32 devices in a mesh: seq: 4 (over y, x), wt: 8 (over z, core).
Axes of the slice: x: 2, y: 2, z: 4, core: 2. Of those that a mesh axis runs over, the one named last changes fastest.
Arguments:
- tokens: bfloat16 [24576, 768], P(('wt', 'seq')), may hold values from -6 to 6
- output_cotangent: bfloat16 [24576, 768], P(('wt', 'seq')), may hold values from -6 to 6
- attention_weight: bfloat16 [768, 2304], P('wt'), may hold values from -0.21875 to 0.21875
- query_bias: bfloat16 [768], replicated, may hold values from -3 to 3
- value_bias: bfloat16 [768], replicated, may hold values from -3 to 3
- output_weight: bfloat16 [768, 768], P('wt'), may hold values from -6 to 6
- output_bias: bfloat16 [768], replicated, may hold values from -3 to 3
- first_gain: bfloat16 [768], replicated, may hold values from 0.5 to 1.5
- first_shift: bfloat16 [768], replicated, may hold values from -3 to 3
- expand_weight: bfloat16 [768, 3072], P('wt'), may hold values from -0.21875 to 0.21875
- expand_bias: bfloat16 [3072], replicated, may hold values from -3 to 3
- contract_weight: bfloat16 [3072, 768], P('wt'), may hold values from -0.109375 to 0.109375
- contract_bias: bfloat16 [768], replicated, may hold values from -3 to 3
- second_gain: bfloat16 [768], replicated, may hold values from 0.5 to 1.5
- second_shift: bfloat16 [768], replicated, may hold values from -3 to 3
- head_gate: float32 [12], replicated, may hold values from 0.5 to 1.5
- hidden_gate: float32 [768], replicated, may hold values from 0.5 to 1.5
- unit_gate: float32 [3072], replicated, may hold values from 0.5 to 1.5
- head_mask: int32 [12], replicated, may hold values 0 or 1
- hidden_mask: int32 [768], replicated, may hold values 0 or 1
- unit_mask: int32 [3072], replicated, may hold values 0 or 1
- attention_mask: int32 [8], replicated, may hold values 0 or 1
- feedforward_mask: int32 [8], replicated, may hold values 0 or 1
- continuation_lengths: int32 [8, 2], replicated, may hold values from 512 to 1536, as said below
Outputs:
- layer_output: bfloat16 [24576, 768], P(('wt', 'seq'))
- tokens_grad: float32 [24576, 768], P(('wt', 'seq'))
- attention_weight_grad: float32 [768, 2304], P('wt')
- query_bias_grad: float32 [768], P('wt')
- value_bias_grad: float32 [768], P('wt')
- output_weight_grad: float32 [768, 768], P('wt')
- output_bias_grad: float32 [768], P('wt')
- first_gain_grad: float32 [768], P('wt')
- first_shift_grad: float32 [768], P('wt')
- expand_weight_grad: float32 [768, 3072], P('wt')
- expand_bias_grad: float32 [3072], P('wt')
- contract_weight_grad: float32 [3072, 768], P('wt')
- contract_bias_grad: float32 [768], P('wt')
- second_gain_grad: float32 [768], P('wt')
- second_shift_grad: float32 [768], P('wt')
- head_gate_grad: float32 [12], replicated
- hidden_gate_grad: float32 [768], P('wt')
- unit_gate_grad: float32 [3072], P('wt')
The draws below stay inside these ranges and needn't reach their ends.
Inputs may be any that keep to these rules, and one draw needn't show every extreme that they name: `continuation_lengths`: row g lists the lengths of group g's 2 continuations; in every row one continuation, at a place drawn from the seed, has exactly 1536 tokens, and the others share the remaining 2 * 1024 - 1536 tokens evenly, any remainder on the last of them.
All inputs are finite; a program needn't handle non-finite values.
Results may differ from the reference program's by a relative error of at most 0.018.
Values may be sent and summed in bfloat16 or wider, within the bound.
A program may use at most 192 MiB of HBM per device.

```python
import jax
import jax.numpy as jnp
from jax import lax

D = 768
H = 12
HD = 64
FF = 3072
PROMPT = 1024
CONT = 1024
NCONT = 2
GLEN = 3072
CMOST = 1536
GROUPS = 8
TOKENS = 24576


def draw_continuation_lengths(key, part):
    longest_place = jax.random.randint(jax.random.fold_in(key, 11), (GROUPS,), 0, NCONT, dtype=jnp.int32)
    remaining = NCONT * CONT - CMOST
    others = NCONT - 1
    share = remaining // others
    extra = remaining - share * others
    column = jnp.arange(NCONT, dtype=jnp.int32)[None, :]
    place = longest_place[:, None]
    rest_index = jnp.where(column > place, column - 1, column)
    rest_value = share + jnp.where(rest_index == others - 1, extra, 0)
    return jnp.where(column == place, CMOST, rest_value).astype(jnp.int32)


def touch_ends(drawn, stream_key, least, largest):
    extent = drawn.shape
    spot = [jax.random.randint(jax.random.fold_in(stream_key, axis), (), 0, extent[axis]) for axis in range(len(extent))]
    drawn = drawn.at[tuple(spot)].set(least)
    longest = extent.index(max(extent))
    spot[longest] = (spot[longest] + 1) % extent[longest]
    return drawn.at[tuple(spot)].set(largest)


def strengthened(values, key, source, target, blocks, factor):
    def block_of(axis_at):
        return (jnp.arange(values.shape[axis_at]) // (values.shape[axis_at] // blocks)).reshape((-1,) + (1,) * (values.ndim - 1 - axis_at))

    near = jax.random.permutation(key, blocks)[block_of(target)]
    second = (block_of(target) + blocks // 2) % blocks
    return jnp.where((block_of(source) == near) | (block_of(source) == second), factor * values, values)


def level_of(rng, shape, cuts, least, high):
    loudness = 1.0
    for dim, parts in cuts:
        draws = jax.random.uniform(jax.random.fold_in(jax.random.fold_in(rng, 6), dim), (parts,), jnp.float32, least / len(cuts), high / len(cuts))
        loudness = loudness * jnp.repeat(jnp.exp(draws), shape[dim] // parts).reshape((-1,) + (1,) * (len(shape) - 1 - dim))
    return loudness


def normal_values(rng, dims, spread, most, cuts=(), kind=jnp.bfloat16):
    loudness = level_of(rng, dims, cuts, -0.22, 0.18) if cuts else 1.0
    values = jax.random.normal(rng, dims, jnp.float32) * spread * loudness
    return jnp.minimum(jnp.maximum(values, -most), most).astype(kind)


def heavy_noise(stream_key, shape, spread, most, pieces, heavy, held_as=jnp.bfloat16):
    entries = spread * jax.random.normal(stream_key, shape, jnp.float32)
    if pieces:
        entries = entries * level_of(stream_key, shape, pieces, -0.22, 0.18)
    return jnp.clip(strengthened(entries, jax.random.fold_in(stream_key, 3), *heavy), -most, most).astype(held_as)


def setup_inputs(seed: int = 0) -> dict:
    keys = jax.random.split(jax.random.key(seed), 25)
    tokens = heavy_noise(keys[0], (TOKENS, D), 1.0, 6.0, ((0, 32),), (0, 1, 32, 2.75))
    output_cotangent = normal_values(keys[1], (TOKENS, D), 1.0, 6.0, ((0, 32),))
    attention_weight = normal_values(keys[2], (D, 3 * D), D ** -0.5, 0.21875, ((0, 8),))
    query_bias = normal_values(keys[3], (D,), 0.5, 3.0)
    value_bias = normal_values(keys[4], (D,), 0.5, 3.0)
    output_weight = normal_values(keys[5], (D, D), (max(1, 4 * D // GLEN)) ** -0.5, 6.0, ((0, 8),))
    output_bias = normal_values(keys[6], (D,), 0.5, 3.0)
    first_gain = jnp.clip(1.0 + 0.1 * jax.random.normal(keys[7], (D,), jnp.float32), 0.5, 1.5).astype(jnp.bfloat16)
    first_shift = normal_values(keys[8], (D,), 0.5, 3.0)
    expand_weight = normal_values(keys[9], (D, FF), D ** -0.5, 0.21875, ((0, 8),))
    expand_bias = normal_values(keys[10], (FF,), 0.5, 3.0)
    contract_weight = normal_values(keys[11], (FF, D), FF ** -0.5, 0.109375, ((0, 8),))
    contract_bias = normal_values(keys[12], (D,), 0.5, 3.0)
    second_gain = jnp.clip(1.0 + 0.1 * jax.random.normal(keys[13], (D,), jnp.float32), 0.5, 1.5).astype(jnp.bfloat16)
    second_shift = normal_values(keys[14], (D,), 0.5, 3.0)
    head_gate = jnp.clip(jax.random.uniform(keys[15], (H,), jnp.float32, 0.5, 1.5), 0.5, 1.5)
    hidden_gate = jnp.clip(jax.random.uniform(keys[16], (D,), jnp.float32, 0.5, 1.5), 0.5, 1.5)
    unit_gate = jnp.clip(jax.random.uniform(keys[17], (FF,), jnp.float32, 0.5, 1.5), 0.5, 1.5)
    head_mask = touch_ends((jax.random.randint(keys[18], (H,), 0, 4) < 3).astype(jnp.int32), jax.random.fold_in(keys[18], 1), 0, 1)
    hidden_mask = touch_ends((jax.random.randint(keys[19], (D,), 0, 8) < 7).astype(jnp.int32), jax.random.fold_in(keys[19], 1), 0, 1)
    unit_mask = touch_ends((jax.random.randint(keys[20], (FF,), 0, 4) < 3).astype(jnp.int32), jax.random.fold_in(keys[20], 1), 0, 1)
    attention_mask = touch_ends((jax.random.randint(keys[21], (GROUPS,), 0, 4) < 3).astype(jnp.int32), jax.random.fold_in(keys[21], 1), 0, 1)
    feedforward_mask = touch_ends((jax.random.randint(keys[22], (GROUPS,), 0, 4) < 3).astype(jnp.int32), jax.random.fold_in(keys[22], 1), 0, 1)
    continuation_lengths = draw_continuation_lengths(jax.random.fold_in(keys[24], 71), 0)
    return dict(tokens=tokens, output_cotangent=output_cotangent, attention_weight=attention_weight, query_bias=query_bias, value_bias=value_bias, output_weight=output_weight, output_bias=output_bias, first_gain=first_gain, first_shift=first_shift, expand_weight=expand_weight, expand_bias=expand_bias, contract_weight=contract_weight, contract_bias=contract_bias, second_gain=second_gain, second_shift=second_shift, head_gate=head_gate, hidden_gate=hidden_gate, unit_gate=unit_gate, head_mask=head_mask, hidden_mask=hidden_mask, unit_mask=unit_mask, attention_mask=attention_mask, feedforward_mask=feedforward_mask, continuation_lengths=continuation_lengths)


epsilon = 1e-06
score_scale = 0.125

@jax.custom_vjp
def low(v):
    return lax.optimization_barrier(v.astype(jnp.bfloat16)).astype(jnp.float32)

@jax.custom_vjp
def low_back(v):
    return v

def low_keep(v):
    return (low(v), None)

def low_pass(kept, grad):
    return (grad,)

def back_keep(v):
    return (v, None)

def back_low(kept, grad):
    return (low(grad),)
low.defvjp(low_keep, low_pass)
low_back.defvjp(back_keep, back_low)

def product(left, right):
    return jnp.dot(left, right, precision=lax.Precision.HIGHEST, preferred_element_type=jnp.float32)

def layer_norm(summed, gain_vec, shift_vec):
    centre = summed - lax.optimization_barrier(jnp.mean(summed, axis=-1, keepdims=True))
    inverse = lax.rsqrt(lax.optimization_barrier(jnp.mean(centre * centre, axis=-1, keepdims=True)) + epsilon)
    return centre * inverse * gain_vec + shift_vec

def segment_ids(lengths_row):
    position = jnp.arange(GLEN, dtype=jnp.int32)
    seg_ends = PROMPT + jnp.cumsum(lengths_row, dtype=jnp.int32)
    counted = lax.optimization_barrier(jnp.sum((position[:, None] >= seg_ends[None, :-1]).astype(jnp.int32), axis=1))
    return jnp.where(position < PROMPT, 0, 1 + counted).astype(jnp.int32)

def group_attention(packed, segments):
    queries = packed[:, :, 0, :]
    keys_all = packed[:, :, 1, :]
    values = packed[:, :, 2, :]
    block_rows = min(512, GLEN)

    def one_block(offset):
        query_rows = lax.dynamic_slice_in_dim(queries, offset, block_rows, 0)
        query_segments = lax.dynamic_slice_in_dim(segments, offset, block_rows, 0)
        scores = low_back(jnp.einsum('qhd,khd->hqk', query_rows, keys_all, precision=lax.Precision.HIGHEST) * score_scale)
        allowed = (segments[None, :] == query_segments[:, None]) | (segments[None, :] == 0)
        scores = jnp.where(allowed[None, :, :], scores, -jnp.inf)
        row_max = lax.optimization_barrier(jnp.max(scores, axis=-1, keepdims=True))
        weights = jnp.exp(scores - row_max)
        attn_probs = low(weights / lax.optimization_barrier(jnp.sum(weights, axis=-1, keepdims=True)))
        return jnp.einsum('hqk,khd->qhd', attn_probs, values, precision=lax.Precision.HIGHEST)
    offsets = jnp.arange(GLEN // block_rows, dtype=jnp.int32) * block_rows
    mixed_rows = lax.map(jax.checkpoint(one_block), offsets)
    return mixed_rows.reshape(GLEN, H, HD)

def group_step(group_item):
    return group_attention(group_item[0], group_item[1])

def forward(inputs_float, integers):
    tokens, attention_weight, query_bias, value_bias, output_weight, output_bias, first_gain, first_shift, expand_weight, expand_bias, contract_weight, contract_bias, second_gain, second_shift, head_gate, hidden_gate, unit_gate = inputs_float
    head_mask, hidden_mask, unit_mask, attention_mask, feedforward_mask, continuation_lengths = integers
    group_of = jnp.arange(TOKENS, dtype=jnp.int32) // GLEN
    attention_rows = attention_mask.astype(jnp.float32)[group_of]
    feedforward_rows = feedforward_mask.astype(jnp.float32)[group_of]
    head_scale = head_mask.astype(jnp.float32) * head_gate
    hidden_scale = hidden_mask.astype(jnp.float32) * hidden_gate
    unit_scale = unit_mask.astype(jnp.float32) * unit_gate
    bias_table = jnp.stack([query_bias.reshape(H, HD), jnp.zeros((H, HD), jnp.float32), value_bias.reshape(H, HD)], axis=1)
    projected = low_back(product(tokens, attention_weight).reshape(TOKENS, H, 3, HD) + bias_table)
    value_scale = head_scale[None, :] * attention_rows[:, None]
    constant_rows = jnp.ones_like(value_scale)
    factor = jnp.stack([constant_rows, constant_rows, value_scale], axis=2)[..., None]
    packed = low_back(low(projected * factor))
    segments = jax.vmap(segment_ids)(continuation_lengths)
    context = lax.map(jax.checkpoint(group_step), (packed.reshape(GROUPS, GLEN, H, 3, HD), segments))
    context = low_back(low(context.reshape(TOKENS, D)))
    attn_out = low_back(product(context, output_weight) + output_bias)
    first_out = layer_norm(tokens + attn_out, first_gain, first_shift) * hidden_scale
    hidden = low_back(product(low(first_out), expand_weight) + expand_bias)
    activated = low(jax.nn.gelu(hidden, approximate=False) * unit_scale[None, :] * feedforward_rows[:, None])
    branch = low_back(product(activated, contract_weight) + contract_bias)
    return layer_norm(first_out + branch, second_gain, second_shift) * hidden_scale

def reference(tokens, output_cotangent, attention_weight, query_bias, value_bias, output_weight, output_bias, first_gain, first_shift, expand_weight, expand_bias, contract_weight, contract_bias, second_gain, second_shift, head_gate, hidden_gate, unit_gate, head_mask, hidden_mask, unit_mask, attention_mask, feedforward_mask, continuation_lengths):
    inputs_float = tuple((array.astype(jnp.float32) for array in (tokens, attention_weight, query_bias, value_bias, output_weight, output_bias, first_gain, first_shift, expand_weight, expand_bias, contract_weight, contract_bias, second_gain, second_shift, head_gate, hidden_gate, unit_gate)))
    integers = (head_mask, hidden_mask, unit_mask, attention_mask, feedforward_mask, continuation_lengths)

    def layer_call(*arrays):
        return forward(arrays, integers)
    result, pullback = jax.vjp(layer_call, *inputs_float)
    gradients = pullback(output_cotangent.astype(jnp.float32))
    return (result.astype(jnp.bfloat16), gradients[0], gradients[1], gradients[2], gradients[3], gradients[4], gradients[5], gradients[6], gradients[7], gradients[8], gradients[9], gradients[10], gradients[11], gradients[12], gradients[13], gradients[14], gradients[15], gradients[16])
```

```python
import functools

import jax
import jax.numpy as jnp
from jax import lax
from jax.experimental import pallas as pl
from jax.experimental.pallas import tpu as pltpu
from jax.sharding import PartitionSpec as P

PROMPT = 1024
GRP_WT = 1
GLEN = 3072
SHORT = 512
LONG = 1536
HD = 64
TQ = 512
KC = 512

epsilon = 1e-06
score_scale = 0.125
exp2_scale = 0.125 * 1.4426950408889634
root_half = 0.7071067811865476
density_scale = 0.3989422804014327
bf16 = jnp.bfloat16
f32 = jnp.float32

NT = (((1,), (1,)), ((), ()))
NN = (((1,), (0,)), ((), ()))


def mm(a, b, dims=NN):
    return lax.dot_general(a, b, dims, preferred_element_type=f32)


def query_tiles(short_first, tile):
    short_at = pl.multiple_of(jnp.where(short_first, PROMPT, PROMPT + LONG), SHORT)
    long_at = pl.multiple_of(jnp.where(short_first, PROMPT + SHORT, PROMPT), SHORT)
    for base, own_at, own_len, rows in (
        (0, 0, 0, PROMPT),
        (short_at, short_at, SHORT, SHORT),
        (long_at, long_at, LONG, LONG),
    ):

        def step(i, carry, base=base, own_at=own_at, own_len=own_len):
            tile(pl.multiple_of(base + i * TQ, TQ), own_at, own_len)
            return carry

        lax.fori_loop(0, rows // TQ, step, 0)


def attend_kernel(
    heads, lens_ref, tok_ref, w_ref, vec_ref, packed_ref, ctx_ref, lse_ref, q_sc, k_sc, vt_sc, ot_sc
):
    def project(i, carry):
        rows = pl.ds(pl.multiple_of(i * TQ, TQ), TQ)
        x = mm(tok_ref[rows, :], w_ref[...]) + vec_ref[0:1, :]
        x = (x * vec_ref[1:2, :]).astype(bf16)
        packed_ref[rows, :] = x
        for h in range(heads):
            at = 3 * HD * h
            q_sc[h, rows, :] = x[:, at : at + HD]
            k_sc[h, rows, :] = x[:, at + HD : at + 2 * HD]
            vt_sc[h, 0:HD, rows] = x[:, at + 2 * HD : at + 3 * HD].T
        return carry

    lax.fori_loop(0, GLEN // TQ, project, 0)
    for h in range(heads):
        vt_sc[h, HD : HD + 16, :] = jnp.ones((16, GLEN), bf16)

    def one_head(h, carry):
        def tile(q_at, own_at, own_len):
            rows = pl.ds(q_at, TQ)
            q = q_sc[h, rows, :]
            s1 = mm(k_sc[h, 0:PROMPT, :], q, NT)
            top = jnp.max(s1, axis=0, keepdims=True)
            if own_len:
                own = pl.ds(own_at, own_len)
                s2 = mm(k_sc[h, own, :], q, NT)
                top = jnp.maximum(top, jnp.max(s2, axis=0, keepdims=True))
            top = top * exp2_scale
            p1 = jnp.exp2(s1 * exp2_scale - top)
            o = mm(vt_sc[h, :, 0:PROMPT], p1.astype(bf16))
            total = jnp.sum(p1, axis=0, keepdims=True)
            if own_len:
                p2 = jnp.exp2(s2 * exp2_scale - top)
                o = o + mm(vt_sc[h, :, own], p2.astype(bf16))
                total = total + jnp.sum(p2, axis=0, keepdims=True)
            ot_sc[h, :, rows] = o[0:HD, :] / total
            lse_ref[h, :, rows] = top + jnp.log2(total)

        query_tiles(lens_ref[0] == SHORT, tile)
        return carry

    lax.fori_loop(0, heads, one_head, 0)

    def place(i, carry):
        rows = pl.ds(pl.multiple_of(i * TQ, TQ), TQ)
        for h in range(heads):
            ctx_ref[rows, HD * h : HD * (h + 1)] = ot_sc[h, :, rows].T.astype(bf16)
        return carry

    lax.fori_loop(0, GLEN // TQ, place, 0)


def attend(lens, tokens_all, weight, vec, heads):
    width = 3 * HD * heads
    whole = pl.BlockSpec(memory_space=pltpu.VMEM)
    return pl.pallas_call(
        functools.partial(attend_kernel, heads),
        out_shape=(
            jax.ShapeDtypeStruct((GLEN, width), bf16),
            jax.ShapeDtypeStruct((GLEN, HD * heads), bf16),
            jax.ShapeDtypeStruct((heads, 1, GLEN), f32),
        ),
        in_specs=[pl.BlockSpec(memory_space=pltpu.SMEM), whole, whole, whole],
        out_specs=(whole, whole, whole),
        scratch_shapes=[
            pltpu.VMEM((heads, GLEN, HD), bf16),
            pltpu.VMEM((heads, GLEN, HD), bf16),
            pltpu.VMEM((heads, HD + 16, GLEN), bf16),
            pltpu.VMEM((heads, HD, GLEN), f32),
        ],
        compiler_params=pltpu.CompilerParams(vmem_limit_bytes=56 * 2**20),
        cost_estimate=pl.CostEstimate(
            flops=2 * GLEN * 768 * width + heads * 4 * 256 * 5767168,
            bytes_accessed=2 * GLEN * (768 + width),
            transcendentals=heads * 5767168,
        ),
        name="attend",
    )(lens, tokens_all, weight, vec)


def attend_back_kernel(
    heads, lens_ref, packed_ref, ctx_ref, gctx_ref, lse_ref, scale_ref,
    out_ref, sums_ref, gate_ref,
    q_sc, k_sc, v_sc, kt_sc, g_sc, delta_sc, dqt_sc, dk_sc, dv_sc,
):
    def split(i, carry):
        rows = pl.ds(pl.multiple_of(i * TQ, TQ), TQ)
        x = packed_ref[rows, :]
        g = gctx_ref[rows, :]
        inner = (g.astype(f32) * ctx_ref[rows, :].astype(f32)).T
        for h in range(heads):
            at = 3 * HD * h
            q_sc[h, rows, :] = x[:, at : at + HD]
            k = x[:, at + HD : at + 2 * HD]
            k_sc[h, rows, :] = k
            kt_sc[h, :, rows] = k.T
            v_sc[h, rows, :] = x[:, at + 2 * HD : at + 3 * HD]
            g_sc[h, rows, :] = g[:, HD * h : HD * (h + 1)]
            delta_sc[h, :, rows] = jnp.sum(inner[HD * h : HD * (h + 1), :], axis=0, keepdims=True)
        return carry

    lax.fori_loop(0, GLEN // TQ, split, 0)
    dk_sc[...] = jnp.zeros_like(dk_sc)
    dv_sc[...] = jnp.zeros_like(dv_sc)

    def one_head(h, carry):
        def tile(q_at, own_at, own_len):
            rows = pl.ds(q_at, TQ)
            q = q_sc[h, rows, :]
            g = g_sc[h, rows, :]
            lse = lse_ref[h, :, rows]
            delta = delta_sc[h, :, rows]
            dq = jnp.zeros((HD, TQ), f32)
            pieces = [(j * KC, PROMPT // KC) for j in range(PROMPT // KC)]
            pieces = [c for c, _ in pieces] + [own_at + j * KC for j in range(own_len // KC)]
            for start in pieces:
                keys = pl.ds(start, KC)
                s = mm(k_sc[h, keys, :], q, NT)
                p = jnp.exp2(s * exp2_scale - lse)
                dp = mm(v_sc[h, keys, :], g, NT)
                ds = (p * (dp - delta)).astype(bf16)
                dv_sc[h, keys, :] += mm(p.astype(bf16), g)
                dk_sc[h, keys, :] += mm(ds, q)
                dq = dq + mm(kt_sc[h, :, keys], ds)
            dqt_sc[h, :, rows] = dq * score_scale

        query_tiles(lens_ref[0] == SHORT, tile)
        return carry

    lax.fori_loop(0, heads, one_head, 0)
    sums_ref[...] = jnp.zeros_like(sums_ref)
    gate_ref[...] = jnp.zeros_like(gate_ref)

    def place(i, carry):
        rows = pl.ds(pl.multiple_of(i * TQ, TQ), TQ)
        for h in range(heads):
            at = 3 * HD * h
            dq = dqt_sc[h, :, rows].T.astype(bf16)
            dk = (dk_sc[h, rows, :] * score_scale).astype(bf16)
            dv = dv_sc[h, rows, :].astype(bf16).astype(f32)
            gate_ref[0:1, HD * h : HD * (h + 1)] += jnp.sum(
                dv * v_sc[h, rows, :].astype(f32), axis=0, keepdims=True
            )
            dv = (dv * scale_ref[:, at + 2 * HD : at + 3 * HD]).astype(bf16)
            out_ref[rows, at : at + HD] = dq
            out_ref[rows, at + HD : at + 2 * HD] = dk
            out_ref[rows, at + 2 * HD : at + 3 * HD] = dv
            sums_ref[0:1, at : at + HD] += jnp.sum(dq.astype(f32), axis=0, keepdims=True)
            sums_ref[0:1, at + 2 * HD : at + 3 * HD] += jnp.sum(
                dv.astype(f32), axis=0, keepdims=True
            )
        return carry

    lax.fori_loop(0, GLEN // TQ, place, 0)


def attend_back(lens, packed, ctx, gctx, lse, scale, heads):
    width = 3 * HD * heads
    whole = pl.BlockSpec(memory_space=pltpu.VMEM)
    rows64 = pltpu.VMEM((heads, GLEN, HD), bf16)
    rows64f = pltpu.VMEM((heads, GLEN, HD), f32)
    return pl.pallas_call(
        functools.partial(attend_back_kernel, heads),
        out_shape=(
            jax.ShapeDtypeStruct((GLEN, width), bf16),
            jax.ShapeDtypeStruct((8, width), f32),
            jax.ShapeDtypeStruct((8, HD * heads), f32),
        ),
        in_specs=[pl.BlockSpec(memory_space=pltpu.SMEM)] + [whole] * 5,
        out_specs=(whole, whole, whole),
        scratch_shapes=[
            rows64,
            rows64,
            rows64,
            pltpu.VMEM((heads, HD, GLEN), bf16),
            rows64,
            pltpu.VMEM((heads, 1, GLEN), f32),
            pltpu.VMEM((heads, HD, GLEN), f32),
            rows64f,
            rows64f,
        ],
        compiler_params=pltpu.CompilerParams(vmem_limit_bytes=56 * 2**20),
        cost_estimate=pl.CostEstimate(
            flops=heads * 10 * 256 * 5767168,
            bytes_accessed=2 * GLEN * (3 * width),
            transcendentals=heads * 5767168,
        ),
        name="attend_back",
    )(lens, packed, ctx, gctx, lse, scale)


def norm_parts(summed):
    centre = summed - jnp.mean(summed, axis=-1, keepdims=True)
    inverse = lax.rsqrt(jnp.mean(centre * centre, axis=-1, keepdims=True) + epsilon)
    return (centre * inverse, inverse)


def norm_back(grad_normed, normed, inverse):
    return inverse * (
        grad_normed
        - jnp.mean(grad_normed, axis=-1, keepdims=True)
        - normed * jnp.mean(grad_normed * normed, axis=-1, keepdims=True)
    )


def local(
    tokens,
    output_cotangent,
    attention_weight,
    query_bias,
    value_bias,
    output_weight,
    output_bias,
    first_gain,
    first_shift,
    expand_weight,
    expand_bias,
    contract_weight,
    contract_bias,
    second_gain,
    second_shift,
    head_gate,
    hidden_gate,
    unit_gate,
    head_mask,
    hidden_mask,
    unit_mask,
    attention_mask,
    feedforward_mask,
    continuation_lengths,
):
    row_count = tokens.shape[0]
    seq_count = lax.axis_size("seq")
    head_count = head_gate.shape[0]
    model_width = hidden_gate.shape[0]
    head_size = model_width // head_count
    local_heads = head_count // seq_count
    seq_index = lax.axis_index("seq")
    wt_index = lax.axis_index("wt")
    local_width = 3 * head_size * local_heads
    tokens_all = lax.all_gather(tokens, "seq", axis=0, tiled=True)
    own_columns = lax.dynamic_slice_in_dim(attention_weight, seq_index * local_width, local_width, 1)
    own_weight = lax.all_gather(own_columns, "wt", axis=0, tiled=True)
    full_output, full_expand, full_contract, full_attention = (
        lax.all_gather(output_weight, "wt", axis=0, tiled=True),
        lax.all_gather(expand_weight, "wt", axis=0, tiled=True),
        lax.all_gather(contract_weight, "wt", axis=0, tiled=True),
        lax.all_gather(attention_weight, "wt", axis=0, tiled=True),
    )
    position = seq_index * row_count + jnp.arange(row_count, dtype=jnp.int32)
    group_local = position // GLEN
    own_groups = jnp.arange(GRP_WT, dtype=jnp.int32)
    chosen = group_local[:, None] == own_groups[None, :]
    first_group = wt_index * GRP_WT
    own_attention = lax.dynamic_slice_in_dim(attention_mask, first_group, GRP_WT, 0).astype(
        jnp.float32
    )
    own_feedforward = lax.dynamic_slice_in_dim(feedforward_mask, first_group, GRP_WT, 0).astype(
        jnp.float32
    )
    attention_rows = jnp.sum(jnp.where(chosen, own_attention[None, :], 0.0), axis=1)
    feedforward_rows = jnp.sum(jnp.where(chosen, own_feedforward[None, :], 0.0), axis=1)
    head_scale = head_mask.astype(jnp.float32) * head_gate
    hidden_scale = hidden_mask.astype(jnp.float32) * hidden_gate
    unit_scale = unit_mask.astype(jnp.float32) * unit_gate
    first_gain_f = first_gain.astype(jnp.float32)
    second_gain_f = second_gain.astype(jnp.float32)
    bias_table = jnp.stack(
        [
            query_bias.astype(jnp.float32).reshape(head_count, head_size),
            jnp.zeros((head_count, head_size), jnp.float32),
            value_bias.astype(jnp.float32).reshape(head_count, head_size),
        ],
        axis=1,
    )
    own_scale = lax.dynamic_slice_in_dim(head_scale, seq_index * local_heads, local_heads, 0)
    own_scale = own_scale * own_attention[0]
    own_mask = lax.dynamic_slice_in_dim(head_mask, seq_index * local_heads, local_heads, 0)
    own_gate = lax.dynamic_slice_in_dim(head_gate, seq_index * local_heads, local_heads, 0)
    own_bias = lax.dynamic_slice_in_dim(bias_table, seq_index * local_heads, local_heads, 0)
    constant = jnp.ones((local_heads, head_size), jnp.float32)
    factor = jnp.stack([constant, constant, constant * own_scale[:, None]], axis=1)
    vec = jnp.stack([own_bias.reshape(local_width), factor.reshape(local_width)], axis=0)
    lens = lax.dynamic_slice_in_dim(continuation_lengths, first_group, GRP_WT, 0)[0]
    packed, mixed_heads, log_sums = attend(lens, tokens_all, own_weight, vec, local_heads)
    context = lax.all_to_all(
        mixed_heads.reshape(GLEN, 1, local_heads * head_size), "seq", split_axis=0, concat_axis=1, tiled=True
    ).reshape(row_count, model_width)
    attn_out = jnp.dot(
        context, full_output, preferred_element_type=jnp.float32
    ) + output_bias.astype(jnp.float32)
    normed_one, inverse_one = norm_parts(tokens.astype(jnp.float32) + attn_out)
    shaped_one = normed_one * first_gain_f + first_shift.astype(jnp.float32)
    first_out = shaped_one * hidden_scale
    first_low = first_out.astype(jnp.bfloat16)
    hidden = jnp.dot(
        first_low, full_expand, preferred_element_type=jnp.float32
    ) + expand_bias.astype(jnp.float32)
    gelu_out = jax.nn.gelu(hidden, approximate=False)
    unit_rows_scale = unit_scale[None, :] * feedforward_rows[:, None]
    activated = (gelu_out * unit_rows_scale).astype(jnp.bfloat16)
    branch = jnp.dot(
        activated, full_contract, preferred_element_type=jnp.float32
    ) + contract_bias.astype(jnp.float32)
    normed_two, inverse_two = norm_parts(first_out + branch)
    shaped_two = normed_two * second_gain_f + second_shift.astype(jnp.float32)
    layer_output = (shaped_two * hidden_scale).astype(jnp.bfloat16)
    back_attention, back_output, back_expand, back_contract = (
        full_attention,
        full_output,
        full_expand,
        full_contract,
    )
    cotangent = output_cotangent.astype(jnp.float32)
    grad_shaped_two = cotangent * hidden_scale
    second_gain_grad = jnp.sum(grad_shaped_two * normed_two, axis=0)
    second_shift_grad = jnp.sum(grad_shaped_two, axis=0)
    grad_total_two = norm_back(grad_shaped_two * second_gain_f, normed_two, inverse_two)
    grad_branch = grad_total_two.astype(jnp.bfloat16)
    contract_bias_grad = jnp.sum(grad_branch.astype(jnp.float32), axis=0)
    contract_weight_grad = jnp.einsum(
        "ti,td->id", activated, grad_branch, preferred_element_type=jnp.float32
    )
    grad_activated = jnp.einsum(
        "td,id->ti", grad_branch, back_contract, preferred_element_type=jnp.float32
    )
    unit_gate_grad = unit_mask.astype(jnp.float32) * jnp.sum(
        grad_activated * gelu_out * feedforward_rows[:, None], axis=0
    )
    cumulative = 0.5 * (1.0 + lax.erf(hidden * root_half))
    gelu_slope = cumulative + hidden * jnp.exp(-0.5 * hidden * hidden) * density_scale
    grad_hidden = (grad_activated * unit_rows_scale * gelu_slope).astype(jnp.bfloat16)
    expand_bias_grad = jnp.sum(grad_hidden.astype(jnp.float32), axis=0)
    expand_weight_grad = jnp.einsum(
        "td,tf->df", first_low, grad_hidden, preferred_element_type=jnp.float32
    )
    grad_first = grad_total_two + jnp.einsum(
        "tf,df->td", grad_hidden, back_expand, preferred_element_type=jnp.float32
    )
    grad_shaped_one = grad_first * hidden_scale
    first_gain_grad = jnp.sum(grad_shaped_one * normed_one, axis=0)
    first_shift_grad = jnp.sum(grad_shaped_one, axis=0)
    hidden_gate_grad = hidden_mask.astype(jnp.float32) * jnp.sum(
        cotangent * shaped_two + grad_first * shaped_one, axis=0
    )
    grad_total_one = norm_back(grad_shaped_one * first_gain_f, normed_one, inverse_one)
    grad_attn = grad_total_one.astype(jnp.bfloat16)
    output_bias_grad = jnp.sum(grad_attn.astype(jnp.float32), axis=0)
    output_weight_grad = jnp.einsum(
        "ti,td->id", context, grad_attn, preferred_element_type=jnp.float32
    )
    grad_context = jnp.einsum(
        "td,id->ti", grad_attn, back_output, preferred_element_type=jnp.float32
    ).astype(jnp.bfloat16)
    arriving = lax.all_to_all(
        grad_context.reshape(row_count, seq_count, local_heads * head_size),
        "seq",
        split_axis=1,
        concat_axis=0,
        tiled=True,
    )
    grad_packed, sums, gate_sums = attend_back(
        lens,
        packed,
        mixed_heads,
        arriving.reshape(GLEN, local_heads * head_size),
        log_sums,
        vec[1:2],
        local_heads,
    )
    head_own = own_mask.astype(jnp.float32) * own_attention[0] / own_gate
    head_own = head_own * jnp.sum(gate_sums[0].reshape(local_heads, head_size), axis=1)
    head_partial = lax.dynamic_update_slice_in_dim(
        jnp.zeros((head_count,), jnp.float32), head_own, seq_index * local_heads, 0
    )
    sums = sums[0].reshape(local_heads, 3, head_size)
    zeros_wide = jnp.zeros((model_width,), jnp.float32)
    at_own = seq_index * local_heads * head_size
    query_bias_grad = lax.dynamic_update_slice_in_dim(zeros_wide, sums[:, 0].reshape(-1), at_own, 0)
    value_bias_grad = lax.dynamic_update_slice_in_dim(zeros_wide, sums[:, 2].reshape(-1), at_own, 0)
    grad_flat = lax.all_to_all(
        grad_packed.reshape(GLEN, 1, local_width), "seq", split_axis=0, concat_axis=1, tiled=True
    ).reshape(row_count, 3 * model_width)
    attention_weight_grad = jnp.einsum(
        "td,tc->dc", tokens_all, grad_packed, preferred_element_type=jnp.float32
    )
    tokens_grad = grad_total_one + jnp.einsum(
        "tc,dc->td", grad_flat, back_attention, preferred_element_type=jnp.float32
    )
    head_gate_grad = lax.psum(head_partial, ("seq", "wt"))
    width_vectors = jnp.stack(
        [
            query_bias_grad,
            value_bias_grad,
            output_bias_grad,
            first_gain_grad,
            first_shift_grad,
            contract_bias_grad,
            second_gain_grad,
            second_shift_grad,
            hidden_gate_grad,
        ],
        axis=1,
    )
    unit_vectors = jnp.stack([expand_bias_grad, unit_gate_grad], axis=1)
    pieces = (
        lax.psum_scatter(attention_weight_grad.astype(bf16), "wt", scatter_dimension=0, tiled=True),
        lax.psum_scatter(output_weight_grad.astype(bf16), "wt", scatter_dimension=0, tiled=True),
        lax.psum_scatter(expand_weight_grad.astype(bf16), "wt", scatter_dimension=0, tiled=True),
        lax.psum_scatter(contract_weight_grad.astype(bf16), "wt", scatter_dimension=0, tiled=True),
        lax.psum_scatter(width_vectors, "wt", scatter_dimension=0, tiled=True),
        lax.psum_scatter(unit_vectors, "wt", scatter_dimension=0, tiled=True),
    )
    shards = (
        lax.all_gather(pieces[0], "seq", axis=1, tiled=True).astype(jnp.float32),
        lax.psum(pieces[1], "seq").astype(jnp.float32),
        lax.psum(pieces[2], "seq").astype(jnp.float32),
        lax.psum(pieces[3], "seq").astype(jnp.float32),
        lax.psum(pieces[4], "seq"),
        lax.psum(pieces[5], "seq"),
    )
    width_shard = shards[4]
    unit_shard = shards[5]
    return (
        layer_output,
        tokens_grad,
        shards[0],
        width_shard[:, 0],
        width_shard[:, 1],
        shards[1],
        width_shard[:, 2],
        width_shard[:, 3],
        width_shard[:, 4],
        shards[2],
        unit_shard[:, 0],
        shards[3],
        width_shard[:, 5],
        width_shard[:, 6],
        width_shard[:, 7],
        head_gate_grad,
        width_shard[:, 8],
        unit_shard[:, 1],
    )


def solution(mesh):
    return jax.shard_map(
        local,
        mesh=mesh,
        in_specs=(
            P(("wt", "seq"), None),
            P(("wt", "seq"), None),
            P("wt", None),
            P(),
            P(),
            P("wt", None),
            P(),
            P(),
            P(),
            P("wt", None),
            P(),
            P("wt", None),
            P(),
            P(),
            P(),
            P(),
            P(),
            P(),
            P(),
            P(),
            P(),
            P(),
            P(),
            P(),
        ),
        out_specs=(
            P(("wt", "seq"), None),
            P(("wt", "seq"), None),
            P("wt", None),
            P("wt"),
            P("wt"),
            P("wt", None),
            P("wt"),
            P("wt"),
            P("wt"),
            P("wt", None),
            P("wt"),
            P("wt", None),
            P("wt"),
            P("wt"),
            P("wt"),
            P(),
            P("wt"),
            P("wt"),
        ),
        check_vma=False,
    )
```

```python
import functools

import jax
import jax.numpy as jnp
from jax import lax
from jax.experimental import pallas as pl
from jax.experimental.pallas import tpu as pltpu
from jax.sharding import PartitionSpec as P

PROMPT = 1024
GRP_WT = 1
GLEN = 3072
SHORT = 512
LONG = 1536
HD = 64
TQ = 512
KC = 512

epsilon = 1e-06
score_scale = 0.125
exp2_scale = 0.125 * 1.4426950408889634
root_half = 0.7071067811865476
density_scale = 0.3989422804014327
bf16 = jnp.bfloat16
f32 = jnp.float32

NT = (((1,), (1,)), ((), ()))
NN = (((1,), (0,)), ((), ()))


def mm(a, b, dims=NN):
    return lax.dot_general(a, b, dims, preferred_element_type=f32)


def query_tiles(short_first, tile):
    short_at = pl.multiple_of(jnp.where(short_first, PROMPT, PROMPT + LONG), SHORT)
    long_at = pl.multiple_of(jnp.where(short_first, PROMPT + SHORT, PROMPT), SHORT)
    for base, own_at, own_len, rows in (
        (0, 0, 0, PROMPT),
        (short_at, short_at, SHORT, SHORT),
        (long_at, long_at, LONG, LONG),
    ):

        def step(i, carry, base=base, own_at=own_at, own_len=own_len):
            tile(pl.multiple_of(base + i * TQ, TQ), own_at, own_len)
            return carry

        lax.fori_loop(0, rows // TQ, step, 0)


def attend_kernel(
    heads, lens_ref, tok_ref, w_ref, vec_ref, packed_ref, ctx_ref, lse_ref, q_sc, k_sc, vt_sc
):
    def project(i, carry):
        rows = pl.ds(pl.multiple_of(i * TQ, TQ), TQ)
        x = mm(tok_ref[rows, :], w_ref[...]) + vec_ref[0:1, :]
        x = (x * vec_ref[1:2, :]).astype(bf16)
        packed_ref[rows, :] = x
        for h in range(heads):
            at = 3 * HD * h
            q_sc[h, rows, :] = x[:, at : at + HD]
            k_sc[h, rows, :] = x[:, at + HD : at + 2 * HD]
            vt_sc[h, 0:HD, rows] = x[:, at + 2 * HD : at + 3 * HD].T
        return carry

    lax.fori_loop(0, GLEN // TQ, project, 0)
    for h in range(heads):
        vt_sc[h, HD : HD + 16, :] = jnp.ones((16, GLEN), bf16)

    def one_head(h, carry):
        def tile(q_at, own_at, own_len):
            rows = pl.ds(q_at, TQ)
            q = q_sc[h, rows, :]
            s1 = mm(k_sc[h, 0:PROMPT, :], q, NT)
            top = jnp.max(s1, axis=0, keepdims=True)
            if own_len:
                own = pl.ds(own_at, own_len)
                s2 = mm(k_sc[h, own, :], q, NT)
                top = jnp.maximum(top, jnp.max(s2, axis=0, keepdims=True))
            top = top * exp2_scale
            p1 = jnp.exp2(s1 * exp2_scale - top)
            o = mm(vt_sc[h, :, 0:PROMPT], p1.astype(bf16))
            total = jnp.sum(p1, axis=0, keepdims=True)
            if own_len:
                p2 = jnp.exp2(s2 * exp2_scale - top)
                o = o + mm(vt_sc[h, :, own], p2.astype(bf16))
                total = total + jnp.sum(p2, axis=0, keepdims=True)
            ctx_ref[pl.ds(pl.multiple_of(HD * h, HD), HD), rows] = (o[0:HD, :] / total).astype(bf16)
            lse_ref[h, :, rows] = top + jnp.log2(total)

        query_tiles(lens_ref[0] == SHORT, tile)
        return carry

    lax.fori_loop(0, heads, one_head, 0)


def attend(lens, tokens_all, weight, vec, heads):
    width = 3 * HD * heads
    whole = pl.BlockSpec(memory_space=pltpu.VMEM)
    return pl.pallas_call(
        functools.partial(attend_kernel, heads),
        out_shape=(
            jax.ShapeDtypeStruct((GLEN, width), bf16),
            jax.ShapeDtypeStruct((HD * heads, GLEN), bf16),
            jax.ShapeDtypeStruct((heads, 1, GLEN), f32),
        ),
        in_specs=[pl.BlockSpec(memory_space=pltpu.SMEM), whole, whole, whole],
        out_specs=(whole, whole, whole),
        scratch_shapes=[
            pltpu.VMEM((heads, GLEN, HD), bf16),
            pltpu.VMEM((heads, GLEN, HD), bf16),
            pltpu.VMEM((heads, HD + 16, GLEN), bf16),
        ],
        compiler_params=pltpu.CompilerParams(vmem_limit_bytes=56 * 2**20),
        cost_estimate=pl.CostEstimate(
            flops=2 * GLEN * 768 * width + heads * 4 * 256 * 5767168,
            bytes_accessed=2 * GLEN * (768 + width),
            transcendentals=heads * 5767168,
        ),
        name="attend",
    )(lens, tokens_all, weight, vec)


def attend_back_kernel(
    heads, lens_ref, packed_ref, ctx_ref, gctx_ref, lse_ref, scale_ref,
    out_ref, sums_ref, gate_ref,
    q_sc, k_sc, v_sc, kt_sc, g_sc, delta_sc, dqt_sc, dk_sc, dv_sc,
):
    def split(i, carry):
        rows = pl.ds(pl.multiple_of(i * TQ, TQ), TQ)
        x = packed_ref[rows, :]
        inner = gctx_ref[:, rows].astype(f32) * ctx_ref[:, rows].astype(f32)
        for h in range(heads):
            at = 3 * HD * h
            q_sc[h, rows, :] = x[:, at : at + HD]
            k = x[:, at + HD : at + 2 * HD]
            k_sc[h, rows, :] = k
            kt_sc[h, :, rows] = k.T
            v_sc[h, rows, :] = x[:, at + 2 * HD : at + 3 * HD]
            g_sc[h, :, rows] = gctx_ref[HD * h : HD * (h + 1), rows]
            delta_sc[h, :, rows] = jnp.sum(inner[HD * h : HD * (h + 1), :], axis=0, keepdims=True)
        return carry

    lax.fori_loop(0, GLEN // TQ, split, 0)
    dk_sc[...] = jnp.zeros_like(dk_sc)
    dv_sc[...] = jnp.zeros_like(dv_sc)

    def one_head(h, carry):
        def tile(q_at, own_at, own_len):
            rows = pl.ds(q_at, TQ)
            q = q_sc[h, rows, :]
            g = g_sc[h, :, rows]
            lse = lse_ref[h, :, rows]
            delta = delta_sc[h, :, rows]
            dq = jnp.zeros((HD, TQ), f32)
            pieces = [(j * KC, PROMPT // KC) for j in range(PROMPT // KC)]
            pieces = [c for c, _ in pieces] + [own_at + j * KC for j in range(own_len // KC)]
            for start in pieces:
                keys = pl.ds(start, KC)
                s = mm(k_sc[h, keys, :], q, NT)
                p = jnp.exp2(s * exp2_scale - lse)
                dp = mm(v_sc[h, keys, :], g)
                ds = (p * (dp - delta)).astype(bf16)
                dv_sc[h, keys, :] += mm(p.astype(bf16), g, NT)
                dk_sc[h, keys, :] += mm(ds, q)
                dq = dq + mm(kt_sc[h, :, keys], ds)
            dqt_sc[h, :, rows] = dq * score_scale

        query_tiles(lens_ref[0] == SHORT, tile)
        return carry

    lax.fori_loop(0, heads, one_head, 0)
    sums_ref[...] = jnp.zeros_like(sums_ref)
    gate_ref[...] = jnp.zeros_like(gate_ref)

    def place(i, carry):
        rows = pl.ds(pl.multiple_of(i * TQ, TQ), TQ)
        for h in range(heads):
            at = 3 * HD * h
            dq = dqt_sc[h, :, rows].T.astype(bf16)
            dk = (dk_sc[h, rows, :] * score_scale).astype(bf16)
            dv = dv_sc[h, rows, :].astype(bf16).astype(f32)
            gate_ref[0:1, HD * h : HD * (h + 1)] += jnp.sum(
                dv * v_sc[h, rows, :].astype(f32), axis=0, keepdims=True
            )
            dv = (dv * scale_ref[:, at + 2 * HD : at + 3 * HD]).astype(bf16)
            out_ref[rows, at : at + HD] = dq
            out_ref[rows, at + HD : at + 2 * HD] = dk
            out_ref[rows, at + 2 * HD : at + 3 * HD] = dv
            sums_ref[0:1, at : at + HD] += jnp.sum(dq.astype(f32), axis=0, keepdims=True)
            sums_ref[0:1, at + 2 * HD : at + 3 * HD] += jnp.sum(
                dv.astype(f32), axis=0, keepdims=True
            )
        return carry

    lax.fori_loop(0, GLEN // TQ, place, 0)


def attend_back(lens, packed, ctx, gctx, lse, scale, heads):
    width = 3 * HD * heads
    whole = pl.BlockSpec(memory_space=pltpu.VMEM)
    rows64 = pltpu.VMEM((heads, GLEN, HD), bf16)
    rows64f = pltpu.VMEM((heads, GLEN, HD), f32)
    return pl.pallas_call(
        functools.partial(attend_back_kernel, heads),
        out_shape=(
            jax.ShapeDtypeStruct((GLEN, width), bf16),
            jax.ShapeDtypeStruct((8, width), f32),
            jax.ShapeDtypeStruct((8, HD * heads), f32),
        ),
        in_specs=[pl.BlockSpec(memory_space=pltpu.SMEM)] + [whole] * 5,
        out_specs=(whole, whole, whole),
        scratch_shapes=[
            rows64,
            rows64,
            rows64,
            pltpu.VMEM((heads, HD, GLEN), bf16),
            pltpu.VMEM((heads, HD, GLEN), bf16),
            pltpu.VMEM((heads, 1, GLEN), f32),
            pltpu.VMEM((heads, HD, GLEN), f32),
            rows64f,
            rows64f,
        ],
        compiler_params=pltpu.CompilerParams(vmem_limit_bytes=56 * 2**20),
        cost_estimate=pl.CostEstimate(
            flops=heads * 10 * 256 * 5767168,
            bytes_accessed=2 * GLEN * (3 * width),
            transcendentals=heads * 5767168,
        ),
        name="attend_back",
    )(lens, packed, ctx, gctx, lse, scale)


def send(src, dst, sems, k, peer):
    copy = pltpu.make_async_remote_copy(
        src_ref=src,
        dst_ref=dst,
        send_sem=sems[0].at[k],
        recv_sem=sems[1].at[k],
        device_id=peer,
        device_id_type=pl.DeviceIdType.MESH,
    )
    copy.start()
    return copy


def meet(peers):
    barrier = pltpu.get_barrier_semaphore()
    for peer in peers:
        pl.semaphore_signal(barrier, inc=1, device_id=peer, device_id_type=pl.DeviceIdType.MESH)
    pl.semaphore_wait(barrier, len(peers))


def flip(index, bits):
    for bit in (1, 2):
        if bits & bit:
            index = index + bit - 2 * bit * ((index // bit) % 2)
    return index


def remote_params(number):
    return pltpu.CompilerParams(
        collective_id=number, has_side_effects=True, vmem_limit_bytes=56 * 2**20
    )


ANYWHERE = pl.BlockSpec(memory_space=pl.ANY)
IN_VMEM = pl.BlockSpec(memory_space=pltpu.VMEM)


def dma_sems(count):
    return [pltpu.SemaphoreType.DMA((count,)), pltpu.SemaphoreType.DMA((count,))]


def gather_kernel(
    n, tok_ref, cols_ref, out_ref, tok_all, cols_all, out_all,
    tok_buf, cols_buf, out_buf, local_sem, s_tok, r_tok, s_w, r_w, s_f, r_f,
):
    s, w = lax.axis_index("seq"), lax.axis_index("wt")
    rows = tok_ref.shape[0]
    half = rows // 2
    by_x, by_y, mate = (flip(s, 1), w), (flip(s, 2), w), (s, flip(w, 1))
    far = [(s, lax.rem(w + 2 * j, n)) for j in range(1, n // 2)]
    meet([by_x, by_y, mate] + far)

    def part(owner, k):
        return pl.ds(pl.multiple_of(owner * rows + k * half, half), half)

    tok = (s_tok, r_tok)
    first = [pl.ds(0, half), pl.ds(half, half)]
    x0 = send(tok_ref.at[first[0]], tok_all.at[part(s, 0)], tok, 0, by_x)
    y1 = send(tok_ref.at[first[1]], tok_all.at[part(s, 1)], tok, 1, by_y)
    x1 = send(tok_ref.at[first[1]], tok_all.at[part(s, 1)], tok, 2, by_x)
    y0 = send(tok_ref.at[first[0]], tok_all.at[part(s, 0)], tok, 3, by_y)
    held = []
    for k, peer in enumerate(far + [mate]):
        for i, (src, dst) in enumerate(((cols_ref, cols_all), (out_ref, out_all))):
            held.append(send(src, dst.at[w], (s_w, r_w), 2 * k + i, peer))
    own = []
    for i, (src, buf) in enumerate(((tok_ref, tok_buf), (cols_ref, cols_buf), (out_ref, out_buf))):
        own.append(pltpu.make_async_copy(src, buf, local_sem.at[i]))
        own[-1].start()
    for copy in own:
        copy.wait()
    targets = (
        (tok_buf, tok_all.at[pl.ds(pl.multiple_of(s * rows, rows), rows)]),
        (cols_buf, cols_all.at[w]),
        (out_buf, out_all.at[w]),
    )
    own = []
    for i, (buf, dst) in enumerate(targets):
        own.append(pltpu.make_async_copy(buf, dst, local_sem.at[3 + i]))
        own[-1].start()
    passed = []
    x0.wait_recv()
    there = tok_all.at[part(flip(s, 1), 0)]
    passed.append(send(there, there, tok, 4, by_y))
    y1.wait_recv()
    there = tok_all.at[part(flip(s, 2), 1)]
    passed.append(send(there, there, tok, 5, by_x))
    for j in range(1, n // 2):
        origin = lax.rem(w + n - 2 * j, n)
        for i, dst in enumerate((cols_all, out_all)):
            k = 2 * (j - 1) + i
            held[k].wait_recv()
            passed.append(send(dst.at[origin], dst.at[origin], (s_f, r_f), k, mate))
    for copy in own:
        copy.wait()
    x1.wait_recv()
    y0.wait_recv()
    for copy in held[n - 2 :]:
        copy.wait_recv()
    for copy in passed:
        copy.wait_recv()
    for copy in [x0, x1, y0, y1] + held + passed:
        copy.wait_send()


def gather_in(n, tokens, own_columns, output_weight):
    rows, d = tokens.shape
    return pl.pallas_call(
        functools.partial(gather_kernel, n),
        out_shape=(
            jax.ShapeDtypeStruct((4 * rows, d), bf16),
            jax.ShapeDtypeStruct((n,) + own_columns.shape, bf16),
            jax.ShapeDtypeStruct((n,) + output_weight.shape, bf16),
        ),
        in_specs=[ANYWHERE] * 3,
        out_specs=(ANYWHERE,) * 3,
        scratch_shapes=[
            pltpu.VMEM(tokens.shape, bf16),
            pltpu.VMEM(own_columns.shape, bf16),
            pltpu.VMEM(output_weight.shape, bf16),
            pltpu.SemaphoreType.DMA((6,)),
        ]
        + dma_sems(6)
        + dma_sems(n)
        + dma_sems(n - 2),
        compiler_params=remote_params(0),
        name="gather_in",
    )(tokens, own_columns, output_weight)


def exchange_kernel(src_of, dst_of, x_ref, o_ref, buf, local_sem, s_sem, r_sem):
    s, w = lax.axis_index("seq"), lax.axis_index("wt")
    others = [flip(s, k) for k in (1, 2, 3)]
    meet([(p, w) for p in others])
    copies = [
        send(src_of(x_ref, p), dst_of(o_ref, s), (s_sem, r_sem), k, (p, w))
        for k, p in enumerate(others)
    ]
    come = pltpu.make_async_copy(src_of(x_ref, s), buf, local_sem.at[0])
    come.start()
    come.wait()
    go = pltpu.make_async_copy(buf, dst_of(o_ref, s), local_sem.at[1])
    go.start()
    go.wait()
    for copy in copies:
        copy.wait()


def exchange(x, out_shape, part_shape, src_of, dst_of, number, name):
    return pl.pallas_call(
        functools.partial(exchange_kernel, src_of, dst_of),
        out_shape=jax.ShapeDtypeStruct(out_shape, x.dtype),
        in_specs=[ANYWHERE],
        out_specs=ANYWHERE,
        scratch_shapes=[pltpu.VMEM(part_shape, x.dtype), pltpu.SemaphoreType.DMA((2,))] + dma_sems(3),
        compiler_params=remote_params(number),
        name=name,
    )(x)


def reduce_kernel(
    n, con_ref, exp_ref, out_ref, att_ref, vec_ref, con_o, exp_o, out_o, att_o, vec_o,
    r_con, r_exp, r_out, h_att, m_att, r_att, r_vec, r_vec2, m_vec, m_ce, g_ce, m_row, g_att,
    s_a, r_a, s_b, r_b, s_c, r_c, s_d, r_d, s_e, r_e, s_f, r_f, s_g, r_g, s_h, r_h, s_i, r_i,
):
    s, w = lax.axis_index("seq"), lax.axis_index("wt")
    z, c = w // 2, lax.rem(w, 2)
    others = [flip(s, k) for k in (1, 2, 3)]
    seq_peers = [(p, w) for p in others]
    mate = (s, flip(w, 1))
    wt_peers = [(s, lax.rem(w + j, n)) for j in range(1, n)]
    meet(seq_peers + wt_peers)
    wide = exp_ref.shape[1] // 4

    def lanes(p):
        return pl.ds(pl.multiple_of(p * wide, 128), wide)

    pair = [
        send(att_ref.at[2 * k + 1 - c], h_att.at[k], (s_a, r_a), k, mate) for k in range(n // 2)
    ]
    vecs = [
        send(vec_ref.at[lax.rem(w + j, n)], r_vec.at[w], (s_b, r_b), j - 1, wt_peers[j - 1])
        for j in range(1, n)
    ]
    cons = [
        send(con_ref.at[p], r_con.at[s], (s_c, r_c), k, (p, w)) for k, p in enumerate(others)
    ]
    exps = [
        send(exp_ref.at[:, lanes(p)], r_exp.at[s], (s_d, r_d), k, (p, w))
        for k, p in enumerate(others)
    ]
    outs = [send(out_ref, r_out.at[s], (s_e, r_e), k, (p, w)) for k, p in enumerate(others)]
    r_con[s] = con_ref[s]
    r_exp[s] = exp_ref[:, lanes(s)]
    r_out[s] = out_ref[...]
    r_vec[w] = vec_ref[w]
    for copy in pair:
        copy.wait_recv()
    for k in range(n // 2):
        m_att[k] = (att_ref[2 * k + c].astype(f32) + h_att[k].astype(f32)).astype(bf16)
    zs = [lax.rem(z + j, n // 2) for j in range(1, n // 2)]
    atts = [
        send(m_att.at[k], r_att.at[z], (s_f, r_f), j, (s, 2 * k + c)) for j, k in enumerate(zs)
    ]
    r_att[z] = m_att[z]
    for copy in vecs:
        copy.wait_recv()
    total = r_vec[0]
    for k in range(1, n):
        total = total + r_vec[k]
    m_vec[...] = total
    vecs2 = [send(m_vec, r_vec2.at[s], (s_g, r_g), k, p) for k, p in enumerate(seq_peers)]
    r_vec2[s] = total

    def add4(ref):
        t = [ref[k].astype(f32) for k in range(4)]
        return (t[0] + t[1]) + (t[2] + t[3])

    for copy in cons:
        copy.wait_recv()
    m_ce[0] = add4(r_con).astype(bf16)
    for copy in exps:
        copy.wait_recv()
    m_ce[1] = add4(r_exp).astype(bf16)
    g_ce[s] = m_ce[...]
    ces = [send(m_ce, g_ce.at[s], (s_h, r_h), k, p) for k, p in enumerate(seq_peers)]
    for copy in atts:
        copy.wait_recv()
    row = r_att[0].astype(f32)
    for k in range(1, n // 2):
        row = row + r_att[k].astype(f32)
    m_row[...] = row.astype(bf16)
    g_att[s] = m_row[...]
    rows = [send(m_row, g_att.at[s], (s_i, r_i), k, p) for k, p in enumerate(seq_peers)]
    for copy in outs:
        copy.wait_recv()
    out_o[...] = add4(r_out)
    for copy in vecs2:
        copy.wait_recv()
    vec_o[...] = (r_vec2[0] + r_vec2[1]) + (r_vec2[2] + r_vec2[3])
    for copy in ces:
        copy.wait_recv()
    for k in range(4):
        con_o[k] = g_ce[k, 0].astype(f32)
        exp_o[:, k * wide : (k + 1) * wide] = g_ce[k, 1].astype(f32)
    for copy in rows:
        copy.wait_recv()
    cols = g_att.shape[2]
    for k in range(4):
        att_o[:, k * cols : (k + 1) * cols] = g_att[k].astype(f32)
    for copy in pair + vecs + cons + exps + outs + atts + vecs2 + ces + rows:
        copy.wait_send()


def reduce_out(n, con, expand, out, att, vec):
    r, d = out.shape
    cols = att.shape[2]
    vshape = vec.shape[1:]
    counts = (n // 2, n - 1, 3, 3, 3, n // 2 - 1, 3, 3, 3)
    return pl.pallas_call(
        functools.partial(reduce_kernel, n),
        out_shape=(
            jax.ShapeDtypeStruct(con.shape, f32),
            jax.ShapeDtypeStruct(expand.shape, f32),
            jax.ShapeDtypeStruct(out.shape, f32),
            jax.ShapeDtypeStruct((r, 4 * cols), f32),
            jax.ShapeDtypeStruct(vshape, f32),
        ),
        in_specs=[IN_VMEM] * 5,
        out_specs=(IN_VMEM,) * 5,
        scratch_shapes=[
            pltpu.VMEM((4, r, d), bf16),
            pltpu.VMEM((4, r, d), bf16),
            pltpu.VMEM((4, r, d), bf16),
            pltpu.VMEM((n // 2, r, cols), bf16),
            pltpu.VMEM((n // 2, r, cols), bf16),
            pltpu.VMEM((n // 2, r, cols), bf16),
            pltpu.VMEM((n,) + vshape, f32),
            pltpu.VMEM((4,) + vshape, f32),
            pltpu.VMEM(vshape, f32),
            pltpu.VMEM((2, r, d), bf16),
            pltpu.VMEM((4, 2, r, d), bf16),
            pltpu.VMEM((r, cols), bf16),
            pltpu.VMEM((4, r, cols), bf16),
        ]
        + [sem for count in counts for sem in dma_sems(count)],
        compiler_params=remote_params(4),
        name="reduce_out",
    )(con, expand, out, att, vec)


def tokens_grad_kernel(base_ref, g_ref, w_ref, o_ref):
    cols = g_ref.shape[2]
    total = base_ref[...]
    for k in range(4):
        total = total + mm(g_ref[k], w_ref[:, k * cols : (k + 1) * cols], NT)
    o_ref[...] = total


def tokens_back(base, g, weight):
    rows, d = base.shape
    cols = g.shape[2]
    block = rows // 3
    return pl.pallas_call(
        tokens_grad_kernel,
        out_shape=jax.ShapeDtypeStruct((rows, d), f32),
        grid=(3,),
        in_specs=[
            pl.BlockSpec((block, d), lambda i: (i, 0)),
            pl.BlockSpec((4, block, cols), lambda i: (0, i, 0)),
            pl.BlockSpec(weight.shape, lambda i: (0, 0)),
        ],
        out_specs=pl.BlockSpec((block, d), lambda i: (i, 0)),
        compiler_params=pltpu.CompilerParams(vmem_limit_bytes=48 * 2**20),
        cost_estimate=pl.CostEstimate(
            flops=8 * rows * d * cols, bytes_accessed=8 * rows * d + 8 * d * cols, transcendentals=0
        ),
        name="tokens_back",
    )(base, g, weight)


def norm_parts(summed):
    centre = summed - jnp.mean(summed, axis=-1, keepdims=True)
    inverse = lax.rsqrt(jnp.mean(centre * centre, axis=-1, keepdims=True) + epsilon)
    return (centre * inverse, inverse)


def norm_back(grad_normed, normed, inverse):
    return inverse * (
        grad_normed
        - jnp.mean(grad_normed, axis=-1, keepdims=True)
        - normed * jnp.mean(grad_normed * normed, axis=-1, keepdims=True)
    )


def local(
    tokens,
    output_cotangent,
    attention_weight,
    query_bias,
    value_bias,
    output_weight,
    output_bias,
    first_gain,
    first_shift,
    expand_weight,
    expand_bias,
    contract_weight,
    contract_bias,
    second_gain,
    second_shift,
    head_gate,
    hidden_gate,
    unit_gate,
    head_mask,
    hidden_mask,
    unit_mask,
    attention_mask,
    feedforward_mask,
    continuation_lengths,
):
    row_count = tokens.shape[0]
    seq_count = lax.axis_size("seq")
    head_count = head_gate.shape[0]
    model_width = hidden_gate.shape[0]
    head_size = model_width // head_count
    local_heads = head_count // seq_count
    seq_index = lax.axis_index("seq")
    wt_index = lax.axis_index("wt")
    local_width = 3 * head_size * local_heads
    wt_count = lax.axis_size("wt")
    own_columns = lax.dynamic_slice_in_dim(attention_weight, seq_index * local_width, local_width, 1)
    tokens_all, own_weight, full_output = gather_in(wt_count, tokens, own_columns, output_weight)
    own_weight = own_weight.reshape(model_width, local_width)
    full_output = full_output.reshape(model_width, model_width)
    full_expand = lax.all_gather(expand_weight, "wt", axis=0, tiled=True)
    full_contract = lax.all_gather(contract_weight, "wt", axis=0, tiled=True)
    full_attention = lax.all_gather(attention_weight, "wt", axis=0, tiled=True)
    position = seq_index * row_count + jnp.arange(row_count, dtype=jnp.int32)
    group_local = position // GLEN
    own_groups = jnp.arange(GRP_WT, dtype=jnp.int32)
    chosen = group_local[:, None] == own_groups[None, :]
    first_group = wt_index * GRP_WT
    own_attention = lax.dynamic_slice_in_dim(attention_mask, first_group, GRP_WT, 0).astype(
        jnp.float32
    )
    own_feedforward = lax.dynamic_slice_in_dim(feedforward_mask, first_group, GRP_WT, 0).astype(
        jnp.float32
    )
    attention_rows = jnp.sum(jnp.where(chosen, own_attention[None, :], 0.0), axis=1)
    feedforward_rows = jnp.sum(jnp.where(chosen, own_feedforward[None, :], 0.0), axis=1)
    head_scale = head_mask.astype(jnp.float32) * head_gate
    hidden_scale = hidden_mask.astype(jnp.float32) * hidden_gate
    unit_scale = unit_mask.astype(jnp.float32) * unit_gate
    first_gain_f = first_gain.astype(jnp.float32)
    second_gain_f = second_gain.astype(jnp.float32)
    bias_table = jnp.stack(
        [
            query_bias.astype(jnp.float32).reshape(head_count, head_size),
            jnp.zeros((head_count, head_size), jnp.float32),
            value_bias.astype(jnp.float32).reshape(head_count, head_size),
        ],
        axis=1,
    )
    own_scale = lax.dynamic_slice_in_dim(head_scale, seq_index * local_heads, local_heads, 0)
    own_scale = own_scale * own_attention[0]
    own_mask = lax.dynamic_slice_in_dim(head_mask, seq_index * local_heads, local_heads, 0)
    own_gate = lax.dynamic_slice_in_dim(head_gate, seq_index * local_heads, local_heads, 0)
    own_bias = lax.dynamic_slice_in_dim(bias_table, seq_index * local_heads, local_heads, 0)
    constant = jnp.ones((local_heads, head_size), jnp.float32)
    factor = jnp.stack([constant, constant, constant * own_scale[:, None]], axis=1)
    vec = jnp.stack([own_bias.reshape(local_width), factor.reshape(local_width)], axis=0)
    lens = lax.dynamic_slice_in_dim(continuation_lengths, first_group, GRP_WT, 0)[0]
    packed, mixed_heads, log_sums = attend(lens, tokens_all, own_weight, vec, local_heads)
    local_ctx = local_heads * head_size
    context_t = exchange(
        mixed_heads,
        (model_width, row_count),
        (local_ctx, row_count),
        lambda ref, p: ref.at[:, pl.ds(pl.multiple_of(p * row_count, 128), row_count)],
        lambda ref, p: ref.at[pl.ds(pl.multiple_of(p * local_ctx, 16), local_ctx), :],
        1,
        "context_out",
    )
    attn_out = jnp.einsum(
        "it,id->td", context_t, full_output, preferred_element_type=jnp.float32
    ) + output_bias.astype(jnp.float32)
    normed_one, inverse_one = norm_parts(tokens.astype(jnp.float32) + attn_out)
    shaped_one = normed_one * first_gain_f + first_shift.astype(jnp.float32)
    first_out = shaped_one * hidden_scale
    first_low = first_out.astype(jnp.bfloat16)
    hidden = jnp.dot(
        first_low, full_expand, preferred_element_type=jnp.float32
    ) + expand_bias.astype(jnp.float32)
    gelu_out = jax.nn.gelu(hidden, approximate=False)
    unit_rows_scale = unit_scale[None, :] * feedforward_rows[:, None]
    activated = (gelu_out * unit_rows_scale).astype(jnp.bfloat16)
    branch = jnp.dot(
        activated, full_contract, preferred_element_type=jnp.float32
    ) + contract_bias.astype(jnp.float32)
    normed_two, inverse_two = norm_parts(first_out + branch)
    shaped_two = normed_two * second_gain_f + second_shift.astype(jnp.float32)
    layer_output = (shaped_two * hidden_scale).astype(jnp.bfloat16)
    back_attention, back_output, back_expand, back_contract = (
        full_attention,
        full_output,
        full_expand,
        full_contract,
    )
    cotangent = output_cotangent.astype(jnp.float32)
    grad_shaped_two = cotangent * hidden_scale
    second_gain_grad = jnp.sum(grad_shaped_two * normed_two, axis=0)
    second_shift_grad = jnp.sum(grad_shaped_two, axis=0)
    grad_total_two = norm_back(grad_shaped_two * second_gain_f, normed_two, inverse_two)
    grad_branch = grad_total_two.astype(jnp.bfloat16)
    contract_bias_grad = jnp.sum(grad_branch.astype(jnp.float32), axis=0)
    contract_weight_grad = jnp.einsum(
        "ti,td->id", activated, grad_branch, preferred_element_type=jnp.float32
    )
    grad_activated = jnp.einsum(
        "td,id->ti", grad_branch, back_contract, preferred_element_type=jnp.float32
    )
    unit_gate_grad = unit_mask.astype(jnp.float32) * jnp.sum(
        grad_activated * gelu_out * feedforward_rows[:, None], axis=0
    )
    cumulative = 0.5 * (1.0 + lax.erf(hidden * root_half))
    gelu_slope = cumulative + hidden * jnp.exp(-0.5 * hidden * hidden) * density_scale
    grad_hidden = (grad_activated * unit_rows_scale * gelu_slope).astype(jnp.bfloat16)
    expand_bias_grad = jnp.sum(grad_hidden.astype(jnp.float32), axis=0)
    expand_weight_grad = jnp.einsum(
        "td,tf->df", first_low, grad_hidden, preferred_element_type=jnp.float32
    )
    grad_first = grad_total_two + jnp.einsum(
        "tf,df->td", grad_hidden, back_expand, preferred_element_type=jnp.float32
    )
    grad_shaped_one = grad_first * hidden_scale
    first_gain_grad = jnp.sum(grad_shaped_one * normed_one, axis=0)
    first_shift_grad = jnp.sum(grad_shaped_one, axis=0)
    hidden_gate_grad = hidden_mask.astype(jnp.float32) * jnp.sum(
        cotangent * shaped_two + grad_first * shaped_one, axis=0
    )
    grad_total_one = norm_back(grad_shaped_one * first_gain_f, normed_one, inverse_one)
    grad_attn = grad_total_one.astype(jnp.bfloat16)
    output_bias_grad = jnp.sum(grad_attn.astype(jnp.float32), axis=0)
    output_weight_grad = jnp.einsum(
        "it,td->id", context_t, grad_attn, preferred_element_type=jnp.float32
    )
    grad_context_t = jnp.einsum(
        "td,id->it", grad_attn, back_output, preferred_element_type=jnp.float32
    ).astype(jnp.bfloat16)
    arriving = exchange(
        grad_context_t,
        (local_ctx, GLEN),
        (local_ctx, row_count),
        lambda ref, p: ref.at[pl.ds(pl.multiple_of(p * local_ctx, 16), local_ctx), :],
        lambda ref, p: ref.at[:, pl.ds(pl.multiple_of(p * row_count, 128), row_count)],
        2,
        "context_grad_in",
    )
    grad_packed, sums, gate_sums = attend_back(
        lens,
        packed,
        mixed_heads,
        arriving,
        log_sums,
        vec[1:2],
        local_heads,
    )
    head_own = own_mask.astype(jnp.float32) * own_attention[0] / own_gate
    head_own = head_own * jnp.sum(gate_sums[0].reshape(local_heads, head_size), axis=1)
    head_partial = lax.dynamic_update_slice_in_dim(
        jnp.zeros((head_count,), jnp.float32), head_own, seq_index * local_heads, 0
    )
    sums = sums[0].reshape(local_heads, 3, head_size)
    zeros_wide = jnp.zeros((model_width,), jnp.float32)
    at_own = seq_index * local_heads * head_size
    query_bias_grad = lax.dynamic_update_slice_in_dim(zeros_wide, sums[:, 0].reshape(-1), at_own, 0)
    value_bias_grad = lax.dynamic_update_slice_in_dim(zeros_wide, sums[:, 2].reshape(-1), at_own, 0)
    grad_pieces = exchange(
        grad_packed.reshape(seq_count, row_count, local_width),
        (seq_count, row_count, local_width),
        (row_count, local_width),
        lambda ref, p: ref.at[p],
        lambda ref, p: ref.at[p],
        3,
        "packed_grad_out",
    )
    attention_weight_grad = jnp.einsum(
        "td,tc->dc", tokens_all, grad_packed, preferred_element_type=jnp.float32
    )
    tokens_grad = tokens_back(grad_total_one, grad_pieces, back_attention)
    width_rows = jnp.stack(
        [
            query_bias_grad,
            value_bias_grad,
            output_bias_grad,
            first_gain_grad,
            first_shift_grad,
            contract_bias_grad,
            second_gain_grad,
            second_shift_grad,
            hidden_gate_grad,
        ],
        axis=0,
    )
    unit_rows = jnp.stack([expand_bias_grad, unit_gate_grad], axis=0)
    own_wide, own_units = model_width // wt_count, unit_gate.shape[0] // wt_count
    by_shard = jnp.concatenate(
        [
            width_rows.reshape(9, wt_count, own_wide).transpose(1, 0, 2).reshape(wt_count, -1),
            unit_rows.reshape(2, wt_count, own_units).transpose(1, 0, 2).reshape(wt_count, -1),
            jnp.broadcast_to(head_partial[None, :], (wt_count, head_count)),
        ],
        axis=1,
    )
    used = by_shard.shape[1]
    by_shard = jnp.pad(by_shard, ((0, 0), (0, -used % 1024))).reshape(wt_count, -1, 128)
    con_piece = lax.psum_scatter(
        contract_weight_grad.astype(bf16), "wt", scatter_dimension=0, tiled=True
    )
    exp_piece = lax.psum_scatter(
        expand_weight_grad.astype(bf16), "wt", scatter_dimension=0, tiled=True
    )
    out_piece = lax.psum_scatter(
        output_weight_grad.astype(bf16), "wt", scatter_dimension=0, tiled=True
    )
    con_sum, exp_sum, out_sum, att_sum, vec_sum = reduce_out(
        wt_count,
        con_piece.reshape(seq_count, own_wide, model_width),
        exp_piece,
        out_piece,
        attention_weight_grad.astype(bf16).reshape(wt_count, own_wide, local_width),
        by_shard,
    )
    vec_sum = vec_sum.reshape(-1)
    wide = [vec_sum[k * own_wide : (k + 1) * own_wide] for k in range(9)]
    base = 9 * own_wide
    units = [vec_sum[base + k * own_units : base + (k + 1) * own_units] for k in range(2)]
    head_gate_grad = vec_sum[base + 2 * own_units : used]
    return (
        layer_output,
        tokens_grad,
        att_sum,
        wide[0],
        wide[1],
        out_sum,
        wide[2],
        wide[3],
        wide[4],
        exp_sum,
        units[0],
        con_sum.reshape(seq_count * own_wide, model_width),
        wide[5],
        wide[6],
        wide[7],
        head_gate_grad,
        wide[8],
        units[1],
    )


def solution(mesh):
    return jax.shard_map(
        local,
        mesh=mesh,
        in_specs=(
            P(("wt", "seq"), None),
            P(("wt", "seq"), None),
            P("wt", None),
            P(),
            P(),
            P("wt", None),
            P(),
            P(),
            P(),
            P("wt", None),
            P(),
            P("wt", None),
            P(),
            P(),
            P(),
            P(),
            P(),
            P(),
            P(),
            P(),
            P(),
            P(),
            P(),
            P(),
        ),
        out_specs=(
            P(("wt", "seq"), None),
            P(("wt", "seq"), None),
            P("wt", None),
            P("wt"),
            P("wt"),
            P("wt", None),
            P("wt"),
            P("wt"),
            P("wt"),
            P("wt", None),
            P("wt"),
            P("wt", None),
            P("wt"),
            P("wt"),
            P("wt"),
            P(),
            P("wt"),
            P("wt"),
        ),
        check_vma=False,
    )
```

```python
import functools

import jax
import jax.numpy as jnp
from jax import lax
from jax.experimental import pallas as pl
from jax.experimental.pallas import tpu as pltpu
from jax.sharding import PartitionSpec as P

PROMPT = 1024
GRP_WT = 1
GLEN = 3072
SHORT = 512
LONG = 1536
HD = 64
TQ = 512
KC = 512

epsilon = 1e-06
score_scale = 0.125
exp2_scale = 0.125 * 1.4426950408889634
root_half = 0.7071067811865476
density_scale = 0.3989422804014327
bf16 = jnp.bfloat16
f32 = jnp.float32

NT = (((1,), (1,)), ((), ()))
NN = (((1,), (0,)), ((), ()))
TN = (((0,), (0,)), ((), ()))


def mm(a, b, dims=NN):
    return lax.dot_general(a, b, dims, preferred_element_type=f32)


def query_tiles(short_first, tile):
    short_at = pl.multiple_of(jnp.where(short_first, PROMPT, PROMPT + LONG), SHORT)
    long_at = pl.multiple_of(jnp.where(short_first, PROMPT + SHORT, PROMPT), SHORT)
    for base, own_at, own_len, rows in (
        (0, 0, 0, PROMPT),
        (short_at, short_at, SHORT, SHORT),
        (long_at, long_at, LONG, LONG),
    ):

        def step(i, carry, base=base, own_at=own_at, own_len=own_len):
            tile(pl.multiple_of(base + i * TQ, TQ), own_at, own_len)
            return carry

        lax.fori_loop(0, rows // TQ, step, 0)


def attend_kernel(
    heads, lens_ref, tok_ref, w_ref, vec_ref, packed_ref, ctx_ref, lse_ref, q_sc, k_sc, vt_sc
):
    def project(i, carry):
        rows = pl.ds(pl.multiple_of(i * TQ, TQ), TQ)
        x = mm(tok_ref[rows, :], w_ref[...]) + vec_ref[0:1, :]
        x = (x * vec_ref[1:2, :]).astype(bf16)
        packed_ref[rows, :] = x
        for h in range(heads):
            at = 3 * HD * h
            q_sc[h, rows, :] = x[:, at : at + HD]
            k_sc[h, rows, :] = x[:, at + HD : at + 2 * HD]
            vt_sc[h, 0:HD, rows] = x[:, at + 2 * HD : at + 3 * HD].T
        return carry

    lax.fori_loop(0, GLEN // TQ, project, 0)
    for h in range(heads):
        vt_sc[h, HD : HD + 16, :] = jnp.ones((16, GLEN), bf16)

    def one_head(h, carry):
        def tile(q_at, own_at, own_len):
            rows = pl.ds(q_at, TQ)
            q = q_sc[h, rows, :]
            s1 = mm(k_sc[h, 0:PROMPT, :], q, NT)
            top = jnp.max(s1, axis=0, keepdims=True)
            if own_len:
                own = pl.ds(own_at, own_len)
                s2 = mm(k_sc[h, own, :], q, NT)
                top = jnp.maximum(top, jnp.max(s2, axis=0, keepdims=True))
            top = top * exp2_scale
            p1 = jnp.exp2(s1 * exp2_scale - top)
            o = mm(vt_sc[h, :, 0:PROMPT], p1.astype(bf16))
            total = jnp.sum(p1, axis=0, keepdims=True)
            if own_len:
                p2 = jnp.exp2(s2 * exp2_scale - top)
                o = o + mm(vt_sc[h, :, own], p2.astype(bf16))
                total = total + jnp.sum(p2, axis=0, keepdims=True)
            ctx_ref[pl.ds(pl.multiple_of(HD * h, HD), HD), rows] = (o[0:HD, :] / total).astype(bf16)
            lse_ref[h, :, rows] = top + jnp.log2(total)

        query_tiles(lens_ref[0] == SHORT, tile)
        return carry

    lax.fori_loop(0, heads, one_head, 0)


def attend(lens, tokens_all, weight, vec, heads):
    width = 3 * HD * heads
    whole = pl.BlockSpec(memory_space=pltpu.VMEM)
    return pl.pallas_call(
        functools.partial(attend_kernel, heads),
        out_shape=(
            jax.ShapeDtypeStruct((GLEN, width), bf16),
            jax.ShapeDtypeStruct((HD * heads, GLEN), bf16),
            jax.ShapeDtypeStruct((heads, 1, GLEN), f32),
        ),
        in_specs=[pl.BlockSpec(memory_space=pltpu.SMEM), whole, whole, whole],
        out_specs=(whole, whole, whole),
        scratch_shapes=[
            pltpu.VMEM((heads, GLEN, HD), bf16),
            pltpu.VMEM((heads, GLEN, HD), bf16),
            pltpu.VMEM((heads, HD + 16, GLEN), bf16),
        ],
        compiler_params=pltpu.CompilerParams(vmem_limit_bytes=56 * 2**20),
        cost_estimate=pl.CostEstimate(
            flops=2 * GLEN * 768 * width + heads * 4 * 256 * 5767168,
            bytes_accessed=2 * GLEN * (768 + width),
            transcendentals=heads * 5767168,
        ),
        name="attend",
    )(lens, tokens_all, weight, vec)


def attend_back_kernel(
    heads, lens_ref, packed_ref, ctx_ref, gctx_ref, lse_ref, scale_ref,
    out_ref, sums_ref, gate_ref,
    q_sc, k_sc, v_sc, kt_sc, g_sc, delta_sc, dqt_sc, dk_sc, dv_sc,
):
    def split(i, carry):
        rows = pl.ds(pl.multiple_of(i * TQ, TQ), TQ)
        x = packed_ref[rows, :]
        inner = gctx_ref[:, rows].astype(f32) * ctx_ref[:, rows].astype(f32)
        for h in range(heads):
            at = 3 * HD * h
            q_sc[h, rows, :] = x[:, at : at + HD]
            k = x[:, at + HD : at + 2 * HD]
            k_sc[h, rows, :] = k
            kt_sc[h, :, rows] = k.T
            v_sc[h, rows, :] = x[:, at + 2 * HD : at + 3 * HD]
            g_sc[h, :, rows] = gctx_ref[HD * h : HD * (h + 1), rows]
            delta_sc[h, :, rows] = jnp.sum(inner[HD * h : HD * (h + 1), :], axis=0, keepdims=True)
        return carry

    lax.fori_loop(0, GLEN // TQ, split, 0)
    dk_sc[...] = jnp.zeros_like(dk_sc)
    dv_sc[...] = jnp.zeros_like(dv_sc)

    def one_head(h, carry):
        def tile(q_at, own_at, own_len):
            rows = pl.ds(q_at, TQ)
            q = q_sc[h, rows, :]
            g = g_sc[h, :, rows]
            lse = lse_ref[h, :, rows]
            delta = delta_sc[h, :, rows]
            dq = jnp.zeros((HD, TQ), f32)
            pieces = [(j * KC, PROMPT // KC) for j in range(PROMPT // KC)]
            pieces = [c for c, _ in pieces] + [own_at + j * KC for j in range(own_len // KC)]
            for start in pieces:
                keys = pl.ds(start, KC)
                s = mm(k_sc[h, keys, :], q, NT)
                p = jnp.exp2(s * exp2_scale - lse)
                dp = mm(v_sc[h, keys, :], g)
                ds = (p * (dp - delta)).astype(bf16)
                dv_sc[h, keys, :] += mm(p.astype(bf16), g, NT)
                dk_sc[h, keys, :] += mm(ds, q)
                dq = dq + mm(kt_sc[h, :, keys], ds)
            dqt_sc[h, :, rows] = dq * score_scale

        query_tiles(lens_ref[0] == SHORT, tile)
        return carry

    lax.fori_loop(0, heads, one_head, 0)
    sums_ref[...] = jnp.zeros_like(sums_ref)
    gate_ref[...] = jnp.zeros_like(gate_ref)

    def place(i, carry):
        rows = pl.ds(pl.multiple_of(i * TQ, TQ), TQ)
        for h in range(heads):
            at = 3 * HD * h
            dq = dqt_sc[h, :, rows].T.astype(bf16)
            dk = (dk_sc[h, rows, :] * score_scale).astype(bf16)
            dv = dv_sc[h, rows, :].astype(bf16).astype(f32)
            gate_ref[0:1, HD * h : HD * (h + 1)] += jnp.sum(
                dv * v_sc[h, rows, :].astype(f32), axis=0, keepdims=True
            )
            dv = (dv * scale_ref[:, at + 2 * HD : at + 3 * HD]).astype(bf16)
            out_ref[rows, at : at + HD] = dq
            out_ref[rows, at + HD : at + 2 * HD] = dk
            out_ref[rows, at + 2 * HD : at + 3 * HD] = dv
            sums_ref[0:1, at : at + HD] += jnp.sum(dq.astype(f32), axis=0, keepdims=True)
            sums_ref[0:1, at + 2 * HD : at + 3 * HD] += jnp.sum(
                dv.astype(f32), axis=0, keepdims=True
            )
        return carry

    lax.fori_loop(0, GLEN // TQ, place, 0)


def attend_back(lens, packed, ctx, gctx, lse, scale, heads):
    width = 3 * HD * heads
    whole = pl.BlockSpec(memory_space=pltpu.VMEM)
    rows64 = pltpu.VMEM((heads, GLEN, HD), bf16)
    rows64f = pltpu.VMEM((heads, GLEN, HD), f32)
    return pl.pallas_call(
        functools.partial(attend_back_kernel, heads),
        out_shape=(
            jax.ShapeDtypeStruct((GLEN, width), bf16),
            jax.ShapeDtypeStruct((8, width), f32),
            jax.ShapeDtypeStruct((8, HD * heads), f32),
        ),
        in_specs=[pl.BlockSpec(memory_space=pltpu.SMEM)] + [whole] * 5,
        out_specs=(whole, whole, whole),
        scratch_shapes=[
            rows64,
            rows64,
            rows64,
            pltpu.VMEM((heads, HD, GLEN), bf16),
            pltpu.VMEM((heads, HD, GLEN), bf16),
            pltpu.VMEM((heads, 1, GLEN), f32),
            pltpu.VMEM((heads, HD, GLEN), f32),
            rows64f,
            rows64f,
        ],
        compiler_params=pltpu.CompilerParams(vmem_limit_bytes=56 * 2**20),
        cost_estimate=pl.CostEstimate(
            flops=heads * 10 * 256 * 5767168,
            bytes_accessed=2 * GLEN * (3 * width),
            transcendentals=heads * 5767168,
        ),
        name="attend_back",
    )(lens, packed, ctx, gctx, lse, scale)


def send(src, dst, sems, k, peer):
    copy = pltpu.make_async_remote_copy(
        src_ref=src,
        dst_ref=dst,
        send_sem=sems[0].at[k],
        recv_sem=sems[1].at[k],
        device_id=peer,
        device_id_type=pl.DeviceIdType.MESH,
    )
    copy.start()
    return copy


def meet(peers):
    barrier = pltpu.get_barrier_semaphore()
    for peer in peers:
        pl.semaphore_signal(barrier, inc=1, device_id=peer, device_id_type=pl.DeviceIdType.MESH)
    pl.semaphore_wait(barrier, len(peers))


def flip(index, bits):
    for bit in (1, 2):
        if bits & bit:
            index = index + bit - 2 * bit * ((index // bit) % 2)
    return index


def remote_params(number):
    return pltpu.CompilerParams(
        collective_id=number, has_side_effects=True, vmem_limit_bytes=56 * 2**20
    )


ANYWHERE = pl.BlockSpec(memory_space=pl.ANY)
IN_VMEM = pl.BlockSpec(memory_space=pltpu.VMEM)


def dma_sems(count):
    return [pltpu.SemaphoreType.DMA((count,)), pltpu.SemaphoreType.DMA((count,))]


def gather_kernel(
    n, tok_ref, cols_ref, out_ref, tok_all, cols_all, out_all,
    tok_buf, cols_buf, out_buf, local_sem, s_tok, r_tok, s_w, r_w, s_f, r_f,
):
    s, w = lax.axis_index("seq"), lax.axis_index("wt")
    rows = tok_ref.shape[0]
    half = rows // 2
    by_x, by_y, mate = (flip(s, 1), w), (flip(s, 2), w), (s, flip(w, 1))
    far = [(s, lax.rem(w + 2 * j, n)) for j in range(1, n // 2)]
    meet([by_x, by_y, mate] + far)

    def part(owner, k):
        return pl.ds(pl.multiple_of(owner * rows + k * half, half), half)

    tok = (s_tok, r_tok)
    first = [pl.ds(0, half), pl.ds(half, half)]
    x0 = send(tok_ref.at[first[0]], tok_all.at[part(s, 0)], tok, 0, by_x)
    y1 = send(tok_ref.at[first[1]], tok_all.at[part(s, 1)], tok, 1, by_y)
    x1 = send(tok_ref.at[first[1]], tok_all.at[part(s, 1)], tok, 2, by_x)
    y0 = send(tok_ref.at[first[0]], tok_all.at[part(s, 0)], tok, 3, by_y)
    held = []
    for k, peer in enumerate(far + [mate]):
        for i, (src, dst) in enumerate(((cols_ref, cols_all), (out_ref, out_all))):
            held.append(send(src, dst.at[w], (s_w, r_w), 2 * k + i, peer))
    own = []
    for i, (src, buf) in enumerate(((tok_ref, tok_buf), (cols_ref, cols_buf), (out_ref, out_buf))):
        own.append(pltpu.make_async_copy(src, buf, local_sem.at[i]))
        own[-1].start()
    for copy in own:
        copy.wait()
    targets = (
        (tok_buf, tok_all.at[pl.ds(pl.multiple_of(s * rows, rows), rows)]),
        (cols_buf, cols_all.at[w]),
        (out_buf, out_all.at[w]),
    )
    own = []
    for i, (buf, dst) in enumerate(targets):
        own.append(pltpu.make_async_copy(buf, dst, local_sem.at[3 + i]))
        own[-1].start()
    passed = []
    x0.wait_recv()
    there = tok_all.at[part(flip(s, 1), 0)]
    passed.append(send(there, there, tok, 4, by_y))
    y1.wait_recv()
    there = tok_all.at[part(flip(s, 2), 1)]
    passed.append(send(there, there, tok, 5, by_x))
    for j in range(1, n // 2):
        origin = lax.rem(w + n - 2 * j, n)
        for i, dst in enumerate((cols_all, out_all)):
            k = 2 * (j - 1) + i
            held[k].wait_recv()
            passed.append(send(dst.at[origin], dst.at[origin], (s_f, r_f), k, mate))
    for copy in own:
        copy.wait()
    x1.wait_recv()
    y0.wait_recv()
    for copy in held[n - 2 :]:
        copy.wait_recv()
    for copy in passed:
        copy.wait_recv()
    for copy in [x0, x1, y0, y1] + held + passed:
        copy.wait_send()


def gather_in(n, tokens, own_columns, output_weight):
    rows, d = tokens.shape
    return pl.pallas_call(
        functools.partial(gather_kernel, n),
        out_shape=(
            jax.ShapeDtypeStruct((4 * rows, d), bf16),
            jax.ShapeDtypeStruct((n,) + own_columns.shape, bf16),
            jax.ShapeDtypeStruct((n,) + output_weight.shape, bf16),
        ),
        in_specs=[ANYWHERE] * 3,
        out_specs=(ANYWHERE,) * 3,
        scratch_shapes=[
            pltpu.VMEM(tokens.shape, bf16),
            pltpu.VMEM(own_columns.shape, bf16),
            pltpu.VMEM(output_weight.shape, bf16),
            pltpu.SemaphoreType.DMA((6,)),
        ]
        + dma_sems(6)
        + dma_sems(n)
        + dma_sems(n - 2),
        compiler_params=remote_params(0),
        name="gather_in",
    )(tokens, own_columns, output_weight)


def exchange_kernel(src_of, dst_of, x_ref, o_ref, buf, local_sem, s_sem, r_sem):
    s, w = lax.axis_index("seq"), lax.axis_index("wt")
    others = [flip(s, k) for k in (1, 2, 3)]
    meet([(p, w) for p in others])
    copies = [
        send(src_of(x_ref, p), dst_of(o_ref, s), (s_sem, r_sem), k, (p, w))
        for k, p in enumerate(others)
    ]
    come = pltpu.make_async_copy(src_of(x_ref, s), buf, local_sem.at[0])
    come.start()
    come.wait()
    go = pltpu.make_async_copy(buf, dst_of(o_ref, s), local_sem.at[1])
    go.start()
    go.wait()
    for copy in copies:
        copy.wait()


def exchange(x, out_shape, part_shape, src_of, dst_of, number, name):
    return pl.pallas_call(
        functools.partial(exchange_kernel, src_of, dst_of),
        out_shape=jax.ShapeDtypeStruct(out_shape, x.dtype),
        in_specs=[ANYWHERE],
        out_specs=ANYWHERE,
        scratch_shapes=[pltpu.VMEM(part_shape, x.dtype), pltpu.SemaphoreType.DMA((2,))] + dma_sems(3),
        compiler_params=remote_params(number),
        name=name,
    )(x)


def reduce_kernel(
    n, con_ref, exp_ref, out_ref, att_ref, vec_ref, con_o, exp_o, out_o, att_o, vec_o,
    r_con, r_exp, r_out, h_att, m_att, r_att, r_vec, r_vec2, m_vec, m_ce, g_ce, m_row, g_att,
    s_a, r_a, s_b, r_b, s_c, r_c, s_d, r_d, s_e, r_e, s_f, r_f, s_g, r_g, s_h, r_h, s_i, r_i,
):
    s, w = lax.axis_index("seq"), lax.axis_index("wt")
    z, c = w // 2, lax.rem(w, 2)
    others = [flip(s, k) for k in (1, 2, 3)]
    seq_peers = [(p, w) for p in others]
    mate = (s, flip(w, 1))
    wt_peers = [(s, lax.rem(w + j, n)) for j in range(1, n)]
    meet(seq_peers + wt_peers)
    wide = exp_ref.shape[1] // 4

    def lanes(p):
        return pl.ds(pl.multiple_of(p * wide, 128), wide)

    pair = [
        send(att_ref.at[2 * k + 1 - c], h_att.at[k], (s_a, r_a), k, mate) for k in range(n // 2)
    ]
    vecs = [
        send(vec_ref.at[lax.rem(w + j, n)], r_vec.at[w], (s_b, r_b), j - 1, wt_peers[j - 1])
        for j in range(1, n)
    ]
    cons = [
        send(con_ref.at[p], r_con.at[s], (s_c, r_c), k, (p, w)) for k, p in enumerate(others)
    ]
    exps = [
        send(exp_ref.at[:, lanes(p)], r_exp.at[s], (s_d, r_d), k, (p, w))
        for k, p in enumerate(others)
    ]
    outs = [send(out_ref, r_out.at[s], (s_e, r_e), k, (p, w)) for k, p in enumerate(others)]
    r_con[s] = con_ref[s]
    r_exp[s] = exp_ref[:, lanes(s)]
    r_out[s] = out_ref[...]
    r_vec[w] = vec_ref[w]
    for copy in pair:
        copy.wait_recv()
    for k in range(n // 2):
        m_att[k] = (att_ref[2 * k + c].astype(f32) + h_att[k].astype(f32)).astype(bf16)
    zs = [lax.rem(z + j, n // 2) for j in range(1, n // 2)]
    atts = [
        send(m_att.at[k], r_att.at[z], (s_f, r_f), j, (s, 2 * k + c)) for j, k in enumerate(zs)
    ]
    r_att[z] = m_att[z]
    for copy in vecs:
        copy.wait_recv()
    total = r_vec[0]
    for k in range(1, n):
        total = total + r_vec[k]
    m_vec[...] = total
    vecs2 = [send(m_vec, r_vec2.at[s], (s_g, r_g), k, p) for k, p in enumerate(seq_peers)]
    r_vec2[s] = total

    def add4(ref):
        t = [ref[k].astype(f32) for k in range(4)]
        return (t[0] + t[1]) + (t[2] + t[3])

    for copy in cons:
        copy.wait_recv()
    m_ce[0] = add4(r_con).astype(bf16)
    for copy in exps:
        copy.wait_recv()
    m_ce[1] = add4(r_exp).astype(bf16)
    g_ce[s] = m_ce[...]
    ces = [send(m_ce, g_ce.at[s], (s_h, r_h), k, p) for k, p in enumerate(seq_peers)]
    for copy in atts:
        copy.wait_recv()
    row = r_att[0].astype(f32)
    for k in range(1, n // 2):
        row = row + r_att[k].astype(f32)
    m_row[...] = row.astype(bf16)
    g_att[s] = m_row[...]
    rows = [send(m_row, g_att.at[s], (s_i, r_i), k, p) for k, p in enumerate(seq_peers)]
    for copy in outs:
        copy.wait_recv()
    out_o[...] = add4(r_out)
    for copy in vecs2:
        copy.wait_recv()
    vec_o[...] = (r_vec2[0] + r_vec2[1]) + (r_vec2[2] + r_vec2[3])
    for copy in ces:
        copy.wait_recv()
    for k in range(4):
        con_o[k] = g_ce[k, 0].astype(f32)
        exp_o[:, k * wide : (k + 1) * wide] = g_ce[k, 1].astype(f32)
    for copy in rows:
        copy.wait_recv()
    cols = g_att.shape[2]
    for k in range(4):
        att_o[:, k * cols : (k + 1) * cols] = g_att[k].astype(f32)
    for copy in pair + vecs + cons + exps + outs + atts + vecs2 + ces + rows:
        copy.wait_send()


def reduce_out(n, con, expand, out, att, vec):
    r, d = out.shape
    cols = att.shape[2]
    vshape = vec.shape[1:]
    counts = (n // 2, n - 1, 3, 3, 3, n // 2 - 1, 3, 3, 3)
    return pl.pallas_call(
        functools.partial(reduce_kernel, n),
        out_shape=(
            jax.ShapeDtypeStruct(con.shape, f32),
            jax.ShapeDtypeStruct(expand.shape, f32),
            jax.ShapeDtypeStruct(out.shape, f32),
            jax.ShapeDtypeStruct((r, 4 * cols), f32),
            jax.ShapeDtypeStruct(vshape, f32),
        ),
        in_specs=[IN_VMEM] * 5,
        out_specs=(IN_VMEM,) * 5,
        scratch_shapes=[
            pltpu.VMEM((4, r, d), bf16),
            pltpu.VMEM((4, r, d), bf16),
            pltpu.VMEM((4, r, d), bf16),
            pltpu.VMEM((n // 2, r, cols), bf16),
            pltpu.VMEM((n // 2, r, cols), bf16),
            pltpu.VMEM((n // 2, r, cols), bf16),
            pltpu.VMEM((n,) + vshape, f32),
            pltpu.VMEM((4,) + vshape, f32),
            pltpu.VMEM(vshape, f32),
            pltpu.VMEM((2, r, d), bf16),
            pltpu.VMEM((4, 2, r, d), bf16),
            pltpu.VMEM((r, cols), bf16),
            pltpu.VMEM((4, r, cols), bf16),
        ]
        + [sem for count in counts for sem in dma_sems(count)],
        compiler_params=remote_params(4),
        name="reduce_out",
    )(con, expand, out, att, vec)


def tokens_grad_kernel(base_ref, g_ref, w_ref, o_ref):
    cols = g_ref.shape[2]
    total = base_ref[...]
    for k in range(4):
        total = total + mm(g_ref[k], w_ref[:, k * cols : (k + 1) * cols], NT)
    o_ref[...] = total


def tokens_back(base, g, weight):
    rows, d = base.shape
    cols = g.shape[2]
    block = rows // 3
    return pl.pallas_call(
        tokens_grad_kernel,
        out_shape=jax.ShapeDtypeStruct((rows, d), f32),
        grid=(3,),
        in_specs=[
            pl.BlockSpec((block, d), lambda i: (i, 0)),
            pl.BlockSpec((4, block, cols), lambda i: (0, i, 0)),
            pl.BlockSpec(weight.shape, lambda i: (0, 0)),
        ],
        out_specs=pl.BlockSpec((block, d), lambda i: (i, 0)),
        compiler_params=pltpu.CompilerParams(vmem_limit_bytes=48 * 2**20),
        cost_estimate=pl.CostEstimate(
            flops=8 * rows * d * cols, bytes_accessed=8 * rows * d + 8 * d * cols, transcendentals=0
        ),
        name="tokens_back",
    )(base, g, weight)


(OUT_BIAS, GAIN1, SHIFT1, HIDDEN_SCALE, CON_BIAS, GAIN2, SHIFT2) = range(7)
(S_OUT_BIAS, S_GAIN1, S_SHIFT1, S_CON_BIAS, S_GAIN2, S_SHIFT2, S_HIDDEN) = range(7)


def gelu_parts(x):
    bell = jnp.exp(-0.5 * (x * x))
    t = 1.0 / (1.0 + (0.3275911 * root_half) * jnp.abs(x))
    poly = t * (
        0.127414796 + t * (-0.142248368 + t * (0.7107068705 + t * (-0.7265760135 + t * 0.5307027145)))
    )
    tail = poly * bell
    cumulative = jnp.where(x < 0.0, tail, 1.0 - tail)
    return x * cumulative, cumulative + x * bell * density_scale


def norm_parts(summed):
    centre = summed - jnp.mean(summed, axis=-1, keepdims=True)
    inverse = lax.rsqrt(jnp.mean(centre * centre, axis=-1, keepdims=True) + epsilon)
    return (centre * inverse, inverse)


def norm_back(grad_normed, normed, inverse):
    return inverse * (
        grad_normed
        - jnp.mean(grad_normed, axis=-1, keepdims=True)
        - normed * jnp.mean(grad_normed * normed, axis=-1, keepdims=True)
    )


def feed_forward_kernel(
    steps, chunk,
    ctx_ref, tok_ref, cot_ref, wo_ref, we_ref, wc_ref, wide_ref, unit_ref,
    lo_ref, dt1_ref, gctx_ref, sw_ref, su_ref, dwc_ref, dwe_ref, dwo_ref,
    act_sc, gh_sc, low_sc, gb_sc, ga_sc, ctx_sc, gelu_sc, slope_sc,
):
    i = pl.program_id(0)
    block = tok_ref.shape[0]
    units = we_ref.shape[1]
    rows = pl.ds(pl.multiple_of(i * block, block), block)

    @pl.when(i == 0)
    def _():
        sw_ref[...] = jnp.zeros_like(sw_ref)
        su_ref[...] = jnp.zeros_like(su_ref)

    def wide(k):
        return wide_ref[k : k + 1, :]

    def add_sum(ref, k, cols, value):
        ref[k : k + 1, cols] += jnp.sum(value, axis=0, keepdims=True)

    full = slice(None)
    ctx = ctx_ref[...]
    ctx_sc[:, rows] = ctx
    summed = mm(ctx, wo_ref[...], TN) + wide(OUT_BIAS) + tok_ref[...].astype(f32)
    n1, inv1 = norm_parts(summed)
    s1 = n1 * wide(GAIN1) + wide(SHIFT1)
    hs = wide(HIDDEN_SCALE)
    first = s1 * hs
    low = first.astype(bf16)
    low_sc[rows, :] = low
    branch = first + wide(CON_BIAS)
    for j in range(units // chunk):
        cols = slice(j * chunk, (j + 1) * chunk)
        hidden = mm(low, we_ref[:, cols]) + unit_ref[0:1, cols]
        gelu, slope = gelu_parts(hidden)
        scale = unit_ref[1:2, cols]
        gelu_sc[:, cols] = gelu.astype(gelu_sc.dtype)
        slope_sc[:, cols] = (slope * scale).astype(slope_sc.dtype)
        act = (gelu * scale).astype(bf16)
        act_sc[rows, cols] = act
        branch = branch + mm(act, wc_ref[cols, :])
    n2, inv2 = norm_parts(branch)
    s2 = n2 * wide(GAIN2) + wide(SHIFT2)
    lo_ref[...] = (s2 * hs).astype(bf16)
    dy = cot_ref[...].astype(f32)
    e2 = dy * hs
    add_sum(sw_ref, S_GAIN2, full, e2 * n2)
    add_sum(sw_ref, S_SHIFT2, full, e2)
    dt2 = norm_back(e2 * wide(GAIN2), n2, inv2)
    gb = dt2.astype(bf16)
    gb_sc[rows, :] = gb
    add_sum(sw_ref, S_CON_BIAS, full, gb.astype(f32))
    d_first = dt2
    for j in range(units // chunk):
        cols = slice(j * chunk, (j + 1) * chunk)
        d_act = mm(gb, wc_ref[cols, :], NT)
        add_sum(su_ref, 1, cols, d_act * gelu_sc[:, cols].astype(f32))
        gh = d_act * slope_sc[:, cols].astype(f32)
        add_sum(su_ref, 0, cols, gh)
        gh = gh.astype(bf16)
        gh_sc[rows, cols] = gh
        d_first = d_first + mm(gh, we_ref[:, cols], NT)
    e1 = d_first * hs
    add_sum(sw_ref, S_GAIN1, full, e1 * n1)
    add_sum(sw_ref, S_SHIFT1, full, e1)
    add_sum(sw_ref, S_HIDDEN, full, dy * s2 + d_first * s1)
    dt1 = norm_back(e1 * wide(GAIN1), n1, inv1)
    dt1_ref[...] = dt1
    ga = dt1.astype(bf16)
    ga_sc[rows, :] = ga
    add_sum(sw_ref, S_OUT_BIAS, full, ga.astype(f32))
    gctx_ref[...] = mm(wo_ref[...], ga, NT).astype(bf16)

    @pl.when(i == steps - 1)
    def _():
        for j in range(units // chunk):
            cols = slice(j * chunk, (j + 1) * chunk)
            dwc_ref[cols, :] = mm(act_sc[:, cols], gb_sc[...], TN).astype(bf16)
            dwe_ref[:, cols] = mm(low_sc[...], gh_sc[:, cols], TN).astype(bf16)
        dwo_ref[...] = mm(ctx_sc[...], ga_sc[...]).astype(bf16)


def feed_forward(ctx_t, tokens, cotangent, wo, we, wc, wide, unit, steps=3, chunk=1024, keep=f32):
    rows, d = tokens.shape
    units = we.shape[1]
    block = rows // steps
    tile = pl.BlockSpec((block, d), lambda i: (i, 0))
    lanes = pl.BlockSpec((d, block), lambda i: (0, i))

    def once(shape):
        return pl.BlockSpec(shape, lambda i: (0, 0), pipeline_mode=pl.Buffered(1))

    def const(shape):
        return pl.BlockSpec(shape, lambda i: (0, 0))

    return pl.pallas_call(
        functools.partial(feed_forward_kernel, steps, chunk),
        out_shape=(
            jax.ShapeDtypeStruct((rows, d), bf16),
            jax.ShapeDtypeStruct((rows, d), f32),
            jax.ShapeDtypeStruct((d, rows), bf16),
            jax.ShapeDtypeStruct((8, d), f32),
            jax.ShapeDtypeStruct((8, units), f32),
            jax.ShapeDtypeStruct((units, d), bf16),
            jax.ShapeDtypeStruct((d, units), bf16),
            jax.ShapeDtypeStruct((d, d), bf16),
        ),
        grid=(steps,),
        in_specs=[
            lanes, tile, tile, once((d, d)), once((d, units)), once((units, d)), once((8, d)), once((8, units)),
        ],
        out_specs=(
            tile, tile, lanes, once((8, d)), once((8, units)), once((units, d)), once((d, units)), once((d, d)),
        ),
        scratch_shapes=[
            pltpu.VMEM((rows, units), bf16),
            pltpu.VMEM((rows, units), bf16),
            pltpu.VMEM((rows, d), bf16),
            pltpu.VMEM((rows, d), bf16),
            pltpu.VMEM((rows, d), bf16),
            pltpu.VMEM((d, rows), bf16),
            pltpu.VMEM((block, units), keep),
            pltpu.VMEM((block, units), keep),
        ],
        compiler_params=pltpu.CompilerParams(vmem_limit_bytes=60 * 2**20),
        cost_estimate=pl.CostEstimate(
            flops=rows * d * (12 * units + 6 * d),
            bytes_accessed=4 * d * (4 * units + 2 * d) + 12 * rows * d,
            transcendentals=2 * rows * units,
        ),
        name="feed_forward",
    )(ctx_t, tokens, cotangent, wo, we, wc, wide, unit)


def local(
    tokens,
    output_cotangent,
    attention_weight,
    query_bias,
    value_bias,
    output_weight,
    output_bias,
    first_gain,
    first_shift,
    expand_weight,
    expand_bias,
    contract_weight,
    contract_bias,
    second_gain,
    second_shift,
    head_gate,
    hidden_gate,
    unit_gate,
    head_mask,
    hidden_mask,
    unit_mask,
    attention_mask,
    feedforward_mask,
    continuation_lengths,
):
    row_count = tokens.shape[0]
    seq_count = lax.axis_size("seq")
    head_count = head_gate.shape[0]
    model_width = hidden_gate.shape[0]
    head_size = model_width // head_count
    local_heads = head_count // seq_count
    seq_index = lax.axis_index("seq")
    wt_index = lax.axis_index("wt")
    local_width = 3 * head_size * local_heads
    wt_count = lax.axis_size("wt")
    own_columns = lax.dynamic_slice_in_dim(attention_weight, seq_index * local_width, local_width, 1)
    tokens_all, own_weight, full_output = gather_in(wt_count, tokens, own_columns, output_weight)
    own_weight = own_weight.reshape(model_width, local_width)
    full_output = full_output.reshape(model_width, model_width)
    full_expand = lax.all_gather(expand_weight, "wt", axis=0, tiled=True)
    full_contract = lax.all_gather(contract_weight, "wt", axis=0, tiled=True)
    full_attention = lax.all_gather(attention_weight, "wt", axis=0, tiled=True)
    first_group = wt_index * GRP_WT
    own_attention = lax.dynamic_slice_in_dim(attention_mask, first_group, GRP_WT, 0).astype(
        jnp.float32
    )
    own_feedforward = lax.dynamic_slice_in_dim(feedforward_mask, first_group, GRP_WT, 0).astype(
        jnp.float32
    )
    head_scale = head_mask.astype(jnp.float32) * head_gate
    hidden_scale = hidden_mask.astype(jnp.float32) * hidden_gate
    unit_scale = unit_mask.astype(jnp.float32) * unit_gate
    wide_table = jnp.stack(
        [
            output_bias.astype(f32),
            first_gain.astype(f32),
            first_shift.astype(f32),
            hidden_scale,
            contract_bias.astype(f32),
            second_gain.astype(f32),
            second_shift.astype(f32),
            hidden_scale,
        ],
        axis=0,
    )
    unit_row = unit_scale * own_feedforward[0]
    unit_table = jnp.stack([expand_bias.astype(f32)] + [unit_row] * 7, axis=0)
    bias_table = jnp.stack(
        [
            query_bias.astype(jnp.float32).reshape(head_count, head_size),
            jnp.zeros((head_count, head_size), jnp.float32),
            value_bias.astype(jnp.float32).reshape(head_count, head_size),
        ],
        axis=1,
    )
    own_scale = lax.dynamic_slice_in_dim(head_scale, seq_index * local_heads, local_heads, 0)
    own_scale = own_scale * own_attention[0]
    own_mask = lax.dynamic_slice_in_dim(head_mask, seq_index * local_heads, local_heads, 0)
    own_gate = lax.dynamic_slice_in_dim(head_gate, seq_index * local_heads, local_heads, 0)
    own_bias = lax.dynamic_slice_in_dim(bias_table, seq_index * local_heads, local_heads, 0)
    constant = jnp.ones((local_heads, head_size), jnp.float32)
    factor = jnp.stack([constant, constant, constant * own_scale[:, None]], axis=1)
    vec = jnp.stack([own_bias.reshape(local_width), factor.reshape(local_width)], axis=0)
    lens = lax.dynamic_slice_in_dim(continuation_lengths, first_group, GRP_WT, 0)[0]
    packed, mixed_heads, log_sums = attend(lens, tokens_all, own_weight, vec, local_heads)
    local_ctx = local_heads * head_size
    context_t = exchange(
        mixed_heads,
        (model_width, row_count),
        (local_ctx, row_count),
        lambda ref, p: ref.at[:, pl.ds(pl.multiple_of(p * row_count, 128), row_count)],
        lambda ref, p: ref.at[pl.ds(pl.multiple_of(p * local_ctx, 16), local_ctx), :],
        1,
        "context_out",
    )
    (
        layer_output,
        grad_total_one,
        grad_context_t,
        wide_sums,
        unit_sums,
        contract_weight_grad,
        expand_weight_grad,
        output_weight_grad,
    ) = feed_forward(
        context_t, tokens, output_cotangent, full_output, full_expand, full_contract, wide_table, unit_table
    )
    con_piece = lax.psum_scatter(contract_weight_grad, "wt", scatter_dimension=0, tiled=True)
    exp_piece = lax.psum_scatter(expand_weight_grad, "wt", scatter_dimension=0, tiled=True)
    out_piece = lax.psum_scatter(output_weight_grad, "wt", scatter_dimension=0, tiled=True)
    arriving = exchange(
        grad_context_t,
        (local_ctx, GLEN),
        (local_ctx, row_count),
        lambda ref, p: ref.at[pl.ds(pl.multiple_of(p * local_ctx, 16), local_ctx), :],
        lambda ref, p: ref.at[:, pl.ds(pl.multiple_of(p * row_count, 128), row_count)],
        2,
        "context_grad_in",
    )
    grad_packed, sums, gate_sums = attend_back(
        lens,
        packed,
        mixed_heads,
        arriving,
        log_sums,
        vec[1:2],
        local_heads,
    )
    head_own = own_mask.astype(jnp.float32) * own_attention[0] / own_gate
    head_own = head_own * jnp.sum(gate_sums[0].reshape(local_heads, head_size), axis=1)
    head_partial = lax.dynamic_update_slice_in_dim(
        jnp.zeros((head_count,), jnp.float32), head_own, seq_index * local_heads, 0
    )
    sums = sums[0].reshape(local_heads, 3, head_size)
    zeros_wide = jnp.zeros((model_width,), jnp.float32)
    at_own = seq_index * local_heads * head_size
    query_bias_grad = lax.dynamic_update_slice_in_dim(zeros_wide, sums[:, 0].reshape(-1), at_own, 0)
    value_bias_grad = lax.dynamic_update_slice_in_dim(zeros_wide, sums[:, 2].reshape(-1), at_own, 0)
    grad_pieces = exchange(
        grad_packed.reshape(seq_count, row_count, local_width),
        (seq_count, row_count, local_width),
        (row_count, local_width),
        lambda ref, p: ref.at[p],
        lambda ref, p: ref.at[p],
        3,
        "packed_grad_out",
    )
    attention_weight_grad = jnp.einsum(
        "td,tc->dc", tokens_all, grad_packed, preferred_element_type=jnp.float32
    )
    tokens_grad = tokens_back(grad_total_one, grad_pieces, full_attention)
    width_rows = jnp.stack(
        [
            query_bias_grad,
            value_bias_grad,
            wide_sums[S_OUT_BIAS],
            wide_sums[S_GAIN1],
            wide_sums[S_SHIFT1],
            wide_sums[S_CON_BIAS],
            wide_sums[S_GAIN2],
            wide_sums[S_SHIFT2],
            wide_sums[S_HIDDEN] * hidden_mask.astype(f32),
        ],
        axis=0,
    )
    unit_rows = jnp.stack(
        [unit_sums[0], unit_sums[1] * (unit_mask.astype(f32) * own_feedforward[0])], axis=0
    )
    own_wide, own_units = model_width // wt_count, unit_gate.shape[0] // wt_count
    by_shard = jnp.concatenate(
        [
            width_rows.reshape(9, wt_count, own_wide).transpose(1, 0, 2).reshape(wt_count, -1),
            unit_rows.reshape(2, wt_count, own_units).transpose(1, 0, 2).reshape(wt_count, -1),
            jnp.broadcast_to(head_partial[None, :], (wt_count, head_count)),
        ],
        axis=1,
    )
    used = by_shard.shape[1]
    by_shard = jnp.pad(by_shard, ((0, 0), (0, -used % 1024))).reshape(wt_count, -1, 128)
    con_sum, exp_sum, out_sum, att_sum, vec_sum = reduce_out(
        wt_count,
        con_piece.reshape(seq_count, own_wide, model_width),
        exp_piece,
        out_piece,
        attention_weight_grad.astype(bf16).reshape(wt_count, own_wide, local_width),
        by_shard,
    )
    vec_sum = vec_sum.reshape(-1)
    wide = [vec_sum[k * own_wide : (k + 1) * own_wide] for k in range(9)]
    base = 9 * own_wide
    units = [vec_sum[base + k * own_units : base + (k + 1) * own_units] for k in range(2)]
    head_gate_grad = vec_sum[base + 2 * own_units : used]
    return (
        layer_output,
        tokens_grad,
        att_sum,
        wide[0],
        wide[1],
        out_sum,
        wide[2],
        wide[3],
        wide[4],
        exp_sum,
        units[0],
        con_sum.reshape(seq_count * own_wide, model_width),
        wide[5],
        wide[6],
        wide[7],
        head_gate_grad,
        wide[8],
        units[1],
    )


def solution(mesh):
    return jax.shard_map(
        local,
        mesh=mesh,
        in_specs=(
            P(("wt", "seq"), None),
            P(("wt", "seq"), None),
            P("wt", None),
            P(),
            P(),
            P("wt", None),
            P(),
            P(),
            P(),
            P("wt", None),
            P(),
            P("wt", None),
            P(),
            P(),
            P(),
            P(),
            P(),
            P(),
            P(),
            P(),
            P(),
            P(),
            P(),
            P(),
        ),
        out_specs=(
            P(("wt", "seq"), None),
            P(("wt", "seq"), None),
            P("wt", None),
            P("wt"),
            P("wt"),
            P("wt", None),
            P("wt"),
            P("wt"),
            P("wt"),
            P("wt", None),
            P("wt"),
            P("wt", None),
            P("wt"),
            P("wt"),
            P("wt"),
            P(),
            P("wt"),
            P("wt"),
        ),
        check_vma=False,
    )
```

```python
import functools

import jax
import jax.numpy as jnp
from jax import lax
from jax.experimental import pallas as pl
from jax.experimental.pallas import tpu as pltpu
from jax.sharding import PartitionSpec as P

PROMPT = 1024
GRP_WT = 1
GLEN = 3072
SHORT = 512
LONG = 1536
HD = 64
TQ = 512
KC = 512

epsilon = 1e-06
score_scale = 0.125
exp2_scale = 0.125 * 1.4426950408889634
root_half = 0.7071067811865476
density_scale = 0.3989422804014327
bf16 = jnp.bfloat16
f32 = jnp.float32

NT = (((1,), (1,)), ((), ()))
NN = (((1,), (0,)), ((), ()))
TN = (((0,), (0,)), ((), ()))


def mm(a, b, dims=NN):
    return lax.dot_general(a, b, dims, preferred_element_type=f32)


def query_tiles(short_first, tile):
    short_at = pl.multiple_of(jnp.where(short_first, PROMPT, PROMPT + LONG), SHORT)
    long_at = pl.multiple_of(jnp.where(short_first, PROMPT + SHORT, PROMPT), SHORT)
    for base, own_at, own_len, rows in (
        (0, 0, 0, PROMPT),
        (short_at, short_at, SHORT, SHORT),
        (long_at, long_at, LONG, LONG),
    ):

        def step(i, carry, base=base, own_at=own_at, own_len=own_len):
            tile(pl.multiple_of(base + i * TQ, TQ), own_at, own_len)
            return carry

        lax.fori_loop(0, rows // TQ, step, 0)


def attend_kernel(
    heads, lens_ref, tok_ref, w_ref, vec_ref, packed_ref, ctx_ref, lse_ref, q_sc, k_sc, vt_sc
):
    def project(i, carry):
        rows = pl.ds(pl.multiple_of(i * TQ, TQ), TQ)
        x = mm(tok_ref[rows, :], w_ref[...]) + vec_ref[0:1, :]
        x = (x * vec_ref[1:2, :]).astype(bf16)
        for h in range(heads):
            at = 3 * HD * h
            packed_ref[h, rows, :] = x[:, at : at + 3 * HD]
            q_sc[h, rows, :] = x[:, at : at + HD]
            k_sc[h, rows, :] = x[:, at + HD : at + 2 * HD]
            vt_sc[h, 0:HD, rows] = x[:, at + 2 * HD : at + 3 * HD].T
        return carry

    lax.fori_loop(0, GLEN // TQ, project, 0)
    for h in range(heads):
        vt_sc[h, HD : HD + 16, :] = jnp.ones((16, GLEN), bf16)

    def one_head(h, carry):
        def tile(q_at, own_at, own_len):
            rows = pl.ds(q_at, TQ)
            q = q_sc[h, rows, :]
            s1 = mm(k_sc[h, 0:PROMPT, :], q, NT)
            top = jnp.max(s1, axis=0, keepdims=True)
            if own_len:
                own = pl.ds(own_at, own_len)
                s2 = mm(k_sc[h, own, :], q, NT)
                top = jnp.maximum(top, jnp.max(s2, axis=0, keepdims=True))
            top = top * exp2_scale
            p1 = jnp.exp2(s1 * exp2_scale - top)
            o = mm(vt_sc[h, :, 0:PROMPT], p1.astype(bf16))
            total = jnp.sum(p1, axis=0, keepdims=True)
            if own_len:
                p2 = jnp.exp2(s2 * exp2_scale - top)
                o = o + mm(vt_sc[h, :, own], p2.astype(bf16))
                total = total + jnp.sum(p2, axis=0, keepdims=True)
            ctx_ref[pl.ds(pl.multiple_of(HD * h, HD), HD), rows] = (o[0:HD, :] / total).astype(bf16)
            lse_ref[h, :, rows] = top + jnp.log2(total)

        query_tiles(lens_ref[0] == SHORT, tile)
        return carry

    lax.fori_loop(0, heads, one_head, 0)


def attend(lens, tokens_all, weight, vec, heads):
    width = 3 * HD * heads
    whole = pl.BlockSpec(memory_space=pltpu.VMEM)
    return pl.pallas_call(
        functools.partial(attend_kernel, heads),
        out_shape=(
            jax.ShapeDtypeStruct((heads, GLEN, 3 * HD), bf16),
            jax.ShapeDtypeStruct((HD * heads, GLEN), bf16),
            jax.ShapeDtypeStruct((heads, 1, GLEN), f32),
        ),
        in_specs=[pl.BlockSpec(memory_space=pltpu.SMEM), whole, whole, whole],
        out_specs=(whole, whole, whole),
        scratch_shapes=[
            pltpu.VMEM((heads, GLEN, HD), bf16),
            pltpu.VMEM((heads, GLEN, HD), bf16),
            pltpu.VMEM((heads, HD + 16, GLEN), bf16),
        ],
        compiler_params=pltpu.CompilerParams(vmem_limit_bytes=56 * 2**20),
        cost_estimate=pl.CostEstimate(
            flops=2 * GLEN * 768 * width + heads * 4 * 256 * 5767168,
            bytes_accessed=2 * GLEN * (768 + width),
            transcendentals=heads * 5767168,
        ),
        name="attend",
    )(lens, tokens_all, weight, vec)


def attend_back_kernel(
    place_ref, packed_ref, ctx_ref, gctx_ref, lse_ref, scale_ref,
    out_ref, own_ref, p1_ref, p2_ref, p3_ref, sums_ref, gate_ref,
    q_sc, k_sc, v_sc, kt_sc, delta_sc, dqt_sc, dk_sc, dv_sc,
):
    def split(i, carry):
        rows = pl.ds(pl.multiple_of(i * TQ, TQ), TQ)
        x = packed_ref[0, rows, :]
        inner = gctx_ref[:, rows].astype(f32) * ctx_ref[:, rows].astype(f32)
        delta_sc[:, rows] = jnp.sum(inner, axis=0, keepdims=True)
        q_sc[rows, :] = x[:, 0:HD]
        k = x[:, HD : 2 * HD]
        k_sc[rows, :] = k
        kt_sc[:, rows] = k.T
        v_sc[rows, :] = x[:, 2 * HD : 3 * HD]
        return carry

    lax.fori_loop(0, GLEN // TQ, split, 0)
    dk_sc[...] = jnp.zeros_like(dk_sc)
    dv_sc[...] = jnp.zeros_like(dv_sc)

    def tile(q_at, own_at, own_len):
        rows = pl.ds(q_at, TQ)
        q = q_sc[rows, :]
        g = gctx_ref[:, rows]
        lse = lse_ref[0, :, rows]
        delta = delta_sc[:, rows]
        dq = jnp.zeros((HD, TQ), f32)
        starts = [j * KC for j in range(PROMPT // KC)]
        starts = starts + [own_at + j * KC for j in range(own_len // KC)]
        for start in starts:
            keys = pl.ds(start, KC)
            s = mm(k_sc[keys, :], q, NT)
            p = jnp.exp2(s * exp2_scale - lse)
            dp = mm(v_sc[keys, :], g)
            ds = (p * (dp - delta)).astype(bf16)
            dv_sc[keys, :] += mm(p.astype(bf16), g, NT)
            dk_sc[keys, :] += mm(ds, q)
            dq = dq + mm(kt_sc[:, keys], ds)
        dqt_sc[:, rows] = dq * score_scale

    query_tiles(place_ref[1] == SHORT, tile)
    sums_ref[...] = jnp.zeros_like(sums_ref)
    gate_ref[...] = jnp.zeros_like(gate_ref)

    def place(i, carry):
        rows = pl.ds(pl.multiple_of(i * TQ, TQ), TQ)
        dq = dqt_sc[:, rows].T.astype(bf16)
        dk = (dk_sc[rows, :] * score_scale).astype(bf16)
        dv = dv_sc[rows, :].astype(bf16).astype(f32)
        gate_ref[0:1, :] += jnp.sum(dv * v_sc[rows, :].astype(f32), axis=0, keepdims=True)
        dv = (dv * scale_ref[0]).astype(bf16)
        out_ref[rows, 0:HD] = dq
        out_ref[rows, HD : 2 * HD] = dk
        out_ref[rows, 2 * HD : 3 * HD] = dv
        sums_ref[0:1, :] += jnp.sum(dq.astype(f32), axis=0, keepdims=True)
        sums_ref[1:2, :] += jnp.sum(dv.astype(f32), axis=0, keepdims=True)
        return carry

    lax.fori_loop(0, GLEN // TQ, place, 0)
    s = place_ref[0]
    count = own_ref.shape[0]
    for k, ref in enumerate((own_ref, p1_ref, p2_ref, p3_ref)):
        ref[...] = out_ref[pl.ds(pl.multiple_of(flip(s, k) * count, count), count), :]


def attend_back(place, packed, ctx, gctx, lse, scale, h):
    heads = packed.shape[0]
    rows64 = pltpu.VMEM((GLEN, HD), bf16)
    piece = (GLEN // 4, 3 * HD)

    def spec(shape, at):
        return pl.BlockSpec(shape, lambda i: at)

    return pl.pallas_call(
        attend_back_kernel,
        grid=(1,),
        out_shape=(jax.ShapeDtypeStruct((GLEN, 3 * HD), bf16),)
        + (jax.ShapeDtypeStruct(piece, bf16),) * 4
        + (jax.ShapeDtypeStruct((8, HD), f32), jax.ShapeDtypeStruct((8, HD), f32)),
        in_specs=[
            pl.BlockSpec(memory_space=pltpu.SMEM),
            spec((1, GLEN, 3 * HD), (h, 0, 0)),
            spec((HD, GLEN), (h, 0)),
            spec((HD, GLEN), (h, 0)),
            spec((1, 1, GLEN), (h, 0, 0)),
            spec((1, 1, HD), (h, 0, 0)),
        ],
        out_specs=(spec((GLEN, 3 * HD), (0, 0)),)
        + (spec(piece, (0, 0)),) * 4
        + (spec((8, HD), (0, 0)),) * 2,
        scratch_shapes=[
            rows64,
            rows64,
            rows64,
            pltpu.VMEM((HD, GLEN), bf16),
            pltpu.VMEM((1, GLEN), f32),
            pltpu.VMEM((HD, GLEN), f32),
            pltpu.VMEM((GLEN, HD), f32),
            pltpu.VMEM((GLEN, HD), f32),
        ],
        compiler_params=pltpu.CompilerParams(vmem_limit_bytes=48 * 2**20),
        cost_estimate=pl.CostEstimate(
            flops=10 * 256 * 5767168, bytes_accessed=2 * GLEN * (9 * HD), transcendentals=5767168
        ),
        name="attend_back",
    )(place, packed, ctx, gctx, lse, scale)


def projection_grad_kernel(steps, n, tok_ref, *refs):
    g_refs, out_ref, acc = refs[:-2], refs[-2], refs[-1]
    i = pl.program_id(0)

    @pl.when(i == 0)
    def _():
        acc[...] = jnp.zeros_like(acc)

    cols = 3 * HD
    for h, g_ref in enumerate(g_refs):
        acc[:, cols * h : cols * (h + 1)] += mm(tok_ref[...], g_ref[...], TN)

    @pl.when(i == steps - 1)
    def _():
        own = out_ref.shape[1]
        for k in range(n):
            out_ref[k] = acc[k * own : (k + 1) * own, :].astype(bf16)


def projection_grad(n, tokens_all, grads):
    rows, d = tokens_all.shape
    steps = 4
    block = rows // steps
    width = 3 * HD * len(grads)
    return pl.pallas_call(
        functools.partial(projection_grad_kernel, steps, n),
        out_shape=jax.ShapeDtypeStruct((n, d // n, width), bf16),
        grid=(steps,),
        in_specs=[pl.BlockSpec((block, d), lambda i: (i, 0))]
        + [pl.BlockSpec((block, 3 * HD), lambda i: (i, 0))] * len(grads),
        out_specs=pl.BlockSpec((n, d // n, width), lambda i: (0, 0, 0)),
        scratch_shapes=[pltpu.VMEM((d, width), f32)],
        compiler_params=pltpu.CompilerParams(vmem_limit_bytes=48 * 2**20),
        cost_estimate=pl.CostEstimate(
            flops=2 * rows * d * width, bytes_accessed=2 * rows * (d + width), transcendentals=0
        ),
        name="projection_grad",
    )(tokens_all, *grads)


def send(src, dst, sems, k, peer):
    copy = pltpu.make_async_remote_copy(
        src_ref=src,
        dst_ref=dst,
        send_sem=sems[0].at[k],
        recv_sem=sems[1].at[k],
        device_id=peer,
        device_id_type=pl.DeviceIdType.MESH,
    )
    copy.start()
    return copy


def meet(peers):
    barrier = pltpu.get_barrier_semaphore()
    for peer in peers:
        pl.semaphore_signal(barrier, inc=1, device_id=peer, device_id_type=pl.DeviceIdType.MESH)
    pl.semaphore_wait(barrier, len(peers))


def flip(index, bits):
    for bit in (1, 2):
        if bits & bit:
            index = index + bit - 2 * bit * ((index // bit) % 2)
    return index


def remote_params(number):
    return pltpu.CompilerParams(
        collective_id=number, has_side_effects=True, vmem_limit_bytes=56 * 2**20
    )


ANYWHERE = pl.BlockSpec(memory_space=pl.ANY)
IN_VMEM = pl.BlockSpec(memory_space=pltpu.VMEM)


def dma_sems(count):
    return [pltpu.SemaphoreType.DMA((count,)), pltpu.SemaphoreType.DMA((count,))]


def gather_kernel(
    n, tok_ref, cols_ref, out_ref, tok_all, cols_all, out_all,
    tok_buf, cols_buf, out_buf, local_sem, s_tok, r_tok, s_w, r_w, s_f, r_f,
):
    s, w = lax.axis_index("seq"), lax.axis_index("wt")
    rows = tok_ref.shape[0]
    half = rows // 2
    by_x, by_y, mate = (flip(s, 1), w), (flip(s, 2), w), (s, flip(w, 1))
    far = [(s, lax.rem(w + 2 * j, n)) for j in range(1, n // 2)]
    meet([by_x, by_y, mate] + far)

    def part(owner, k):
        return pl.ds(pl.multiple_of(owner * rows + k * half, half), half)

    tok = (s_tok, r_tok)
    first = [pl.ds(0, half), pl.ds(half, half)]
    x0 = send(tok_ref.at[first[0]], tok_all.at[part(s, 0)], tok, 0, by_x)
    y1 = send(tok_ref.at[first[1]], tok_all.at[part(s, 1)], tok, 1, by_y)
    x1 = send(tok_ref.at[first[1]], tok_all.at[part(s, 1)], tok, 2, by_x)
    y0 = send(tok_ref.at[first[0]], tok_all.at[part(s, 0)], tok, 3, by_y)
    held = []
    for k, peer in enumerate(far + [mate]):
        for i, (src, dst) in enumerate(((cols_ref, cols_all), (out_ref, out_all))):
            held.append(send(src, dst.at[w], (s_w, r_w), 2 * k + i, peer))
    own = []
    for i, (src, buf) in enumerate(((tok_ref, tok_buf), (cols_ref, cols_buf), (out_ref, out_buf))):
        own.append(pltpu.make_async_copy(src, buf, local_sem.at[i]))
        own[-1].start()
    for copy in own:
        copy.wait()
    targets = (
        (tok_buf, tok_all.at[pl.ds(pl.multiple_of(s * rows, rows), rows)]),
        (cols_buf, cols_all.at[w]),
        (out_buf, out_all.at[w]),
    )
    own = []
    for i, (buf, dst) in enumerate(targets):
        own.append(pltpu.make_async_copy(buf, dst, local_sem.at[3 + i]))
        own[-1].start()
    passed = []
    x0.wait_recv()
    there = tok_all.at[part(flip(s, 1), 0)]
    passed.append(send(there, there, tok, 4, by_y))
    y1.wait_recv()
    there = tok_all.at[part(flip(s, 2), 1)]
    passed.append(send(there, there, tok, 5, by_x))
    for j in range(1, n // 2):
        origin = lax.rem(w + n - 2 * j, n)
        for i, dst in enumerate((cols_all, out_all)):
            k = 2 * (j - 1) + i
            held[k].wait_recv()
            passed.append(send(dst.at[origin], dst.at[origin], (s_f, r_f), k, mate))
    for copy in own:
        copy.wait()
    x1.wait_recv()
    y0.wait_recv()
    for copy in held[n - 2 :]:
        copy.wait_recv()
    for copy in passed:
        copy.wait_recv()
    for copy in [x0, x1, y0, y1] + held + passed:
        copy.wait_send()


def gather_in(n, tokens, own_columns, output_weight):
    rows, d = tokens.shape
    return pl.pallas_call(
        functools.partial(gather_kernel, n),
        out_shape=(
            jax.ShapeDtypeStruct((4 * rows, d), bf16),
            jax.ShapeDtypeStruct((n,) + own_columns.shape, bf16),
            jax.ShapeDtypeStruct((n,) + output_weight.shape, bf16),
        ),
        in_specs=[ANYWHERE] * 3,
        out_specs=(ANYWHERE,) * 3,
        scratch_shapes=[
            pltpu.VMEM(tokens.shape, bf16),
            pltpu.VMEM(own_columns.shape, bf16),
            pltpu.VMEM(output_weight.shape, bf16),
            pltpu.SemaphoreType.DMA((6,)),
        ]
        + dma_sems(6)
        + dma_sems(n)
        + dma_sems(n - 2),
        compiler_params=remote_params(0),
        name="gather_in",
    )(tokens, own_columns, output_weight)


def exchange_kernel(src_of, dst_of, x_ref, o_ref, buf, local_sem, s_sem, r_sem):
    s, w = lax.axis_index("seq"), lax.axis_index("wt")
    others = [flip(s, k) for k in (1, 2, 3)]
    meet([(p, w) for p in others])
    copies = [
        send(src_of(x_ref, p), dst_of(o_ref, s), (s_sem, r_sem), k, (p, w))
        for k, p in enumerate(others)
    ]
    come = pltpu.make_async_copy(src_of(x_ref, s), buf, local_sem.at[0])
    come.start()
    come.wait()
    go = pltpu.make_async_copy(buf, dst_of(o_ref, s), local_sem.at[1])
    go.start()
    go.wait()
    for copy in copies:
        copy.wait()


def exchange(x, out_shape, part_shape, src_of, dst_of, number, name):
    return pl.pallas_call(
        functools.partial(exchange_kernel, src_of, dst_of),
        out_shape=jax.ShapeDtypeStruct(out_shape, x.dtype),
        in_specs=[ANYWHERE],
        out_specs=ANYWHERE,
        scratch_shapes=[pltpu.VMEM(part_shape, x.dtype), pltpu.SemaphoreType.DMA((2,))] + dma_sems(3),
        compiler_params=remote_params(number),
        name=name,
    )(x)


def reduce_kernel(
    n, con_ref, out_ref, att_ref, vec_ref, con_o, out_o, att_o, vec_o,
    r_con, r_out, h_att, m_att, r_att, r_vec, r_vec2, m_vec, m_ce, g_ce, m_row, g_att,
    s_a, r_a, s_b, r_b, s_c, r_c, s_e, r_e, s_f, r_f, s_g, r_g, s_h, r_h, s_i, r_i,
):
    s, w = lax.axis_index("seq"), lax.axis_index("wt")
    z, c = w // 2, lax.rem(w, 2)
    others = [flip(s, k) for k in (1, 2, 3)]
    seq_peers = [(p, w) for p in others]
    mate = (s, flip(w, 1))
    wt_peers = [(s, lax.rem(w + j, n)) for j in range(1, n)]
    meet(seq_peers + wt_peers)
    pair = [
        send(att_ref.at[2 * k + 1 - c], h_att.at[k], (s_a, r_a), k, mate) for k in range(n // 2)
    ]
    vecs = [
        send(vec_ref.at[lax.rem(w + j, n)], r_vec.at[w], (s_b, r_b), j - 1, wt_peers[j - 1])
        for j in range(1, n)
    ]
    cons = [
        send(con_ref.at[p], r_con.at[s], (s_c, r_c), k, (p, w)) for k, p in enumerate(others)
    ]
    outs = [send(out_ref, r_out.at[s], (s_e, r_e), k, (p, w)) for k, p in enumerate(others)]
    r_con[s] = con_ref[s]
    r_out[s] = out_ref[...]
    r_vec[w] = vec_ref[w]
    for copy in pair:
        copy.wait_recv()
    for k in range(n // 2):
        m_att[k] = (att_ref[2 * k + c].astype(f32) + h_att[k].astype(f32)).astype(bf16)
    zs = [lax.rem(z + j, n // 2) for j in range(1, n // 2)]
    atts = [
        send(m_att.at[k], r_att.at[z], (s_f, r_f), j, (s, 2 * k + c)) for j, k in enumerate(zs)
    ]
    r_att[z] = m_att[z]
    for copy in vecs:
        copy.wait_recv()
    total = r_vec[0]
    for k in range(1, n):
        total = total + r_vec[k]
    m_vec[...] = total
    vecs2 = [send(m_vec, r_vec2.at[s], (s_g, r_g), k, p) for k, p in enumerate(seq_peers)]
    r_vec2[s] = total

    def add4(ref):
        t = [ref[k].astype(f32) for k in range(4)]
        return (t[0] + t[1]) + (t[2] + t[3])

    for copy in cons:
        copy.wait_recv()
    m_ce[...] = add4(r_con).astype(bf16)
    g_ce[s] = m_ce[...]
    ces = [send(m_ce, g_ce.at[s], (s_h, r_h), k, p) for k, p in enumerate(seq_peers)]
    for copy in atts:
        copy.wait_recv()
    row = r_att[0].astype(f32)
    for k in range(1, n // 2):
        row = row + r_att[k].astype(f32)
    m_row[...] = row.astype(bf16)
    g_att[s] = m_row[...]
    rows = [send(m_row, g_att.at[s], (s_i, r_i), k, p) for k, p in enumerate(seq_peers)]
    for copy in outs:
        copy.wait_recv()
    out_o[...] = add4(r_out)
    for copy in vecs2:
        copy.wait_recv()
    vec_o[...] = (r_vec2[0] + r_vec2[1]) + (r_vec2[2] + r_vec2[3])
    for copy in ces:
        copy.wait_recv()
    for k in range(4):
        con_o[k] = g_ce[k].astype(f32)
    for copy in rows:
        copy.wait_recv()
    cols = g_att.shape[2]
    for k in range(4):
        att_o[:, k * cols : (k + 1) * cols] = g_att[k].astype(f32)
    for copy in pair + vecs + cons + outs + atts + vecs2 + ces + rows:
        copy.wait_send()


def reduce_out(n, con, out, att, vec):
    r, d = out.shape
    cols = att.shape[2]
    vshape = vec.shape[1:]
    counts = (n // 2, n - 1, 3, 3, n // 2 - 1, 3, 3, 3)
    return pl.pallas_call(
        functools.partial(reduce_kernel, n),
        out_shape=(
            jax.ShapeDtypeStruct(con.shape, f32),
            jax.ShapeDtypeStruct(out.shape, f32),
            jax.ShapeDtypeStruct((r, 4 * cols), f32),
            jax.ShapeDtypeStruct(vshape, f32),
        ),
        in_specs=[IN_VMEM] * 4,
        out_specs=(IN_VMEM,) * 4,
        scratch_shapes=[
            pltpu.VMEM((4, r, d), bf16),
            pltpu.VMEM((4, r, d), bf16),
            pltpu.VMEM((n // 2, r, cols), bf16),
            pltpu.VMEM((n // 2, r, cols), bf16),
            pltpu.VMEM((n // 2, r, cols), bf16),
            pltpu.VMEM((n,) + vshape, f32),
            pltpu.VMEM((4,) + vshape, f32),
            pltpu.VMEM(vshape, f32),
            pltpu.VMEM((r, d), bf16),
            pltpu.VMEM((4, r, d), bf16),
            pltpu.VMEM((r, cols), bf16),
            pltpu.VMEM((4, r, cols), bf16),
        ]
        + [sem for count in counts for sem in dma_sems(count)],
        compiler_params=remote_params(4),
        name="reduce_out",
    )(con, out, att, vec)


def tokens_back_kernel(heads, place_ref, base_ref, w_ref, *refs):
    o_ref, pieces = refs[-1], refs[:-1]
    cols = 3 * HD
    for s in range(4):

        @pl.when(place_ref[0] == s)
        def _(s=s):
            total = base_ref[...]
            for h in range(heads):
                for k in range(4):
                    at = (heads * (s ^ k) + h) * cols
                    total = total + mm(pieces[4 * h + k][...], w_ref[:, at : at + cols], NT)
            o_ref[...] = total


def tokens_back(place, base, weight, pieces):
    rows, d = base.shape
    block = rows // 3
    cols = 3 * HD
    return pl.pallas_call(
        functools.partial(tokens_back_kernel, len(pieces) // 4),
        out_shape=jax.ShapeDtypeStruct((rows, d), f32),
        grid=(3,),
        in_specs=[
            pl.BlockSpec(memory_space=pltpu.SMEM),
            pl.BlockSpec((block, d), lambda i: (i, 0)),
            pl.BlockSpec(weight.shape, lambda i: (0, 0)),
        ]
        + [pl.BlockSpec((block, cols), lambda i: (i, 0))] * len(pieces),
        out_specs=pl.BlockSpec((block, d), lambda i: (i, 0)),
        compiler_params=pltpu.CompilerParams(vmem_limit_bytes=48 * 2**20),
        cost_estimate=pl.CostEstimate(
            flops=2 * rows * d * cols * len(pieces),
            bytes_accessed=8 * rows * d + 8 * d * cols * len(pieces),
            transcendentals=0,
        ),
        name="tokens_back",
    )(place, base, weight, *pieces)


(OUT_BIAS, GAIN1, SHIFT1, HIDDEN_SCALE, CON_BIAS, GAIN2, SHIFT2) = range(7)
(S_OUT_BIAS, S_GAIN1, S_SHIFT1, S_CON_BIAS, S_GAIN2, S_SHIFT2, S_HIDDEN) = range(7)


def gelu_parts(x):
    bell = jnp.exp(-0.5 * (x * x))
    t = 1.0 / (1.0 + (0.3275911 * root_half) * jnp.abs(x))
    poly = t * (
        0.127414796 + t * (-0.142248368 + t * (0.7107068705 + t * (-0.7265760135 + t * 0.5307027145)))
    )
    tail = poly * bell
    cumulative = jnp.where(x < 0.0, tail, 1.0 - tail)
    return x * cumulative, cumulative + x * bell * density_scale


def norm_parts(summed):
    centre = summed - jnp.mean(summed, axis=-1, keepdims=True)
    inverse = lax.rsqrt(jnp.mean(centre * centre, axis=-1, keepdims=True) + epsilon)
    return (centre * inverse, inverse)


def norm_back(grad_normed, normed, inverse):
    return inverse * (
        grad_normed
        - jnp.mean(grad_normed, axis=-1, keepdims=True)
        - normed * jnp.mean(grad_normed * normed, axis=-1, keepdims=True)
    )


def feed_forward_kernel(
    steps, chunk,
    place_ref, ctx_ref, tok_ref, cot_ref, wo_ref, we_ref, wc_ref, wide_ref, unit_ref,
    lo_ref, dt1_ref, gctx_ref, sw_ref, su_ref, dwc_ref, mine_ref, mate_ref, dwo_ref,
    act_sc, gh_sc, low_sc, gb_sc, ga_sc, ctx_sc, gelu_sc, slope_sc,
):
    i = pl.program_id(0)
    block = tok_ref.shape[0]
    units = we_ref.shape[1]
    rows = pl.ds(pl.multiple_of(i * block, block), block)

    @pl.when(i == 0)
    def _():
        sw_ref[...] = jnp.zeros_like(sw_ref)
        su_ref[...] = jnp.zeros_like(su_ref)

    def wide(k):
        return wide_ref[k : k + 1, :]

    def add_sum(ref, k, cols, value):
        ref[k : k + 1, cols] += jnp.sum(value, axis=0, keepdims=True)

    full = slice(None)
    ctx = ctx_ref[...]
    ctx_sc[:, rows] = ctx
    summed = mm(ctx, wo_ref[...], TN) + wide(OUT_BIAS) + tok_ref[...].astype(f32)
    n1, inv1 = norm_parts(summed)
    s1 = n1 * wide(GAIN1) + wide(SHIFT1)
    hs = wide(HIDDEN_SCALE)
    first = s1 * hs
    low = first.astype(bf16)
    low_sc[rows, :] = low
    branch = first + wide(CON_BIAS)
    for j in range(units // chunk):
        cols = slice(j * chunk, (j + 1) * chunk)
        hidden = mm(low, we_ref[:, cols]) + unit_ref[0:1, cols]
        gelu, slope = gelu_parts(hidden)
        scale = unit_ref[1:2, cols]
        gelu_sc[:, cols] = gelu.astype(gelu_sc.dtype)
        slope_sc[:, cols] = (slope * scale).astype(slope_sc.dtype)
        act = (gelu * scale).astype(bf16)
        act_sc[rows, cols] = act
        branch = branch + mm(act, wc_ref[cols, :])
    n2, inv2 = norm_parts(branch)
    s2 = n2 * wide(GAIN2) + wide(SHIFT2)
    lo_ref[...] = (s2 * hs).astype(bf16)
    dy = cot_ref[...].astype(f32)
    e2 = dy * hs
    add_sum(sw_ref, S_GAIN2, full, e2 * n2)
    add_sum(sw_ref, S_SHIFT2, full, e2)
    dt2 = norm_back(e2 * wide(GAIN2), n2, inv2)
    gb = dt2.astype(bf16)
    gb_sc[rows, :] = gb
    add_sum(sw_ref, S_CON_BIAS, full, gb.astype(f32))
    d_first = dt2
    for j in range(units // chunk):
        cols = slice(j * chunk, (j + 1) * chunk)
        d_act = mm(gb, wc_ref[cols, :], NT)
        add_sum(su_ref, 1, cols, d_act * gelu_sc[:, cols].astype(f32))
        gh = d_act * slope_sc[:, cols].astype(f32)
        add_sum(su_ref, 0, cols, gh)
        gh = gh.astype(bf16)
        gh_sc[rows, cols] = gh
        d_first = d_first + mm(gh, we_ref[:, cols], NT)
    e1 = d_first * hs
    add_sum(sw_ref, S_GAIN1, full, e1 * n1)
    add_sum(sw_ref, S_SHIFT1, full, e1)
    add_sum(sw_ref, S_HIDDEN, full, dy * s2 + d_first * s1)
    dt1 = norm_back(e1 * wide(GAIN1), n1, inv1)
    dt1_ref[...] = dt1
    ga = dt1.astype(bf16)
    ga_sc[rows, :] = ga
    add_sum(sw_ref, S_OUT_BIAS, full, ga.astype(f32))
    gctx_ref[...] = mm(wo_ref[...], ga, NT).astype(bf16)

    @pl.when(i == steps - 1)
    def _():
        for j in range(units // chunk):
            cols = slice(j * chunk, (j + 1) * chunk)
            dwc_ref[cols, :] = mm(act_sc[:, cols], gb_sc[...], TN).astype(bf16)
            part = mm(low_sc[...], gh_sc[:, cols], TN).astype(bf16)
            own, wide_cols = mine_ref.shape[2:]
            for c in range(2):

                @pl.when(place_ref[2] == c)
                def _(part=part, j=j, c=c):
                    for q in range(chunk // wide_cols):
                        at = j * (chunk // wide_cols) + q
                        inner = slice(q * wide_cols, (q + 1) * wide_cols)
                        for z in range(mine_ref.shape[1]):
                            mine = (2 * z + c) * own
                            mate = (2 * z + 1 - c) * own
                            mine_ref[at, z] = part[mine : mine + own, inner]
                            mate_ref[at, z] = part[mate : mate + own, inner]

        dwo_ref[...] = mm(ctx_sc[...], ga_sc[...]).astype(bf16)


def feed_forward(n, place, ctx_t, tokens, cotangent, wo, we, wc, wide, unit):
    steps, chunk, keep = 3, 768, f32
    rows, d = tokens.shape
    units = we.shape[1]
    block = rows // steps
    halves = (4, n // 2, d // n, units // 4)
    tile = pl.BlockSpec((block, d), lambda i: (i, 0))
    lanes = pl.BlockSpec((d, block), lambda i: (0, i))

    def once(shape):
        return pl.BlockSpec(shape, lambda i: (0, 0), pipeline_mode=pl.Buffered(1))

    def once4(shape):
        return pl.BlockSpec(shape, lambda i: (0, 0, 0, 0), pipeline_mode=pl.Buffered(1))

    return pl.pallas_call(
        functools.partial(feed_forward_kernel, steps, chunk),
        out_shape=(
            jax.ShapeDtypeStruct((rows, d), bf16),
            jax.ShapeDtypeStruct((rows, d), f32),
            jax.ShapeDtypeStruct((d, rows), bf16),
            jax.ShapeDtypeStruct((8, d), f32),
            jax.ShapeDtypeStruct((8, units), f32),
            jax.ShapeDtypeStruct((units, d), bf16),
            jax.ShapeDtypeStruct(halves, bf16),
            jax.ShapeDtypeStruct(halves, bf16),
            jax.ShapeDtypeStruct((d, d), bf16),
        ),
        grid=(steps,),
        in_specs=[
            pl.BlockSpec(memory_space=pltpu.SMEM),
            lanes, tile, tile, once((d, d)), once((d, units)), once((units, d)), once((8, d)), once((8, units)),
        ],
        out_specs=(
            tile, tile, lanes, once((8, d)), once((8, units)), once((units, d)),
            once4(halves), once4(halves), once((d, d)),
        ),
        scratch_shapes=[
            pltpu.VMEM((rows, units), bf16),
            pltpu.VMEM((rows, units), bf16),
            pltpu.VMEM((rows, d), bf16),
            pltpu.VMEM((rows, d), bf16),
            pltpu.VMEM((rows, d), bf16),
            pltpu.VMEM((d, rows), bf16),
            pltpu.VMEM((block, units), keep),
            pltpu.VMEM((block, units), keep),
        ],
        compiler_params=pltpu.CompilerParams(vmem_limit_bytes=60 * 2**20),
        cost_estimate=pl.CostEstimate(
            flops=rows * d * (12 * units + 6 * d),
            bytes_accessed=4 * d * (4 * units + 2 * d) + 12 * rows * d,
            transcendentals=2 * rows * units,
        ),
        name="feed_forward",
    )(place, ctx_t, tokens, cotangent, wo, we, wc, wide, unit)


def expand_reduce(mine, got, s, w, n):
    z = w // 2

    def at(q):
        return lax.dynamic_index_in_dim(mine, q, 0, False).astype(f32) + lax.dynamic_index_in_dim(
            got, q, 0, False
        ).astype(f32)

    own = at(s)
    for k in (1, 2, 3):
        piece = at(s ^ k).astype(bf16)
        own = own + lax.ppermute(piece, "seq", [(j, j ^ k) for j in range(4)]).astype(f32)
    total = lax.dynamic_index_in_dim(own, z, 0, False)
    for j in range(1, n // 2):
        piece = lax.dynamic_index_in_dim(own, lax.rem(z + j, n // 2), 0, False).astype(bf16)
        total = total + lax.ppermute(piece, "wt", [(k, (k + 2 * j) % n) for k in range(n)]).astype(f32)
    total = total.astype(bf16)
    parts = [total] + [lax.ppermute(total, "seq", [(j, j ^ k) for j in range(4)]) for k in (1, 2, 3)]
    parts = jnp.stack(parts)
    return jnp.concatenate(
        [lax.dynamic_index_in_dim(parts, s ^ q, 0, False) for q in range(4)], axis=1
    ).astype(f32)


def local(
    tokens,
    output_cotangent,
    attention_weight,
    query_bias,
    value_bias,
    output_weight,
    output_bias,
    first_gain,
    first_shift,
    expand_weight,
    expand_bias,
    contract_weight,
    contract_bias,
    second_gain,
    second_shift,
    head_gate,
    hidden_gate,
    unit_gate,
    head_mask,
    hidden_mask,
    unit_mask,
    attention_mask,
    feedforward_mask,
    continuation_lengths,
):
    row_count = tokens.shape[0]
    seq_count = lax.axis_size("seq")
    head_count = head_gate.shape[0]
    model_width = hidden_gate.shape[0]
    head_size = model_width // head_count
    local_heads = head_count // seq_count
    seq_index = lax.axis_index("seq")
    wt_index = lax.axis_index("wt")
    local_width = 3 * head_size * local_heads
    wt_count = lax.axis_size("wt")
    own_columns = lax.dynamic_slice_in_dim(attention_weight, seq_index * local_width, local_width, 1)
    tokens_all, own_weight, full_output = gather_in(wt_count, tokens, own_columns, output_weight)
    own_weight = own_weight.reshape(model_width, local_width)
    full_output = full_output.reshape(model_width, model_width)
    full_expand = lax.all_gather(expand_weight, "wt", axis=0, tiled=True)
    full_contract = lax.all_gather(contract_weight, "wt", axis=0, tiled=True)
    full_attention = lax.all_gather(attention_weight, "wt", axis=0, tiled=True)
    first_group = wt_index * GRP_WT
    own_attention = lax.dynamic_slice_in_dim(attention_mask, first_group, GRP_WT, 0).astype(
        jnp.float32
    )
    own_feedforward = lax.dynamic_slice_in_dim(feedforward_mask, first_group, GRP_WT, 0).astype(
        jnp.float32
    )
    head_scale = head_mask.astype(jnp.float32) * head_gate
    hidden_scale = hidden_mask.astype(jnp.float32) * hidden_gate
    unit_scale = unit_mask.astype(jnp.float32) * unit_gate
    wide_table = jnp.stack(
        [
            output_bias.astype(f32),
            first_gain.astype(f32),
            first_shift.astype(f32),
            hidden_scale,
            contract_bias.astype(f32),
            second_gain.astype(f32),
            second_shift.astype(f32),
            hidden_scale,
        ],
        axis=0,
    )
    unit_row = unit_scale * own_feedforward[0]
    unit_table = jnp.stack([expand_bias.astype(f32)] + [unit_row] * 7, axis=0)
    bias_table = jnp.stack(
        [
            query_bias.astype(jnp.float32).reshape(head_count, head_size),
            jnp.zeros((head_count, head_size), jnp.float32),
            value_bias.astype(jnp.float32).reshape(head_count, head_size),
        ],
        axis=1,
    )
    own_scale = lax.dynamic_slice_in_dim(head_scale, seq_index * local_heads, local_heads, 0)
    own_scale = own_scale * own_attention[0]
    own_mask = lax.dynamic_slice_in_dim(head_mask, seq_index * local_heads, local_heads, 0)
    own_gate = lax.dynamic_slice_in_dim(head_gate, seq_index * local_heads, local_heads, 0)
    own_bias = lax.dynamic_slice_in_dim(bias_table, seq_index * local_heads, local_heads, 0)
    constant = jnp.ones((local_heads, head_size), jnp.float32)
    factor = jnp.stack([constant, constant, constant * own_scale[:, None]], axis=1)
    vec = jnp.stack([own_bias.reshape(local_width), factor.reshape(local_width)], axis=0)
    lens = lax.dynamic_slice_in_dim(continuation_lengths, first_group, GRP_WT, 0)[0]
    place = jnp.stack([seq_index, lens[0], lax.rem(wt_index, 2)])
    packed, mixed_heads, log_sums = attend(lens, tokens_all, own_weight, vec, local_heads)
    local_ctx = local_heads * head_size
    context_t = exchange(
        mixed_heads,
        (model_width, row_count),
        (local_ctx, row_count),
        lambda ref, p: ref.at[:, pl.ds(pl.multiple_of(p * row_count, 128), row_count)],
        lambda ref, p: ref.at[pl.ds(pl.multiple_of(p * local_ctx, 16), local_ctx), :],
        1,
        "context_out",
    )
    (
        layer_output,
        grad_total_one,
        grad_context_t,
        wide_sums,
        unit_sums,
        contract_weight_grad,
        exp_mine,
        exp_mate,
        output_weight_grad,
    ) = feed_forward(
        wt_count, place, context_t, tokens, output_cotangent, full_output, full_expand, full_contract, wide_table, unit_table
    )
    con_piece = lax.psum_scatter(contract_weight_grad, "wt", scatter_dimension=0, tiled=True)
    output_weight_grad, con_piece = lax.optimization_barrier((output_weight_grad, con_piece))
    out_piece = lax.psum_scatter(output_weight_grad, "wt", scatter_dimension=0, tiled=True)
    arriving = exchange(
        grad_context_t,
        (local_ctx, GLEN),
        (local_ctx, row_count),
        lambda ref, p: ref.at[pl.ds(pl.multiple_of(p * local_ctx, 16), local_ctx), :],
        lambda ref, p: ref.at[:, pl.ds(pl.multiple_of(p * row_count, 128), row_count)],
        2,
        "context_grad_in",
    )
    exp_got = lax.ppermute(exp_mate, "wt", [(k, k ^ 1) for k in range(wt_count)])
    value_scale = factor[:, 2:3, :]
    backs, pieces, exp_own = [], [], None
    for h in range(local_heads):
        back = attend_back(place, packed, mixed_heads, arriving, log_sums, value_scale, h)
        backs.append(back)
        pieces.append(back[1])
        for k in (1, 2, 3):
            pieces.append(lax.ppermute(back[1 + k], "seq", [(j, j ^ k) for j in range(4)]))
    exp_sum = expand_reduce(exp_mine, exp_got, seq_index, wt_index, wt_count)
    sums = jnp.stack([back[5] for back in backs])
    gate_sums = jnp.stack([back[6] for back in backs])
    head_own = own_mask.astype(jnp.float32) * own_attention[0] / own_gate
    head_own = head_own * jnp.sum(gate_sums[:, 0], axis=1)
    head_partial = lax.dynamic_update_slice_in_dim(
        jnp.zeros((head_count,), jnp.float32), head_own, seq_index * local_heads, 0
    )
    zeros_wide = jnp.zeros((model_width,), jnp.float32)
    at_own = seq_index * local_heads * head_size
    query_bias_grad = lax.dynamic_update_slice_in_dim(zeros_wide, sums[:, 0].reshape(-1), at_own, 0)
    value_bias_grad = lax.dynamic_update_slice_in_dim(zeros_wide, sums[:, 1].reshape(-1), at_own, 0)
    attention_weight_grad = projection_grad(wt_count, tokens_all, [back[0] for back in backs])
    tokens_grad = tokens_back(place, grad_total_one, full_attention, pieces)
    width_rows = jnp.stack(
        [
            query_bias_grad,
            value_bias_grad,
            wide_sums[S_OUT_BIAS],
            wide_sums[S_GAIN1],
            wide_sums[S_SHIFT1],
            wide_sums[S_CON_BIAS],
            wide_sums[S_GAIN2],
            wide_sums[S_SHIFT2],
            wide_sums[S_HIDDEN] * hidden_mask.astype(f32),
        ],
        axis=0,
    )
    unit_rows = jnp.stack(
        [unit_sums[0], unit_sums[1] * (unit_mask.astype(f32) * own_feedforward[0])], axis=0
    )
    own_wide, own_units = model_width // wt_count, unit_gate.shape[0] // wt_count
    by_shard = jnp.concatenate(
        [
            width_rows.reshape(9, wt_count, own_wide).transpose(1, 0, 2).reshape(wt_count, -1),
            unit_rows.reshape(2, wt_count, own_units).transpose(1, 0, 2).reshape(wt_count, -1),
            jnp.broadcast_to(head_partial[None, :], (wt_count, head_count)),
        ],
        axis=1,
    )
    used = by_shard.shape[1]
    by_shard = jnp.pad(by_shard, ((0, 0), (0, -used % 1024))).reshape(wt_count, -1, 128)
    con_sum, out_sum, att_sum, vec_sum = reduce_out(
        wt_count,
        con_piece.reshape(seq_count, own_wide, model_width),
        out_piece,
        attention_weight_grad,
        by_shard,
    )
    vec_sum = vec_sum.reshape(-1)
    wide = [vec_sum[k * own_wide : (k + 1) * own_wide] for k in range(9)]
    base = 9 * own_wide
    units = [vec_sum[base + k * own_units : base + (k + 1) * own_units] for k in range(2)]
    head_gate_grad = vec_sum[base + 2 * own_units : used]
    return (
        layer_output,
        tokens_grad,
        att_sum,
        wide[0],
        wide[1],
        out_sum,
        wide[2],
        wide[3],
        wide[4],
        exp_sum,
        units[0],
        con_sum.reshape(seq_count * own_wide, model_width),
        wide[5],
        wide[6],
        wide[7],
        head_gate_grad,
        wide[8],
        units[1],
    )


def solution(mesh):
    return jax.shard_map(
        local,
        mesh=mesh,
        in_specs=(
            P(("wt", "seq"), None),
            P(("wt", "seq"), None),
            P("wt", None),
            P(),
            P(),
            P("wt", None),
            P(),
            P(),
            P(),
            P("wt", None),
            P(),
            P("wt", None),
            P(),
            P(),
            P(),
            P(),
            P(),
            P(),
            P(),
            P(),
            P(),
            P(),
            P(),
            P(),
        ),
        out_specs=(
            P(("wt", "seq"), None),
            P(("wt", "seq"), None),
            P("wt", None),
            P("wt"),
            P("wt"),
            P("wt", None),
            P("wt"),
            P("wt"),
            P("wt"),
            P("wt", None),
            P("wt"),
            P("wt", None),
            P("wt"),
            P("wt"),
            P("wt"),
            P(),
            P("wt"),
            P("wt"),
        ),
        check_vma=False,
    )
```

```python
import functools

import jax
import jax.numpy as jnp
from jax import lax
from jax.experimental import pallas as pl
from jax.experimental.pallas import tpu as pltpu
from jax.sharding import PartitionSpec as P

PROMPT = 1024
GRP_WT = 1
GLEN = 3072
SHORT = 512
LONG = 1536
HD = 64
TQ = 512
KC = 512

epsilon = 1e-06
score_scale = 0.125
exp2_scale = 0.125 * 1.4426950408889634
root_half = 0.7071067811865476
density_scale = 0.3989422804014327
bf16 = jnp.bfloat16
f32 = jnp.float32

NT = (((1,), (1,)), ((), ()))
NN = (((1,), (0,)), ((), ()))
TN = (((0,), (0,)), ((), ()))


def mm(a, b, dims=NN):
    return lax.dot_general(a, b, dims, preferred_element_type=f32)


def natural_at(short_first, i):
    other = jnp.where(i == 2, 5, i - 1)
    return jnp.where(short_first | (i < 2), i, other)


def ordered_at(short_first, j):
    other = jnp.where(j == 5, 2, j + 1)
    return jnp.where(short_first | (j < 2), j, other)


def query_tiles(tile):
    def prompt(i, carry):
        tile(i, ())
        return carry

    def longer(i, carry):
        tile(i, (3, 4, 5))
        return carry

    lax.fori_loop(0, 2, prompt, 0)
    tile(2, (2,))
    lax.fori_loop(3, 6, longer, 0)


def remote(src, dst, sems, k, peer):
    return pltpu.make_async_remote_copy(
        src_ref=src,
        dst_ref=dst,
        send_sem=sems[0].at[k],
        recv_sem=sems[1].at[k],
        device_id=peer,
        device_id_type=pl.DeviceIdType.MESH,
    )


def send(src, dst, sems, k, peer):
    copy = remote(src, dst, sems, k, peer)
    copy.start()
    return copy


def attend_kernel(
    heads, lens_ref, tok_ref, w_ref, vec_ref, packed_ref, ctx_ref, lse_ref, full_ref,
    q_sc, k_sc, vt_sc, ct_sc, local_sem, s_sem, r_sem,
):
    s, w = lax.axis_index("seq"), lax.axis_index("wt")
    others = [flip(s, k) for k in (1, 2, 3)]
    short_first = lens_ref[0] == SHORT
    meet([(p, w) for p in others])
    width = heads * HD
    count = GLEN // 4

    def project(i, carry):
        rows = pl.ds(pl.multiple_of(i * TQ, TQ), TQ)
        x = mm(tok_ref[natural_at(short_first, i)], w_ref[...]) + vec_ref[0:1, :]
        x = (x * vec_ref[1:2, :]).astype(bf16)
        for h in range(heads):
            at = 3 * HD * h
            packed_ref[h, rows, :] = x[:, at : at + 3 * HD]
            q_sc[h, rows, :] = x[:, at : at + HD]
            k_sc[h, rows, :] = x[:, at + HD : at + 2 * HD]
            vt_sc[h, :, rows] = x[:, at + 2 * HD : at + 3 * HD].T
        return carry

    lax.fori_loop(0, GLEN // TQ, project, 0)

    def leaving(h):
        rows = pl.ds(pl.multiple_of(h * HD, HD), HD)
        there = full_ref.at[pl.ds(pl.multiple_of(s * width + h * HD, HD), HD), :]

        def part(p):
            return ctx_ref.at[rows, pl.ds(pl.multiple_of(p * count, 128), count)]

        copies = [
            remote(part(p), there, (s_sem, r_sem), 3 * h + k, (p, w)) for k, p in enumerate(others)
        ]
        return copies, pltpu.make_async_copy(part(s), there, local_sem.at[h])

    def one_head(h, carry):
        def tile(i, own_blocks):
            rows = pl.ds(pl.multiple_of(i * TQ, TQ), TQ)
            q = q_sc[h, rows, :]
            s1 = mm(k_sc[h, 0:PROMPT, :], q, NT)
            top = jnp.max(s1, axis=0, keepdims=True)
            if own_blocks:
                own = slice(own_blocks[0] * KC, (own_blocks[-1] + 1) * KC)
                s2 = mm(k_sc[h, own, :], q, NT)
                top = jnp.maximum(top, jnp.max(s2, axis=0, keepdims=True))
            top = top * exp2_scale
            p1 = jnp.exp2(s1 * exp2_scale - top)
            o = mm(vt_sc[h, :, 0:PROMPT], p1.astype(bf16))
            total = jnp.sum(p1, axis=0, keepdims=True)
            if own_blocks:
                p2 = jnp.exp2(s2 * exp2_scale - top)
                o = o + mm(vt_sc[h, :, own], p2.astype(bf16))
                total = total + jnp.sum(p2, axis=0, keepdims=True)
            ct_sc[i] = (o / total).astype(bf16)
            lse_ref[h, :, rows] = top + jnp.log2(total)

        query_tiles(tile)

        def settle(j, carry):
            rows = pl.ds(pl.multiple_of(h * HD, HD), HD)
            lanes = pl.ds(pl.multiple_of(j * SHORT, SHORT), SHORT)
            ctx_ref[rows, lanes] = ct_sc[ordered_at(short_first, j)]
            return carry

        lax.fori_loop(0, GLEN // SHORT, settle, 0)
        copies, own = leaving(h)
        for copy in copies:
            copy.start()
        own.start()
        return carry

    lax.fori_loop(0, heads, one_head, 0)
    for h in range(heads):
        copies, own = leaving(h)
        own.wait()
        for copy in copies:
            copy.wait()


def attend(lens, tokens_all, weight, vec, heads):
    width = 3 * HD * heads
    return pl.pallas_call(
        functools.partial(attend_kernel, heads),
        out_shape=(
            jax.ShapeDtypeStruct((heads, GLEN, 3 * HD), bf16),
            jax.ShapeDtypeStruct((HD * heads, GLEN), bf16),
            jax.ShapeDtypeStruct((heads, 1, GLEN), f32),
            jax.ShapeDtypeStruct((4 * HD * heads, GLEN // 4), bf16),
        ),
        in_specs=[pl.BlockSpec(memory_space=pltpu.SMEM), IN_VMEM, IN_VMEM, IN_VMEM],
        out_specs=(IN_VMEM, IN_VMEM, IN_VMEM, ANYWHERE),
        scratch_shapes=[
            pltpu.VMEM((heads, GLEN, HD), bf16),
            pltpu.VMEM((heads, GLEN, HD), bf16),
            pltpu.VMEM((heads, HD, GLEN), bf16),
            pltpu.VMEM((GLEN // TQ, HD, TQ), bf16),
            pltpu.SemaphoreType.DMA((heads,)),
        ]
        + dma_sems(3 * heads),
        compiler_params=remote_params(1),
        cost_estimate=pl.CostEstimate(
            flops=2 * GLEN * 768 * width + heads * 4 * 256 * 5767168,
            bytes_accessed=2 * GLEN * (768 + width),
            transcendentals=heads * 5767168,
        ),
        name="attend",
    )(lens, tokens_all.reshape(GLEN // TQ, TQ, -1), weight, vec)


def attend_back_kernel(
    heads, n, lens_ref, packed_hbm, ctx_ref, g_hbm, lse_ref, scale_ref, tok_hbm, mine_hbm, mate_hbm,
    pieces_o, dw_o, exp_o, late_o,
    packed_v, tok_v, mine_v, got, e2, gh0, gh1, gh2, st0, st1, st2,
    q_sc, k_sc, v_sc, kt_sc, g_sc, g_nat, delta_sc, delta_nat, dqt_sc, dk_sc, dv_sc, acc,
    l_in, l_g, l_out, s_g, r_g, s_p, r_p, s_c, r_c, s_e, r_e,
):
    s, w = lax.axis_index("seq"), lax.axis_index("wt")
    others = [flip(s, k) for k in (1, 2, 3)]
    mate = (s, flip(w, 1))
    short_first = lens_ref[0] == SHORT
    count = GLEN // 4
    width = heads * HD
    gh, stage = (gh0, gh1, gh2)[:heads], (st0, st1, st2)[:heads]
    loads = [
        pltpu.make_async_copy(packed_hbm.at[h], packed_v.at[h], l_in.at[h]) for h in range(heads)
    ] + [
        pltpu.make_async_copy(mine_hbm, mine_v, l_in.at[heads]),
        pltpu.make_async_copy(tok_hbm, tok_v, l_in.at[heads + 1]),
    ]
    for copy in loads:
        copy.start()
    meet([(p, w) for p in others] + [mate])

    def coming(h, own=False):
        def part(p):
            return g_hbm.at[pl.ds(pl.multiple_of(p * width + h * HD, HD), HD), :]

        there = gh[h].at[:, pl.ds(pl.multiple_of(s * count, 128), count)]
        if own:
            return pltpu.make_async_copy(part(s), there, l_g.at[h])
        return [remote(part(p), there, (s_g, r_g), 3 * h + k, (p, w)) for k, p in enumerate(others)]

    def leaving(h):
        copies = [
            remote(stage[h].at[p], pieces_o.at[h, s], (s_p, r_p), 3 * h + k, (p, w))
            for k, p in enumerate(others)
        ]
        return copies, pltpu.make_async_copy(stage[h].at[s], pieces_o.at[h, s], l_out.at[h])

    over_pair = remote(mate_hbm, got, (s_c, r_c), 0, mate)
    over_plane = [
        remote(got.at[p], e2.at[s], (s_e, r_e), k, (p, w)) for k, p in enumerate(others)
    ]
    for h in range(heads):
        for copy in coming(h) + [coming(h, True)]:
            copy.start()
        if h == 0:
            over_pair.start()
    late_o[...] = jnp.zeros_like(late_o)
    zs = exp_o.shape[0]

    def prologue(h):
        loads[h].wait()

        def split(i, carry):
            rows = pl.ds(pl.multiple_of(i * TQ, TQ), TQ)
            x = packed_v[h, rows, :]
            q_sc[i] = x[:, 0:HD]
            k = x[:, HD : 2 * HD]
            k_sc[i] = k
            kt_sc[i] = k.T
            v_sc[i] = x[:, 2 * HD : 3 * HD]
            return carry

        lax.fori_loop(0, GLEN // TQ, split, 0)
        dk_sc[...] = jnp.zeros_like(dk_sc)
        dv_sc[...] = jnp.zeros_like(dv_sc)
        if h == 0:
            loads[heads].wait()
            over_pair.wait_recv()

            def pair_sum(i, carry):
                q, z = i // zs, lax.rem(i, zs)
                got[q, z] = (got[q, z].astype(f32) + mine_v[q, z].astype(f32)).astype(bf16)
                return carry

            lax.fori_loop(0, 4 * zs, pair_sum, 0)
        coming(h, True).wait()
        for copy in coming(h):
            copy.wait_recv()
        if h == 0:
            for copy in over_plane:
                copy.start()
            e2[s] = got[s]

        def inner(j, carry):
            lanes = pl.ds(pl.multiple_of(j * TQ, TQ), TQ)
            g = gh[h][:, lanes]
            g_nat[j] = g
            product = g.astype(f32) * ctx_ref[HD * h : HD * (h + 1), lanes].astype(f32)
            delta_nat[j] = jnp.sum(product, axis=0, keepdims=True)
            return carry

        def order(i, carry):
            g_sc[i] = g_nat[natural_at(short_first, i)]
            delta_sc[i] = delta_nat[natural_at(short_first, i)]
            return carry

        lax.fori_loop(0, GLEN // TQ, inner, 0)
        lax.fori_loop(0, GLEN // TQ, order, 0)

    def epilogue(h):
        half = SHORT // 2
        lanes = slice(HD * h, HD * (h + 1))

        def settle(j, carry):
            i = ordered_at(short_first, j)
            dq = dqt_sc[i].T.astype(bf16)
            dk = (dk_sc[i] * score_scale).astype(bf16)
            dv = dv_sc[i].astype(bf16).astype(f32)
            late_o[2:3, lanes] += jnp.sum(dv * v_sc[i].astype(f32), axis=0, keepdims=True)
            dv = (dv * scale_ref[h]).astype(bf16)
            late_o[0:1, lanes] += jnp.sum(dq.astype(f32), axis=0, keepdims=True)
            late_o[1:2, lanes] += jnp.sum(dv.astype(f32), axis=0, keepdims=True)
            for r in range(2):
                u = 2 * j + r
                p, there = u // 3, pl.ds(pl.multiple_of(lax.rem(u, 3) * half, half), half)
                rows = slice(r * half, (r + 1) * half)
                stage[h][p, there, 0:HD] = dq[rows]
                stage[h][p, there, HD : 2 * HD] = dk[rows]
                stage[h][p, there, 2 * HD : 3 * HD] = dv[rows]
            return carry

        lax.fori_loop(0, GLEN // SHORT, settle, 0)
        copies, own = leaving(h)
        for copy in copies:
            copy.start()
        own.start()

    def tile_of(h):
        def tile(i, own_blocks):
            q = q_sc[i]
            g = g_sc[i]
            lse = lse_ref[h, :, pl.ds(pl.multiple_of(i * TQ, TQ), TQ)]
            delta = delta_sc[i]
            dq = jnp.zeros((HD, TQ), f32)
            for j in (0, 1) + own_blocks:
                sc = mm(k_sc[j], q, NT)
                p = jnp.exp2(sc * exp2_scale - lse)
                dp = mm(v_sc[j], g)
                ds = (p * (dp - delta)).astype(bf16)
                dv_sc[j] += mm(p.astype(bf16), g, NT)
                dk_sc[j] += mm(ds, q)
                dq = dq + mm(kt_sc[j], ds)
            dqt_sc[i] = dq * score_scale

        return tile

    def one_head(h, carry):
        for j in range(heads):

            @pl.when(h == j)
            def _(j=j):
                prologue(j)

        query_tiles(tile_of(h))
        for j in range(heads):

            @pl.when(h == j)
            def _(j=j):
                epilogue(j)

        return carry

    lax.fori_loop(0, heads, one_head, 0)
    loads[heads + 1].wait()
    acc[...] = jnp.zeros_like(acc)

    def weight_grad(p, carry):
        x = tok_v[pl.ds(pl.multiple_of(p * count, count), count), :]
        for h in range(heads):
            acc[:, 3 * HD * h : 3 * HD * (h + 1)] += mm(x, stage[h][p], TN)
        return carry

    lax.fori_loop(0, 4, weight_grad, 0)
    own_rows = dw_o.shape[1]
    for k in range(n):
        dw_o[k] = acc[k * own_rows : (k + 1) * own_rows, :].astype(bf16)
    for copy in over_plane:
        copy.wait_recv()

    def plane_sum(z, carry):
        t = [e2[q, z].astype(f32) for q in range(4)]
        exp_o[z] = ((t[0] + t[1]) + (t[2] + t[3])).astype(bf16)
        return carry

    lax.fori_loop(0, zs, plane_sum, 0)
    for h in range(heads):
        copies, own = leaving(h)
        own.wait()
        for copy in copies:
            copy.wait()
        for copy in coming(h):
            copy.wait_send()
    over_pair.wait_send()
    for copy in over_plane:
        copy.wait_send()


def attend_back(n, lens, packed, ctx, g, lse, scale, tokens_all, mine, mate):
    heads = packed.shape[0]
    width = 3 * HD * heads
    d = tokens_all.shape[1]
    count = GLEN // 4
    _, zs, own, wide = mine.shape
    blocks = GLEN // TQ
    rows64 = pltpu.VMEM((blocks, TQ, HD), bf16)
    blocks64 = pltpu.VMEM((blocks, HD, TQ), bf16)
    lanes64 = pltpu.VMEM((HD, GLEN), bf16)
    return pl.pallas_call(
        functools.partial(attend_back_kernel, heads, n),
        out_shape=(
            jax.ShapeDtypeStruct((heads, 4, count, 3 * HD), bf16),
            jax.ShapeDtypeStruct((n, d // n, width), bf16),
            jax.ShapeDtypeStruct((zs, own, wide), bf16),
            jax.ShapeDtypeStruct((8, HD * heads), f32),
        ),
        in_specs=[pl.BlockSpec(memory_space=pltpu.SMEM)]
        + [ANYWHERE, IN_VMEM, ANYWHERE, IN_VMEM, IN_VMEM, ANYWHERE, ANYWHERE, ANYWHERE],
        out_specs=(ANYWHERE, IN_VMEM, IN_VMEM, IN_VMEM),
        scratch_shapes=[
            pltpu.VMEM(packed.shape, bf16),
            pltpu.VMEM(tokens_all.shape, bf16),
            pltpu.VMEM(mine.shape, bf16),
            pltpu.VMEM(mine.shape, bf16),
            pltpu.VMEM(mine.shape, bf16),
            lanes64,
            lanes64,
            lanes64,
        ]
        + [pltpu.VMEM((4, count, 3 * HD), bf16)] * 3
        + [
            rows64,
            rows64,
            rows64,
            blocks64,
            blocks64,
            blocks64,
            pltpu.VMEM((blocks, 1, TQ), f32),
            pltpu.VMEM((blocks, 1, TQ), f32),
            pltpu.VMEM((blocks, HD, TQ), f32),
            pltpu.VMEM((blocks, TQ, HD), f32),
            pltpu.VMEM((blocks, TQ, HD), f32),
            pltpu.VMEM((d, width), f32),
            pltpu.SemaphoreType.DMA((heads + 2,)),
            pltpu.SemaphoreType.DMA((heads,)),
            pltpu.SemaphoreType.DMA((heads,)),
        ]
        + dma_sems(3 * heads)
        + dma_sems(3 * heads)
        + dma_sems(1)
        + dma_sems(3),
        compiler_params=remote_params(2),
        cost_estimate=pl.CostEstimate(
            flops=heads * 10 * 256 * 5767168 + 2 * GLEN * d * width,
            bytes_accessed=2 * GLEN * (3 * width + d),
            transcendentals=heads * 5767168,
        ),
        name="attend_back",
    )(lens, packed, ctx, g, lse, scale, tokens_all, mine, mate)


def meet(peers):
    barrier = pltpu.get_barrier_semaphore()
    for peer in peers:
        pl.semaphore_signal(barrier, inc=1, device_id=peer, device_id_type=pl.DeviceIdType.MESH)
    pl.semaphore_wait(barrier, len(peers))


def flip(index, bits):
    for bit in (1, 2):
        if bits & bit:
            index = index + bit - 2 * bit * ((index // bit) % 2)
    return index


def remote_params(number):
    return pltpu.CompilerParams(
        collective_id=number, has_side_effects=True, vmem_limit_bytes=56 * 2**20
    )


ANYWHERE = pl.BlockSpec(memory_space=pl.ANY)
IN_VMEM = pl.BlockSpec(memory_space=pltpu.VMEM)


def dma_sems(count):
    return [pltpu.SemaphoreType.DMA((count,)), pltpu.SemaphoreType.DMA((count,))]


def gather_kernel(
    n, tok_ref, cols_ref, out_ref, tok_all, cols_all, out_all,
    tok_buf, cols_buf, out_buf, local_sem, s_tok, r_tok, s_w, r_w, s_f, r_f,
):
    s, w = lax.axis_index("seq"), lax.axis_index("wt")
    rows = tok_ref.shape[0]
    half = rows // 2
    by_x, by_y, mate = (flip(s, 1), w), (flip(s, 2), w), (s, flip(w, 1))
    far = [(s, lax.rem(w + 2 * j, n)) for j in range(1, n // 2)]
    meet([by_x, by_y, mate] + far)

    def part(owner, k):
        return pl.ds(pl.multiple_of(owner * rows + k * half, half), half)

    tok = (s_tok, r_tok)
    first = [pl.ds(0, half), pl.ds(half, half)]
    x0 = send(tok_ref.at[first[0]], tok_all.at[part(s, 0)], tok, 0, by_x)
    y1 = send(tok_ref.at[first[1]], tok_all.at[part(s, 1)], tok, 1, by_y)
    x1 = send(tok_ref.at[first[1]], tok_all.at[part(s, 1)], tok, 2, by_x)
    y0 = send(tok_ref.at[first[0]], tok_all.at[part(s, 0)], tok, 3, by_y)
    held = []
    for k, peer in enumerate(far + [mate]):
        for i, (src, dst) in enumerate(((cols_ref, cols_all), (out_ref, out_all))):
            held.append(send(src, dst.at[w], (s_w, r_w), 2 * k + i, peer))
    own = []
    for i, (src, buf) in enumerate(((tok_ref, tok_buf), (cols_ref, cols_buf), (out_ref, out_buf))):
        own.append(pltpu.make_async_copy(src, buf, local_sem.at[i]))
        own[-1].start()
    for copy in own:
        copy.wait()
    targets = (
        (tok_buf, tok_all.at[pl.ds(pl.multiple_of(s * rows, rows), rows)]),
        (cols_buf, cols_all.at[w]),
        (out_buf, out_all.at[w]),
    )
    own = []
    for i, (buf, dst) in enumerate(targets):
        own.append(pltpu.make_async_copy(buf, dst, local_sem.at[3 + i]))
        own[-1].start()
    passed = []
    x0.wait_recv()
    there = tok_all.at[part(flip(s, 1), 0)]
    passed.append(send(there, there, tok, 4, by_y))
    y1.wait_recv()
    there = tok_all.at[part(flip(s, 2), 1)]
    passed.append(send(there, there, tok, 5, by_x))
    for j in range(1, n // 2):
        origin = lax.rem(w + n - 2 * j, n)
        for i, dst in enumerate((cols_all, out_all)):
            k = 2 * (j - 1) + i
            held[k].wait_recv()
            passed.append(send(dst.at[origin], dst.at[origin], (s_f, r_f), k, mate))
    for copy in own:
        copy.wait()
    x1.wait_recv()
    y0.wait_recv()
    for copy in held[n - 2 :]:
        copy.wait_recv()
    for copy in passed:
        copy.wait_recv()
    for copy in [x0, x1, y0, y1] + held + passed:
        copy.wait_send()


def gather_in(n, tokens, own_columns, output_weight):
    rows, d = tokens.shape
    return pl.pallas_call(
        functools.partial(gather_kernel, n),
        out_shape=(
            jax.ShapeDtypeStruct((4 * rows, d), bf16),
            jax.ShapeDtypeStruct((n,) + own_columns.shape, bf16),
            jax.ShapeDtypeStruct((n,) + output_weight.shape, bf16),
        ),
        in_specs=[ANYWHERE] * 3,
        out_specs=(ANYWHERE,) * 3,
        scratch_shapes=[
            pltpu.VMEM(tokens.shape, bf16),
            pltpu.VMEM(own_columns.shape, bf16),
            pltpu.VMEM(output_weight.shape, bf16),
            pltpu.SemaphoreType.DMA((6,)),
        ]
        + dma_sems(6)
        + dma_sems(n)
        + dma_sems(n - 2),
        compiler_params=remote_params(0),
        name="gather_in",
    )(tokens, own_columns, output_weight)


def final_kernel(
    heads, n, base_hbm, pieces_hbm, w_hbm, con_ref, out_ref, att_ref, exp_ref, vec_ref, late_ref,
    tok_o, g_con, r_out, g_exp, g_att, r_vec2, r_late2,
    base_v, pieces_v, w_v, r_con, h_att, m_att, r_att, r_exp, r_vec, r_late,
    l_in, *sems,
):
    s, w = lax.axis_index("seq"), lax.axis_index("wt")
    z, c = w // 2, lax.rem(w, 2)
    nz = n // 2
    others = [flip(s, k) for k in (1, 2, 3)]
    seq_peers = [(p, w) for p in others]
    mate = (s, flip(w, 1))
    wt_peers = [(s, lax.rem(w + j, n)) for j in range(1, n)]
    names = ("pair", "vec", "late", "con", "exp", "out", "att", "vec2", "late2", "con2", "exp2", "att2")
    sem = {name: (sems[2 * k], sems[2 * k + 1]) for k, name in enumerate(names)}
    loads = [
        pltpu.make_async_copy(src, dst, l_in.at[k])
        for k, (src, dst) in enumerate(((pieces_hbm, pieces_v), (w_hbm, w_v), (base_hbm, base_v)))
    ]
    for copy in loads:
        copy.start()
    meet(seq_peers + wt_peers)
    pair = [send(att_ref.at[2 * k + 1 - c], h_att.at[k], sem["pair"], k, mate) for k in range(nz)]
    cons = [send(con_ref.at[p], r_con.at[s], sem["con"], k, (p, w)) for k, p in enumerate(others)]
    far = [lax.rem(z + j, nz) for j in range(1, nz)]
    exps = [
        send(exp_ref.at[k], r_exp.at[z], sem["exp"], j, (s, 2 * k + c)) for j, k in enumerate(far)
    ]
    vecs = [
        send(vec_ref.at[lax.rem(w + j, n)], r_vec.at[w], sem["vec"], j - 1, wt_peers[j - 1])
        for j in range(1, n)
    ]
    lates = [send(late_ref, r_late.at[w], sem["late"], j, p) for j, p in enumerate(wt_peers)]
    outs = [send(out_ref, r_out.at[s], sem["out"], k, p) for k, p in enumerate(seq_peers)]
    r_con[s] = con_ref[s]
    r_exp[z] = exp_ref[z]
    r_vec[w] = vec_ref[w]
    r_late[w] = late_ref[...]
    r_out[s] = out_ref[...]
    for copy in pair:
        copy.wait_recv()
    for k in range(nz):
        m_att[k] = (att_ref[2 * k + c].astype(f32) + h_att[k].astype(f32)).astype(bf16)
    atts = [send(m_att.at[k], r_att.at[z], sem["att"], j, (s, 2 * k + c)) for j, k in enumerate(far)]
    r_att[z] = m_att[z]
    for copy in loads:
        copy.wait()
    cols = 3 * HD
    rows = tok_o.shape[0]
    block = rows // 3

    def tokens_block(i, carry):
        there = pl.ds(pl.multiple_of(i * block, block), block)
        total = base_v[there, :]
        for h in range(heads):
            for k in range(4):
                at = (heads * k + h) * cols
                total = total + mm(pieces_v[h, k, there, :], w_v[:, at : at + cols], NT)
        tok_o[there, :] = total
        return carry

    lax.fori_loop(0, 1, tokens_block, 0)

    def total_of(ref, count):
        total = ref[0].astype(f32)
        for k in range(1, count):
            total = total + ref[k].astype(f32)
        return total

    for copy in cons:
        copy.wait_recv()
    g_con[s] = total_of(r_con, 4).astype(bf16)
    con2 = [send(g_con.at[s], g_con.at[s], sem["con2"], k, p) for k, p in enumerate(seq_peers)]
    for copy in vecs + lates:
        copy.wait_recv()
    r_vec2[s] = total_of(r_vec, n)
    r_late2[s] = total_of(r_late, n)
    vec2 = [send(r_vec2.at[s], r_vec2.at[s], sem["vec2"], k, p) for k, p in enumerate(seq_peers)]
    late2 = [send(r_late2.at[s], r_late2.at[s], sem["late2"], k, p) for k, p in enumerate(seq_peers)]
    lax.fori_loop(1, 2, tokens_block, 0)
    for copy in exps:
        copy.wait_recv()
    g_exp[s] = total_of(r_exp, nz).astype(bf16)
    exp2 = [send(g_exp.at[s], g_exp.at[s], sem["exp2"], k, p) for k, p in enumerate(seq_peers)]
    for copy in atts:
        copy.wait_recv()
    g_att[s] = total_of(r_att, nz).astype(bf16)
    att2 = [send(g_att.at[s], g_att.at[s], sem["att2"], k, p) for k, p in enumerate(seq_peers)]
    lax.fori_loop(2, 3, tokens_block, 0)
    for copy in outs + con2 + vec2 + late2 + exp2 + att2:
        copy.wait_recv()
    for copy in pair + cons + exps + vecs + lates + outs + atts + con2 + vec2 + late2 + exp2 + att2:
        copy.wait_send()


def final(n, base, pieces, weight, con, out, att, exp_part, vec, late):
    heads = pieces.shape[0]
    r, d = out.shape
    cols = att.shape[2]
    nz = n // 2
    wide = exp_part.shape[2]
    counts = (nz, n - 1, n - 1, 3, nz - 1, 3, nz - 1, 3, 3, 3, 3, 3)
    return pl.pallas_call(
        functools.partial(final_kernel, heads, n),
        out_shape=(
            jax.ShapeDtypeStruct(base.shape, f32),
            jax.ShapeDtypeStruct((4, r, d), bf16),
            jax.ShapeDtypeStruct((4, r, d), bf16),
            jax.ShapeDtypeStruct((4, r, wide), bf16),
            jax.ShapeDtypeStruct((4, r, cols), bf16),
            jax.ShapeDtypeStruct((4,) + vec.shape[1:], f32),
            jax.ShapeDtypeStruct((4,) + late.shape, f32),
        ),
        in_specs=[ANYWHERE] * 3 + [IN_VMEM] * 6,
        out_specs=(IN_VMEM,) * 7,
        scratch_shapes=[
            pltpu.VMEM(base.shape, f32),
            pltpu.VMEM(pieces.shape, bf16),
            pltpu.VMEM(weight.shape, bf16),
            pltpu.VMEM((4, r, d), bf16),
            pltpu.VMEM((nz, r, cols), bf16),
            pltpu.VMEM((nz, r, cols), bf16),
            pltpu.VMEM((nz, r, cols), bf16),
            pltpu.VMEM((nz, r, wide), bf16),
            pltpu.VMEM((n,) + vec.shape[1:], f32),
            pltpu.VMEM((n,) + late.shape, f32),
            pltpu.SemaphoreType.DMA((3,)),
        ]
        + [sem for count in counts for sem in dma_sems(count)],
        compiler_params=remote_params(3),
        cost_estimate=pl.CostEstimate(
            flops=8 * base.shape[0] * d * cols, bytes_accessed=8 * d * cols, transcendentals=0
        ),
        name="final",
    )(base, pieces, weight, con, out, att, exp_part, vec, late)


def finish_kernel(
    n, heads, place_ref, head_ref, con_ref, out_ref, exp_ref, att_ref, vec_ref, late_ref,
    con_o, out_o, exp_o, att_o, *rest,
):
    vec_os, unit_os, query_o, value_o, gate_o = rest[:7], rest[7:9], rest[9], rest[10], rest[11]

    def add4(parts):
        return (parts[0] + parts[1]) + (parts[2] + parts[3])

    out_o[...] = add4([out_ref[k].astype(f32) for k in range(4)])
    wide, cols = exp_ref.shape[2], att_ref.shape[2]
    for k in range(4):
        con_o[k] = con_ref[k].astype(f32)
        exp_o[:, k * wide : (k + 1) * wide] = exp_ref[k].astype(f32)
        att_o[:, k * cols : (k + 1) * cols] = att_ref[k].astype(f32)
    vec = add4([vec_ref[k] for k in range(4)])
    own = vec_os[0].shape[1]
    for k, ref in enumerate(vec_os):
        ref[...] = vec[k : k + 1, 0:own]
    for k, ref in enumerate(unit_os):
        ref[...] = vec[8 + k : 9 + k, :]
    rows = [jnp.concatenate([late_ref[k, j : j + 1, :] for k in range(4)], axis=1) for j in range(2)]
    for k in range(n):

        @pl.when(place_ref[3] == k)
        def _(k=k):
            query_o[...] = rows[0][:, k * own : (k + 1) * own]
            value_o[...] = rows[1][:, k * own : (k + 1) * own]

    gates = []
    for k in range(4):
        for h in range(heads):
            part = late_ref[k, 2:3, HD * h : HD * (h + 1)]
            gates.append(jnp.sum(part, axis=1, keepdims=True))
    gate_o[...] = jnp.concatenate(gates, axis=1) * head_ref[...]


def finish(n, heads, place, head_row, con, out, exp_all, att, vec, late):
    r, d = out.shape[1:]
    wide, cols = exp_all.shape[2], att.shape[2]
    units = vec.shape[2]
    row = jax.ShapeDtypeStruct((1, r), f32)
    return pl.pallas_call(
        functools.partial(finish_kernel, n, heads),
        out_shape=(
            jax.ShapeDtypeStruct(con.shape, f32),
            jax.ShapeDtypeStruct((r, d), f32),
            jax.ShapeDtypeStruct((r, 4 * wide), f32),
            jax.ShapeDtypeStruct((r, 4 * cols), f32),
        )
        + (row,) * 7
        + (jax.ShapeDtypeStruct((1, units), f32),) * 2
        + (row,) * 2
        + (jax.ShapeDtypeStruct((1, 4 * heads), f32),),
        in_specs=[pl.BlockSpec(memory_space=pltpu.SMEM)] + [IN_VMEM] * 7,
        out_specs=(IN_VMEM,) * 16,
        compiler_params=pltpu.CompilerParams(vmem_limit_bytes=32 * 2**20),
        name="finish",
    )(place, head_row, con, out, exp_all, att, vec, late)


(OUT_BIAS, GAIN1, SHIFT1, HIDDEN_SCALE, CON_BIAS, GAIN2, SHIFT2, HIDDEN_MASK) = range(8)
(S_OUT_BIAS, S_GAIN1, S_SHIFT1, S_CON_BIAS, S_GAIN2, S_SHIFT2, S_HIDDEN) = range(7)


def gelu_parts(x):
    bell = jnp.exp(-0.5 * (x * x))
    t = 1.0 / (1.0 + (0.3275911 * root_half) * jnp.abs(x))
    poly = t * (
        0.127414796 + t * (-0.142248368 + t * (0.7107068705 + t * (-0.7265760135 + t * 0.5307027145)))
    )
    tail = poly * bell
    cumulative = jnp.where(x < 0.0, tail, 1.0 - tail)
    return x * cumulative, cumulative + x * bell * density_scale


def norm_parts(summed):
    centre = summed - jnp.mean(summed, axis=-1, keepdims=True)
    inverse = lax.rsqrt(jnp.mean(centre * centre, axis=-1, keepdims=True) + epsilon)
    return (centre * inverse, inverse)


def norm_back(grad_normed, normed, inverse):
    return inverse * (
        grad_normed
        - jnp.mean(grad_normed, axis=-1, keepdims=True)
        - normed * jnp.mean(grad_normed * normed, axis=-1, keepdims=True)
    )


def feed_forward_kernel(
    steps, chunk,
    place_ref, ctx_ref, tok_ref, cot_ref, wo_ref, we_ref, wc_ref, wide_ref, unit_ref,
    lo_ref, dt1_ref, gctx_ref, vec_ref, dwc_ref, mine_ref, mate_ref, dwo_ref,
    sw_ref, su_ref, act_sc, gh_sc, low_sc, gb_sc, ga_sc, ctx_sc, gelu_sc, slope_sc,
):
    i = pl.program_id(0)
    block = tok_ref.shape[0]
    units = we_ref.shape[1]
    rows = pl.ds(pl.multiple_of(i * block, block), block)

    @pl.when(i == 0)
    def _():
        sw_ref[...] = jnp.zeros_like(sw_ref)
        su_ref[...] = jnp.zeros_like(su_ref)

    def wide(k):
        return wide_ref[k : k + 1, :]

    def add_sum(ref, k, cols, value):
        ref[k : k + 1, cols] += jnp.sum(value, axis=0, keepdims=True)

    full = slice(None)
    ctx = ctx_ref[...]
    ctx_sc[:, rows] = ctx
    summed = mm(ctx, wo_ref[...], TN) + wide(OUT_BIAS) + tok_ref[...].astype(f32)
    n1, inv1 = norm_parts(summed)
    s1 = n1 * wide(GAIN1) + wide(SHIFT1)
    hs = wide(HIDDEN_SCALE)
    first = s1 * hs
    low = first.astype(bf16)
    low_sc[rows, :] = low
    branch = first + wide(CON_BIAS)
    for j in range(units // chunk):
        cols = slice(j * chunk, (j + 1) * chunk)
        hidden = mm(low, we_ref[:, cols]) + unit_ref[0:1, cols]
        gelu, slope = gelu_parts(hidden)
        scale = unit_ref[1:2, cols]
        gelu_sc[:, cols] = gelu.astype(gelu_sc.dtype)
        slope_sc[:, cols] = (slope * scale).astype(slope_sc.dtype)
        act = (gelu * scale).astype(bf16)
        act_sc[rows, cols] = act
        branch = branch + mm(act, wc_ref[cols, :])
    n2, inv2 = norm_parts(branch)
    s2 = n2 * wide(GAIN2) + wide(SHIFT2)
    lo_ref[...] = (s2 * hs).astype(bf16)
    dy = cot_ref[...].astype(f32)
    e2 = dy * hs
    add_sum(sw_ref, S_GAIN2, full, e2 * n2)
    add_sum(sw_ref, S_SHIFT2, full, e2)
    dt2 = norm_back(e2 * wide(GAIN2), n2, inv2)
    gb = dt2.astype(bf16)
    gb_sc[rows, :] = gb
    add_sum(sw_ref, S_CON_BIAS, full, gb.astype(f32))
    d_first = dt2
    for j in range(units // chunk):
        cols = slice(j * chunk, (j + 1) * chunk)
        d_act = mm(gb, wc_ref[cols, :], NT)
        add_sum(su_ref, 1, cols, d_act * gelu_sc[:, cols].astype(f32))
        gh = d_act * slope_sc[:, cols].astype(f32)
        add_sum(su_ref, 0, cols, gh)
        gh = gh.astype(bf16)
        gh_sc[rows, cols] = gh
        d_first = d_first + mm(gh, we_ref[:, cols], NT)
    e1 = d_first * hs
    add_sum(sw_ref, S_GAIN1, full, e1 * n1)
    add_sum(sw_ref, S_SHIFT1, full, e1)
    add_sum(sw_ref, S_HIDDEN, full, dy * s2 + d_first * s1)
    dt1 = norm_back(e1 * wide(GAIN1), n1, inv1)
    dt1_ref[...] = dt1
    ga = dt1.astype(bf16)
    ga_sc[rows, :] = ga
    add_sum(sw_ref, S_OUT_BIAS, full, ga.astype(f32))
    gctx_ref[...] = mm(wo_ref[...], ga, NT).astype(bf16)

    @pl.when(i == steps - 1)
    def _():
        for j in range(units // chunk):
            cols = slice(j * chunk, (j + 1) * chunk)
            dwc_ref[cols, :] = mm(act_sc[:, cols], gb_sc[...], TN).astype(bf16)
            part = mm(low_sc[...], gh_sc[:, cols], TN).astype(bf16)
            own, wide_cols = mine_ref.shape[2:]
            for c in range(2):

                @pl.when(place_ref[2] == c)
                def _(part=part, j=j, c=c):
                    for q in range(chunk // wide_cols):
                        at = j * (chunk // wide_cols) + q
                        inner = slice(q * wide_cols, (q + 1) * wide_cols)
                        for z in range(mine_ref.shape[1]):
                            mine = (2 * z + c) * own
                            mate = (2 * z + 1 - c) * own
                            mine_ref[at, z] = part[mine : mine + own, inner]
                            mate_ref[at, z] = part[mate : mate + own, inner]

        dwo_ref[...] = mm(ctx_sc[...], ga_sc[...]).astype(bf16)
        vec_ref[...] = jnp.zeros_like(vec_ref)
        sw_ref[S_HIDDEN : S_HIDDEN + 1, :] *= wide(HIDDEN_MASK)
        su_ref[1:2, :] *= unit_ref[2:3, :]
        own_wide, own_units = mine_ref.shape[2], vec_ref.shape[2]
        for k in range(vec_ref.shape[0]):
            vec_ref[k, 0:8, 0:own_wide] = sw_ref[:, k * own_wide : (k + 1) * own_wide]
            vec_ref[k, 8:16, :] = su_ref[:, k * own_units : (k + 1) * own_units]


def feed_forward(n, place, ctx_t, tokens, cotangent, wo, we, wc, wide, unit):
    steps, chunk, keep = 3, 768, f32
    rows, d = tokens.shape
    units = we.shape[1]
    block = rows // steps
    halves = (4, n // 2, d // n, units // 4)
    tile = pl.BlockSpec((block, d), lambda i: (i, 0))
    lanes = pl.BlockSpec((d, block), lambda i: (0, i))

    def once(shape):
        return pl.BlockSpec(shape, lambda i: (0, 0), pipeline_mode=pl.Buffered(1))

    def once3(shape):
        return pl.BlockSpec(shape, lambda i: (0, 0, 0), pipeline_mode=pl.Buffered(1))

    def once4(shape):
        return pl.BlockSpec(shape, lambda i: (0, 0, 0, 0), pipeline_mode=pl.Buffered(1))

    return pl.pallas_call(
        functools.partial(feed_forward_kernel, steps, chunk),
        out_shape=(
            jax.ShapeDtypeStruct((rows, d), bf16),
            jax.ShapeDtypeStruct((rows, d), f32),
            jax.ShapeDtypeStruct((d, rows), bf16),
            jax.ShapeDtypeStruct((n, 16, units // n), f32),
            jax.ShapeDtypeStruct((units, d), bf16),
            jax.ShapeDtypeStruct(halves, bf16),
            jax.ShapeDtypeStruct(halves, bf16),
            jax.ShapeDtypeStruct((d, d), bf16),
        ),
        grid=(steps,),
        in_specs=[
            pl.BlockSpec(memory_space=pltpu.SMEM),
            lanes, tile, tile, once((d, d)), once((d, units)), once((units, d)), once((8, d)), once((8, units)),
        ],
        out_specs=(
            tile, tile, lanes, once3((n, 16, units // n)), once((units, d)),
            once4(halves), once4(halves), once((d, d)),
        ),
        scratch_shapes=[
            pltpu.VMEM((8, d), f32),
            pltpu.VMEM((8, units), f32),
            pltpu.VMEM((rows, units), bf16),
            pltpu.VMEM((rows, units), bf16),
            pltpu.VMEM((rows, d), bf16),
            pltpu.VMEM((rows, d), bf16),
            pltpu.VMEM((rows, d), bf16),
            pltpu.VMEM((d, rows), bf16),
            pltpu.VMEM((block, units), keep),
            pltpu.VMEM((block, units), keep),
        ],
        compiler_params=pltpu.CompilerParams(vmem_limit_bytes=60 * 2**20),
        cost_estimate=pl.CostEstimate(
            flops=rows * d * (12 * units + 6 * d),
            bytes_accessed=4 * d * (4 * units + 2 * d) + 12 * rows * d,
            transcendentals=2 * rows * units,
        ),
        name="feed_forward",
    )(place, ctx_t, tokens, cotangent, wo, we, wc, wide, unit)


def local(
    tokens,
    output_cotangent,
    attention_weight,
    query_bias,
    value_bias,
    output_weight,
    output_bias,
    first_gain,
    first_shift,
    expand_weight,
    expand_bias,
    contract_weight,
    contract_bias,
    second_gain,
    second_shift,
    head_gate,
    hidden_gate,
    unit_gate,
    head_mask,
    hidden_mask,
    unit_mask,
    attention_mask,
    feedforward_mask,
    continuation_lengths,
):
    row_count = tokens.shape[0]
    seq_count = lax.axis_size("seq")
    head_count = head_gate.shape[0]
    model_width = hidden_gate.shape[0]
    head_size = model_width // head_count
    local_heads = head_count // seq_count
    seq_index = lax.axis_index("seq")
    wt_index = lax.axis_index("wt")
    local_width = 3 * head_size * local_heads
    wt_count = lax.axis_size("wt")
    own_columns = lax.dynamic_slice_in_dim(attention_weight, seq_index * local_width, local_width, 1)
    tokens_all, own_weight, full_output = gather_in(wt_count, tokens, own_columns, output_weight)
    own_weight = own_weight.reshape(model_width, local_width)
    full_output = full_output.reshape(model_width, model_width)
    full_expand = lax.all_gather(expand_weight, "wt", axis=0, tiled=True)
    full_contract = lax.all_gather(contract_weight, "wt", axis=0, tiled=True)
    full_attention = lax.all_gather(attention_weight, "wt", axis=0, tiled=True)
    first_group = wt_index * GRP_WT
    own_attention = lax.dynamic_slice_in_dim(attention_mask, first_group, GRP_WT, 0).astype(
        jnp.float32
    )
    own_feedforward = lax.dynamic_slice_in_dim(feedforward_mask, first_group, GRP_WT, 0).astype(
        jnp.float32
    )
    head_scale = head_mask.astype(jnp.float32) * head_gate
    hidden_scale = hidden_mask.astype(jnp.float32) * hidden_gate
    unit_scale = unit_mask.astype(jnp.float32) * unit_gate
    wide_table = jnp.stack(
        [
            output_bias.astype(f32),
            first_gain.astype(f32),
            first_shift.astype(f32),
            hidden_scale,
            contract_bias.astype(f32),
            second_gain.astype(f32),
            second_shift.astype(f32),
            hidden_mask.astype(f32),
        ],
        axis=0,
    )
    unit_row = unit_scale * own_feedforward[0]
    unit_kept = unit_mask.astype(f32) * own_feedforward[0]
    unit_table = jnp.stack([expand_bias.astype(f32), unit_row] + [unit_kept] * 6, axis=0)
    bias_table = jnp.stack(
        [
            query_bias.astype(jnp.float32).reshape(head_count, head_size),
            jnp.zeros((head_count, head_size), jnp.float32),
            value_bias.astype(jnp.float32).reshape(head_count, head_size),
        ],
        axis=1,
    )
    own_scale = lax.dynamic_slice_in_dim(head_scale, seq_index * local_heads, local_heads, 0)
    own_scale = own_scale * own_attention[0]
    own_mask = lax.dynamic_slice_in_dim(head_mask, seq_index * local_heads, local_heads, 0)
    own_gate = lax.dynamic_slice_in_dim(head_gate, seq_index * local_heads, local_heads, 0)
    own_bias = lax.dynamic_slice_in_dim(bias_table, seq_index * local_heads, local_heads, 0)
    constant = jnp.ones((local_heads, head_size), jnp.float32)
    factor = jnp.stack([constant, constant, constant * own_scale[:, None]], axis=1)
    vec = jnp.stack([own_bias.reshape(local_width), factor.reshape(local_width)], axis=0)
    lens = lax.dynamic_slice_in_dim(continuation_lengths, first_group, GRP_WT, 0)[0]
    place = jnp.stack([seq_index, lens[0], lax.rem(wt_index, 2), wt_index])
    packed, own_context, log_sums, context_t = attend(lens, tokens_all, own_weight, vec, local_heads)
    (
        layer_output,
        grad_total_one,
        grad_context_t,
        vec_sums,
        contract_weight_grad,
        exp_mine,
        exp_mate,
        output_weight_grad,
    ) = feed_forward(
        wt_count, place, context_t, tokens, output_cotangent, full_output, full_expand, full_contract, wide_table, unit_table
    )
    con_piece = lax.psum_scatter(contract_weight_grad, "wt", scatter_dimension=0, tiled=True)
    output_weight_grad, con_piece = lax.optimization_barrier((output_weight_grad, con_piece))
    out_piece = lax.psum_scatter(output_weight_grad, "wt", scatter_dimension=0, tiled=True)
    pieces, projection_grad, exp_part, late_sums = attend_back(
        wt_count,
        lens,
        packed,
        own_context,
        grad_context_t,
        log_sums,
        factor[:, 2:3, :],
        tokens_all,
        exp_mine,
        exp_mate,
    )
    own_wide = model_width // wt_count
    tokens_grad, con_all, out_all, exp_all, att_all, vec_all, late_all = final(
        wt_count,
        grad_total_one,
        pieces,
        full_attention,
        con_piece.reshape(seq_count, own_wide, model_width),
        out_piece,
        projection_grad,
        exp_part,
        vec_sums,
        late_sums,
    )
    head_row = (head_mask.astype(f32) / head_gate).reshape(1, head_count)
    con_sum, out_sum, exp_sum, att_sum, *rows = finish(
        wt_count, local_heads, place, head_row, con_all, out_all, exp_all, att_all, vec_all, late_all
    )
    wide = [row.reshape(own_wide) for row in rows[:7]]
    units = [row.reshape(-1) for row in rows[7:9]]
    return (
        layer_output,
        tokens_grad,
        att_sum,
        rows[9].reshape(own_wide),
        rows[10].reshape(own_wide),
        out_sum,
        wide[S_OUT_BIAS],
        wide[S_GAIN1],
        wide[S_SHIFT1],
        exp_sum,
        units[0],
        con_sum.reshape(seq_count * own_wide, model_width),
        wide[S_CON_BIAS],
        wide[S_GAIN2],
        wide[S_SHIFT2],
        rows[11].reshape(head_count),
        wide[S_HIDDEN],
        units[1],
    )


def solution(mesh):
    return jax.shard_map(
        local,
        mesh=mesh,
        in_specs=(
            P(("wt", "seq"), None),
            P(("wt", "seq"), None),
            P("wt", None),
            P(),
            P(),
            P("wt", None),
            P(),
            P(),
            P(),
            P("wt", None),
            P(),
            P("wt", None),
            P(),
            P(),
            P(),
            P(),
            P(),
            P(),
            P(),
            P(),
            P(),
            P(),
            P(),
            P(),
        ),
        out_specs=(
            P(("wt", "seq"), None),
            P(("wt", "seq"), None),
            P("wt", None),
            P("wt"),
            P("wt"),
            P("wt", None),
            P("wt"),
            P("wt"),
            P("wt"),
            P("wt", None),
            P("wt"),
            P("wt", None),
            P("wt"),
            P("wt"),
            P("wt"),
            P(),
            P("wt"),
            P("wt"),
        ),
        check_vma=False,
    )
```

```python
import functools

import jax
import jax.numpy as jnp
from jax import lax
from jax.experimental import pallas as pl
from jax.experimental.pallas import tpu as pltpu
from jax.sharding import PartitionSpec as P

PROMPT = 1024
GRP_WT = 1
GLEN = 3072
SHORT = 512
LONG = 1536
HD = 64
TQ = 512
KC = 512

epsilon = 1e-06
score_scale = 0.125
exp2_scale = 0.125 * 1.4426950408889634
root_half = 0.7071067811865476
density_scale = 0.3989422804014327
bf16 = jnp.bfloat16
f32 = jnp.float32

NT = (((1,), (1,)), ((), ()))
NN = (((1,), (0,)), ((), ()))
TN = (((0,), (0,)), ((), ()))


def mm(a, b, dims=NN):
    return lax.dot_general(a, b, dims, preferred_element_type=f32)


def natural_at(short_first, i):
    other = jnp.where(i == 2, 5, i - 1)
    return jnp.where(short_first | (i < 2), i, other)


def ordered_at(short_first, j):
    other = jnp.where(j == 5, 2, j + 1)
    return jnp.where(short_first | (j < 2), j, other)


def query_tiles(tile):
    def prompt(i, carry):
        tile(i, ())
        return carry

    def longer(i, carry):
        tile(i, (3, 4, 5))
        return carry

    lax.fori_loop(0, 2, prompt, 0)
    tile(2, (2,))
    lax.fori_loop(3, 6, longer, 0)


def remote(src, dst, sems, k, peer):
    return pltpu.make_async_remote_copy(
        src_ref=src,
        dst_ref=dst,
        send_sem=sems[0].at[k],
        recv_sem=sems[1].at[k],
        device_id=peer,
        device_id_type=pl.DeviceIdType.MESH,
    )


def send(src, dst, sems, k, peer):
    copy = remote(src, dst, sems, k, peer)
    copy.start()
    return copy


def value_scale(head, group, kept_ref, gate_ref, mask_ref):
    return mask_ref[head].astype(f32) * gate_ref[head] * kept_ref[group].astype(f32)


def attend_kernel(
    heads, n, lens_ref, kept_ref, gate_ref, mask_ref, qb_ref, vb_ref, tok_ref, w_ref, wo_ref,
    packed_ref, ctx_ref, lse_ref, full_ref, wo_all,
    q_sc, k_sc, vt_sc, ct_sc, vec_ref, wo_buf, local_sem, s_sem, r_sem, s_w, r_w, s_f, r_f,
):
    s, w = lax.axis_index("seq"), lax.axis_index("wt")
    others = [flip(s, k) for k in (1, 2, 3)]
    mate = (s, flip(w, 1))
    far = [(s, lax.rem(w + 2 * j, n)) for j in range(1, n // 2)]
    short_first = lens_ref[w, 0] == SHORT
    come = pltpu.make_async_copy(wo_ref, wo_buf, local_sem.at[heads])
    come.start()
    meet([(p, w) for p in others] + [mate] + far)
    held = [send(wo_ref, wo_all.at[w], (s_w, r_w), k, peer) for k, peer in enumerate(far + [mate])]
    width = heads * HD
    count = GLEN // 4
    vec_ref[...] = jnp.zeros_like(vec_ref)
    for k in range(4):

        @pl.when(s == k)
        def _(k=k):
            query = qb_ref[...].astype(f32).reshape(1, 4 * width)
            value = vb_ref[...].astype(f32).reshape(1, 4 * width)
            for h in range(heads):
                own = slice(k * width + h * HD, k * width + (h + 1) * HD)
                at = 3 * HD * h
                vec_ref[0:1, at : at + HD] = query[:, own]
                vec_ref[0:1, at + 2 * HD : at + 3 * HD] = value[:, own]

    for h in range(heads):
        at = 3 * HD * h
        vec_ref[1:2, at : at + 2 * HD] = jnp.ones((1, 2 * HD), f32)
        scale = value_scale(s * heads + h, w, kept_ref, gate_ref, mask_ref)
        vec_ref[1:2, at + 2 * HD : at + 3 * HD] = jnp.full((1, HD), scale, f32)
    come.wait()
    wo_own = pltpu.make_async_copy(wo_buf, wo_all.at[w], local_sem.at[heads])
    wo_own.start()

    def project(i, carry):
        rows = pl.ds(pl.multiple_of(i * TQ, TQ), TQ)
        x = mm(tok_ref[natural_at(short_first, i)], w_ref[...]) + vec_ref[0:1, :]
        x = (x * vec_ref[1:2, :]).astype(bf16)
        for h in range(heads):
            at = 3 * HD * h
            packed_ref[h, rows, :] = x[:, at : at + 3 * HD]
            q_sc[h, rows, :] = x[:, at : at + HD]
            k_sc[h, rows, :] = x[:, at + HD : at + 2 * HD]
            vt_sc[h, :, rows] = x[:, at + 2 * HD : at + 3 * HD].T
        return carry

    lax.fori_loop(0, GLEN // TQ, project, 0)

    def leaving(h):
        rows = pl.ds(pl.multiple_of(h * HD, HD), HD)
        there = full_ref.at[pl.ds(pl.multiple_of(s * width + h * HD, HD), HD), :]

        def part(p):
            return ctx_ref.at[rows, pl.ds(pl.multiple_of(p * count, 128), count)]

        copies = [
            remote(part(p), there, (s_sem, r_sem), 3 * h + k, (p, w)) for k, p in enumerate(others)
        ]
        return copies, pltpu.make_async_copy(part(s), there, local_sem.at[h])

    def one_head(h, carry):
        def tile(i, own_blocks):
            rows = pl.ds(pl.multiple_of(i * TQ, TQ), TQ)
            q = q_sc[h, rows, :]
            s1 = mm(k_sc[h, 0:PROMPT, :], q, NT)
            top = jnp.max(s1, axis=0, keepdims=True)
            if own_blocks:
                own = slice(own_blocks[0] * KC, (own_blocks[-1] + 1) * KC)
                s2 = mm(k_sc[h, own, :], q, NT)
                top = jnp.maximum(top, jnp.max(s2, axis=0, keepdims=True))
            top = top * exp2_scale
            p1 = jnp.exp2(s1 * exp2_scale - top)
            o = mm(vt_sc[h, :, 0:PROMPT], p1.astype(bf16))
            total = jnp.sum(p1, axis=0, keepdims=True)
            if own_blocks:
                p2 = jnp.exp2(s2 * exp2_scale - top)
                o = o + mm(vt_sc[h, :, own], p2.astype(bf16))
                total = total + jnp.sum(p2, axis=0, keepdims=True)
            ct_sc[i] = (o / total).astype(bf16)
            lse_ref[h, :, rows] = top + jnp.log2(total)

        query_tiles(tile)

        def settle(j, carry):
            rows = pl.ds(pl.multiple_of(h * HD, HD), HD)
            lanes = pl.ds(pl.multiple_of(j * SHORT, SHORT), SHORT)
            ctx_ref[rows, lanes] = ct_sc[ordered_at(short_first, j)]
            return carry

        lax.fori_loop(0, GLEN // SHORT, settle, 0)
        copies, own = leaving(h)
        for copy in copies:
            copy.start()
        own.start()
        return carry

    lax.fori_loop(0, heads - 1, one_head, 0)
    passed = []
    for j in range(1, n // 2):
        origin = lax.rem(w + n - 2 * j, n)
        held[j - 1].wait_recv()
        passed.append(send(wo_all.at[origin], wo_all.at[origin], (s_f, r_f), j - 1, mate))
    lax.fori_loop(heads - 1, heads, one_head, 0)
    wo_own.wait()
    held[-1].wait_recv()
    for copy in passed:
        copy.wait()
    for copy in held:
        copy.wait_send()
    for h in range(heads):
        copies, own = leaving(h)
        own.wait()
        for copy in copies:
            copy.wait()


def attend(n, lens, kept, gate, mask, query_bias, value_bias, tokens_all, weight, wo, heads):
    width = 3 * HD * heads
    return pl.pallas_call(
        functools.partial(attend_kernel, heads, n),
        out_shape=(
            jax.ShapeDtypeStruct((heads, GLEN, 3 * HD), bf16),
            jax.ShapeDtypeStruct((HD * heads, GLEN), bf16),
            jax.ShapeDtypeStruct((heads, 1, GLEN), f32),
            jax.ShapeDtypeStruct((4 * HD * heads, GLEN // 4), bf16),
            jax.ShapeDtypeStruct((n,) + wo.shape, bf16),
        ),
        in_specs=[IN_SMEM] * 4 + [IN_VMEM] * 4 + [ANYWHERE],
        out_specs=(IN_VMEM, IN_VMEM, IN_VMEM, ANYWHERE, ANYWHERE),
        scratch_shapes=[
            pltpu.VMEM((heads, GLEN, HD), bf16),
            pltpu.VMEM((heads, GLEN, HD), bf16),
            pltpu.VMEM((heads, HD, GLEN), bf16),
            pltpu.VMEM((GLEN // TQ, HD, TQ), bf16),
            pltpu.VMEM((2, width), f32),
            pltpu.VMEM(wo.shape, bf16),
            pltpu.SemaphoreType.DMA((heads + 1,)),
        ]
        + dma_sems(3 * heads)
        + dma_sems(n // 2)
        + dma_sems(n // 2 - 1),
        compiler_params=remote_params(1),
        cost_estimate=pl.CostEstimate(
            flops=2 * GLEN * 768 * width + heads * 4 * 256 * 5767168,
            bytes_accessed=2 * GLEN * (768 + width),
            transcendentals=heads * 5767168,
        ),
        name="attend",
    )(
        lens, kept, gate, mask, query_bias, value_bias,
        tokens_all.reshape(GLEN // TQ, TQ, -1), weight, wo,
    )


def attend_back_kernel(
    heads, n, lens_ref, kept_ref, gate_ref, mask_ref, packed_hbm, ctx_ref, g_hbm, lse_ref, tok_hbm,
    e_mine, e_mate, o_mine, o_mate, pieces_o, dw_o, exp_o, out_o, late_o,
    packed_v, tok_v, e_own, o_own, e_got, o_got, e_all, o_all, e_sum, o_sum, e_z, o_z, gh0, gh1, gh2, st0, st1, st2,
    q_sc, k_sc, v_sc, kt_sc, g_sc, g_nat, delta_sc, delta_nat, dqt_sc, dk_sc, dv_sc, acc,
    l_in, l_g, l_out, s_g, r_g, s_p, r_p, s_c, r_c, s_e, r_e, s_z, r_z,
):
    s, w = lax.axis_index("seq"), lax.axis_index("wt")
    others = [flip(s, k) for k in (1, 2, 3)]
    mate = (s, flip(w, 1))
    z, c, nz = w // 2, lax.rem(w, 2), n // 2
    far = [lax.rem(z + j, nz) for j in range(1, nz)]
    short_first = lens_ref[w, 0] == SHORT
    count = GLEN // 4
    width = heads * HD
    gh, stage = (gh0, gh1, gh2)[:heads], (st0, st1, st2)[:heads]
    loads = [
        pltpu.make_async_copy(packed_hbm.at[h], packed_v.at[h], l_in.at[h]) for h in range(heads)
    ] + [
        pltpu.make_async_copy(e_mine, e_own, l_in.at[heads]),
        pltpu.make_async_copy(o_mine, o_own, l_in.at[heads + 1]),
        pltpu.make_async_copy(tok_hbm, tok_v, l_in.at[heads + 2]),
    ]
    for copy in loads:
        copy.start()
    meet([(p, w) for p in others] + [mate] + [(s, 2 * k + c) for k in far])

    def coming(h, own=False):
        def part(p):
            return g_hbm.at[pl.ds(pl.multiple_of(p * width + h * HD, HD), HD), :]

        there = gh[h].at[:, pl.ds(pl.multiple_of(s * count, 128), count)]
        if own:
            return pltpu.make_async_copy(part(s), there, l_g.at[h])
        return [remote(part(p), there, (s_g, r_g), 3 * h + k, (p, w)) for k, p in enumerate(others)]

    def leaving(h):
        copies = [
            remote(stage[h].at[p], pieces_o.at[h, s], (s_p, r_p), 3 * h + k, (p, w))
            for k, p in enumerate(others)
        ]
        return copies, pltpu.make_async_copy(stage[h].at[s], pieces_o.at[h, s], l_out.at[h])

    over_pair = [
        remote(e_mate, e_got, (s_c, r_c), 0, mate),
        remote(o_mate, o_got, (s_c, r_c), 1, mate),
    ]
    over_plane = [
        remote(e_got.at[p], e_all.at[s], (s_e, r_e), k, (p, w)) for k, p in enumerate(others)
    ] + [remote(o_got.at[p], o_all.at[s], (s_e, r_e), 3 + k, (p, w)) for k, p in enumerate(others)]
    over_z = [
        remote(e_sum.at[k], e_z.at[z], (s_z, r_z), j, (s, 2 * k + c)) for j, k in enumerate(far)
    ] + [
        remote(o_sum.at[k], o_z.at[z], (s_z, r_z), nz - 1 + j, (s, 2 * k + c))
        for j, k in enumerate(far)
    ]
    for h in range(heads):
        for copy in coming(h) + [coming(h, True)]:
            copy.start()
        if h == 0:
            for copy in over_pair:
                copy.start()
    late_o[...] = jnp.zeros_like(late_o)

    def prologue(h):
        loads[h].wait()

        def split(i, carry):
            rows = pl.ds(pl.multiple_of(i * TQ, TQ), TQ)
            x = packed_v[h, rows, :]
            q_sc[i] = x[:, 0:HD]
            k = x[:, HD : 2 * HD]
            k_sc[i] = k
            kt_sc[i] = k.T
            v_sc[i] = x[:, 2 * HD : 3 * HD]
            return carry

        lax.fori_loop(0, GLEN // TQ, split, 0)
        dk_sc[...] = jnp.zeros_like(dk_sc)
        dv_sc[...] = jnp.zeros_like(dv_sc)
        if h == 0:
            loads[heads].wait()
            loads[heads + 1].wait()
            for copy in over_pair:
                copy.wait_recv()

            def pair_sum(i, carry):
                q, k = i // nz, lax.rem(i, nz)
                e_got[q, k] = (e_got[q, k].astype(f32) + e_own[q, k].astype(f32)).astype(bf16)
                o_got[q, k] = (o_got[q, k].astype(f32) + o_own[q, k].astype(f32)).astype(bf16)
                return carry

            lax.fori_loop(0, 4 * nz, pair_sum, 0)
        coming(h, True).wait()
        for copy in coming(h):
            copy.wait_recv()
        if h == 0:
            for copy in over_plane:
                copy.start()
            e_all[s] = e_got[s]
            o_all[s] = o_got[s]

        def inner(j, carry):
            lanes = pl.ds(pl.multiple_of(j * TQ, TQ), TQ)
            g = gh[h][:, lanes]
            g_nat[j] = g
            product = g.astype(f32) * ctx_ref[HD * h : HD * (h + 1), lanes].astype(f32)
            delta_nat[j] = jnp.sum(product, axis=0, keepdims=True)
            return carry

        def order(i, carry):
            g_sc[i] = g_nat[natural_at(short_first, i)]
            delta_sc[i] = delta_nat[natural_at(short_first, i)]
            return carry

        lax.fori_loop(0, GLEN // TQ, inner, 0)
        lax.fori_loop(0, GLEN // TQ, order, 0)

    def epilogue(h):
        half = SHORT // 2
        lanes = slice(HD * h, HD * (h + 1))

        scale = value_scale(s * heads + h, w, kept_ref, gate_ref, mask_ref)

        def settle(j, carry):
            i = ordered_at(short_first, j)
            dq = dqt_sc[i].T.astype(bf16)
            dk = (dk_sc[i] * score_scale).astype(bf16)
            dv = dv_sc[i].astype(bf16).astype(f32)
            late_o[2:3, lanes] += jnp.sum(dv * v_sc[i].astype(f32), axis=0, keepdims=True)
            dv = (dv * scale).astype(bf16)
            late_o[0:1, lanes] += jnp.sum(dq.astype(f32), axis=0, keepdims=True)
            late_o[1:2, lanes] += jnp.sum(dv.astype(f32), axis=0, keepdims=True)
            for r in range(2):
                u = 2 * j + r
                p, there = u // 3, pl.ds(pl.multiple_of(lax.rem(u, 3) * half, half), half)
                rows = slice(r * half, (r + 1) * half)
                stage[h][p, there, 0:HD] = dq[rows]
                stage[h][p, there, HD : 2 * HD] = dk[rows]
                stage[h][p, there, 2 * HD : 3 * HD] = dv[rows]
            return carry

        lax.fori_loop(0, GLEN // SHORT, settle, 0)
        copies, own = leaving(h)
        for copy in copies:
            copy.start()
        own.start()

    def tile_of(h):
        def tile(i, own_blocks):
            q = q_sc[i]
            g = g_sc[i]
            lse = lse_ref[h, :, pl.ds(pl.multiple_of(i * TQ, TQ), TQ)]
            delta = delta_sc[i]
            dq = jnp.zeros((HD, TQ), f32)
            for j in (0, 1) + own_blocks:
                sc = mm(k_sc[j], q, NT)
                p = jnp.exp2(sc * exp2_scale - lse)
                dp = mm(v_sc[j], g)
                ds = (p * (dp - delta)).astype(bf16)
                dv_sc[j] += mm(p.astype(bf16), g, NT)
                dk_sc[j] += mm(ds, q)
                dq = dq + mm(kt_sc[j], ds)
            dqt_sc[i] = dq * score_scale

        return tile

    def one_head(h, carry):
        for j in range(heads):

            @pl.when(h == j)
            def _(j=j):
                prologue(j)

        query_tiles(tile_of(h))
        for j in range(heads):

            @pl.when(h == j)
            def _(j=j):
                epilogue(j)

        return carry

    lax.fori_loop(0, heads, one_head, 0)
    for copy in over_plane:
        copy.wait_recv()

    def add4(ref, k):
        t = [ref[q, k].astype(f32) for q in range(4)]
        return ((t[0] + t[1]) + (t[2] + t[3])).astype(bf16)

    def plane_sum(k, carry):
        e_sum[k] = add4(e_all, k)
        o_sum[k] = add4(o_all, k)
        return carry

    lax.fori_loop(0, nz, plane_sum, 0)
    for copy in over_z:
        copy.start()
    e_z[z] = e_sum[z]
    o_z[z] = o_sum[z]
    loads[heads + 2].wait()
    acc[...] = jnp.zeros_like(acc)

    def weight_grad(p, carry):
        x = tok_v[pl.ds(pl.multiple_of(p * count, count), count), :]
        for h in range(heads):
            acc[:, 3 * HD * h : 3 * HD * (h + 1)] += mm(x, stage[h][p], TN)
        return carry

    lax.fori_loop(0, 4, weight_grad, 0)
    own_rows = dw_o.shape[1]
    for k in range(n):
        dw_o[k] = acc[k * own_rows : (k + 1) * own_rows, :].astype(bf16)
    for copy in over_z:
        copy.wait_recv()
    for ref, out in ((e_z, exp_o), (o_z, out_o)):
        total = ref[0].astype(f32)
        for k in range(1, nz):
            total = total + ref[k].astype(f32)
        out[...] = total.astype(bf16)
    for h in range(heads):
        copies, own = leaving(h)
        own.wait()
        for copy in copies:
            copy.wait()
        for copy in coming(h):
            copy.wait_send()
    for copy in over_pair + over_plane + over_z:
        copy.wait_send()


def attend_back(n, lens, kept, gate, mask, packed, ctx, g, lse, tokens_all, e_mine, e_mate, o_mine, o_mate):
    heads = packed.shape[0]
    width = 3 * HD * heads
    d = tokens_all.shape[1]
    count = GLEN // 4
    nz = n // 2
    own, wide = e_mine.shape[2:]
    part = o_mine.shape[3]
    blocks = GLEN // TQ
    rows64 = pltpu.VMEM((blocks, TQ, HD), bf16)
    blocks64 = pltpu.VMEM((blocks, HD, TQ), bf16)
    lanes64 = pltpu.VMEM((HD, GLEN), bf16)
    quarters = [pltpu.VMEM(e_mine.shape, bf16), pltpu.VMEM(o_mine.shape, bf16)]
    return pl.pallas_call(
        functools.partial(attend_back_kernel, heads, n),
        out_shape=(
            jax.ShapeDtypeStruct((heads, 4, count, 3 * HD), bf16),
            jax.ShapeDtypeStruct((n, d // n, width), bf16),
            jax.ShapeDtypeStruct((own, wide), bf16),
            jax.ShapeDtypeStruct((own, part), bf16),
            jax.ShapeDtypeStruct((8, HD * heads), f32),
        ),
        in_specs=[IN_SMEM] * 4
        + [ANYWHERE, IN_VMEM, ANYWHERE, IN_VMEM, ANYWHERE]
        + [ANYWHERE] * 4,
        out_specs=(ANYWHERE, IN_VMEM, IN_VMEM, IN_VMEM, IN_VMEM),
        scratch_shapes=[
            pltpu.VMEM(packed.shape, bf16),
            pltpu.VMEM(tokens_all.shape, bf16),
        ]
        + quarters * 3
        + [pltpu.VMEM((nz, own, wide), bf16), pltpu.VMEM((nz, own, part), bf16)] * 2
        + [lanes64] * 3
        + [pltpu.VMEM((4, count, 3 * HD), bf16)] * 3
        + [
            rows64,
            rows64,
            rows64,
            blocks64,
            blocks64,
            blocks64,
            pltpu.VMEM((blocks, 1, TQ), f32),
            pltpu.VMEM((blocks, 1, TQ), f32),
            pltpu.VMEM((blocks, HD, TQ), f32),
            pltpu.VMEM((blocks, TQ, HD), f32),
            pltpu.VMEM((blocks, TQ, HD), f32),
            pltpu.VMEM((d, width), f32),
            pltpu.SemaphoreType.DMA((heads + 3,)),
            pltpu.SemaphoreType.DMA((heads,)),
            pltpu.SemaphoreType.DMA((heads,)),
        ]
        + dma_sems(3 * heads)
        + dma_sems(3 * heads)
        + dma_sems(2)
        + dma_sems(6)
        + dma_sems(2 * nz - 2),
        compiler_params=remote_params(2),
        cost_estimate=pl.CostEstimate(
            flops=heads * 10 * 256 * 5767168 + 2 * GLEN * d * width,
            bytes_accessed=2 * GLEN * (3 * width + d),
            transcendentals=heads * 5767168,
        ),
        name="attend_back",
    )(lens, kept, gate, mask, packed, ctx, g, lse, tokens_all, e_mine, e_mate, o_mine, o_mate)


def meet(peers):
    barrier = pltpu.get_barrier_semaphore()
    for peer in peers:
        pl.semaphore_signal(barrier, inc=1, device_id=peer, device_id_type=pl.DeviceIdType.MESH)
    pl.semaphore_wait(barrier, len(peers))


def flip(index, bits):
    for bit in (1, 2):
        if bits & bit:
            index = index + bit - 2 * bit * ((index // bit) % 2)
    return index


def remote_params(number):
    return pltpu.CompilerParams(
        collective_id=number, has_side_effects=True, vmem_limit_bytes=56 * 2**20
    )


ANYWHERE = pl.BlockSpec(memory_space=pl.ANY)
IN_VMEM = pl.BlockSpec(memory_space=pltpu.VMEM)
IN_SMEM = pl.BlockSpec(memory_space=pltpu.SMEM)


def dma_sems(count):
    return [pltpu.SemaphoreType.DMA((count,)), pltpu.SemaphoreType.DMA((count,))]


def gather_kernel(
    n, tok_ref, weight_ref, tok_all, cols_all, tok_buf, cols_buf, local_sem, s_tok, r_tok, s_w, r_w, s_f, r_f
):
    s, w = lax.axis_index("seq"), lax.axis_index("wt")
    rows = tok_ref.shape[0]
    half = rows // 2
    wide = cols_buf.shape[1]
    for k in range(4):

        @pl.when(s == k)
        def _(k=k):
            cols_buf[...] = weight_ref[:, k * wide : (k + 1) * wide]

    by_x, by_y, mate = (flip(s, 1), w), (flip(s, 2), w), (s, flip(w, 1))
    far = [(s, lax.rem(w + 2 * j, n)) for j in range(1, n // 2)]
    come = pltpu.make_async_copy(tok_ref, tok_buf, local_sem.at[0])
    come.start()
    meet([by_x, by_y, mate] + far)

    def part(owner, k):
        return pl.ds(pl.multiple_of(owner * rows + k * half, half), half)

    tok = (s_tok, r_tok)
    first = [pl.ds(0, half), pl.ds(half, half)]
    x0 = send(tok_ref.at[first[0]], tok_all.at[part(s, 0)], tok, 0, by_x)
    y1 = send(tok_ref.at[first[1]], tok_all.at[part(s, 1)], tok, 1, by_y)
    x1 = send(tok_ref.at[first[1]], tok_all.at[part(s, 1)], tok, 2, by_x)
    y0 = send(tok_ref.at[first[0]], tok_all.at[part(s, 0)], tok, 3, by_y)
    held = [
        send(cols_buf, cols_all.at[w], (s_w, r_w), k, peer) for k, peer in enumerate(far + [mate])
    ]
    come.wait()
    own = [
        pltpu.make_async_copy(
            tok_buf, tok_all.at[pl.ds(pl.multiple_of(s * rows, rows), rows)], local_sem.at[0]
        ),
        pltpu.make_async_copy(cols_buf, cols_all.at[w], local_sem.at[1]),
    ]
    for copy in own:
        copy.start()
    passed = []
    for j in range(1, n // 2):
        origin = lax.rem(w + n - 2 * j, n)
        held[j - 1].wait_recv()
        passed.append(send(cols_all.at[origin], cols_all.at[origin], (s_f, r_f), j - 1, mate))
    x0.wait_recv()
    there = tok_all.at[part(flip(s, 1), 0)]
    passed.append(send(there, there, tok, 4, by_y))
    y1.wait_recv()
    there = tok_all.at[part(flip(s, 2), 1)]
    passed.append(send(there, there, tok, 5, by_x))
    for copy in own:
        copy.wait()
    for copy in [x1, y0, held[-1]] + passed:
        copy.wait_recv()
    for copy in [x0, x1, y0, y1] + held + passed:
        copy.wait_send()


def gather_in(n, tokens, attention_weight):
    rows, d = tokens.shape
    own, width = attention_weight.shape
    return pl.pallas_call(
        functools.partial(gather_kernel, n),
        out_shape=(
            jax.ShapeDtypeStruct((4 * rows, d), bf16),
            jax.ShapeDtypeStruct((n, own, width // 4), bf16),
        ),
        in_specs=[ANYWHERE, IN_VMEM],
        out_specs=(ANYWHERE,) * 2,
        scratch_shapes=[
            pltpu.VMEM(tokens.shape, bf16),
            pltpu.VMEM((own, width // 4), bf16),
            pltpu.SemaphoreType.DMA((2,)),
        ]
        + dma_sems(6)
        + dma_sems(n // 2)
        + dma_sems(n // 2 - 1),
        compiler_params=remote_params(0),
        name="gather_in",
    )(tokens, attention_weight)


def final_kernel(
    heads, n, base_hbm, pieces_hbm, w_hbm, con_ref, out_ref, att_ref, exp_ref, vec_ref, late_ref,
    tok_o, g_con, g_out, g_exp, g_att, r_vec2, r_late2,
    base_v, pieces_v, w_v, r_con, h_att, m_att, r_att, r_vec, r_late,
    l_in, *sems,
):
    s, w = lax.axis_index("seq"), lax.axis_index("wt")
    z, c = w // 2, lax.rem(w, 2)
    nz = n // 2
    others = [flip(s, k) for k in (1, 2, 3)]
    seq_peers = [(p, w) for p in others]
    mate = (s, flip(w, 1))
    wt_peers = [(s, lax.rem(w + j, n)) for j in range(1, n)]
    names = ("pair", "vec", "late", "con", "out2", "att", "vec2", "late2", "con2", "exp2", "att2")
    sem = {name: (sems[2 * k], sems[2 * k + 1]) for k, name in enumerate(names)}
    loads = [
        pltpu.make_async_copy(src, dst, l_in.at[k])
        for k, (src, dst) in enumerate(((pieces_hbm, pieces_v), (w_hbm, w_v), (base_hbm, base_v)))
    ]
    for copy in loads:
        copy.start()
    meet(seq_peers + wt_peers)
    pair = [send(att_ref.at[2 * k + 1 - c], h_att.at[k], sem["pair"], k, mate) for k in range(nz)]
    cons = [send(con_ref.at[p], r_con.at[s], sem["con"], k, (p, w)) for k, p in enumerate(others)]
    far = [lax.rem(z + j, nz) for j in range(1, nz)]
    exp2 = [send(exp_ref, g_exp.at[s], sem["exp2"], k, p) for k, p in enumerate(seq_peers)]
    out2 = [send(out_ref, g_out.at[s], sem["out2"], k, p) for k, p in enumerate(seq_peers)]
    vecs = [
        send(vec_ref.at[lax.rem(w + j, n)], r_vec.at[w], sem["vec"], j - 1, wt_peers[j - 1])
        for j in range(1, n)
    ]
    lates = [send(late_ref, r_late.at[w], sem["late"], j, p) for j, p in enumerate(wt_peers)]
    r_con[s] = con_ref[s]
    g_exp[s] = exp_ref[...]
    r_vec[w] = vec_ref[w]
    r_late[w] = late_ref[...]
    g_out[s] = out_ref[...]
    for copy in pair:
        copy.wait_recv()
    for k in range(nz):
        m_att[k] = (att_ref[2 * k + c].astype(f32) + h_att[k].astype(f32)).astype(bf16)
    atts = [send(m_att.at[k], r_att.at[z], sem["att"], j, (s, 2 * k + c)) for j, k in enumerate(far)]
    r_att[z] = m_att[z]
    for copy in loads:
        copy.wait()
    cols = 3 * HD
    rows = tok_o.shape[0]
    block = rows // 3

    def tokens_block(i, carry):
        there = pl.ds(pl.multiple_of(i * block, block), block)
        total = base_v[there, :]
        for h in range(heads):
            for k in range(4):
                at = (heads * k + h) * cols
                total = total + mm(pieces_v[h, k, there, :], w_v[:, at : at + cols], NT)
        tok_o[there, :] = total
        return carry

    lax.fori_loop(0, 1, tokens_block, 0)

    def total_of(ref, count):
        total = ref[0].astype(f32)
        for k in range(1, count):
            total = total + ref[k].astype(f32)
        return total

    for copy in cons:
        copy.wait_recv()
    g_con[s] = total_of(r_con, 4).astype(bf16)
    con2 = [send(g_con.at[s], g_con.at[s], sem["con2"], k, p) for k, p in enumerate(seq_peers)]
    for copy in vecs + lates:
        copy.wait_recv()
    r_vec2[s] = total_of(r_vec, n)
    r_late2[s] = total_of(r_late, n)
    vec2 = [send(r_vec2.at[s], r_vec2.at[s], sem["vec2"], k, p) for k, p in enumerate(seq_peers)]
    late2 = [send(r_late2.at[s], r_late2.at[s], sem["late2"], k, p) for k, p in enumerate(seq_peers)]
    lax.fori_loop(1, 2, tokens_block, 0)
    for copy in atts:
        copy.wait_recv()
    g_att[s] = total_of(r_att, nz).astype(bf16)
    att2 = [send(g_att.at[s], g_att.at[s], sem["att2"], k, p) for k, p in enumerate(seq_peers)]
    lax.fori_loop(2, 3, tokens_block, 0)
    for copy in out2 + con2 + vec2 + late2 + exp2 + att2:
        copy.wait_recv()
    for copy in pair + cons + vecs + lates + atts + con2 + vec2 + late2 + exp2 + out2 + att2:
        copy.wait_send()


def final(n, base, pieces, weight, con, out, att, exp_part, vec, late):
    heads = pieces.shape[0]
    r, d = con.shape[1:]
    cols = att.shape[2]
    nz = n // 2
    counts = (nz, n - 1, n - 1, 3, 3, nz - 1, 3, 3, 3, 3, 3)
    return pl.pallas_call(
        functools.partial(final_kernel, heads, n),
        out_shape=(
            jax.ShapeDtypeStruct(base.shape, f32),
            jax.ShapeDtypeStruct((4, r, d), bf16),
            jax.ShapeDtypeStruct((4,) + out.shape, bf16),
            jax.ShapeDtypeStruct((4,) + exp_part.shape, bf16),
            jax.ShapeDtypeStruct((4, r, cols), bf16),
            jax.ShapeDtypeStruct((4,) + vec.shape[1:], f32),
            jax.ShapeDtypeStruct((4,) + late.shape, f32),
        ),
        in_specs=[ANYWHERE] * 3 + [IN_VMEM] * 6,
        out_specs=(IN_VMEM,) * 7,
        scratch_shapes=[
            pltpu.VMEM(base.shape, f32),
            pltpu.VMEM(pieces.shape, bf16),
            pltpu.VMEM(weight.shape, bf16),
            pltpu.VMEM((4, r, d), bf16),
            pltpu.VMEM((nz, r, cols), bf16),
            pltpu.VMEM((nz, r, cols), bf16),
            pltpu.VMEM((nz, r, cols), bf16),
            pltpu.VMEM((n,) + vec.shape[1:], f32),
            pltpu.VMEM((n,) + late.shape, f32),
            pltpu.SemaphoreType.DMA((3,)),
        ]
        + [sem for count in counts for sem in dma_sems(count)],
        compiler_params=remote_params(3),
        cost_estimate=pl.CostEstimate(
            flops=8 * base.shape[0] * d * cols, bytes_accessed=8 * d * cols, transcendentals=0
        ),
        name="final",
    )(base, pieces, weight, con, out, att, exp_part, vec, late)


def finish_kernel(n, heads, gate_ref, mask_ref, *refs):
    sources, rest = refs[:7], refs[7:]
    con_o, out_o, exp_o, att_o, tok_o = rest[:5]
    vec_os, unit_os, query_o, value_o, gate_o = rest[5:12], rest[12:14], rest[14], rest[15], rest[16]
    con_v, out_v, exp_v, att_v, vec_v, late_v, sem = rest[17:]
    loads = [
        pltpu.make_async_copy(src, dst, sem.at[k])
        for k, (src, dst) in enumerate(
            zip(sources, (con_v, out_v, exp_v, att_v, vec_v, late_v, tok_o), strict=True)
        )
    ]
    for copy in loads:
        copy.start()

    def add4(parts):
        return (parts[0] + parts[1]) + (parts[2] + parts[3])

    for copy in loads:
        copy.wait()
    wide, cols, part = exp_v.shape[2], att_v.shape[2], out_v.shape[2]
    for k in range(4):
        con_o[k] = con_v[k].astype(f32)
        exp_o[:, k * wide : (k + 1) * wide] = exp_v[k].astype(f32)
        att_o[:, k * cols : (k + 1) * cols] = att_v[k].astype(f32)
        out_o[:, k * part : (k + 1) * part] = out_v[k].astype(f32)
    vec = add4([vec_v[k] for k in range(4)])
    own = vec_os[0].shape[0]
    for k, ref in enumerate(vec_os):
        ref[...] = vec[k, 0:own]
    for k, ref in enumerate(unit_os):
        ref[...] = vec[8 + k]
    rows = [jnp.concatenate([late_v[k, j : j + 1, :] for k in range(4)], axis=1) for j in range(2)]
    for k in range(n):

        @pl.when(lax.axis_index("wt") == k)
        def _(k=k):
            query_o[...] = rows[0][0, k * own : (k + 1) * own]
            value_o[...] = rows[1][0, k * own : (k + 1) * own]

    gates = []
    for k in range(4):
        for h in range(heads):
            part_sum = jnp.sum(late_v[k, 2:3, HD * h : HD * (h + 1)], axis=1, keepdims=True)
            kept = mask_ref[heads * k + h].astype(f32) / gate_ref[heads * k + h]
            gates.append(part_sum * kept)
    gate_o[...] = jnp.concatenate(gates, axis=1)[0]


def finish(n, heads, gate, mask, con, out, exp_all, att, vec, late, tok):
    r = out.shape[1]
    wide, cols, part = exp_all.shape[2], att.shape[2], out.shape[2]
    units = vec.shape[2]
    row = jax.ShapeDtypeStruct((r,), f32)
    return pl.pallas_call(
        functools.partial(finish_kernel, n, heads),
        out_shape=(
            jax.ShapeDtypeStruct(con.shape, f32),
            jax.ShapeDtypeStruct((r, 4 * part), f32),
            jax.ShapeDtypeStruct((r, 4 * wide), f32),
            jax.ShapeDtypeStruct((r, 4 * cols), f32),
            jax.ShapeDtypeStruct(tok.shape, f32),
        )
        + (row,) * 7
        + (jax.ShapeDtypeStruct((units,), f32),) * 2
        + (row,) * 2
        + (jax.ShapeDtypeStruct((4 * heads,), f32),),
        in_specs=[IN_SMEM] * 2 + [ANYWHERE] * 7,
        out_specs=(IN_VMEM,) * 17,
        scratch_shapes=[pltpu.VMEM(x.shape, x.dtype) for x in (con, out, exp_all, att, vec, late)]
        + [pltpu.SemaphoreType.DMA((7,))],
        compiler_params=pltpu.CompilerParams(vmem_limit_bytes=56 * 2**20),
        name="finish",
    )(gate, mask, con, out, exp_all, att, vec, late, tok)


(OUT_BIAS, GAIN1, SHIFT1, HIDDEN_SCALE, CON_BIAS, GAIN2, SHIFT2, HIDDEN_MASK) = range(8)
(S_OUT_BIAS, S_GAIN1, S_SHIFT1, S_CON_BIAS, S_GAIN2, S_SHIFT2, S_HIDDEN) = range(7)


def gelu_parts(x):
    bell = jnp.exp(-0.5 * (x * x))
    t = 1.0 / (1.0 + (0.3275911 * root_half) * jnp.abs(x))
    poly = t * (
        0.127414796 + t * (-0.142248368 + t * (0.7107068705 + t * (-0.7265760135 + t * 0.5307027145)))
    )
    tail = poly * bell
    cumulative = jnp.where(x < 0.0, tail, 1.0 - tail)
    return x * cumulative, cumulative + x * bell * density_scale


def norm_parts(summed):
    centre = summed - jnp.mean(summed, axis=-1, keepdims=True)
    inverse = lax.rsqrt(jnp.mean(centre * centre, axis=-1, keepdims=True) + epsilon)
    return (centre * inverse, inverse)


def norm_back(grad_normed, normed, inverse):
    return inverse * (
        grad_normed
        - jnp.mean(grad_normed, axis=-1, keepdims=True)
        - normed * jnp.mean(grad_normed * normed, axis=-1, keepdims=True)
    )


def feed_forward_kernel(
    steps, chunk,
    kept_ref, ctx_ref, tok_ref, cot_ref, wo_ref, we_ref, wc_ref,
    ob_ref, g1_ref, t1_ref, hg_ref, hm_ref, cb_ref, g2_ref, t2_ref, eb_ref, ug_ref, um_ref,
    lo_ref, dt1_ref, gctx_ref, vec_ref, dwc_ref, mine_ref, mate_ref, omine_ref, omate_ref,
    wide_ref, unit_ref, sw_ref, su_ref, act_sc, gh_sc, low_sc, gb_sc, ga_sc, ctx_sc, gelu_sc, slope_sc,
):
    i = pl.program_id(0)
    block = tok_ref.shape[0]
    units = we_ref.shape[1]
    rows = pl.ds(pl.multiple_of(i * block, block), block)
    core = lax.rem(lax.axis_index("wt"), 2)

    @pl.when(i == 0)
    def _():
        sw_ref[...] = jnp.zeros_like(sw_ref)
        su_ref[...] = jnp.zeros_like(su_ref)

        def row(ref):
            return ref[...].astype(f32).reshape(1, ref.shape[0])

        plain = ((OUT_BIAS, ob_ref), (GAIN1, g1_ref), (SHIFT1, t1_ref), (CON_BIAS, cb_ref))
        for k, ref in plain + ((GAIN2, g2_ref), (SHIFT2, t2_ref), (HIDDEN_MASK, hm_ref)):
            wide_ref[k : k + 1, :] = row(ref)
        wide_ref[HIDDEN_SCALE : HIDDEN_SCALE + 1, :] = row(hm_ref) * row(hg_ref)
        kept = row(um_ref) * kept_ref[lax.axis_index("wt")].astype(f32)
        unit_ref[0:1, :] = row(eb_ref)
        unit_ref[1:2, :] = kept * row(ug_ref)
        unit_ref[2:3, :] = kept

    def wide(k):
        return wide_ref[k : k + 1, :]

    def add_sum(ref, k, cols, value):
        ref[k : k + 1, cols] += jnp.sum(value, axis=0, keepdims=True)

    full = slice(None)
    ctx = ctx_ref[...]
    ctx_sc[:, rows] = ctx
    summed = mm(ctx, wo_ref[...], TN) + wide(OUT_BIAS) + tok_ref[...].astype(f32)
    n1, inv1 = norm_parts(summed)
    s1 = n1 * wide(GAIN1) + wide(SHIFT1)
    hs = wide(HIDDEN_SCALE)
    first = s1 * hs
    low = first.astype(bf16)
    low_sc[rows, :] = low
    branch = first + wide(CON_BIAS)
    for j in range(units // chunk):
        cols = slice(j * chunk, (j + 1) * chunk)
        hidden = mm(low, we_ref[:, cols]) + unit_ref[0:1, cols]
        gelu, slope = gelu_parts(hidden)
        scale = unit_ref[1:2, cols]
        gelu_sc[:, cols] = gelu.astype(gelu_sc.dtype)
        slope_sc[:, cols] = (slope * scale).astype(slope_sc.dtype)
        act = (gelu * scale).astype(bf16)
        act_sc[rows, cols] = act
        branch = branch + mm(act, wc_ref[cols, :])
    n2, inv2 = norm_parts(branch)
    s2 = n2 * wide(GAIN2) + wide(SHIFT2)
    lo_ref[...] = (s2 * hs).astype(bf16)
    dy = cot_ref[...].astype(f32)
    e2 = dy * hs
    add_sum(sw_ref, S_GAIN2, full, e2 * n2)
    add_sum(sw_ref, S_SHIFT2, full, e2)
    dt2 = norm_back(e2 * wide(GAIN2), n2, inv2)
    gb = dt2.astype(bf16)
    gb_sc[rows, :] = gb
    add_sum(sw_ref, S_CON_BIAS, full, gb.astype(f32))
    d_first = dt2
    for j in range(units // chunk):
        cols = slice(j * chunk, (j + 1) * chunk)
        d_act = mm(gb, wc_ref[cols, :], NT)
        add_sum(su_ref, 1, cols, d_act * gelu_sc[:, cols].astype(f32))
        gh = d_act * slope_sc[:, cols].astype(f32)
        add_sum(su_ref, 0, cols, gh)
        gh = gh.astype(bf16)
        gh_sc[rows, cols] = gh
        d_first = d_first + mm(gh, we_ref[:, cols], NT)
    e1 = d_first * hs
    add_sum(sw_ref, S_GAIN1, full, e1 * n1)
    add_sum(sw_ref, S_SHIFT1, full, e1)
    add_sum(sw_ref, S_HIDDEN, full, dy * s2 + d_first * s1)
    dt1 = norm_back(e1 * wide(GAIN1), n1, inv1)
    dt1_ref[...] = dt1
    ga = dt1.astype(bf16)
    ga_sc[rows, :] = ga
    add_sum(sw_ref, S_OUT_BIAS, full, ga.astype(f32))
    gctx_ref[...] = mm(wo_ref[...], ga, NT).astype(bf16)

    @pl.when(i == steps - 1)
    def _():
        for j in range(units // chunk):
            cols = slice(j * chunk, (j + 1) * chunk)
            dwc_ref[cols, :] = mm(act_sc[:, cols], gb_sc[...], TN).astype(bf16)
            part = mm(low_sc[...], gh_sc[:, cols], TN).astype(bf16)
            own, wide_cols = mine_ref.shape[2:]
            for c in range(2):

                @pl.when(core == c)
                def _(part=part, j=j, c=c):
                    for q in range(chunk // wide_cols):
                        at = j * (chunk // wide_cols) + q
                        inner = slice(q * wide_cols, (q + 1) * wide_cols)
                        for z in range(mine_ref.shape[1]):
                            mine = (2 * z + c) * own
                            mate = (2 * z + 1 - c) * own
                            mine_ref[at, z] = part[mine : mine + own, inner]
                            mate_ref[at, z] = part[mate : mate + own, inner]

        part = mm(ctx_sc[...], ga_sc[...]).astype(bf16)
        own, part_cols = omine_ref.shape[2:]
        for c in range(2):

            @pl.when(core == c)
            def _(part=part, c=c):
                for q in range(4):
                    inner = slice(q * part_cols, (q + 1) * part_cols)
                    for z in range(omine_ref.shape[1]):
                        mine = (2 * z + c) * own
                        mate = (2 * z + 1 - c) * own
                        omine_ref[q, z] = part[mine : mine + own, inner]
                        omate_ref[q, z] = part[mate : mate + own, inner]

        vec_ref[...] = jnp.zeros_like(vec_ref)
        sw_ref[S_HIDDEN : S_HIDDEN + 1, :] *= wide(HIDDEN_MASK)
        su_ref[1:2, :] *= unit_ref[2:3, :]
        own_wide, own_units = mine_ref.shape[2], vec_ref.shape[2]
        for k in range(vec_ref.shape[0]):
            vec_ref[k, 0:8, 0:own_wide] = sw_ref[:, k * own_wide : (k + 1) * own_wide]
            vec_ref[k, 8:16, :] = su_ref[:, k * own_units : (k + 1) * own_units]


def feed_forward(n, kept, ctx_t, tokens, cotangent, wo, we, wc, *vectors):
    steps, chunk, keep = 3, 768, f32
    rows, d = tokens.shape
    units = we.shape[1]
    block = rows // steps
    halves = (4, n // 2, d // n, units // 4)
    out_halves = (4, n // 2, d // n, d // 4)
    tile = pl.BlockSpec((block, d), lambda i: (i, 0))
    lanes = pl.BlockSpec((d, block), lambda i: (0, i))

    def once(shape):
        return pl.BlockSpec(shape, lambda i: (0, 0), pipeline_mode=pl.Buffered(1))

    def once3(shape):
        return pl.BlockSpec(shape, lambda i: (0, 0, 0), pipeline_mode=pl.Buffered(1))

    def once4(shape):
        return pl.BlockSpec(shape, lambda i: (0, 0, 0, 0), pipeline_mode=pl.Buffered(1))

    return pl.pallas_call(
        functools.partial(feed_forward_kernel, steps, chunk),
        out_shape=(
            jax.ShapeDtypeStruct((rows, d), bf16),
            jax.ShapeDtypeStruct((rows, d), f32),
            jax.ShapeDtypeStruct((d, rows), bf16),
            jax.ShapeDtypeStruct((n, 16, units // n), f32),
            jax.ShapeDtypeStruct((units, d), bf16),
            jax.ShapeDtypeStruct(halves, bf16),
            jax.ShapeDtypeStruct(halves, bf16),
            jax.ShapeDtypeStruct(out_halves, bf16),
            jax.ShapeDtypeStruct(out_halves, bf16),
        ),
        grid=(steps,),
        in_specs=[
            pl.BlockSpec(memory_space=pltpu.SMEM),
            lanes, tile, tile, once((d, d)), once((d, units)), once((units, d)),
        ]
        + [IN_VMEM] * len(vectors),
        out_specs=(
            tile, tile, lanes, once3((n, 16, units // n)), once((units, d)),
            once4(halves), once4(halves), once4(out_halves), once4(out_halves),
        ),
        scratch_shapes=[
            pltpu.VMEM((8, d), f32),
            pltpu.VMEM((8, units), f32),
            pltpu.VMEM((8, d), f32),
            pltpu.VMEM((8, units), f32),
            pltpu.VMEM((rows, units), bf16),
            pltpu.VMEM((rows, units), bf16),
            pltpu.VMEM((rows, d), bf16),
            pltpu.VMEM((rows, d), bf16),
            pltpu.VMEM((rows, d), bf16),
            pltpu.VMEM((d, rows), bf16),
            pltpu.VMEM((block, units), keep),
            pltpu.VMEM((block, units), keep),
        ],
        compiler_params=pltpu.CompilerParams(vmem_limit_bytes=60 * 2**20),
        cost_estimate=pl.CostEstimate(
            flops=rows * d * (12 * units + 6 * d),
            bytes_accessed=4 * d * (4 * units + 2 * d) + 12 * rows * d,
            transcendentals=2 * rows * units,
        ),
        name="feed_forward",
    )(kept, ctx_t, tokens, cotangent, wo, we, wc, *vectors)


def local(
    tokens,
    output_cotangent,
    attention_weight,
    query_bias,
    value_bias,
    output_weight,
    output_bias,
    first_gain,
    first_shift,
    expand_weight,
    expand_bias,
    contract_weight,
    contract_bias,
    second_gain,
    second_shift,
    head_gate,
    hidden_gate,
    unit_gate,
    head_mask,
    hidden_mask,
    unit_mask,
    attention_mask,
    feedforward_mask,
    continuation_lengths,
):
    seq_count = lax.axis_size("seq")
    wt_count = lax.axis_size("wt")
    model_width = hidden_gate.shape[0]
    local_heads = head_gate.shape[0] // seq_count
    own_wide = model_width // wt_count
    tokens_all, own_weight = gather_in(wt_count, tokens, attention_weight)
    full_expand = lax.all_gather(expand_weight, "wt", axis=0, tiled=True)
    full_contract = lax.all_gather(contract_weight, "wt", axis=0, tiled=True)
    full_attention = lax.all_gather(attention_weight, "wt", axis=0, tiled=True)
    packed, own_context, log_sums, context_t, full_output = attend(
        wt_count,
        continuation_lengths,
        attention_mask,
        head_gate,
        head_mask,
        query_bias,
        value_bias,
        tokens_all,
        own_weight.reshape(model_width, -1),
        output_weight,
        local_heads,
    )
    (
        layer_output,
        grad_total_one,
        grad_context_t,
        vec_sums,
        contract_weight_grad,
        exp_mine,
        exp_mate,
        out_mine,
        out_mate,
    ) = feed_forward(
        wt_count,
        feedforward_mask,
        context_t,
        tokens,
        output_cotangent,
        full_output.reshape(model_width, model_width),
        full_expand,
        full_contract,
        output_bias,
        first_gain,
        first_shift,
        hidden_gate,
        hidden_mask,
        contract_bias,
        second_gain,
        second_shift,
        expand_bias,
        unit_gate,
        unit_mask,
    )
    con_piece = lax.psum_scatter(contract_weight_grad, "wt", scatter_dimension=0, tiled=True)
    pieces, projection_grad, exp_part, out_part, late_sums = attend_back(
        wt_count,
        continuation_lengths,
        attention_mask,
        head_gate,
        head_mask,
        packed,
        own_context,
        grad_context_t,
        log_sums,
        tokens_all,
        exp_mine,
        exp_mate,
        out_mine,
        out_mate,
    )
    tokens_grad, con_all, out_all, exp_all, att_all, vec_all, late_all = final(
        wt_count,
        grad_total_one,
        pieces,
        full_attention,
        con_piece.reshape(seq_count, own_wide, model_width),
        out_part,
        projection_grad,
        exp_part,
        vec_sums,
        late_sums,
    )
    con_sum, out_sum, exp_sum, att_sum, tokens_grad, *rows = finish(
        wt_count,
        local_heads,
        head_gate,
        head_mask,
        con_all,
        out_all,
        exp_all,
        att_all,
        vec_all,
        late_all,
        tokens_grad,
    )
    return (
        layer_output,
        tokens_grad,
        att_sum,
        rows[9],
        rows[10],
        out_sum,
        rows[S_OUT_BIAS],
        rows[S_GAIN1],
        rows[S_SHIFT1],
        exp_sum,
        rows[7],
        con_sum.reshape(seq_count * own_wide, model_width),
        rows[S_CON_BIAS],
        rows[S_GAIN2],
        rows[S_SHIFT2],
        rows[11],
        rows[S_HIDDEN],
        rows[8],
    )


def solution(mesh):
    return jax.shard_map(
        local,
        mesh=mesh,
        in_specs=(
            P(("wt", "seq"), None),
            P(("wt", "seq"), None),
            P("wt", None),
            P(),
            P(),
            P("wt", None),
            P(),
            P(),
            P(),
            P("wt", None),
            P(),
            P("wt", None),
            P(),
            P(),
            P(),
            P(),
            P(),
            P(),
            P(),
            P(),
            P(),
            P(),
            P(),
            P(),
        ),
        out_specs=(
            P(("wt", "seq"), None),
            P(("wt", "seq"), None),
            P("wt", None),
            P("wt"),
            P("wt"),
            P("wt", None),
            P("wt"),
            P("wt"),
            P("wt"),
            P("wt", None),
            P("wt"),
            P("wt", None),
            P("wt"),
            P("wt"),
            P("wt"),
            P(),
            P("wt"),
            P("wt"),
        ),
        check_vma=False,
    )
```

```python
import functools

import jax
import jax.numpy as jnp
from jax import lax
from jax.experimental import pallas as pl
from jax.experimental.pallas import tpu as pltpu
from jax.sharding import PartitionSpec as P

PROMPT = 1024
GRP_WT = 1
GLEN = 3072
SHORT = 512
LONG = 1536
HD = 64
TQ = 512
KC = 512

epsilon = 1e-06
score_scale = 0.125
exp2_scale = 0.125 * 1.4426950408889634
root_half = 0.7071067811865476
density_scale = 0.3989422804014327
bf16 = jnp.bfloat16
f32 = jnp.float32

NT = (((1,), (1,)), ((), ()))
NN = (((1,), (0,)), ((), ()))
TN = (((0,), (0,)), ((), ()))


def mm(a, b, dims=NN):
    return lax.dot_general(a, b, dims, preferred_element_type=f32)


def natural_at(short_first, i):
    other = jnp.where(i == 2, 5, i - 1)
    return jnp.where(short_first | (i < 2), i, other)


def ordered_at(short_first, j):
    other = jnp.where(j == 5, 2, j + 1)
    return jnp.where(short_first | (j < 2), j, other)


def query_tiles(tile):
    def prompt(i, carry):
        tile(i, ())
        return carry

    def longer(i, carry):
        tile(i, (3, 4, 5))
        return carry

    lax.fori_loop(0, 2, prompt, 0)
    tile(2, (2,))
    lax.fori_loop(3, 6, longer, 0)


def remote(src, dst, sems, k, peer):
    return pltpu.make_async_remote_copy(
        src_ref=src,
        dst_ref=dst,
        send_sem=sems[0].at[k],
        recv_sem=sems[1].at[k],
        device_id=peer,
        device_id_type=pl.DeviceIdType.MESH,
    )


def send(src, dst, sems, k, peer):
    copy = remote(src, dst, sems, k, peer)
    copy.start()
    return copy


def value_scale(head, group, kept_ref, gate_ref, mask_ref):
    return mask_ref[head].astype(f32) * gate_ref[head] * kept_ref[group].astype(f32)


def attend_kernel(
    heads, n, lens_ref, kept_ref, gate_ref, mask_ref, qb_ref, vb_ref, tok_ref, w_ref, wo_ref, exp_ref,
    packed_ref, ctx_ref, lse_ref, full_ref, wo_all, exp_all,
    q_sc, k_sc, vt_sc, ct_sc, vec_ref, wo_buf, exp_buf,
    local_sem, s_sem, r_sem, s_w, r_w, s_f, r_f, s_e, r_e,
):
    s, w = lax.axis_index("seq"), lax.axis_index("wt")
    others = [flip(s, k) for k in (1, 2, 3)]
    mate = (s, flip(w, 1))
    far = [(s, lax.rem(w + 2 * j, n)) for j in range(1, n // 2)]
    short_first = lens_ref[w, 0] == SHORT
    come = [
        pltpu.make_async_copy(wo_ref, wo_buf, local_sem.at[heads]),
        pltpu.make_async_copy(exp_ref, exp_buf, local_sem.at[heads + 1]),
    ]
    for copy in come:
        copy.start()
    meet([(p, w) for p in others] + [mate] + far)
    core, quarter = lax.rem(w, 2), exp_ref.shape[2]

    def exp_place(p):
        return exp_all.at[:, core, :, pl.ds(pl.multiple_of(p * quarter, 128), quarter)]

    spread = [
        send(exp_ref, exp_place(s), (s_e, r_e), k, (p, w)) for k, p in enumerate(others)
    ] + [send(exp_ref, exp_place(s), (s_e, r_e), 3, mate)]
    held = [send(wo_ref, wo_all.at[w], (s_w, r_w), k, peer) for k, peer in enumerate(far + [mate])]
    width = heads * HD
    count = GLEN // 4
    vec_ref[...] = jnp.zeros_like(vec_ref)
    for k in range(4):

        @pl.when(s == k)
        def _(k=k):
            query = qb_ref[...].astype(f32).reshape(1, 4 * width)
            value = vb_ref[...].astype(f32).reshape(1, 4 * width)
            for h in range(heads):
                own = slice(k * width + h * HD, k * width + (h + 1) * HD)
                at = 3 * HD * h
                vec_ref[0:1, at : at + HD] = query[:, own]
                vec_ref[0:1, at + 2 * HD : at + 3 * HD] = value[:, own]

    for h in range(heads):
        at = 3 * HD * h
        vec_ref[1:2, at : at + 2 * HD] = jnp.ones((1, 2 * HD), f32)
        scale = value_scale(s * heads + h, w, kept_ref, gate_ref, mask_ref)
        vec_ref[1:2, at + 2 * HD : at + 3 * HD] = jnp.full((1, HD), scale, f32)
    for copy in come:
        copy.wait()
    own_parts = [
        pltpu.make_async_copy(wo_buf, wo_all.at[w], local_sem.at[heads]),
        pltpu.make_async_copy(exp_buf, exp_place(s), local_sem.at[heads + 1]),
    ]
    for copy in own_parts:
        copy.start()

    def project(i, carry):
        rows = pl.ds(pl.multiple_of(i * TQ, TQ), TQ)
        x = mm(tok_ref[natural_at(short_first, i)], w_ref[...]) + vec_ref[0:1, :]
        x = (x * vec_ref[1:2, :]).astype(bf16)
        for h in range(heads):
            at = 3 * HD * h
            packed_ref[h, rows, :] = x[:, at : at + 3 * HD]
            q_sc[h, rows, :] = x[:, at : at + HD]
            k_sc[h, rows, :] = x[:, at + HD : at + 2 * HD]
            vt_sc[h, :, rows] = x[:, at + 2 * HD : at + 3 * HD].T
        return carry

    lax.fori_loop(0, GLEN // TQ, project, 0)

    def leaving(h):
        rows = pl.ds(pl.multiple_of(h * HD, HD), HD)
        there = full_ref.at[pl.ds(pl.multiple_of(s * width + h * HD, HD), HD), :]

        def part(p):
            return ctx_ref.at[rows, pl.ds(pl.multiple_of(p * count, 128), count)]

        copies = [
            remote(part(p), there, (s_sem, r_sem), 3 * h + k, (p, w)) for k, p in enumerate(others)
        ]
        return copies, pltpu.make_async_copy(part(s), there, local_sem.at[h])

    def one_head(h, carry):
        def tile(i, own_blocks):
            rows = pl.ds(pl.multiple_of(i * TQ, TQ), TQ)
            q = q_sc[h, rows, :]
            s1 = mm(k_sc[h, 0:PROMPT, :], q, NT)
            top = jnp.max(s1, axis=0, keepdims=True)
            if own_blocks:
                own = slice(own_blocks[0] * KC, (own_blocks[-1] + 1) * KC)
                s2 = mm(k_sc[h, own, :], q, NT)
                top = jnp.maximum(top, jnp.max(s2, axis=0, keepdims=True))
            top = top * exp2_scale
            p1 = jnp.exp2(s1 * exp2_scale - top)
            o = mm(vt_sc[h, :, 0:PROMPT], p1.astype(bf16))
            total = jnp.sum(p1, axis=0, keepdims=True)
            if own_blocks:
                p2 = jnp.exp2(s2 * exp2_scale - top)
                o = o + mm(vt_sc[h, :, own], p2.astype(bf16))
                total = total + jnp.sum(p2, axis=0, keepdims=True)
            ct_sc[i] = (o / total).astype(bf16)
            lse_ref[h, :, rows] = top + jnp.log2(total)

        query_tiles(tile)

        def settle(j, carry):
            rows = pl.ds(pl.multiple_of(h * HD, HD), HD)
            lanes = pl.ds(pl.multiple_of(j * SHORT, SHORT), SHORT)
            ctx_ref[rows, lanes] = ct_sc[ordered_at(short_first, j)]
            return carry

        lax.fori_loop(0, GLEN // SHORT, settle, 0)
        copies, own = leaving(h)
        for copy in copies:
            copy.start()
        own.start()
        return carry

    lax.fori_loop(0, heads - 1, one_head, 0)
    passed = []
    for j in range(1, n // 2):
        origin = lax.rem(w + n - 2 * j, n)
        held[j - 1].wait_recv()
        passed.append(send(wo_all.at[origin], wo_all.at[origin], (s_f, r_f), j - 1, mate))
    for k, p in enumerate(others):
        spread[k].wait_recv()
        passed.append(send(exp_place(p), exp_place(p), (s_e, r_e), 4 + k, mate))
    lax.fori_loop(heads - 1, heads, one_head, 0)
    for copy in own_parts:
        copy.wait()
    for copy in (held[-1], spread[3]):
        copy.wait_recv()
    for copy in passed:
        copy.wait()
    for copy in held + spread:
        copy.wait_send()
    for h in range(heads):
        copies, own = leaving(h)
        own.wait()
        for copy in copies:
            copy.wait()


def attend(n, lens, kept, gate, mask, query_bias, value_bias, tokens_all, weight, wo, exp_part, heads):
    width = 3 * HD * heads
    return pl.pallas_call(
        functools.partial(attend_kernel, heads, n),
        out_shape=(
            jax.ShapeDtypeStruct((heads, GLEN, 3 * HD), bf16),
            jax.ShapeDtypeStruct((HD * heads, GLEN), bf16),
            jax.ShapeDtypeStruct((heads, 1, GLEN), f32),
            jax.ShapeDtypeStruct((4 * HD * heads, GLEN // 4), bf16),
            jax.ShapeDtypeStruct((n,) + wo.shape, bf16),
            jax.ShapeDtypeStruct((n // 2, 2, exp_part.shape[1], 4 * exp_part.shape[2]), bf16),
        ),
        in_specs=[IN_SMEM] * 4 + [IN_VMEM] * 4 + [ANYWHERE] * 2,
        out_specs=(IN_VMEM, IN_VMEM, IN_VMEM, ANYWHERE, ANYWHERE, ANYWHERE),
        scratch_shapes=[
            pltpu.VMEM((heads, GLEN, HD), bf16),
            pltpu.VMEM((heads, GLEN, HD), bf16),
            pltpu.VMEM((heads, HD, GLEN), bf16),
            pltpu.VMEM((GLEN // TQ, HD, TQ), bf16),
            pltpu.VMEM((2, width), f32),
            pltpu.VMEM(wo.shape, bf16),
            pltpu.VMEM(exp_part.shape, bf16),
            pltpu.SemaphoreType.DMA((heads + 2,)),
        ]
        + dma_sems(3 * heads)
        + dma_sems(n // 2)
        + dma_sems(n // 2 - 1)
        + dma_sems(7),
        compiler_params=remote_params(1),
        cost_estimate=pl.CostEstimate(
            flops=2 * GLEN * 768 * width + heads * 4 * 256 * 5767168,
            bytes_accessed=2 * GLEN * (768 + width),
            transcendentals=heads * 5767168,
        ),
        name="attend",
    )(
        lens, kept, gate, mask, query_bias, value_bias,
        tokens_all.reshape(GLEN // TQ, TQ, -1), weight, wo, exp_part,
    )


def attend_back_kernel(
    heads, n, lens_ref, kept_ref, gate_ref, mask_ref, packed_hbm, ctx_ref, g_hbm, lse_ref, tok_hbm,
    e_hbm, o_hbm, pieces_o, dw_o, exp_o, out_o, late_o,
    packed_v, tok_v, e_own, o_own, e_got, o_got, e_all, o_all, e_sum, o_sum, e_z, o_z, gh0, gh1, gh2, st0, st1, st2,
    q_sc, k_sc, v_sc, kt_sc, g_sc, g_nat, delta_sc, delta_nat, dqt_sc, dk_sc, dv_sc, acc,
    l_in, l_g, l_out, s_g, r_g, s_p, r_p, s_c, r_c, s_e, r_e, s_z, r_z,
):
    s, w = lax.axis_index("seq"), lax.axis_index("wt")
    others = [flip(s, k) for k in (1, 2, 3)]
    mate = (s, flip(w, 1))
    z, c, nz = w // 2, lax.rem(w, 2), n // 2
    far = [lax.rem(z + j, nz) for j in range(1, nz)]
    short_first = lens_ref[w, 0] == SHORT
    count = GLEN // 4
    width = heads * HD
    gh, stage = (gh0, gh1, gh2)[:heads], (st0, st1, st2)[:heads]
    loads = [
        pltpu.make_async_copy(packed_hbm.at[h], packed_v.at[h], l_in.at[h]) for h in range(heads)
    ] + [
        pltpu.make_async_copy(e_hbm.at[c], e_own, l_in.at[heads]),
        pltpu.make_async_copy(o_hbm.at[c], o_own, l_in.at[heads + 1]),
        pltpu.make_async_copy(tok_hbm, tok_v, l_in.at[heads + 2]),
    ]
    for copy in loads:
        copy.start()
    meet([(p, w) for p in others] + [mate] + [(s, 2 * k + c) for k in far])

    def coming(h, own=False):
        def part(p):
            return g_hbm.at[pl.ds(pl.multiple_of(p * width + h * HD, HD), HD), :]

        there = gh[h].at[:, pl.ds(pl.multiple_of(s * count, 128), count)]
        if own:
            return pltpu.make_async_copy(part(s), there, l_g.at[h])
        return [remote(part(p), there, (s_g, r_g), 3 * h + k, (p, w)) for k, p in enumerate(others)]

    def leaving(h, own=False):
        if own:
            return pltpu.make_async_copy(stage[h].at[s], pieces_o.at[h, s], l_out.at[h])
        return [
            remote(stage[h].at[p], pieces_o.at[h, s], (s_p, r_p), 3 * h + k, (p, w))
            for k, p in enumerate(others)
        ]

    over_pair = [
        remote(e_hbm.at[1 - c], e_got, (s_c, r_c), 0, mate),
        remote(o_hbm.at[1 - c], o_got, (s_c, r_c), 1, mate),
    ]
    over_plane = [
        remote(e_got.at[p], e_all.at[s], (s_e, r_e), k, (p, w)) for k, p in enumerate(others)
    ] + [remote(o_got.at[p], o_all.at[s], (s_e, r_e), 3 + k, (p, w)) for k, p in enumerate(others)]
    over_z = [
        remote(e_sum.at[k], e_z.at[z], (s_z, r_z), j, (s, 2 * k + c)) for j, k in enumerate(far)
    ] + [
        remote(o_sum.at[k], o_z.at[z], (s_z, r_z), nz - 1 + j, (s, 2 * k + c))
        for j, k in enumerate(far)
    ]
    for h in range(heads):
        for copy in coming(h) + [coming(h, True)]:
            copy.start()
        if h == 0:
            for copy in over_pair:
                copy.start()
    late_o[...] = jnp.zeros_like(late_o)

    def prologue(h):
        loads[h].wait()

        def split(i, carry):
            rows = pl.ds(pl.multiple_of(i * TQ, TQ), TQ)
            x = packed_v[h, rows, :]
            q_sc[i] = x[:, 0:HD]
            k = x[:, HD : 2 * HD]
            k_sc[i] = k
            kt_sc[i] = k.T
            v_sc[i] = x[:, 2 * HD : 3 * HD]
            return carry

        lax.fori_loop(0, GLEN // TQ, split, 0)
        dk_sc[...] = jnp.zeros_like(dk_sc)
        dv_sc[...] = jnp.zeros_like(dv_sc)
        coming(h, True).wait()
        for copy in coming(h):
            copy.wait_recv()

        def inner(j, carry):
            lanes = pl.ds(pl.multiple_of(j * TQ, TQ), TQ)
            g = gh[h][:, lanes]
            g_nat[j] = g
            product = g.astype(f32) * ctx_ref[HD * h : HD * (h + 1), lanes].astype(f32)
            delta_nat[j] = jnp.sum(product, axis=0, keepdims=True)
            return carry

        def order(i, carry):
            g_sc[i] = g_nat[natural_at(short_first, i)]
            delta_sc[i] = delta_nat[natural_at(short_first, i)]
            return carry

        lax.fori_loop(0, GLEN // TQ, inner, 0)
        lax.fori_loop(0, GLEN // TQ, order, 0)

    def halfway(h):
        if h == 0:
            loads[heads].wait()
            loads[heads + 1].wait()
            for copy in over_pair:
                copy.wait_recv()

            def pair_sum(i, carry):
                q, k = i // nz, lax.rem(i, nz)
                e_got[q, k] = (e_got[q, k].astype(f32) + e_own[q, k].astype(f32)).astype(bf16)
                o_got[q, k] = (o_got[q, k].astype(f32) + o_own[q, k].astype(f32)).astype(bf16)
                return carry

            lax.fori_loop(0, 4 * nz, pair_sum, 0)
            for copy in over_plane:
                copy.start()
            e_all[s] = e_got[s]
            o_all[s] = o_got[s]
        if h == heads - 1:
            for copy in over_plane:
                copy.wait_recv()

            def add4(ref, k):
                t = [ref[q, k].astype(f32) for q in range(4)]
                return ((t[0] + t[1]) + (t[2] + t[3])).astype(bf16)

            def plane_sum(k, carry):
                e_sum[k] = add4(e_all, k)
                o_sum[k] = add4(o_all, k)
                return carry

            lax.fori_loop(0, nz, plane_sum, 0)
            for copy in over_z:
                copy.start()
            e_z[z] = e_sum[z]
            o_z[z] = o_sum[z]

    def epilogue(h, first, last):
        half = SHORT // 2
        lanes = slice(HD * h, HD * (h + 1))

        scale = value_scale(s * heads + h, w, kept_ref, gate_ref, mask_ref)

        def settle(j, carry):
            i = ordered_at(short_first, j)
            dq = dqt_sc[i].T.astype(bf16)
            dk = (dk_sc[i] * score_scale).astype(bf16)
            dv = dv_sc[i].astype(bf16).astype(f32)
            late_o[2:3, lanes] += jnp.sum(dv * v_sc[i].astype(f32), axis=0, keepdims=True)
            dv = (dv * scale).astype(bf16)
            late_o[0:1, lanes] += jnp.sum(dq.astype(f32), axis=0, keepdims=True)
            late_o[1:2, lanes] += jnp.sum(dv.astype(f32), axis=0, keepdims=True)
            for r in range(2):
                u = 2 * j + r
                p, there = u // 3, pl.ds(pl.multiple_of(lax.rem(u, 3) * half, half), half)
                rows = slice(r * half, (r + 1) * half)
                stage[h][p, there, 0:HD] = dq[rows]
                stage[h][p, there, HD : 2 * HD] = dk[rows]
                stage[h][p, there, 2 * HD : 3 * HD] = dv[rows]
            return carry

        lax.fori_loop(first, last, settle, 0)
        for p, copy in zip(others, leaving(h), strict=True):

            @pl.when(p // 2 == (0 if first == 0 else 1))
            def _(copy=copy):
                copy.start()

        if first == 0:
            leaving(h, True).start()

    def tile_of(h):
        def tile(i, own_blocks):
            q = q_sc[i]
            g = g_sc[i]
            lse = lse_ref[h, :, pl.ds(pl.multiple_of(i * TQ, TQ), TQ)]
            delta = delta_sc[i]
            dq = jnp.zeros((HD, TQ), f32)
            for j in (0, 1) + own_blocks:
                sc = mm(k_sc[j], q, NT)
                p = jnp.exp2(sc * exp2_scale - lse)
                dp = mm(v_sc[j], g)
                ds = (p * (dp - delta)).astype(bf16)
                dv_sc[j] += mm(p.astype(bf16), g, NT)
                dk_sc[j] += mm(ds, q)
                dq = dq + mm(kt_sc[j], ds)
            dqt_sc[i] = dq * score_scale

        return tile

    def one_head(h, carry):
        for j in range(heads):

            @pl.when(h == j)
            def _(j=j):
                prologue(j)

        def longer(i, carry):
            tile_of(h)(i, (3, 4, 5))
            return carry

        def prompt(i, carry):
            tile_of(h)(i, ())
            return carry

        tile_of(h)(2, (2,))
        for j in (0, heads - 1):

            @pl.when(h == j)
            def _(j=j):
                halfway(j)

        lax.fori_loop(3, 6, longer, 0)
        for j in range(heads):

            @pl.when(h == j)
            def _(j=j):
                epilogue(j, 2, 6)

        lax.fori_loop(0, 2, prompt, 0)
        for j in range(heads):

            @pl.when(h == j)
            def _(j=j):
                epilogue(j, 0, 2)

        return carry

    lax.fori_loop(0, heads, one_head, 0)
    loads[heads + 2].wait()
    acc[...] = jnp.zeros_like(acc)

    def weight_grad(p, carry):
        x = tok_v[pl.ds(pl.multiple_of(p * count, count), count), :]
        for h in range(heads):
            acc[:, 3 * HD * h : 3 * HD * (h + 1)] += mm(x, stage[h][p], TN)
        return carry

    lax.fori_loop(0, 4, weight_grad, 0)
    own_rows = dw_o.shape[1]
    for k in range(n):
        dw_o[k] = acc[k * own_rows : (k + 1) * own_rows, :].astype(bf16)
    for copy in over_z:
        copy.wait_recv()
    for ref, out in ((e_z, exp_o), (o_z, out_o)):
        total = ref[0].astype(f32)
        for k in range(1, nz):
            total = total + ref[k].astype(f32)
        out[...] = total.astype(bf16)
    for h in range(heads):
        for copy in [leaving(h, True)] + leaving(h):
            copy.wait()
        for copy in coming(h):
            copy.wait_send()
    for copy in over_pair + over_plane + over_z:
        copy.wait_send()


def attend_back(n, lens, kept, gate, mask, packed, ctx, g, lse, tokens_all, e_parts, o_parts):
    heads = packed.shape[0]
    width = 3 * HD * heads
    d = tokens_all.shape[1]
    count = GLEN // 4
    nz = n // 2
    own, wide = e_parts.shape[3:]
    part = o_parts.shape[4]
    blocks = GLEN // TQ
    rows64 = pltpu.VMEM((blocks, TQ, HD), bf16)
    blocks64 = pltpu.VMEM((blocks, HD, TQ), bf16)
    lanes64 = pltpu.VMEM((HD, GLEN), bf16)
    quarters = [pltpu.VMEM(e_parts.shape[1:], bf16), pltpu.VMEM(o_parts.shape[1:], bf16)]
    return pl.pallas_call(
        functools.partial(attend_back_kernel, heads, n),
        out_shape=(
            jax.ShapeDtypeStruct((heads, 4, count, 3 * HD), bf16),
            jax.ShapeDtypeStruct((n, d // n, width), bf16),
            jax.ShapeDtypeStruct((own, wide), bf16),
            jax.ShapeDtypeStruct((own, part), bf16),
            jax.ShapeDtypeStruct((8, HD * heads), f32),
        ),
        in_specs=[IN_SMEM] * 4
        + [ANYWHERE, IN_VMEM, ANYWHERE, IN_VMEM, ANYWHERE]
        + [ANYWHERE] * 2,
        out_specs=(ANYWHERE, IN_VMEM, IN_VMEM, IN_VMEM, IN_VMEM),
        scratch_shapes=[
            pltpu.VMEM(packed.shape, bf16),
            pltpu.VMEM(tokens_all.shape, bf16),
        ]
        + quarters * 3
        + [pltpu.VMEM((nz, own, wide), bf16), pltpu.VMEM((nz, own, part), bf16)] * 2
        + [lanes64] * 3
        + [pltpu.VMEM((4, count, 3 * HD), bf16)] * 3
        + [
            rows64,
            rows64,
            rows64,
            blocks64,
            blocks64,
            blocks64,
            pltpu.VMEM((blocks, 1, TQ), f32),
            pltpu.VMEM((blocks, 1, TQ), f32),
            pltpu.VMEM((blocks, HD, TQ), f32),
            pltpu.VMEM((blocks, TQ, HD), f32),
            pltpu.VMEM((blocks, TQ, HD), f32),
            pltpu.VMEM((d, width), f32),
            pltpu.SemaphoreType.DMA((heads + 3,)),
            pltpu.SemaphoreType.DMA((heads,)),
            pltpu.SemaphoreType.DMA((heads,)),
        ]
        + dma_sems(3 * heads)
        + dma_sems(3 * heads)
        + dma_sems(2)
        + dma_sems(6)
        + dma_sems(2 * nz - 2),
        compiler_params=remote_params(2),
        cost_estimate=pl.CostEstimate(
            flops=heads * 10 * 256 * 5767168 + 2 * GLEN * d * width,
            bytes_accessed=2 * GLEN * (3 * width + d),
            transcendentals=heads * 5767168,
        ),
        name="attend_back",
    )(lens, kept, gate, mask, packed, ctx, g, lse, tokens_all, e_parts, o_parts)


def meet(peers):
    barrier = pltpu.get_barrier_semaphore()
    for peer in peers:
        pl.semaphore_signal(barrier, inc=1, device_id=peer, device_id_type=pl.DeviceIdType.MESH)
    pl.semaphore_wait(barrier, len(peers))


def flip(index, bits):
    for bit in (1, 2):
        if bits & bit:
            index = index + bit - 2 * bit * ((index // bit) % 2)
    return index


def remote_params(number):
    return pltpu.CompilerParams(
        collective_id=number, has_side_effects=True, vmem_limit_bytes=56 * 2**20
    )


ANYWHERE = pl.BlockSpec(memory_space=pl.ANY)
IN_VMEM = pl.BlockSpec(memory_space=pltpu.VMEM)
IN_SMEM = pl.BlockSpec(memory_space=pltpu.SMEM)


def dma_sems(count):
    return [pltpu.SemaphoreType.DMA((count,)), pltpu.SemaphoreType.DMA((count,))]


def gather_kernel(
    n, tok_ref, weight_ref, exp_ref, tok_all, cols_all, exp_all, tok_buf, cols_buf, exp_buf,
    local_sem, s_tok, r_tok, s_w, r_w, s_f, r_f, s_e, r_e,
):
    s, w = lax.axis_index("seq"), lax.axis_index("wt")
    rows = tok_ref.shape[0]
    half = rows // 2
    wide = cols_buf.shape[1]
    for k in range(4):

        @pl.when(s == k)
        def _(k=k):
            cols_buf[...] = weight_ref[:, k * wide : (k + 1) * wide]

    by_x, by_y, mate = (flip(s, 1), w), (flip(s, 2), w), (s, flip(w, 1))
    far = [(s, lax.rem(w + 2 * j, n)) for j in range(1, n // 2)]
    quarter = exp_buf.shape[1]
    exp_own = exp_ref.at[:, pl.ds(pl.multiple_of(s * quarter, 128), quarter)]
    come = [
        pltpu.make_async_copy(tok_ref, tok_buf, local_sem.at[0]),
        pltpu.make_async_copy(exp_own, exp_buf, local_sem.at[2]),
    ]
    for copy in come:
        copy.start()
    meet([by_x, by_y, mate] + far)

    def part(owner, k):
        return pl.ds(pl.multiple_of(owner * rows + k * half, half), half)

    tok = (s_tok, r_tok)
    first = [pl.ds(0, half), pl.ds(half, half)]
    x0 = send(tok_ref.at[first[0]], tok_all.at[part(s, 0)], tok, 0, by_x)
    y1 = send(tok_ref.at[first[1]], tok_all.at[part(s, 1)], tok, 1, by_y)
    x1 = send(tok_ref.at[first[1]], tok_all.at[part(s, 1)], tok, 2, by_x)
    y0 = send(tok_ref.at[first[0]], tok_all.at[part(s, 0)], tok, 3, by_y)
    held = [
        send(cols_buf, cols_all.at[w], (s_w, r_w), k, peer) for k, peer in enumerate(far + [mate])
    ]
    along = [
        send(exp_own, exp_all.at[w // 2], (s_e, r_e), k, peer) for k, peer in enumerate(far)
    ]
    for copy in come:
        copy.wait()
    own = [
        pltpu.make_async_copy(exp_buf, exp_all.at[w // 2], local_sem.at[2]),
        pltpu.make_async_copy(
            tok_buf, tok_all.at[pl.ds(pl.multiple_of(s * rows, rows), rows)], local_sem.at[0]
        ),
        pltpu.make_async_copy(cols_buf, cols_all.at[w], local_sem.at[1]),
    ]
    for copy in own:
        copy.start()
    passed = []
    for j in range(1, n // 2):
        origin = lax.rem(w + n - 2 * j, n)
        held[j - 1].wait_recv()
        passed.append(send(cols_all.at[origin], cols_all.at[origin], (s_f, r_f), j - 1, mate))
    x0.wait_recv()
    there = tok_all.at[part(flip(s, 1), 0)]
    passed.append(send(there, there, tok, 4, by_y))
    y1.wait_recv()
    there = tok_all.at[part(flip(s, 2), 1)]
    passed.append(send(there, there, tok, 5, by_x))
    for copy in own:
        copy.wait()
    for copy in [x1, y0, held[-1]] + passed + along:
        copy.wait_recv()
    for copy in [x0, x1, y0, y1] + held + passed + along:
        copy.wait_send()


def gather_in(n, tokens, attention_weight, expand_weight):
    rows, d = tokens.shape
    own, width = attention_weight.shape
    quarter = expand_weight.shape[1] // 4
    return pl.pallas_call(
        functools.partial(gather_kernel, n),
        out_shape=(
            jax.ShapeDtypeStruct((4 * rows, d), bf16),
            jax.ShapeDtypeStruct((n, own, width // 4), bf16),
            jax.ShapeDtypeStruct((n // 2, own, quarter), bf16),
        ),
        in_specs=[ANYWHERE, IN_VMEM, ANYWHERE],
        out_specs=(ANYWHERE,) * 3,
        scratch_shapes=[
            pltpu.VMEM(tokens.shape, bf16),
            pltpu.VMEM((own, width // 4), bf16),
            pltpu.VMEM((own, quarter), bf16),
            pltpu.SemaphoreType.DMA((3,)),
        ]
        + dma_sems(6)
        + dma_sems(n // 2)
        + dma_sems(n // 2 - 1)
        + dma_sems(n // 2 - 1),
        compiler_params=remote_params(0),
        name="gather_in",
    )(tokens, attention_weight, expand_weight)


def final_kernel(
    heads, n, base_hbm, pieces_hbm, w_hbm, con_ref, out_ref, att_ref, exp_ref, vec_ref, late_ref,
    tok_o, g_con, g_out, g_exp, g_att, r_vec2, r_late2,
    base_v, pieces_v, w_v, r_con, h_att, m_att, r_att, r_vec, r_late,
    l_in, *sems,
):
    s, w = lax.axis_index("seq"), lax.axis_index("wt")
    z, c = w // 2, lax.rem(w, 2)
    nz = n // 2
    others = [flip(s, k) for k in (1, 2, 3)]
    seq_peers = [(p, w) for p in others]
    mate = (s, flip(w, 1))
    wt_peers = [(s, lax.rem(w + j, n)) for j in range(1, n)]
    names = ("pair", "vec", "late", "con", "out2", "att", "vec2", "late2", "con2", "exp2", "att2")
    sem = {name: (sems[2 * k], sems[2 * k + 1]) for k, name in enumerate(names)}
    loads = [
        pltpu.make_async_copy(src, dst, l_in.at[k])
        for k, (src, dst) in enumerate(((pieces_hbm, pieces_v), (w_hbm, w_v), (base_hbm, base_v)))
    ]
    for copy in loads:
        copy.start()
    meet(seq_peers + wt_peers)
    pair = [send(att_ref.at[2 * k + 1 - c], h_att.at[k], sem["pair"], k, mate) for k in range(nz)]
    cons = [send(con_ref.at[p], r_con.at[s], sem["con"], k, (p, w)) for k, p in enumerate(others)]
    far = [lax.rem(z + j, nz) for j in range(1, nz)]
    exp2 = [send(exp_ref, g_exp.at[s], sem["exp2"], k, p) for k, p in enumerate(seq_peers)]
    out2 = [send(out_ref, g_out.at[s], sem["out2"], k, p) for k, p in enumerate(seq_peers)]
    vecs = [
        send(vec_ref.at[lax.rem(w + j, n)], r_vec.at[w], sem["vec"], j - 1, wt_peers[j - 1])
        for j in range(1, n)
    ]
    lates = [send(late_ref, r_late.at[w], sem["late"], j, p) for j, p in enumerate(wt_peers)]
    r_con[s] = con_ref[s]
    g_exp[s] = exp_ref[...]
    r_vec[w] = vec_ref[w]
    r_late[w] = late_ref[...]
    g_out[s] = out_ref[...]
    for copy in pair:
        copy.wait_recv()
    for k in range(nz):
        m_att[k] = (att_ref[2 * k + c].astype(f32) + h_att[k].astype(f32)).astype(bf16)
    atts = [send(m_att.at[k], r_att.at[z], sem["att"], j, (s, 2 * k + c)) for j, k in enumerate(far)]
    r_att[z] = m_att[z]
    for copy in loads:
        copy.wait()
    cols = 3 * HD
    rows = tok_o.shape[0]
    block = rows // 3

    def tokens_block(i, carry):
        there = pl.ds(pl.multiple_of(i * block, block), block)
        total = base_v[there, :]
        for h in range(heads):
            for k in range(4):
                at = (heads * k + h) * cols
                total = total + mm(pieces_v[h, k, there, :], w_v[:, at : at + cols], NT)
        tok_o[there, :] = total
        return carry

    lax.fori_loop(0, 1, tokens_block, 0)

    def total_of(ref, count):
        total = ref[0].astype(f32)
        for k in range(1, count):
            total = total + ref[k].astype(f32)
        return total

    for copy in cons:
        copy.wait_recv()
    g_con[s] = total_of(r_con, 4).astype(bf16)
    con2 = [send(g_con.at[s], g_con.at[s], sem["con2"], k, p) for k, p in enumerate(seq_peers)]
    for copy in vecs + lates:
        copy.wait_recv()
    r_vec2[s] = total_of(r_vec, n)
    r_late2[s] = total_of(r_late, n)
    vec2 = [send(r_vec2.at[s], r_vec2.at[s], sem["vec2"], k, p) for k, p in enumerate(seq_peers)]
    late2 = [send(r_late2.at[s], r_late2.at[s], sem["late2"], k, p) for k, p in enumerate(seq_peers)]
    lax.fori_loop(1, 2, tokens_block, 0)
    for copy in atts:
        copy.wait_recv()
    g_att[s] = total_of(r_att, nz).astype(bf16)
    att2 = [send(g_att.at[s], g_att.at[s], sem["att2"], k, p) for k, p in enumerate(seq_peers)]
    lax.fori_loop(2, 3, tokens_block, 0)
    for copy in out2 + con2 + vec2 + late2 + exp2 + att2:
        copy.wait_recv()
    for copy in pair + cons + vecs + lates + atts + con2 + vec2 + late2 + exp2 + out2 + att2:
        copy.wait_send()


def final(n, base, pieces, weight, con, out, att, exp_part, vec, late):
    heads = pieces.shape[0]
    r, d = con.shape[1:]
    cols = att.shape[2]
    nz = n // 2
    counts = (nz, n - 1, n - 1, 3, 3, nz - 1, 3, 3, 3, 3, 3)
    return pl.pallas_call(
        functools.partial(final_kernel, heads, n),
        out_shape=(
            jax.ShapeDtypeStruct(base.shape, f32),
            jax.ShapeDtypeStruct((4, r, d), bf16),
            jax.ShapeDtypeStruct((4,) + out.shape, bf16),
            jax.ShapeDtypeStruct((4,) + exp_part.shape, bf16),
            jax.ShapeDtypeStruct((4, r, cols), bf16),
            jax.ShapeDtypeStruct((4,) + vec.shape[1:], f32),
            jax.ShapeDtypeStruct((4,) + late.shape, f32),
        ),
        in_specs=[ANYWHERE] * 3 + [IN_VMEM] * 6,
        out_specs=(IN_VMEM,) * 7,
        scratch_shapes=[
            pltpu.VMEM(base.shape, f32),
            pltpu.VMEM(pieces.shape, bf16),
            pltpu.VMEM(weight.shape, bf16),
            pltpu.VMEM((4, r, d), bf16),
            pltpu.VMEM((nz, r, cols), bf16),
            pltpu.VMEM((nz, r, cols), bf16),
            pltpu.VMEM((nz, r, cols), bf16),
            pltpu.VMEM((n,) + vec.shape[1:], f32),
            pltpu.VMEM((n,) + late.shape, f32),
            pltpu.SemaphoreType.DMA((3,)),
        ]
        + [sem for count in counts for sem in dma_sems(count)],
        compiler_params=remote_params(3),
        cost_estimate=pl.CostEstimate(
            flops=8 * base.shape[0] * d * cols, bytes_accessed=8 * d * cols, transcendentals=0
        ),
        name="final",
    )(base, pieces, weight, con, out, att, exp_part, vec, late)


def finish_kernel(n, heads, gate_ref, mask_ref, *refs):
    sources, rest = refs[:7], refs[7:]
    con_o, out_o, exp_o, att_o, tok_o = rest[:5]
    vec_os, unit_os, query_o, value_o, gate_o = rest[5:12], rest[12:14], rest[14], rest[15], rest[16]
    con_v, out_v, exp_v, att_v, vec_v, late_v, sem = rest[17:]
    loads = [
        pltpu.make_async_copy(src, dst, sem.at[k])
        for k, (src, dst) in enumerate(
            zip(sources, (con_v, out_v, exp_v, att_v, vec_v, late_v, tok_o), strict=True)
        )
    ]
    for copy in loads:
        copy.start()

    def add4(parts):
        return (parts[0] + parts[1]) + (parts[2] + parts[3])

    for copy in loads:
        copy.wait()
    wide, cols, part = exp_v.shape[2], att_v.shape[2], out_v.shape[2]
    for k in range(4):
        con_o[k] = con_v[k].astype(f32)
        exp_o[:, k * wide : (k + 1) * wide] = exp_v[k].astype(f32)
        att_o[:, k * cols : (k + 1) * cols] = att_v[k].astype(f32)
        out_o[:, k * part : (k + 1) * part] = out_v[k].astype(f32)
    vec = add4([vec_v[k] for k in range(4)])
    own = vec_os[0].shape[0]
    for k, ref in enumerate(vec_os):
        ref[...] = vec[k, 0:own]
    for k, ref in enumerate(unit_os):
        ref[...] = vec[8 + k]
    rows = [jnp.concatenate([late_v[k, j : j + 1, :] for k in range(4)], axis=1) for j in range(2)]
    for k in range(n):

        @pl.when(lax.axis_index("wt") == k)
        def _(k=k):
            query_o[...] = rows[0][0, k * own : (k + 1) * own]
            value_o[...] = rows[1][0, k * own : (k + 1) * own]

    gates = []
    for k in range(4):
        for h in range(heads):
            part_sum = jnp.sum(late_v[k, 2:3, HD * h : HD * (h + 1)], axis=1, keepdims=True)
            kept = mask_ref[heads * k + h].astype(f32) / gate_ref[heads * k + h]
            gates.append(part_sum * kept)
    gate_o[...] = jnp.concatenate(gates, axis=1)[0]


def finish(n, heads, gate, mask, con, out, exp_all, att, vec, late, tok):
    r = out.shape[1]
    wide, cols, part = exp_all.shape[2], att.shape[2], out.shape[2]
    units = vec.shape[2]
    row = jax.ShapeDtypeStruct((r,), f32)
    return pl.pallas_call(
        functools.partial(finish_kernel, n, heads),
        out_shape=(
            jax.ShapeDtypeStruct(con.shape, f32),
            jax.ShapeDtypeStruct((r, 4 * part), f32),
            jax.ShapeDtypeStruct((r, 4 * wide), f32),
            jax.ShapeDtypeStruct((r, 4 * cols), f32),
            jax.ShapeDtypeStruct(tok.shape, f32),
        )
        + (row,) * 7
        + (jax.ShapeDtypeStruct((units,), f32),) * 2
        + (row,) * 2
        + (jax.ShapeDtypeStruct((4 * heads,), f32),),
        in_specs=[IN_SMEM] * 2 + [ANYWHERE] * 7,
        out_specs=(IN_VMEM,) * 17,
        scratch_shapes=[pltpu.VMEM(x.shape, x.dtype) for x in (con, out, exp_all, att, vec, late)]
        + [pltpu.SemaphoreType.DMA((7,))],
        compiler_params=pltpu.CompilerParams(vmem_limit_bytes=56 * 2**20),
        name="finish",
    )(gate, mask, con, out, exp_all, att, vec, late, tok)


(OUT_BIAS, GAIN1, SHIFT1, HIDDEN_SCALE, CON_BIAS, GAIN2, SHIFT2, HIDDEN_MASK) = range(8)
(S_OUT_BIAS, S_GAIN1, S_SHIFT1, S_CON_BIAS, S_GAIN2, S_SHIFT2, S_HIDDEN) = range(7)


def gelu_parts(x):
    bell = jnp.exp(-0.5 * (x * x))
    t = 1.0 / (1.0 + (0.3275911 * root_half) * jnp.abs(x))
    poly = t * (
        0.127414796 + t * (-0.142248368 + t * (0.7107068705 + t * (-0.7265760135 + t * 0.5307027145)))
    )
    tail = poly * bell
    cumulative = jnp.where(x < 0.0, tail, 1.0 - tail)
    return x * cumulative, cumulative + x * bell * density_scale


def norm_parts(summed):
    centre = summed - jnp.mean(summed, axis=-1, keepdims=True)
    inverse = lax.rsqrt(jnp.mean(centre * centre, axis=-1, keepdims=True) + epsilon)
    return (centre * inverse, inverse)


def norm_back(grad_normed, normed, inverse):
    return inverse * (
        grad_normed
        - jnp.mean(grad_normed, axis=-1, keepdims=True)
        - normed * jnp.mean(grad_normed * normed, axis=-1, keepdims=True)
    )


def feed_forward_kernel(
    steps, chunk,
    kept_ref, ctx_ref, tok_ref, cot_ref, wo_ref, we_ref, wc_ref,
    ob_ref, g1_ref, t1_ref, hg_ref, hm_ref, cb_ref, g2_ref, t2_ref, eb_ref, ug_ref, um_ref,
    lo_ref, dt1_ref, gctx_ref, vec_ref, dwc_ref, dwe_ref, dwo_ref,
    wide_ref, unit_ref, sw_ref, su_ref, act_sc, gh_sc, low_sc, gb_sc, ga_sc, ctx_sc, gelu_sc, slope_sc,
):
    i = pl.program_id(0)
    block = tok_ref.shape[0]
    units = we_ref.shape[1]
    rows = pl.ds(pl.multiple_of(i * block, block), block)

    @pl.when(i == 0)
    def _():
        sw_ref[...] = jnp.zeros_like(sw_ref)
        su_ref[...] = jnp.zeros_like(su_ref)

        def row(ref):
            return ref[...].astype(f32).reshape(1, ref.shape[0])

        plain = ((OUT_BIAS, ob_ref), (GAIN1, g1_ref), (SHIFT1, t1_ref), (CON_BIAS, cb_ref))
        for k, ref in plain + ((GAIN2, g2_ref), (SHIFT2, t2_ref), (HIDDEN_MASK, hm_ref)):
            wide_ref[k : k + 1, :] = row(ref)
        wide_ref[HIDDEN_SCALE : HIDDEN_SCALE + 1, :] = row(hm_ref) * row(hg_ref)
        kept = row(um_ref) * kept_ref[lax.axis_index("wt")].astype(f32)
        unit_ref[0:1, :] = row(eb_ref)
        unit_ref[1:2, :] = kept * row(ug_ref)
        unit_ref[2:3, :] = kept

    def wide(k):
        return wide_ref[k : k + 1, :]

    def add_sum(ref, k, cols, value):
        ref[k : k + 1, cols] += jnp.sum(value, axis=0, keepdims=True)

    full = slice(None)
    ctx = ctx_ref[...]
    ctx_sc[:, rows] = ctx
    summed = mm(ctx, wo_ref[...], TN) + wide(OUT_BIAS) + tok_ref[...].astype(f32)
    n1, inv1 = norm_parts(summed)
    s1 = n1 * wide(GAIN1) + wide(SHIFT1)
    hs = wide(HIDDEN_SCALE)
    first = s1 * hs
    low = first.astype(bf16)
    low_sc[rows, :] = low
    branch = first + wide(CON_BIAS)
    for j in range(units // chunk):
        cols = slice(j * chunk, (j + 1) * chunk)
        hidden = mm(low, we_ref[:, cols]) + unit_ref[0:1, cols]
        gelu, slope = gelu_parts(hidden)
        scale = unit_ref[1:2, cols]
        gelu_sc[:, cols] = gelu.astype(gelu_sc.dtype)
        slope_sc[:, cols] = (slope * scale).astype(slope_sc.dtype)
        act = (gelu * scale).astype(bf16)
        act_sc[rows, cols] = act
        branch = branch + mm(act, wc_ref[cols, :])
    n2, inv2 = norm_parts(branch)
    s2 = n2 * wide(GAIN2) + wide(SHIFT2)
    lo_ref[...] = (s2 * hs).astype(bf16)
    dy = cot_ref[...].astype(f32)
    e2 = dy * hs
    add_sum(sw_ref, S_GAIN2, full, e2 * n2)
    add_sum(sw_ref, S_SHIFT2, full, e2)
    dt2 = norm_back(e2 * wide(GAIN2), n2, inv2)
    gb = dt2.astype(bf16)
    gb_sc[rows, :] = gb
    add_sum(sw_ref, S_CON_BIAS, full, gb.astype(f32))
    d_first = dt2
    for j in range(units // chunk):
        cols = slice(j * chunk, (j + 1) * chunk)
        d_act = mm(gb, wc_ref[cols, :], NT)
        add_sum(su_ref, 1, cols, d_act * gelu_sc[:, cols].astype(f32))
        gh = d_act * slope_sc[:, cols].astype(f32)
        add_sum(su_ref, 0, cols, gh)
        gh = gh.astype(bf16)
        gh_sc[rows, cols] = gh
        d_first = d_first + mm(gh, we_ref[:, cols], NT)
    e1 = d_first * hs
    add_sum(sw_ref, S_GAIN1, full, e1 * n1)
    add_sum(sw_ref, S_SHIFT1, full, e1)
    add_sum(sw_ref, S_HIDDEN, full, dy * s2 + d_first * s1)
    dt1 = norm_back(e1 * wide(GAIN1), n1, inv1)
    dt1_ref[...] = dt1
    ga = dt1.astype(bf16)
    ga_sc[rows, :] = ga
    add_sum(sw_ref, S_OUT_BIAS, full, ga.astype(f32))
    gctx_ref[...] = mm(wo_ref[...], ga, NT).astype(bf16)

    @pl.when(i == steps - 1)
    def _():
        for j in range(units // chunk):
            cols = slice(j * chunk, (j + 1) * chunk)
            dwc_ref[cols, :] = mm(act_sc[:, cols], gb_sc[...], TN).astype(bf16)
            part = mm(low_sc[...], gh_sc[:, cols], TN).astype(bf16)
            own, wide_cols = dwe_ref.shape[3:]
            for q in range(chunk // wide_cols):
                at = j * (chunk // wide_cols) + q
                inner = slice(q * wide_cols, (q + 1) * wide_cols)
                for k in range(2 * dwe_ref.shape[2]):
                    dwe_ref[k % 2, at, k // 2] = part[k * own : (k + 1) * own, inner]
        own, part_cols = dwo_ref.shape[3:]
        for q in range(4):
            part = mm(ctx_sc[...], ga_sc[:, q * part_cols : (q + 1) * part_cols]).astype(bf16)
            for k in range(2 * dwo_ref.shape[2]):
                dwo_ref[k % 2, q, k // 2] = part[k * own : (k + 1) * own]
        vec_ref[...] = jnp.zeros_like(vec_ref)
        sw_ref[S_HIDDEN : S_HIDDEN + 1, :] *= wide(HIDDEN_MASK)
        su_ref[1:2, :] *= unit_ref[2:3, :]
        own_wide, own_units = dwe_ref.shape[3], vec_ref.shape[2]
        for k in range(vec_ref.shape[0]):
            vec_ref[k, 0:8, 0:own_wide] = sw_ref[:, k * own_wide : (k + 1) * own_wide]
            vec_ref[k, 8:16, :] = su_ref[:, k * own_units : (k + 1) * own_units]


def feed_forward(n, kept, ctx_t, tokens, cotangent, wo, we, wc, *vectors):
    steps, chunk, keep = 3, 768, f32
    rows, d = tokens.shape
    units = we.shape[1]
    block = rows // steps
    halves = (2, 4, n // 2, d // n, units // 4)
    out_halves = (2, 4, n // 2, d // n, d // 4)
    tile = pl.BlockSpec((block, d), lambda i: (i, 0))
    lanes = pl.BlockSpec((d, block), lambda i: (0, i))

    def once(shape):
        return pl.BlockSpec(shape, lambda i: (0, 0), pipeline_mode=pl.Buffered(1))

    def once3(shape):
        return pl.BlockSpec(shape, lambda i: (0, 0, 0), pipeline_mode=pl.Buffered(1))

    def once5(shape):
        return pl.BlockSpec(shape, lambda i: (0, 0, 0, 0, 0), pipeline_mode=pl.Buffered(1))

    return pl.pallas_call(
        functools.partial(feed_forward_kernel, steps, chunk),
        out_shape=(
            jax.ShapeDtypeStruct((rows, d), bf16),
            jax.ShapeDtypeStruct((rows, d), f32),
            jax.ShapeDtypeStruct((d, rows), bf16),
            jax.ShapeDtypeStruct((n, 16, units // n), f32),
            jax.ShapeDtypeStruct((units, d), bf16),
            jax.ShapeDtypeStruct(halves, bf16),
            jax.ShapeDtypeStruct(out_halves, bf16),
        ),
        grid=(steps,),
        in_specs=[
            pl.BlockSpec(memory_space=pltpu.SMEM),
            lanes, tile, tile, once((d, d)), once((d, units)), once((units, d)),
        ]
        + [IN_VMEM] * len(vectors),
        out_specs=(
            tile, tile, lanes, once3((n, 16, units // n)), once((units, d)),
            once5(halves), once5(out_halves),
        ),
        scratch_shapes=[
            pltpu.VMEM((8, d), f32),
            pltpu.VMEM((8, units), f32),
            pltpu.VMEM((8, d), f32),
            pltpu.VMEM((8, units), f32),
            pltpu.VMEM((rows, units), bf16),
            pltpu.VMEM((rows, units), bf16),
            pltpu.VMEM((rows, d), bf16),
            pltpu.VMEM((rows, d), bf16),
            pltpu.VMEM((rows, d), bf16),
            pltpu.VMEM((d, rows), bf16),
            pltpu.VMEM((block, units), keep),
            pltpu.VMEM((block, units), keep),
        ],
        compiler_params=pltpu.CompilerParams(vmem_limit_bytes=60 * 2**20),
        cost_estimate=pl.CostEstimate(
            flops=rows * d * (12 * units + 6 * d),
            bytes_accessed=4 * d * (4 * units + 2 * d) + 12 * rows * d,
            transcendentals=2 * rows * units,
        ),
        name="feed_forward",
    )(kept, ctx_t, tokens, cotangent, wo, we, wc, *vectors)


def local(
    tokens,
    output_cotangent,
    attention_weight,
    query_bias,
    value_bias,
    output_weight,
    output_bias,
    first_gain,
    first_shift,
    expand_weight,
    expand_bias,
    contract_weight,
    contract_bias,
    second_gain,
    second_shift,
    head_gate,
    hidden_gate,
    unit_gate,
    head_mask,
    hidden_mask,
    unit_mask,
    attention_mask,
    feedforward_mask,
    continuation_lengths,
):
    seq_count = lax.axis_size("seq")
    wt_count = lax.axis_size("wt")
    model_width = hidden_gate.shape[0]
    local_heads = head_gate.shape[0] // seq_count
    own_wide = model_width // wt_count
    tokens_all, own_weight, exp_quarter = gather_in(wt_count, tokens, attention_weight, expand_weight)
    full_contract = lax.all_gather(contract_weight, "wt", axis=0, tiled=True)
    full_attention = lax.all_gather(attention_weight, "wt", axis=0, tiled=True)
    packed, own_context, log_sums, context_t, full_output, full_expand = attend(
        wt_count,
        continuation_lengths,
        attention_mask,
        head_gate,
        head_mask,
        query_bias,
        value_bias,
        tokens_all,
        own_weight.reshape(model_width, -1),
        output_weight,
        exp_quarter,
        local_heads,
    )
    (
        layer_output,
        grad_total_one,
        grad_context_t,
        vec_sums,
        contract_weight_grad,
        exp_parts,
        out_parts,
    ) = feed_forward(
        wt_count,
        feedforward_mask,
        context_t,
        tokens,
        output_cotangent,
        full_output.reshape(model_width, model_width),
        full_expand.reshape(model_width, -1),
        full_contract,
        output_bias,
        first_gain,
        first_shift,
        hidden_gate,
        hidden_mask,
        contract_bias,
        second_gain,
        second_shift,
        expand_bias,
        unit_gate,
        unit_mask,
    )
    con_piece = lax.psum_scatter(contract_weight_grad, "wt", scatter_dimension=0, tiled=True)
    pieces, projection_grad, exp_part, out_part, late_sums = attend_back(
        wt_count,
        continuation_lengths,
        attention_mask,
        head_gate,
        head_mask,
        packed,
        own_context,
        grad_context_t,
        log_sums,
        tokens_all,
        exp_parts,
        out_parts,
    )
    tokens_grad, con_all, out_all, exp_all, att_all, vec_all, late_all = final(
        wt_count,
        grad_total_one,
        pieces,
        full_attention,
        con_piece.reshape(seq_count, own_wide, model_width),
        out_part,
        projection_grad,
        exp_part,
        vec_sums,
        late_sums,
    )
    con_sum, out_sum, exp_sum, att_sum, tokens_grad, *rows = finish(
        wt_count,
        local_heads,
        head_gate,
        head_mask,
        con_all,
        out_all,
        exp_all,
        att_all,
        vec_all,
        late_all,
        tokens_grad,
    )
    return (
        layer_output,
        tokens_grad,
        att_sum,
        rows[9],
        rows[10],
        out_sum,
        rows[S_OUT_BIAS],
        rows[S_GAIN1],
        rows[S_SHIFT1],
        exp_sum,
        rows[7],
        con_sum.reshape(seq_count * own_wide, model_width),
        rows[S_CON_BIAS],
        rows[S_GAIN2],
        rows[S_SHIFT2],
        rows[11],
        rows[S_HIDDEN],
        rows[8],
    )


def solution(mesh):
    return jax.shard_map(
        local,
        mesh=mesh,
        in_specs=(
            P(("wt", "seq"), None),
            P(("wt", "seq"), None),
            P("wt", None),
            P(),
            P(),
            P("wt", None),
            P(),
            P(),
            P(),
            P("wt", None),
            P(),
            P("wt", None),
            P(),
            P(),
            P(),
            P(),
            P(),
            P(),
            P(),
            P(),
            P(),
            P(),
            P(),
            P(),
        ),
        out_specs=(
            P(("wt", "seq"), None),
            P(("wt", "seq"), None),
            P("wt", None),
            P("wt"),
            P("wt"),
            P("wt", None),
            P("wt"),
            P("wt"),
            P("wt"),
            P("wt", None),
            P("wt"),
            P("wt", None),
            P("wt"),
            P("wt"),
            P("wt"),
            P(),
            P("wt"),
            P("wt"),
        ),
        check_vma=False,
    )
```

```python
import functools

import jax
import jax.numpy as jnp
from jax import lax
from jax.experimental import pallas as pl
from jax.experimental.pallas import tpu as pltpu
from jax.sharding import PartitionSpec as P

PROMPT = 1024
GRP_WT = 1
GLEN = 3072
SHORT = 512
LONG = 1536
HD = 64
TQ = 512
KC = 512

epsilon = 1e-06
score_scale = 0.125
exp2_scale = 0.125 * 1.4426950408889634
root_half = 0.7071067811865476
density_scale = 0.3989422804014327
bf16 = jnp.bfloat16
f32 = jnp.float32

NT = (((1,), (1,)), ((), ()))
NN = (((1,), (0,)), ((), ()))
TN = (((0,), (0,)), ((), ()))


def mm(a, b, dims=NN):
    return lax.dot_general(a, b, dims, preferred_element_type=f32)


def natural_at(short_first, i):
    other = jnp.where(i == 2, 5, i - 1)
    return jnp.where(short_first | (i < 2), i, other)


def ordered_at(short_first, j):
    other = jnp.where(j == 5, 2, j + 1)
    return jnp.where(short_first | (j < 2), j, other)


def query_tiles(tile):
    def prompt(i, carry):
        tile(i, ())
        return carry

    def longer(i, carry):
        tile(i, (3, 4, 5))
        return carry

    lax.fori_loop(0, 2, prompt, 0)
    tile(2, (2,))
    lax.fori_loop(3, 6, longer, 0)


def remote(src, dst, sems, k, peer):
    return pltpu.make_async_remote_copy(
        src_ref=src,
        dst_ref=dst,
        send_sem=sems[0].at[k],
        recv_sem=sems[1].at[k],
        device_id=peer,
        device_id_type=pl.DeviceIdType.MESH,
    )


def send(src, dst, sems, k, peer):
    copy = remote(src, dst, sems, k, peer)
    copy.start()
    return copy


def value_scale(head, group, kept_ref, gate_ref, mask_ref):
    return mask_ref[head].astype(f32) * gate_ref[head] * kept_ref[group].astype(f32)


def attend_kernel(
    heads, n, lens_ref, kept_ref, gate_ref, mask_ref, qb_ref, vb_ref, tok_ref, w_ref, exp_ref,
    packed_ref, ctx_ref, lse_ref, full_ref, exp_all,
    q_sc, k_sc, vt_sc, ct_sc, vec_ref, exp_buf,
    local_sem, s_sem, r_sem, s_e, r_e,
):
    s, w = lax.axis_index("seq"), lax.axis_index("wt")
    others = [flip(s, k) for k in (1, 2, 3)]
    mate = (s, flip(w, 1))
    short_first = lens_ref[w, 0] == SHORT
    come = pltpu.make_async_copy(exp_ref, exp_buf, local_sem.at[heads])
    come.start()
    meet([(p, w) for p in others] + [mate])
    core, quarter = lax.rem(w, 2), exp_ref.shape[2]

    def exp_place(p):
        return exp_all.at[:, core, :, pl.ds(pl.multiple_of(p * quarter, 128), quarter)]

    spread = [
        send(exp_ref, exp_place(s), (s_e, r_e), k, (p, w)) for k, p in enumerate(others)
    ] + [send(exp_ref, exp_place(s), (s_e, r_e), 3, mate)]
    width = heads * HD
    count = GLEN // 4
    vec_ref[...] = jnp.zeros_like(vec_ref)
    for k in range(4):

        @pl.when(s == k)
        def _(k=k):
            query = qb_ref[...].astype(f32).reshape(1, 4 * width)
            value = vb_ref[...].astype(f32).reshape(1, 4 * width)
            for h in range(heads):
                own = slice(k * width + h * HD, k * width + (h + 1) * HD)
                at = 3 * HD * h
                vec_ref[0:1, at : at + HD] = query[:, own]
                vec_ref[0:1, at + 2 * HD : at + 3 * HD] = value[:, own]

    for h in range(heads):
        at = 3 * HD * h
        vec_ref[1:2, at : at + 2 * HD] = jnp.ones((1, 2 * HD), f32)
        scale = value_scale(s * heads + h, w, kept_ref, gate_ref, mask_ref)
        vec_ref[1:2, at + 2 * HD : at + 3 * HD] = jnp.full((1, HD), scale, f32)
    come.wait()
    own_part = pltpu.make_async_copy(exp_buf, exp_place(s), local_sem.at[heads])
    own_part.start()

    def project(i, carry):
        rows = pl.ds(pl.multiple_of(i * TQ, TQ), TQ)
        x = mm(tok_ref[natural_at(short_first, i)], w_ref[...]) + vec_ref[0:1, :]
        x = (x * vec_ref[1:2, :]).astype(bf16)
        for h in range(heads):
            at = 3 * HD * h
            packed_ref[h, rows, :] = x[:, at : at + 3 * HD]
            q_sc[h, rows, :] = x[:, at : at + HD]
            k_sc[h, rows, :] = x[:, at + HD : at + 2 * HD]
            vt_sc[h, :, rows] = x[:, at + 2 * HD : at + 3 * HD].T
        return carry

    lax.fori_loop(0, GLEN // TQ, project, 0)

    def leaving(h):
        rows = pl.ds(pl.multiple_of(h * HD, HD), HD)
        there = full_ref.at[pl.ds(pl.multiple_of(s * width + h * HD, HD), HD), :]

        def part(p):
            return ctx_ref.at[rows, pl.ds(pl.multiple_of(p * count, 128), count)]

        copies = [
            remote(part(p), there, (s_sem, r_sem), 3 * h + k, (p, w)) for k, p in enumerate(others)
        ]
        return copies, pltpu.make_async_copy(part(s), there, local_sem.at[h])

    passed = [
        (spread[k], remote(exp_place(p), exp_place(p), (s_e, r_e), 4 + k, mate))
        for k, p in enumerate(others)
    ]

    def one_head(h, carry):
        @pl.when(h == heads - 1)
        def _():
            for came, copy in passed:
                came.wait_recv()
                copy.start()

        def tile(i, own_blocks):
            rows = pl.ds(pl.multiple_of(i * TQ, TQ), TQ)
            q = q_sc[h, rows, :]
            s1 = mm(k_sc[h, 0:PROMPT, :], q, NT)
            top = jnp.max(s1, axis=0, keepdims=True)
            if own_blocks:
                own = slice(own_blocks[0] * KC, (own_blocks[-1] + 1) * KC)
                s2 = mm(k_sc[h, own, :], q, NT)
                top = jnp.maximum(top, jnp.max(s2, axis=0, keepdims=True))
            top = top * exp2_scale
            p1 = jnp.exp2(s1 * exp2_scale - top)
            o = mm(vt_sc[h, :, 0:PROMPT], p1.astype(bf16))
            total = jnp.sum(p1, axis=0, keepdims=True)
            if own_blocks:
                p2 = jnp.exp2(s2 * exp2_scale - top)
                o = o + mm(vt_sc[h, :, own], p2.astype(bf16))
                total = total + jnp.sum(p2, axis=0, keepdims=True)
            ct_sc[i] = (o / total).astype(bf16)
            lse_ref[h, :, rows] = top + jnp.log2(total)

        query_tiles(tile)

        def settle(j, carry):
            rows = pl.ds(pl.multiple_of(h * HD, HD), HD)
            lanes = pl.ds(pl.multiple_of(j * SHORT, SHORT), SHORT)
            ctx_ref[rows, lanes] = ct_sc[ordered_at(short_first, j)]
            return carry

        lax.fori_loop(0, GLEN // SHORT, settle, 0)
        copies, own = leaving(h)
        for copy in copies:
            copy.start()
        own.start()
        return carry

    lax.fori_loop(0, heads, one_head, 0)
    own_part.wait()
    spread[3].wait_recv()
    for _, copy in passed:
        copy.wait()
    for copy in spread:
        copy.wait_send()
    for h in range(heads):
        copies, own = leaving(h)
        own.wait()
        for copy in copies:
            copy.wait()


def attend(n, lens, kept, gate, mask, query_bias, value_bias, tokens_all, weight, exp_part, heads):
    width = 3 * HD * heads
    return pl.pallas_call(
        functools.partial(attend_kernel, heads, n),
        out_shape=(
            jax.ShapeDtypeStruct((heads, GLEN, 3 * HD), bf16),
            jax.ShapeDtypeStruct((HD * heads, GLEN), bf16),
            jax.ShapeDtypeStruct((heads, 1, GLEN), f32),
            jax.ShapeDtypeStruct((4 * HD * heads, GLEN // 4), bf16),
            jax.ShapeDtypeStruct((n // 2, 2, exp_part.shape[1], 4 * exp_part.shape[2]), bf16),
        ),
        in_specs=[IN_SMEM] * 4 + [IN_VMEM] * 4 + [ANYWHERE],
        out_specs=(IN_VMEM, IN_VMEM, IN_VMEM, ANYWHERE, ANYWHERE),
        scratch_shapes=[
            pltpu.VMEM((heads, GLEN, HD), bf16),
            pltpu.VMEM((heads, GLEN, HD), bf16),
            pltpu.VMEM((heads, HD, GLEN), bf16),
            pltpu.VMEM((GLEN // TQ, HD, TQ), bf16),
            pltpu.VMEM((2, width), f32),
            pltpu.VMEM(exp_part.shape, bf16),
            pltpu.SemaphoreType.DMA((heads + 1,)),
        ]
        + dma_sems(3 * heads)
        + dma_sems(7),
        compiler_params=remote_params(1),
        cost_estimate=pl.CostEstimate(
            flops=2 * GLEN * 768 * width + heads * 4 * 256 * 5767168,
            bytes_accessed=2 * GLEN * (768 + width),
            transcendentals=heads * 5767168,
        ),
        name="attend",
    )(
        lens, kept, gate, mask, query_bias, value_bias,
        tokens_all.reshape(GLEN // TQ, TQ, -1), weight, exp_part,
    )


def attend_back_kernel(
    heads, n, lens_ref, kept_ref, gate_ref, mask_ref, packed_hbm, ctx_ref, g_hbm, lse_ref, tok_hbm,
    e_hbm, o_hbm, pieces_o, dw_o, exp_o, out_o, late_o,
    packed_v, tok_v, e_own, o_own, e_got, o_got, e_all, o_all, e_sum, o_sum, e_z, o_z, gh0, gh1, gh2, stage, late_sc,
    q_sc, k_sc, v_sc, kt_sc, g_sc, g_nat, delta_sc, delta_nat, dqt_sc, dk_sc, dv_sc, acc,
    l_in, l_g, l_out, s_g, r_g, s_p, r_p, s_c, r_c, s_e, r_e, s_z, r_z,
):
    s, w = lax.axis_index("seq"), lax.axis_index("wt")
    others = [flip(s, k) for k in (1, 2, 3)]
    mate = (s, flip(w, 1))
    z, c, nz = w // 2, lax.rem(w, 2), n // 2
    far = [lax.rem(z + j, nz) for j in range(1, nz)]
    short_first = lens_ref[w, 0] == SHORT
    count = GLEN // 4
    width = heads * HD
    gh = (gh0, gh1, gh2)[:heads]
    loads = [
        pltpu.make_async_copy(packed_hbm.at[h], packed_v.at[h], l_in.at[h]) for h in range(heads)
    ] + [
        pltpu.make_async_copy(e_hbm.at[c], e_own, l_in.at[heads]),
        pltpu.make_async_copy(o_hbm.at[c], o_own, l_in.at[heads + 1]),
        pltpu.make_async_copy(tok_hbm, tok_v, l_in.at[heads + 2]),
    ]
    for copy in loads:
        copy.start()
    meet([(p, w) for p in others] + [mate] + [(s, 2 * k + c) for k in far])

    def coming(h, own=False):
        def part(p):
            return g_hbm.at[pl.ds(pl.multiple_of(p * width + h * HD, HD), HD), :]

        there = gh[h].at[:, pl.ds(pl.multiple_of(s * count, 128), count)]
        if own:
            return pltpu.make_async_copy(part(s), there, l_g.at[h])
        return [remote(part(p), there, (s_g, r_g), 3 * h + k, (p, w)) for k, p in enumerate(others)]

    def leaving(h, own=False):
        if own:
            return pltpu.make_async_copy(stage.at[h, s], pieces_o.at[h, s], l_out.at[h])
        return [
            remote(stage.at[h, p], pieces_o.at[h, s], (s_p, r_p), 3 * h + k, (p, w))
            for k, p in enumerate(others)
        ]

    over_pair = [
        remote(e_hbm.at[1 - c], e_got, (s_c, r_c), 0, mate),
        remote(o_hbm.at[1 - c], o_got, (s_c, r_c), 1, mate),
    ]
    over_plane = [
        remote(e_got.at[p], e_all.at[s], (s_e, r_e), k, (p, w)) for k, p in enumerate(others)
    ] + [remote(o_got.at[p], o_all.at[s], (s_e, r_e), 3 + k, (p, w)) for k, p in enumerate(others)]
    over_z = [
        remote(e_sum.at[k], e_z.at[z], (s_z, r_z), j, (s, 2 * k + c)) for j, k in enumerate(far)
    ] + [
        remote(o_sum.at[k], o_z.at[z], (s_z, r_z), nz - 1 + j, (s, 2 * k + c))
        for j, k in enumerate(far)
    ]
    for h in range(heads):
        for copy in coming(h) + [coming(h, True)]:
            copy.start()
        if h == 0:
            for copy in over_pair:
                copy.start()
    late_sc[...] = jnp.zeros_like(late_sc)

    def prologue(h):
        pltpu.make_async_copy(packed_hbm.at[h], packed_v.at[h], l_in.at[h]).wait()

        def split(i, carry):
            rows = pl.ds(pl.multiple_of(i * TQ, TQ), TQ)
            x = packed_v[h, rows, :]
            q_sc[i] = x[:, 0:HD]
            k = x[:, HD : 2 * HD]
            k_sc[i] = k
            kt_sc[i] = k.T
            v_sc[i] = x[:, 2 * HD : 3 * HD]
            return carry

        lax.fori_loop(0, GLEN // TQ, split, 0)
        dk_sc[...] = jnp.zeros_like(dk_sc)
        dv_sc[...] = jnp.zeros_like(dv_sc)
        for j in range(heads):

            @pl.when(h == j)
            def _(j=j):
                coming(j, True).wait()
                for copy in coming(j):
                    copy.wait_recv()

                def take(i, carry):
                    g_nat[i] = gh[j][:, pl.ds(pl.multiple_of(i * TQ, TQ), TQ)]
                    return carry

                lax.fori_loop(0, GLEN // TQ, take, 0)

        def inner(i, carry):
            lanes = pl.ds(pl.multiple_of(i * TQ, TQ), TQ)
            ctx = ctx_ref[pl.ds(pl.multiple_of(h * HD, HD), HD), lanes]
            product = g_nat[i].astype(f32) * ctx.astype(f32)
            delta_nat[i] = jnp.sum(product, axis=0, keepdims=True)
            return carry

        def order(i, carry):
            g_sc[i] = g_nat[natural_at(short_first, i)]
            delta_sc[i] = delta_nat[natural_at(short_first, i)]
            return carry

        lax.fori_loop(0, GLEN // TQ, inner, 0)
        lax.fori_loop(0, GLEN // TQ, order, 0)

    def halfway(h):
        if h == 0:
            loads[heads].wait()
            loads[heads + 1].wait()
            for copy in over_pair:
                copy.wait_recv()

            def pair_sum(i, carry):
                q, k = i // nz, lax.rem(i, nz)
                e_got[q, k] = (e_got[q, k].astype(f32) + e_own[q, k].astype(f32)).astype(bf16)
                o_got[q, k] = (o_got[q, k].astype(f32) + o_own[q, k].astype(f32)).astype(bf16)
                return carry

            lax.fori_loop(0, 4 * nz, pair_sum, 0)
            for copy in over_plane:
                copy.start()
            e_all[s] = e_got[s]
            o_all[s] = o_got[s]
        if h == heads - 1:
            for copy in over_plane:
                copy.wait_recv()

            def add4(ref, k):
                t = [ref[q, k].astype(f32) for q in range(4)]
                return ((t[0] + t[1]) + (t[2] + t[3])).astype(bf16)

            def plane_sum(k, carry):
                e_sum[k] = add4(e_all, k)
                o_sum[k] = add4(o_all, k)
                return carry

            lax.fori_loop(0, nz, plane_sum, 0)
            for copy in over_z:
                copy.start()
            e_z[z] = e_sum[z]
            o_z[z] = o_sum[z]

    def epilogue(h, first, last):
        half = SHORT // 2
        scale = value_scale(s * heads + h, w, kept_ref, gate_ref, mask_ref)

        def settle(j, carry):
            i = ordered_at(short_first, j)
            dq = dqt_sc[i].astype(bf16)
            dk = (dk_sc[i] * score_scale).T.astype(bf16)
            dv = dv_sc[i].T.astype(bf16).astype(f32)
            gate = dv * v_sc[i].T.astype(f32)
            dv = (dv * scale).astype(bf16)
            for row, x in ((0, dq.astype(f32)), (HD, dv.astype(f32)), (2 * HD, gate)):
                x = (x[:, 0:128] + x[:, 128:256]) + (x[:, 256:384] + x[:, 384:512])
                late_sc[h, row : row + HD, :] += x
            for r in range(2):
                u = 2 * j + r
                p, there = u // 3, pl.ds(pl.multiple_of(lax.rem(u, 3) * half, half), half)
                cols = slice(r * half, (r + 1) * half)
                stage[h, p, 0:HD, there] = dq[:, cols]
                stage[h, p, HD : 2 * HD, there] = dk[:, cols]
                stage[h, p, 2 * HD : 3 * HD, there] = dv[:, cols]
            return carry

        lax.fori_loop(first, last, settle, 0)
        for p, copy in zip(others, leaving(h), strict=True):

            @pl.when(p // 2 == (0 if first == 0 else 1))
            def _(copy=copy):
                copy.start()

        if first == 0:
            leaving(h, True).start()

    def tile_of(h):
        def tile(i, own_blocks):
            q = q_sc[i]
            g = g_sc[i]
            lse = lse_ref[h, :, pl.ds(pl.multiple_of(i * TQ, TQ), TQ)]
            delta = delta_sc[i]
            dq = jnp.zeros((HD, TQ), f32)
            for j in (0, 1) + own_blocks:
                sc = mm(k_sc[j], q, NT)
                p = jnp.exp2(sc * exp2_scale - lse)
                dp = mm(v_sc[j], g)
                ds = (p * (dp - delta)).astype(bf16)
                dv_sc[j] += mm(p.astype(bf16), g, NT)
                dk_sc[j] += mm(ds, q)
                dq = dq + mm(kt_sc[j], ds)
            dqt_sc[i] = dq * score_scale

        return tile

    def one_head(h, carry):
        prologue(h)
        def longer(i, carry):
            tile_of(h)(i, (3, 4, 5))
            return carry

        def prompt(i, carry):
            tile_of(h)(i, ())
            return carry

        tile_of(h)(2, (2,))
        for j in (0, heads - 1):

            @pl.when(h == j)
            def _(j=j):
                halfway(j)

        lax.fori_loop(3, 6, longer, 0)
        epilogue(h, 2, 6)
        lax.fori_loop(0, 2, prompt, 0)
        epilogue(h, 0, 2)
        return carry

    lax.fori_loop(0, heads, one_head, 0)
    loads[heads + 2].wait()
    acc[...] = jnp.zeros_like(acc)

    def weight_grad(p, carry):
        x = tok_v[pl.ds(pl.multiple_of(p * count, count), count), :]
        for h in range(heads):
            acc[3 * HD * h : 3 * HD * (h + 1), :] += mm(stage[h, p], x)
        return carry

    lax.fori_loop(0, 4, weight_grad, 0)
    own_rows = dw_o.shape[1]
    grad = acc[...].T.astype(bf16)
    for k in range(n):
        dw_o[k] = grad[k * own_rows : (k + 1) * own_rows, :]
    late_o[...] = jnp.zeros_like(late_o)
    for h in range(heads):
        sums = jnp.sum(late_sc[h].T, axis=0, keepdims=True)
        for k in range(3):
            late_o[k : k + 1, HD * h : HD * (h + 1)] = sums[:, HD * k : HD * (k + 1)]
    for copy in over_z:
        copy.wait_recv()
    for ref, out in ((e_z, exp_o), (o_z, out_o)):
        total = ref[0].astype(f32)
        for k in range(1, nz):
            total = total + ref[k].astype(f32)
        out[...] = total.astype(bf16)
    for h in range(heads):
        for copy in [leaving(h, True)] + leaving(h):
            copy.wait()
        for copy in coming(h):
            copy.wait_send()
    for copy in over_pair + over_plane + over_z:
        copy.wait_send()


def attend_back(n, lens, kept, gate, mask, packed, ctx, g, lse, tokens_all, e_parts, o_parts):
    heads = packed.shape[0]
    width = 3 * HD * heads
    d = tokens_all.shape[1]
    count = GLEN // 4
    nz = n // 2
    own, wide = e_parts.shape[3:]
    part = o_parts.shape[4]
    blocks = GLEN // TQ
    rows64 = pltpu.VMEM((blocks, TQ, HD), bf16)
    blocks64 = pltpu.VMEM((blocks, HD, TQ), bf16)
    lanes64 = pltpu.VMEM((HD, GLEN), bf16)
    quarters = [pltpu.VMEM(e_parts.shape[1:], bf16), pltpu.VMEM(o_parts.shape[1:], bf16)]
    return pl.pallas_call(
        functools.partial(attend_back_kernel, heads, n),
        out_shape=(
            jax.ShapeDtypeStruct((heads, 4, 3 * HD, count), bf16),
            jax.ShapeDtypeStruct((n, d // n, width), bf16),
            jax.ShapeDtypeStruct((own, wide), bf16),
            jax.ShapeDtypeStruct((own, part), bf16),
            jax.ShapeDtypeStruct((8, HD * heads), f32),
        ),
        in_specs=[IN_SMEM] * 4
        + [ANYWHERE, IN_VMEM, ANYWHERE, IN_VMEM, ANYWHERE]
        + [ANYWHERE] * 2,
        out_specs=(ANYWHERE, IN_VMEM, IN_VMEM, IN_VMEM, IN_VMEM),
        scratch_shapes=[
            pltpu.VMEM(packed.shape, bf16),
            pltpu.VMEM(tokens_all.shape, bf16),
        ]
        + quarters * 3
        + [pltpu.VMEM((nz, own, wide), bf16), pltpu.VMEM((nz, own, part), bf16)] * 2
        + [lanes64] * 3
        + [pltpu.VMEM((heads, 4, 3 * HD, count), bf16), pltpu.VMEM((heads, 3 * HD, 128), f32)]
        + [
            rows64,
            rows64,
            rows64,
            blocks64,
            blocks64,
            blocks64,
            pltpu.VMEM((blocks, 1, TQ), f32),
            pltpu.VMEM((blocks, 1, TQ), f32),
            pltpu.VMEM((blocks, HD, TQ), f32),
            pltpu.VMEM((blocks, TQ, HD), f32),
            pltpu.VMEM((blocks, TQ, HD), f32),
            pltpu.VMEM((width, d), f32),
            pltpu.SemaphoreType.DMA((heads + 3,)),
            pltpu.SemaphoreType.DMA((heads,)),
            pltpu.SemaphoreType.DMA((heads,)),
        ]
        + dma_sems(3 * heads)
        + dma_sems(3 * heads)
        + dma_sems(2)
        + dma_sems(6)
        + dma_sems(2 * nz - 2),
        compiler_params=remote_params(2),
        cost_estimate=pl.CostEstimate(
            flops=heads * 10 * 256 * 5767168 + 2 * GLEN * d * width,
            bytes_accessed=2 * GLEN * (3 * width + d),
            transcendentals=heads * 5767168,
        ),
        name="attend_back",
    )(lens, kept, gate, mask, packed, ctx, g, lse, tokens_all, e_parts, o_parts)


def meet(peers):
    barrier = pltpu.get_barrier_semaphore()
    for peer in peers:
        pl.semaphore_signal(barrier, inc=1, device_id=peer, device_id_type=pl.DeviceIdType.MESH)
    pl.semaphore_wait(barrier, len(peers))


def flip(index, bits):
    for bit in (1, 2):
        if bits & bit:
            index = index + bit - 2 * bit * ((index // bit) % 2)
    return index


def remote_params(number):
    return pltpu.CompilerParams(
        collective_id=number, has_side_effects=True, vmem_limit_bytes=56 * 2**20
    )


ANYWHERE = pl.BlockSpec(memory_space=pl.ANY)
IN_VMEM = pl.BlockSpec(memory_space=pltpu.VMEM)
IN_SMEM = pl.BlockSpec(memory_space=pltpu.SMEM)


def dma_sems(count):
    return [pltpu.SemaphoreType.DMA((count,)), pltpu.SemaphoreType.DMA((count,))]


def gather_kernel(
    n, tok_ref, weight_ref, exp_ref, tok_all, cols_all, exp_all, tok_buf, cols_buf, exp_buf,
    local_sem, s_tok, r_tok, s_w, r_w, s_f, r_f, s_e, r_e,
):
    s, w = lax.axis_index("seq"), lax.axis_index("wt")
    rows = tok_ref.shape[0]
    half = rows // 2
    wide = cols_buf.shape[1]
    for k in range(4):

        @pl.when(s == k)
        def _(k=k):
            cols_buf[...] = weight_ref[:, k * wide : (k + 1) * wide]

    by_x, by_y, mate = (flip(s, 1), w), (flip(s, 2), w), (s, flip(w, 1))
    far = [(s, lax.rem(w + 2 * j, n)) for j in range(1, n // 2)]
    quarter = exp_buf.shape[1]
    exp_own = exp_ref.at[:, pl.ds(pl.multiple_of(s * quarter, 128), quarter)]
    come = [
        pltpu.make_async_copy(tok_ref, tok_buf, local_sem.at[0]),
        pltpu.make_async_copy(exp_own, exp_buf, local_sem.at[2]),
    ]
    for copy in come:
        copy.start()
    meet([by_x, by_y, mate] + far)

    def part(owner, k):
        return pl.ds(pl.multiple_of(owner * rows + k * half, half), half)

    tok = (s_tok, r_tok)
    first = [pl.ds(0, half), pl.ds(half, half)]
    x0 = send(tok_ref.at[first[0]], tok_all.at[part(s, 0)], tok, 0, by_x)
    y1 = send(tok_ref.at[first[1]], tok_all.at[part(s, 1)], tok, 1, by_y)
    x1 = send(tok_ref.at[first[1]], tok_all.at[part(s, 1)], tok, 2, by_x)
    y0 = send(tok_ref.at[first[0]], tok_all.at[part(s, 0)], tok, 3, by_y)
    held = [
        send(cols_buf, cols_all.at[w], (s_w, r_w), k, peer) for k, peer in enumerate(far + [mate])
    ]
    along = [
        send(exp_own, exp_all.at[w // 2], (s_e, r_e), k, peer) for k, peer in enumerate(far)
    ]
    for copy in come:
        copy.wait()
    own = [
        pltpu.make_async_copy(exp_buf, exp_all.at[w // 2], local_sem.at[2]),
        pltpu.make_async_copy(
            tok_buf, tok_all.at[pl.ds(pl.multiple_of(s * rows, rows), rows)], local_sem.at[0]
        ),
        pltpu.make_async_copy(cols_buf, cols_all.at[w], local_sem.at[1]),
    ]
    for copy in own:
        copy.start()
    passed = []
    for j in range(1, n // 2):
        origin = lax.rem(w + n - 2 * j, n)
        held[j - 1].wait_recv()
        passed.append(send(cols_all.at[origin], cols_all.at[origin], (s_f, r_f), j - 1, mate))
    x0.wait_recv()
    there = tok_all.at[part(flip(s, 1), 0)]
    passed.append(send(there, there, tok, 4, by_y))
    y1.wait_recv()
    there = tok_all.at[part(flip(s, 2), 1)]
    passed.append(send(there, there, tok, 5, by_x))
    for copy in own:
        copy.wait()
    for copy in [x1, y0, held[-1]] + passed + along:
        copy.wait_recv()
    for copy in [x0, x1, y0, y1] + held + passed + along:
        copy.wait_send()


def gather_in(n, tokens, attention_weight, expand_weight):
    rows, d = tokens.shape
    own, width = attention_weight.shape
    quarter = expand_weight.shape[1] // 4
    return pl.pallas_call(
        functools.partial(gather_kernel, n),
        out_shape=(
            jax.ShapeDtypeStruct((4 * rows, d), bf16),
            jax.ShapeDtypeStruct((n, own, width // 4), bf16),
            jax.ShapeDtypeStruct((n // 2, own, quarter), bf16),
        ),
        in_specs=[ANYWHERE, IN_VMEM, ANYWHERE],
        out_specs=(ANYWHERE,) * 3,
        scratch_shapes=[
            pltpu.VMEM(tokens.shape, bf16),
            pltpu.VMEM((own, width // 4), bf16),
            pltpu.VMEM((own, quarter), bf16),
            pltpu.SemaphoreType.DMA((3,)),
        ]
        + dma_sems(6)
        + dma_sems(n // 2)
        + dma_sems(n // 2 - 1)
        + dma_sems(n // 2 - 1),
        compiler_params=remote_params(0),
        name="gather_in",
    )(tokens, attention_weight, expand_weight)


def final_kernel(
    heads, n, base_hbm, pieces_hbm, w_hbm, con_ref, out_ref, att_ref, exp_ref, vec_ref, late_ref,
    tok_o, g_con, g_out, g_exp, g_att, r_vec2, r_late2,
    base_v, pieces_v, w_v, r_con, h_att, m_att, r_att, r_vec, r_late,
    l_in, *sems,
):
    s, w = lax.axis_index("seq"), lax.axis_index("wt")
    z, c = w // 2, lax.rem(w, 2)
    nz = n // 2
    others = [flip(s, k) for k in (1, 2, 3)]
    seq_peers = [(p, w) for p in others]
    mate = (s, flip(w, 1))
    wt_peers = [(s, lax.rem(w + j, n)) for j in range(1, n)]
    names = ("pair", "vec", "late", "con", "out2", "att", "vec2", "late2", "con2", "exp2", "att2")
    sem = {name: (sems[2 * k], sems[2 * k + 1]) for k, name in enumerate(names)}
    loads = [
        pltpu.make_async_copy(src, dst, l_in.at[k])
        for k, (src, dst) in enumerate(((pieces_hbm, pieces_v), (w_hbm, w_v), (base_hbm, base_v)))
    ]
    for copy in loads:
        copy.start()
    meet(seq_peers + wt_peers)
    pair = [send(att_ref.at[2 * k + 1 - c], h_att.at[k], sem["pair"], k, mate) for k in range(nz)]
    cons = [send(con_ref.at[p], r_con.at[s], sem["con"], k, (p, w)) for k, p in enumerate(others)]
    far = [lax.rem(z + j, nz) for j in range(1, nz)]
    exp2 = [send(exp_ref, g_exp.at[s], sem["exp2"], k, p) for k, p in enumerate(seq_peers)]
    out2 = [send(out_ref, g_out.at[s], sem["out2"], k, p) for k, p in enumerate(seq_peers)]
    vecs = [
        send(vec_ref.at[lax.rem(w + j, n)], r_vec.at[w], sem["vec"], j - 1, wt_peers[j - 1])
        for j in range(1, n)
    ]
    lates = [send(late_ref, r_late.at[w], sem["late"], j, p) for j, p in enumerate(wt_peers)]
    r_con[s] = con_ref[s]
    g_exp[s] = exp_ref[...]
    r_vec[w] = vec_ref[w]
    r_late[w] = late_ref[...]
    g_out[s] = out_ref[...]
    for copy in pair:
        copy.wait_recv()
    for k in range(nz):
        m_att[k] = (att_ref[2 * k + c].astype(f32) + h_att[k].astype(f32)).astype(bf16)
    atts = [send(m_att.at[k], r_att.at[z], sem["att"], j, (s, 2 * k + c)) for j, k in enumerate(far)]
    r_att[z] = m_att[z]
    for copy in loads:
        copy.wait()
    cols = 3 * HD
    rows = tok_o.shape[0]
    block = rows // 3

    def total_of(ref, count):
        total = ref[0].astype(f32)
        for k in range(1, count):
            total = total + ref[k].astype(f32)
        return total

    own = [ref.at[s] for ref in (g_con, r_vec2, r_late2, g_att)]
    con2, vec2, late2, att2 = (
        [remote(ref, ref, sem[name], k, p) for k, p in enumerate(seq_peers)]
        for ref, name in zip(own, ("con2", "vec2", "late2", "att2"), strict=True)
    )

    def tokens_block(i, carry):
        there = pl.ds(pl.multiple_of(i * block, block), block)
        total = base_v[there, :]
        for h in range(heads):
            for k in range(4):
                at = (heads * k + h) * cols
                total = total + mm(pieces_v[h, k, :, there].T, w_v[:, at : at + cols], NT)
        tok_o[there, :] = total

        @pl.when(i == 0)
        def _():
            for copy in cons:
                copy.wait_recv()
            g_con[s] = total_of(r_con, 4).astype(bf16)
            for copy in con2:
                copy.start()
            for copy in vecs + lates:
                copy.wait_recv()
            r_vec2[s] = total_of(r_vec, n)
            r_late2[s] = total_of(r_late, n)
            for copy in vec2 + late2:
                copy.start()

        @pl.when(i == 1)
        def _():
            for copy in atts:
                copy.wait_recv()
            g_att[s] = total_of(r_att, nz).astype(bf16)
            for copy in att2:
                copy.start()

        return carry

    lax.fori_loop(0, 3, tokens_block, 0)
    for copy in out2 + con2 + vec2 + late2 + exp2 + att2:
        copy.wait_recv()
    for copy in pair + cons + vecs + lates + atts + con2 + vec2 + late2 + exp2 + out2 + att2:
        copy.wait_send()


def final(n, base, pieces, weight, con, out, att, exp_part, vec, late):
    heads = pieces.shape[0]
    r, d = con.shape[1:]
    cols = att.shape[2]
    nz = n // 2
    counts = (nz, n - 1, n - 1, 3, 3, nz - 1, 3, 3, 3, 3, 3)
    return pl.pallas_call(
        functools.partial(final_kernel, heads, n),
        out_shape=(
            jax.ShapeDtypeStruct(base.shape, f32),
            jax.ShapeDtypeStruct((4, r, d), bf16),
            jax.ShapeDtypeStruct((4,) + out.shape, bf16),
            jax.ShapeDtypeStruct((4,) + exp_part.shape, bf16),
            jax.ShapeDtypeStruct((4, r, cols), bf16),
            jax.ShapeDtypeStruct((4,) + vec.shape[1:], f32),
            jax.ShapeDtypeStruct((4,) + late.shape, f32),
        ),
        in_specs=[ANYWHERE] * 3 + [IN_VMEM] * 6,
        out_specs=(IN_VMEM,) * 7,
        scratch_shapes=[
            pltpu.VMEM(base.shape, f32),
            pltpu.VMEM(pieces.shape, bf16),
            pltpu.VMEM(weight.shape, bf16),
            pltpu.VMEM((4, r, d), bf16),
            pltpu.VMEM((nz, r, cols), bf16),
            pltpu.VMEM((nz, r, cols), bf16),
            pltpu.VMEM((nz, r, cols), bf16),
            pltpu.VMEM((n,) + vec.shape[1:], f32),
            pltpu.VMEM((n,) + late.shape, f32),
            pltpu.SemaphoreType.DMA((3,)),
        ]
        + [sem for count in counts for sem in dma_sems(count)],
        compiler_params=remote_params(3),
        cost_estimate=pl.CostEstimate(
            flops=8 * base.shape[0] * d * cols, bytes_accessed=8 * d * cols, transcendentals=0
        ),
        name="final",
    )(base, pieces, weight, con, out, att, exp_part, vec, late)


def finish_kernel(n, heads, gate_ref, mask_ref, *refs):
    sources, rest = refs[:7], refs[7:]
    con_o, out_o, exp_o, att_o, tok_o = rest[:5]
    vec_os, unit_os, query_o, value_o, gate_o = rest[5:12], rest[12:14], rest[14], rest[15], rest[16]
    con_v, out_v, exp_v, att_v, vec_v, late_v, sem = rest[17:]
    loads = [
        pltpu.make_async_copy(src, dst, sem.at[k])
        for k, (src, dst) in enumerate(
            zip(sources, (con_v, out_v, exp_v, att_v, vec_v, late_v, tok_o), strict=True)
        )
    ]
    for copy in loads:
        copy.start()

    def add4(parts):
        return (parts[0] + parts[1]) + (parts[2] + parts[3])

    for copy in loads:
        copy.wait()
    wide, cols, part = exp_v.shape[2], att_v.shape[2], out_v.shape[2]
    for k in range(4):
        con_o[k] = con_v[k].astype(f32)
        exp_o[:, k * wide : (k + 1) * wide] = exp_v[k].astype(f32)
        att_o[:, k * cols : (k + 1) * cols] = att_v[k].astype(f32)
        out_o[:, k * part : (k + 1) * part] = out_v[k].astype(f32)
    vec = add4([vec_v[k] for k in range(4)])
    own = vec_os[0].shape[0]
    for k, ref in enumerate(vec_os):
        ref[...] = vec[k, 0:own]
    for k, ref in enumerate(unit_os):
        ref[...] = vec[8 + k]
    rows = [jnp.concatenate([late_v[k, j : j + 1, :] for k in range(4)], axis=1) for j in range(2)]
    for k in range(n):

        @pl.when(lax.axis_index("wt") == k)
        def _(k=k):
            query_o[...] = rows[0][0, k * own : (k + 1) * own]
            value_o[...] = rows[1][0, k * own : (k + 1) * own]

    gates = []
    for k in range(4):
        for h in range(heads):
            part_sum = jnp.sum(late_v[k, 2:3, HD * h : HD * (h + 1)], axis=1, keepdims=True)
            kept = mask_ref[heads * k + h].astype(f32) / gate_ref[heads * k + h]
            gates.append(part_sum * kept)
    gate_o[...] = jnp.concatenate(gates, axis=1)[0]


def finish(n, heads, gate, mask, con, out, exp_all, att, vec, late, tok):
    r = out.shape[1]
    wide, cols, part = exp_all.shape[2], att.shape[2], out.shape[2]
    units = vec.shape[2]
    row = jax.ShapeDtypeStruct((r,), f32)
    return pl.pallas_call(
        functools.partial(finish_kernel, n, heads),
        out_shape=(
            jax.ShapeDtypeStruct(con.shape, f32),
            jax.ShapeDtypeStruct((r, 4 * part), f32),
            jax.ShapeDtypeStruct((r, 4 * wide), f32),
            jax.ShapeDtypeStruct((r, 4 * cols), f32),
            jax.ShapeDtypeStruct(tok.shape, f32),
        )
        + (row,) * 7
        + (jax.ShapeDtypeStruct((units,), f32),) * 2
        + (row,) * 2
        + (jax.ShapeDtypeStruct((4 * heads,), f32),),
        in_specs=[IN_SMEM] * 2 + [ANYWHERE] * 7,
        out_specs=(IN_VMEM,) * 17,
        scratch_shapes=[pltpu.VMEM(x.shape, x.dtype) for x in (con, out, exp_all, att, vec, late)]
        + [pltpu.SemaphoreType.DMA((7,))],
        compiler_params=pltpu.CompilerParams(vmem_limit_bytes=56 * 2**20),
        name="finish",
    )(gate, mask, con, out, exp_all, att, vec, late, tok)


(OUT_BIAS, GAIN1, SHIFT1, HIDDEN_SCALE, CON_BIAS, GAIN2, SHIFT2, HIDDEN_MASK) = range(8)
(S_OUT_BIAS, S_GAIN1, S_SHIFT1, S_CON_BIAS, S_GAIN2, S_SHIFT2, S_HIDDEN) = range(7)


def gelu_parts(x):
    bell = jnp.exp(-0.5 * (x * x))
    t = 1.0 / (1.0 + (0.3275911 * root_half) * jnp.abs(x))
    poly = t * (
        0.127414796 + t * (-0.142248368 + t * (0.7107068705 + t * (-0.7265760135 + t * 0.5307027145)))
    )
    tail = poly * bell
    cumulative = jnp.where(x < 0.0, tail, 1.0 - tail)
    return x * cumulative, cumulative + x * bell * density_scale


def norm_parts(summed):
    centre = summed - jnp.mean(summed, axis=-1, keepdims=True)
    inverse = lax.rsqrt(jnp.mean(centre * centre, axis=-1, keepdims=True) + epsilon)
    return (centre * inverse, inverse)


def norm_back(grad_normed, normed, inverse):
    return inverse * (
        grad_normed
        - jnp.mean(grad_normed, axis=-1, keepdims=True)
        - normed * jnp.mean(grad_normed * normed, axis=-1, keepdims=True)
    )


def feed_forward_kernel(
    steps, chunk,
    kept_ref, ctx_ref, tok_ref, cot_ref, wo_ref, we_ref, wc_ref,
    ob_ref, g1_ref, t1_ref, hg_ref, hm_ref, cb_ref, g2_ref, t2_ref, eb_ref, ug_ref, um_ref,
    lo_ref, dt1_ref, gctx_ref, vec_ref, dwc_ref, dwe_ref, dwo_ref,
    wide_ref, unit_ref, sw_ref, su_ref, act_sc, gh_sc, low_sc, gb_sc, ga_sc, ctx_sc, gelu_sc, slope_sc,
):
    i = pl.program_id(0)
    block = tok_ref.shape[0]
    units = we_ref.shape[1]
    rows = pl.ds(pl.multiple_of(i * block, block), block)

    @pl.when(i == 0)
    def _():
        sw_ref[...] = jnp.zeros_like(sw_ref)
        su_ref[...] = jnp.zeros_like(su_ref)

        def row(ref):
            return ref[...].astype(f32).reshape(1, ref.shape[0])

        plain = ((OUT_BIAS, ob_ref), (GAIN1, g1_ref), (SHIFT1, t1_ref), (CON_BIAS, cb_ref))
        for k, ref in plain + ((GAIN2, g2_ref), (SHIFT2, t2_ref), (HIDDEN_MASK, hm_ref)):
            wide_ref[k : k + 1, :] = row(ref)
        wide_ref[HIDDEN_SCALE : HIDDEN_SCALE + 1, :] = row(hm_ref) * row(hg_ref)
        kept = row(um_ref) * kept_ref[lax.axis_index("wt")].astype(f32)
        unit_ref[0:1, :] = row(eb_ref)
        unit_ref[1:2, :] = kept * row(ug_ref)
        unit_ref[2:3, :] = kept

    def wide(k):
        return wide_ref[k : k + 1, :]

    def add_sum(ref, k, cols, value):
        ref[k : k + 1, cols] += jnp.sum(value, axis=0, keepdims=True)

    full = slice(None)
    ctx = ctx_ref[...]
    ctx_sc[:, rows] = ctx
    summed = mm(ctx, wo_ref[...], TN) + wide(OUT_BIAS) + tok_ref[...].astype(f32)
    n1, inv1 = norm_parts(summed)
    s1 = n1 * wide(GAIN1) + wide(SHIFT1)
    hs = wide(HIDDEN_SCALE)
    first = s1 * hs
    low = first.astype(bf16)
    low_sc[rows, :] = low
    branch = first + wide(CON_BIAS)
    for j in range(units // chunk):
        cols = slice(j * chunk, (j + 1) * chunk)
        hidden = mm(low, we_ref[:, cols]) + unit_ref[0:1, cols]
        gelu, slope = gelu_parts(hidden)
        scale = unit_ref[1:2, cols]
        gelu_sc[:, cols] = gelu.astype(gelu_sc.dtype)
        slope_sc[:, cols] = (slope * scale).astype(slope_sc.dtype)
        act = (gelu * scale).astype(bf16)
        act_sc[rows, cols] = act
        branch = branch + mm(act, wc_ref[cols, :])
    n2, inv2 = norm_parts(branch)
    s2 = n2 * wide(GAIN2) + wide(SHIFT2)
    lo_ref[...] = (s2 * hs).astype(bf16)
    dy = cot_ref[...].astype(f32)
    e2 = dy * hs
    add_sum(sw_ref, S_GAIN2, full, e2 * n2)
    add_sum(sw_ref, S_SHIFT2, full, e2)
    dt2 = norm_back(e2 * wide(GAIN2), n2, inv2)
    gb = dt2.astype(bf16)
    gb_sc[rows, :] = gb
    add_sum(sw_ref, S_CON_BIAS, full, gb.astype(f32))
    d_first = dt2
    for j in range(units // chunk):
        cols = slice(j * chunk, (j + 1) * chunk)
        d_act = mm(gb, wc_ref[cols, :], NT)
        add_sum(su_ref, 1, cols, d_act * gelu_sc[:, cols].astype(f32))
        gh = d_act * slope_sc[:, cols].astype(f32)
        add_sum(su_ref, 0, cols, gh)
        gh = gh.astype(bf16)
        gh_sc[rows, cols] = gh
        d_first = d_first + mm(gh, we_ref[:, cols], NT)
    e1 = d_first * hs
    add_sum(sw_ref, S_GAIN1, full, e1 * n1)
    add_sum(sw_ref, S_SHIFT1, full, e1)
    add_sum(sw_ref, S_HIDDEN, full, dy * s2 + d_first * s1)
    dt1 = norm_back(e1 * wide(GAIN1), n1, inv1)
    dt1_ref[...] = dt1
    ga = dt1.astype(bf16)
    ga_sc[rows, :] = ga
    add_sum(sw_ref, S_OUT_BIAS, full, ga.astype(f32))
    gctx_ref[...] = mm(wo_ref[...], ga, NT).astype(bf16)

    @pl.when(i == steps - 1)
    def _():
        own, wide_cols = dwe_ref.shape[3:]

        def weight_grads(j, carry):
            cols = pl.ds(pl.multiple_of(j * wide_cols, 128), wide_cols)
            dwc_ref[cols, :] = mm(act_sc[:, cols], gb_sc[...], TN).astype(bf16)
            part = mm(low_sc[...], gh_sc[:, cols], TN).astype(bf16)
            for k in range(2 * dwe_ref.shape[2]):
                dwe_ref[k % 2, j, k // 2] = part[k * own : (k + 1) * own]
            return carry

        lax.fori_loop(0, 4, weight_grads, 0)
        own, part_cols = dwo_ref.shape[3:]
        for q in range(4):
            part = mm(ctx_sc[...], ga_sc[:, q * part_cols : (q + 1) * part_cols]).astype(bf16)
            for k in range(2 * dwo_ref.shape[2]):
                dwo_ref[k % 2, q, k // 2] = part[k * own : (k + 1) * own]
        vec_ref[...] = jnp.zeros_like(vec_ref)
        sw_ref[S_HIDDEN : S_HIDDEN + 1, :] *= wide(HIDDEN_MASK)
        su_ref[1:2, :] *= unit_ref[2:3, :]
        own_wide, own_units = dwe_ref.shape[3], vec_ref.shape[2]
        for k in range(vec_ref.shape[0]):
            vec_ref[k, 0:8, 0:own_wide] = sw_ref[:, k * own_wide : (k + 1) * own_wide]
            vec_ref[k, 8:16, :] = su_ref[:, k * own_units : (k + 1) * own_units]


def feed_forward(n, kept, ctx_t, tokens, cotangent, wo, we, wc, *vectors):
    steps, chunk, keep = 3, 768, f32
    rows, d = tokens.shape
    units = we.shape[1]
    block = rows // steps
    halves = (2, 4, n // 2, d // n, units // 4)
    out_halves = (2, 4, n // 2, d // n, d // 4)
    tile = pl.BlockSpec((block, d), lambda i: (i, 0))
    lanes = pl.BlockSpec((d, block), lambda i: (0, i))

    def once(shape):
        return pl.BlockSpec(shape, lambda i: (0, 0), pipeline_mode=pl.Buffered(1))

    def once3(shape):
        return pl.BlockSpec(shape, lambda i: (0, 0, 0), pipeline_mode=pl.Buffered(1))

    def once5(shape):
        return pl.BlockSpec(shape, lambda i: (0, 0, 0, 0, 0), pipeline_mode=pl.Buffered(1))

    return pl.pallas_call(
        functools.partial(feed_forward_kernel, steps, chunk),
        out_shape=(
            jax.ShapeDtypeStruct((rows, d), bf16),
            jax.ShapeDtypeStruct((rows, d), f32),
            jax.ShapeDtypeStruct((d, rows), bf16),
            jax.ShapeDtypeStruct((n, 16, units // n), f32),
            jax.ShapeDtypeStruct((units, d), bf16),
            jax.ShapeDtypeStruct(halves, bf16),
            jax.ShapeDtypeStruct(out_halves, bf16),
        ),
        grid=(steps,),
        in_specs=[
            pl.BlockSpec(memory_space=pltpu.SMEM),
            lanes, tile, tile, once((d, d)), once((d, units)), once((units, d)),
        ]
        + [IN_VMEM] * len(vectors),
        out_specs=(
            tile, tile, lanes, once3((n, 16, units // n)), once((units, d)),
            once5(halves), once5(out_halves),
        ),
        scratch_shapes=[
            pltpu.VMEM((8, d), f32),
            pltpu.VMEM((8, units), f32),
            pltpu.VMEM((8, d), f32),
            pltpu.VMEM((8, units), f32),
            pltpu.VMEM((rows, units), bf16),
            pltpu.VMEM((rows, units), bf16),
            pltpu.VMEM((rows, d), bf16),
            pltpu.VMEM((rows, d), bf16),
            pltpu.VMEM((rows, d), bf16),
            pltpu.VMEM((d, rows), bf16),
            pltpu.VMEM((block, units), keep),
            pltpu.VMEM((block, units), keep),
        ],
        compiler_params=pltpu.CompilerParams(vmem_limit_bytes=60 * 2**20),
        cost_estimate=pl.CostEstimate(
            flops=rows * d * (12 * units + 6 * d),
            bytes_accessed=4 * d * (4 * units + 2 * d) + 12 * rows * d,
            transcendentals=2 * rows * units,
        ),
        name="feed_forward",
    )(kept, ctx_t, tokens, cotangent, wo, we, wc, *vectors)


def local(
    tokens,
    output_cotangent,
    attention_weight,
    query_bias,
    value_bias,
    output_weight,
    output_bias,
    first_gain,
    first_shift,
    expand_weight,
    expand_bias,
    contract_weight,
    contract_bias,
    second_gain,
    second_shift,
    head_gate,
    hidden_gate,
    unit_gate,
    head_mask,
    hidden_mask,
    unit_mask,
    attention_mask,
    feedforward_mask,
    continuation_lengths,
):
    seq_count = lax.axis_size("seq")
    wt_count = lax.axis_size("wt")
    model_width = hidden_gate.shape[0]
    local_heads = head_gate.shape[0] // seq_count
    own_wide = model_width // wt_count
    tokens_all, own_weight, exp_quarter = gather_in(wt_count, tokens, attention_weight, expand_weight)
    contract_weight, own_weight = lax.optimization_barrier((contract_weight, own_weight))
    full_contract = lax.all_gather(contract_weight, "wt", axis=0, tiled=True)
    full_attention = lax.all_gather(attention_weight, "wt", axis=0, tiled=True)
    full_output = lax.all_gather(output_weight, "wt", axis=0, tiled=True)
    packed, own_context, log_sums, context_t, full_expand = attend(
        wt_count,
        continuation_lengths,
        attention_mask,
        head_gate,
        head_mask,
        query_bias,
        value_bias,
        tokens_all,
        own_weight.reshape(model_width, -1),
        exp_quarter,
        local_heads,
    )
    (
        layer_output,
        grad_total_one,
        grad_context_t,
        vec_sums,
        contract_weight_grad,
        exp_parts,
        out_parts,
    ) = feed_forward(
        wt_count,
        feedforward_mask,
        context_t,
        tokens,
        output_cotangent,
        full_output,
        full_expand.reshape(model_width, -1),
        full_contract,
        output_bias,
        first_gain,
        first_shift,
        hidden_gate,
        hidden_mask,
        contract_bias,
        second_gain,
        second_shift,
        expand_bias,
        unit_gate,
        unit_mask,
    )
    con_piece = lax.psum_scatter(contract_weight_grad, "wt", scatter_dimension=0, tiled=True)
    pieces, projection_grad, exp_part, out_part, late_sums = attend_back(
        wt_count,
        continuation_lengths,
        attention_mask,
        head_gate,
        head_mask,
        packed,
        own_context,
        grad_context_t,
        log_sums,
        tokens_all,
        exp_parts,
        out_parts,
    )
    tokens_grad, con_all, out_all, exp_all, att_all, vec_all, late_all = final(
        wt_count,
        grad_total_one,
        pieces,
        full_attention,
        con_piece.reshape(seq_count, own_wide, model_width),
        out_part,
        projection_grad,
        exp_part,
        vec_sums,
        late_sums,
    )
    con_sum, out_sum, exp_sum, att_sum, tokens_grad, *rows = finish(
        wt_count,
        local_heads,
        head_gate,
        head_mask,
        con_all,
        out_all,
        exp_all,
        att_all,
        vec_all,
        late_all,
        tokens_grad,
    )
    return (
        layer_output,
        tokens_grad,
        att_sum,
        rows[9],
        rows[10],
        out_sum,
        rows[S_OUT_BIAS],
        rows[S_GAIN1],
        rows[S_SHIFT1],
        exp_sum,
        rows[7],
        con_sum.reshape(seq_count * own_wide, model_width),
        rows[S_CON_BIAS],
        rows[S_GAIN2],
        rows[S_SHIFT2],
        rows[11],
        rows[S_HIDDEN],
        rows[8],
    )


def solution(mesh):
    return jax.shard_map(
        local,
        mesh=mesh,
        in_specs=(
            P(("wt", "seq"), None),
            P(("wt", "seq"), None),
            P("wt", None),
            P(),
            P(),
            P("wt", None),
            P(),
            P(),
            P(),
            P("wt", None),
            P(),
            P("wt", None),
            P(),
            P(),
            P(),
            P(),
            P(),
            P(),
            P(),
            P(),
            P(),
            P(),
            P(),
            P(),
        ),
        out_specs=(
            P(("wt", "seq"), None),
            P(("wt", "seq"), None),
            P("wt", None),
            P("wt"),
            P("wt"),
            P("wt", None),
            P("wt"),
            P("wt"),
            P("wt"),
            P("wt", None),
            P("wt"),
            P("wt", None),
            P("wt"),
            P("wt"),
            P("wt"),
            P(),
            P("wt"),
            P("wt"),
        ),
        check_vma=False,
    )
```

```python
import functools

import jax
import jax.numpy as jnp
from jax import lax
from jax.experimental import pallas as pl
from jax.experimental.pallas import tpu as pltpu
from jax.sharding import PartitionSpec as P

PROMPT = 1024
GRP_WT = 1
GLEN = 3072
SHORT = 512
LONG = 1536
HD = 64
TQ = 512
KC = 512

epsilon = 1e-06
score_scale = 0.125
exp2_scale = 0.125 * 1.4426950408889634
root_half = 0.7071067811865476
density_scale = 0.3989422804014327
bf16 = jnp.bfloat16
f32 = jnp.float32

NT = (((1,), (1,)), ((), ()))
NN = (((1,), (0,)), ((), ()))
TN = (((0,), (0,)), ((), ()))


def mm(a, b, dims=NN):
    return lax.dot_general(a, b, dims, preferred_element_type=f32)


def natural_at(short_first, i):
    other = jnp.where(i == 2, 5, i - 1)
    return jnp.where(short_first | (i < 2), i, other)


def ordered_at(short_first, j):
    other = jnp.where(j == 5, 2, j + 1)
    return jnp.where(short_first | (j < 2), j, other)


def query_tiles(tile):
    def prompt(i, carry):
        tile(i, ())
        return carry

    def longer(i, carry):
        tile(i, (3, 4, 5))
        return carry

    lax.fori_loop(0, 2, prompt, 0)
    tile(2, (2,))
    lax.fori_loop(3, 6, longer, 0)


def remote(src, dst, sems, k, peer):
    return pltpu.make_async_remote_copy(
        src_ref=src,
        dst_ref=dst,
        send_sem=sems[0].at[k],
        recv_sem=sems[1].at[k],
        device_id=peer,
        device_id_type=pl.DeviceIdType.MESH,
    )


def send(src, dst, sems, k, peer):
    copy = remote(src, dst, sems, k, peer)
    copy.start()
    return copy


def value_scale(head, group, kept_ref, gate_ref, mask_ref):
    return mask_ref[head].astype(f32) * gate_ref[head] * kept_ref[group].astype(f32)


def attend_kernel(
    heads, n, lens_ref, kept_ref, gate_ref, mask_ref, qb_ref, vb_ref, tok_ref, w_ref, exp_ref,
    packed_ref, ctx_ref, lse_ref, full_ref, exp_all,
    q_sc, k_sc, vt_sc, ct_sc, vec_ref, exp_buf,
    local_sem, s_sem, r_sem, s_e, r_e,
):
    s, w = lax.axis_index("seq"), lax.axis_index("wt")
    others = [flip(s, k) for k in (1, 2, 3)]
    mate = (s, flip(w, 1))
    short_first = lens_ref[w, 0] == SHORT
    come = pltpu.make_async_copy(exp_ref, exp_buf, local_sem.at[heads])
    come.start()
    meet([(p, w) for p in others] + [mate])
    core, quarter = lax.rem(w, 2), exp_ref.shape[2]

    def exp_place(p):
        return exp_all.at[:, core, :, pl.ds(pl.multiple_of(p * quarter, 128), quarter)]

    spread = [
        send(exp_ref, exp_place(s), (s_e, r_e), k, (p, w)) for k, p in enumerate(others)
    ] + [send(exp_ref, exp_place(s), (s_e, r_e), 3, mate)]
    width = heads * HD
    count = GLEN // 4
    vec_ref[...] = jnp.zeros_like(vec_ref)
    for k in range(4):

        @pl.when(s == k)
        def _(k=k):
            query = qb_ref[...].astype(f32).reshape(1, 4 * width)
            value = vb_ref[...].astype(f32).reshape(1, 4 * width)
            for h in range(heads):
                own = slice(k * width + h * HD, k * width + (h + 1) * HD)
                at = 3 * HD * h
                vec_ref[0:1, at : at + HD] = query[:, own]
                vec_ref[0:1, at + 2 * HD : at + 3 * HD] = value[:, own]

    for h in range(heads):
        at = 3 * HD * h
        vec_ref[1:2, at : at + 2 * HD] = jnp.ones((1, 2 * HD), f32)
        scale = value_scale(s * heads + h, w, kept_ref, gate_ref, mask_ref)
        vec_ref[1:2, at + 2 * HD : at + 3 * HD] = jnp.full((1, HD), scale, f32)
    come.wait()
    own_part = pltpu.make_async_copy(exp_buf, exp_place(s), local_sem.at[heads])
    own_part.start()

    def project(i, carry):
        rows = pl.ds(pl.multiple_of(i * TQ, TQ), TQ)
        x = mm(tok_ref[natural_at(short_first, i)], w_ref[...]) + vec_ref[0:1, :]
        x = (x * vec_ref[1:2, :]).astype(bf16)
        for h in range(heads):
            at = 3 * HD * h
            packed_ref[h, rows, :] = x[:, at : at + 3 * HD]
            q_sc[h, rows, :] = x[:, at : at + HD]
            k_sc[h, rows, :] = x[:, at + HD : at + 2 * HD]
            vt_sc[h, :, rows] = x[:, at + 2 * HD : at + 3 * HD].T
        return carry

    lax.fori_loop(0, GLEN // TQ, project, 0)

    def leaving(h):
        rows = pl.ds(pl.multiple_of(h * HD, HD), HD)
        there = full_ref.at[pl.ds(pl.multiple_of(s * width + h * HD, HD), HD), :]

        def part(p):
            return ctx_ref.at[rows, pl.ds(pl.multiple_of(p * count, 128), count)]

        copies = [
            remote(part(p), there, (s_sem, r_sem), 3 * h + k, (p, w)) for k, p in enumerate(others)
        ]
        return copies, pltpu.make_async_copy(part(s), there, local_sem.at[h])

    passed = [
        (spread[k], remote(exp_place(p), exp_place(p), (s_e, r_e), 4 + k, mate))
        for k, p in enumerate(others)
    ]

    def one_head(h, carry):
        @pl.when(h == heads - 1)
        def _():
            for came, copy in passed:
                came.wait_recv()
                copy.start()

        def tile(i, own_blocks):
            rows = pl.ds(pl.multiple_of(i * TQ, TQ), TQ)
            q = q_sc[h, rows, :]
            s1 = mm(k_sc[h, 0:PROMPT, :], q, NT)
            top = jnp.max(s1, axis=0, keepdims=True)
            if own_blocks:
                own = slice(own_blocks[0] * KC, (own_blocks[-1] + 1) * KC)
                s2 = mm(k_sc[h, own, :], q, NT)
                top = jnp.maximum(top, jnp.max(s2, axis=0, keepdims=True))
            top = top * exp2_scale
            p1 = jnp.exp2(s1 * exp2_scale - top)
            o = mm(vt_sc[h, :, 0:PROMPT], p1.astype(bf16))
            total = jnp.sum(p1, axis=0, keepdims=True)
            if own_blocks:
                p2 = jnp.exp2(s2 * exp2_scale - top)
                o = o + mm(vt_sc[h, :, own], p2.astype(bf16))
                total = total + jnp.sum(p2, axis=0, keepdims=True)
            ct_sc[i] = (o / total).astype(bf16)
            lse_ref[h, :, rows] = top + jnp.log2(total)

        query_tiles(tile)

        def settle(j, carry):
            rows = pl.ds(pl.multiple_of(h * HD, HD), HD)
            lanes = pl.ds(pl.multiple_of(j * SHORT, SHORT), SHORT)
            ctx_ref[rows, lanes] = ct_sc[ordered_at(short_first, j)]
            return carry

        lax.fori_loop(0, GLEN // SHORT, settle, 0)
        copies, own = leaving(h)
        for copy in copies:
            copy.start()
        own.start()
        return carry

    lax.fori_loop(0, heads, one_head, 0)
    own_part.wait()
    spread[3].wait_recv()
    for _, copy in passed:
        copy.wait()
    for copy in spread:
        copy.wait_send()
    for h in range(heads):
        copies, own = leaving(h)
        own.wait()
        for copy in copies:
            copy.wait()


def attend(n, lens, kept, gate, mask, query_bias, value_bias, tokens_all, weight, exp_part, heads):
    width = 3 * HD * heads
    return pl.pallas_call(
        functools.partial(attend_kernel, heads, n),
        out_shape=(
            jax.ShapeDtypeStruct((heads, GLEN, 3 * HD), bf16),
            jax.ShapeDtypeStruct((HD * heads, GLEN), bf16),
            jax.ShapeDtypeStruct((heads, 1, GLEN), f32),
            jax.ShapeDtypeStruct((4 * HD * heads, GLEN // 4), bf16),
            jax.ShapeDtypeStruct((n // 2, 2, exp_part.shape[1], 4 * exp_part.shape[2]), bf16),
        ),
        in_specs=[IN_SMEM] * 4 + [IN_VMEM] * 4 + [ANYWHERE],
        out_specs=(IN_VMEM, IN_VMEM, IN_VMEM, ANYWHERE, ANYWHERE),
        scratch_shapes=[
            pltpu.VMEM((heads, GLEN, HD), bf16),
            pltpu.VMEM((heads, GLEN, HD), bf16),
            pltpu.VMEM((heads, HD, GLEN), bf16),
            pltpu.VMEM((GLEN // TQ, HD, TQ), bf16),
            pltpu.VMEM((2, width), f32),
            pltpu.VMEM(exp_part.shape, bf16),
            pltpu.SemaphoreType.DMA((heads + 1,)),
        ]
        + dma_sems(3 * heads)
        + dma_sems(7),
        compiler_params=remote_params(1),
        cost_estimate=pl.CostEstimate(
            flops=2 * GLEN * 768 * width + heads * 4 * 256 * 5767168,
            bytes_accessed=2 * GLEN * (768 + width),
            transcendentals=heads * 5767168,
        ),
        name="attend",
    )(
        lens, kept, gate, mask, query_bias, value_bias,
        tokens_all.reshape(GLEN // TQ, TQ, -1), weight, exp_part,
    )


def attend_back_kernel(
    heads, n, lens_ref, kept_ref, gate_ref, mask_ref, packed_hbm, ctx_ref, gctx_ref, lse_ref, tok_hbm,
    e_hbm, o_hbm, pieces_o, dw_o, exp_o, out_o, late_o,
    packed_v, tok_v, e_own, o_own, e_got, o_got, e_all, o_all, e_sum, o_sum, e_z, o_z, stage, late_sc,
    q_sc, k_sc, v_sc, kt_sc, g_sc, g_nat, delta_sc, delta_nat, dqt_sc, dk_sc, dv_sc, acc,
    l_in, l_out, s_p, r_p, s_c, r_c, s_e, r_e, s_z, r_z,
):
    s, w = lax.axis_index("seq"), lax.axis_index("wt")
    others = [flip(s, k) for k in (1, 2, 3)]
    mate = (s, flip(w, 1))
    z, c, nz = w // 2, lax.rem(w, 2), n // 2
    far = [lax.rem(z + j, nz) for j in range(1, nz)]
    short_first = lens_ref[w, 0] == SHORT
    count = GLEN // 4
    width = heads * HD
    loads = [
        pltpu.make_async_copy(packed_hbm.at[h], packed_v.at[h], l_in.at[h]) for h in range(heads)
    ] + [
        pltpu.make_async_copy(e_hbm.at[c], e_own, l_in.at[heads]),
        pltpu.make_async_copy(o_hbm.at[c], o_own, l_in.at[heads + 1]),
        pltpu.make_async_copy(tok_hbm, tok_v, l_in.at[heads + 2]),
    ]
    for copy in loads:
        copy.start()
    meet([(p, w) for p in others] + [mate] + [(s, 2 * k + c) for k in far])

    def leaving(h, own=False):
        if own:
            return pltpu.make_async_copy(stage.at[h, s], pieces_o.at[h, s], l_out.at[h])
        return [
            remote(stage.at[h, p], pieces_o.at[h, s], (s_p, r_p), 3 * h + k, (p, w))
            for k, p in enumerate(others)
        ]

    over_pair = [
        remote(e_hbm.at[1 - c], e_got, (s_c, r_c), 0, mate),
        remote(o_hbm.at[1 - c], o_got, (s_c, r_c), 1, mate),
    ]
    over_plane = [
        remote(e_got.at[p], e_all.at[s], (s_e, r_e), k, (p, w)) for k, p in enumerate(others)
    ] + [remote(o_got.at[p], o_all.at[s], (s_e, r_e), 3 + k, (p, w)) for k, p in enumerate(others)]
    over_z = [
        remote(e_sum.at[k], e_z.at[z], (s_z, r_z), j, (s, 2 * k + c)) for j, k in enumerate(far)
    ] + [
        remote(o_sum.at[k], o_z.at[z], (s_z, r_z), nz - 1 + j, (s, 2 * k + c))
        for j, k in enumerate(far)
    ]
    for copy in over_pair:
        copy.start()
    late_sc[...] = jnp.zeros_like(late_sc)

    def prologue(h):
        pltpu.make_async_copy(packed_hbm.at[h], packed_v.at[h], l_in.at[h]).wait()

        def split(i, carry):
            rows = pl.ds(pl.multiple_of(i * TQ, TQ), TQ)
            x = packed_v[h, rows, :]
            q_sc[i] = x[:, 0:HD]
            k = x[:, HD : 2 * HD]
            k_sc[i] = k
            kt_sc[i] = k.T
            v_sc[i] = x[:, 2 * HD : 3 * HD]
            return carry

        lax.fori_loop(0, GLEN // TQ, split, 0)
        dk_sc[...] = jnp.zeros_like(dk_sc)
        dv_sc[...] = jnp.zeros_like(dv_sc)
        def inner(i, carry):
            lanes = pl.ds(pl.multiple_of(i * TQ, TQ), TQ)
            own = pl.ds(pl.multiple_of(h * HD, HD), HD)
            g_nat[i] = gctx_ref[own, lanes]
            product = g_nat[i].astype(f32) * ctx_ref[own, lanes].astype(f32)
            delta_nat[i] = jnp.sum(product, axis=0, keepdims=True)
            return carry

        def order(i, carry):
            g_sc[i] = g_nat[natural_at(short_first, i)]
            delta_sc[i] = delta_nat[natural_at(short_first, i)]
            return carry

        lax.fori_loop(0, GLEN // TQ, inner, 0)
        lax.fori_loop(0, GLEN // TQ, order, 0)

    def halfway(h):
        if h == 0:
            loads[heads].wait()
            loads[heads + 1].wait()
            for copy in over_pair:
                copy.wait_recv()

            def pair_sum(i, carry):
                q, k = i // nz, lax.rem(i, nz)
                e_got[q, k] = (e_got[q, k].astype(f32) + e_own[q, k].astype(f32)).astype(bf16)
                o_got[q, k] = (o_got[q, k].astype(f32) + o_own[q, k].astype(f32)).astype(bf16)
                return carry

            lax.fori_loop(0, 4 * nz, pair_sum, 0)
            for copy in over_plane:
                copy.start()
            e_all[s] = e_got[s]
            o_all[s] = o_got[s]
        if h == heads - 1:
            for copy in over_plane:
                copy.wait_recv()

            def add4(ref, k):
                t = [ref[q, k].astype(f32) for q in range(4)]
                return ((t[0] + t[1]) + (t[2] + t[3])).astype(bf16)

            def plane_sum(k, carry):
                e_sum[k] = add4(e_all, k)
                o_sum[k] = add4(o_all, k)
                return carry

            lax.fori_loop(0, nz, plane_sum, 0)
            for copy in over_z:
                copy.start()
            e_z[z] = e_sum[z]
            o_z[z] = o_sum[z]

    def epilogue(h, first, last):
        half = SHORT // 2
        scale = value_scale(s * heads + h, w, kept_ref, gate_ref, mask_ref)

        def settle(j, carry):
            i = ordered_at(short_first, j)
            dq = dqt_sc[i].astype(bf16)
            dk = (dk_sc[i] * score_scale).T.astype(bf16)
            dv = dv_sc[i].T.astype(bf16).astype(f32)
            gate = dv * v_sc[i].T.astype(f32)
            dv = (dv * scale).astype(bf16)
            for row, x in ((0, dq.astype(f32)), (HD, dv.astype(f32)), (2 * HD, gate)):
                x = (x[:, 0:128] + x[:, 128:256]) + (x[:, 256:384] + x[:, 384:512])
                late_sc[h, row : row + HD, :] += x
            for r in range(2):
                u = 2 * j + r
                p, there = u // 3, pl.ds(pl.multiple_of(lax.rem(u, 3) * half, half), half)
                cols = slice(r * half, (r + 1) * half)
                stage[h, p, 0:HD, there] = dq[:, cols]
                stage[h, p, HD : 2 * HD, there] = dk[:, cols]
                stage[h, p, 2 * HD : 3 * HD, there] = dv[:, cols]
            return carry

        lax.fori_loop(first, last, settle, 0)
        for p, copy in zip(others, leaving(h), strict=True):

            @pl.when(p // 2 == (0 if first == 0 else 1))
            def _(copy=copy):
                copy.start()

        if first == 0:
            leaving(h, True).start()

    def tile_of(h):
        def tile(i, own_blocks):
            q = q_sc[i]
            g = g_sc[i]
            lse = lse_ref[h, :, pl.ds(pl.multiple_of(i * TQ, TQ), TQ)]
            delta = delta_sc[i]
            dq = jnp.zeros((HD, TQ), f32)
            for j in (0, 1) + own_blocks:
                sc = mm(k_sc[j], q, NT)
                p = jnp.exp2(sc * exp2_scale - lse)
                dp = mm(v_sc[j], g)
                ds = (p * (dp - delta)).astype(bf16)
                dv_sc[j] += mm(p.astype(bf16), g, NT)
                dk_sc[j] += mm(ds, q)
                dq = dq + mm(kt_sc[j], ds)
            dqt_sc[i] = dq * score_scale

        return tile

    def one_head(h, carry):
        prologue(h)
        def longer(i, carry):
            tile_of(h)(i, (3, 4, 5))
            return carry

        def prompt(i, carry):
            tile_of(h)(i, ())
            return carry

        tile_of(h)(2, (2,))
        for j in (0, heads - 1):

            @pl.when(h == j)
            def _(j=j):
                halfway(j)

        lax.fori_loop(3, 6, longer, 0)
        epilogue(h, 2, 6)
        lax.fori_loop(0, 2, prompt, 0)
        epilogue(h, 0, 2)
        return carry

    lax.fori_loop(0, heads, one_head, 0)
    loads[heads + 2].wait()
    acc[...] = jnp.zeros_like(acc)

    def weight_grad(p, carry):
        x = tok_v[pl.ds(pl.multiple_of(p * count, count), count), :]
        for h in range(heads):
            acc[3 * HD * h : 3 * HD * (h + 1), :] += mm(stage[h, p], x)
        return carry

    lax.fori_loop(0, 4, weight_grad, 0)
    own_rows = dw_o.shape[1]
    grad = acc[...].T.astype(bf16)
    for k in range(n):
        dw_o[k] = grad[k * own_rows : (k + 1) * own_rows, :]
    late_o[...] = jnp.zeros_like(late_o)
    for h in range(heads):
        sums = jnp.sum(late_sc[h].T, axis=0, keepdims=True)
        for k in range(3):
            late_o[k : k + 1, HD * h : HD * (h + 1)] = sums[:, HD * k : HD * (k + 1)]
    for copy in over_z:
        copy.wait_recv()
    for ref, out in ((e_z, exp_o), (o_z, out_o)):
        total = ref[0].astype(f32)
        for k in range(1, nz):
            total = total + ref[k].astype(f32)
        out[...] = total.astype(bf16)
    for h in range(heads):
        for copy in [leaving(h, True)] + leaving(h):
            copy.wait()
    for copy in over_pair + over_plane + over_z:
        copy.wait_send()


def attend_back(n, lens, kept, gate, mask, packed, ctx, g, lse, tokens_all, e_parts, o_parts):
    heads = packed.shape[0]
    width = 3 * HD * heads
    d = tokens_all.shape[1]
    count = GLEN // 4
    nz = n // 2
    own, wide = e_parts.shape[3:]
    part = o_parts.shape[4]
    blocks = GLEN // TQ
    rows64 = pltpu.VMEM((blocks, TQ, HD), bf16)
    blocks64 = pltpu.VMEM((blocks, HD, TQ), bf16)
    quarters = [pltpu.VMEM(e_parts.shape[1:], bf16), pltpu.VMEM(o_parts.shape[1:], bf16)]
    return pl.pallas_call(
        functools.partial(attend_back_kernel, heads, n),
        out_shape=(
            jax.ShapeDtypeStruct((heads, 4, 3 * HD, count), bf16),
            jax.ShapeDtypeStruct((n, d // n, width), bf16),
            jax.ShapeDtypeStruct((own, wide), bf16),
            jax.ShapeDtypeStruct((own, part), bf16),
            jax.ShapeDtypeStruct((8, HD * heads), f32),
        ),
        in_specs=[IN_SMEM] * 4
        + [ANYWHERE, IN_VMEM, IN_VMEM, IN_VMEM, ANYWHERE]
        + [ANYWHERE] * 2,
        out_specs=(ANYWHERE, IN_VMEM, IN_VMEM, IN_VMEM, IN_VMEM),
        scratch_shapes=[
            pltpu.VMEM(packed.shape, bf16),
            pltpu.VMEM(tokens_all.shape, bf16),
        ]
        + quarters * 3
        + [pltpu.VMEM((nz, own, wide), bf16), pltpu.VMEM((nz, own, part), bf16)] * 2
        + [pltpu.VMEM((heads, 4, 3 * HD, count), bf16), pltpu.VMEM((heads, 3 * HD, 128), f32)]
        + [
            rows64,
            rows64,
            rows64,
            blocks64,
            blocks64,
            blocks64,
            pltpu.VMEM((blocks, 1, TQ), f32),
            pltpu.VMEM((blocks, 1, TQ), f32),
            pltpu.VMEM((blocks, HD, TQ), f32),
            pltpu.VMEM((blocks, TQ, HD), f32),
            pltpu.VMEM((blocks, TQ, HD), f32),
            pltpu.VMEM((width, d), f32),
            pltpu.SemaphoreType.DMA((heads + 3,)),
            pltpu.SemaphoreType.DMA((heads,)),
        ]
        + dma_sems(3 * heads)
        + dma_sems(2)
        + dma_sems(6)
        + dma_sems(2 * nz - 2),
        compiler_params=remote_params(2),
        cost_estimate=pl.CostEstimate(
            flops=heads * 10 * 256 * 5767168 + 2 * GLEN * d * width,
            bytes_accessed=2 * GLEN * (3 * width + d),
            transcendentals=heads * 5767168,
        ),
        name="attend_back",
    )(lens, kept, gate, mask, packed, ctx, g, lse, tokens_all, e_parts, o_parts)


def meet(peers):
    barrier = pltpu.get_barrier_semaphore()
    for peer in peers:
        pl.semaphore_signal(barrier, inc=1, device_id=peer, device_id_type=pl.DeviceIdType.MESH)
    pl.semaphore_wait(barrier, len(peers))


def flip(index, bits):
    for bit in (1, 2):
        if bits & bit:
            index = index + bit - 2 * bit * ((index // bit) % 2)
    return index


def remote_params(number):
    return pltpu.CompilerParams(
        collective_id=number, has_side_effects=True, vmem_limit_bytes=56 * 2**20
    )


ANYWHERE = pl.BlockSpec(memory_space=pl.ANY)
IN_VMEM = pl.BlockSpec(memory_space=pltpu.VMEM)
IN_SMEM = pl.BlockSpec(memory_space=pltpu.SMEM)


def dma_sems(count):
    return [pltpu.SemaphoreType.DMA((count,)), pltpu.SemaphoreType.DMA((count,))]


def gather_kernel(
    n, tok_ref, weight_ref, exp_ref, tok_all, cols_all, exp_all, tok_buf, cols_buf, exp_buf,
    local_sem, s_tok, r_tok, s_w, r_w, s_f, r_f, s_e, r_e,
):
    s, w = lax.axis_index("seq"), lax.axis_index("wt")
    rows = tok_ref.shape[0]
    half = rows // 2
    wide = cols_buf.shape[1]
    for k in range(4):

        @pl.when(s == k)
        def _(k=k):
            cols_buf[...] = weight_ref[:, k * wide : (k + 1) * wide]

    by_x, by_y, mate = (flip(s, 1), w), (flip(s, 2), w), (s, flip(w, 1))
    far = [(s, lax.rem(w + 2 * j, n)) for j in range(1, n // 2)]
    quarter = exp_buf.shape[1]
    exp_own = exp_ref.at[:, pl.ds(pl.multiple_of(s * quarter, 128), quarter)]
    come = [
        pltpu.make_async_copy(tok_ref, tok_buf, local_sem.at[0]),
        pltpu.make_async_copy(exp_own, exp_buf, local_sem.at[2]),
    ]
    for copy in come:
        copy.start()
    meet([by_x, by_y, mate] + far)

    def part(owner, k):
        return pl.ds(pl.multiple_of(owner * rows + k * half, half), half)

    tok = (s_tok, r_tok)
    first = [pl.ds(0, half), pl.ds(half, half)]
    x0 = send(tok_ref.at[first[0]], tok_all.at[part(s, 0)], tok, 0, by_x)
    y1 = send(tok_ref.at[first[1]], tok_all.at[part(s, 1)], tok, 1, by_y)
    x1 = send(tok_ref.at[first[1]], tok_all.at[part(s, 1)], tok, 2, by_x)
    y0 = send(tok_ref.at[first[0]], tok_all.at[part(s, 0)], tok, 3, by_y)
    held = [
        send(cols_buf, cols_all.at[w], (s_w, r_w), k, peer) for k, peer in enumerate(far + [mate])
    ]
    along = [
        send(exp_own, exp_all.at[w // 2], (s_e, r_e), k, peer) for k, peer in enumerate(far)
    ]
    for copy in come:
        copy.wait()
    own = [
        pltpu.make_async_copy(exp_buf, exp_all.at[w // 2], local_sem.at[2]),
        pltpu.make_async_copy(
            tok_buf, tok_all.at[pl.ds(pl.multiple_of(s * rows, rows), rows)], local_sem.at[0]
        ),
        pltpu.make_async_copy(cols_buf, cols_all.at[w], local_sem.at[1]),
    ]
    for copy in own:
        copy.start()
    passed = []
    for j in range(1, n // 2):
        origin = lax.rem(w + n - 2 * j, n)
        held[j - 1].wait_recv()
        passed.append(send(cols_all.at[origin], cols_all.at[origin], (s_f, r_f), j - 1, mate))
    x0.wait_recv()
    there = tok_all.at[part(flip(s, 1), 0)]
    passed.append(send(there, there, tok, 4, by_y))
    y1.wait_recv()
    there = tok_all.at[part(flip(s, 2), 1)]
    passed.append(send(there, there, tok, 5, by_x))
    for copy in own:
        copy.wait()
    for copy in [x1, y0, held[-1]] + passed + along:
        copy.wait_recv()
    for copy in [x0, x1, y0, y1] + held + passed + along:
        copy.wait_send()


def gather_in(n, tokens, attention_weight, expand_weight):
    rows, d = tokens.shape
    own, width = attention_weight.shape
    quarter = expand_weight.shape[1] // 4
    return pl.pallas_call(
        functools.partial(gather_kernel, n),
        out_shape=(
            jax.ShapeDtypeStruct((4 * rows, d), bf16),
            jax.ShapeDtypeStruct((n, own, width // 4), bf16),
            jax.ShapeDtypeStruct((n // 2, own, quarter), bf16),
        ),
        in_specs=[ANYWHERE, IN_VMEM, ANYWHERE],
        out_specs=(ANYWHERE,) * 3,
        scratch_shapes=[
            pltpu.VMEM(tokens.shape, bf16),
            pltpu.VMEM((own, width // 4), bf16),
            pltpu.VMEM((own, quarter), bf16),
            pltpu.SemaphoreType.DMA((3,)),
        ]
        + dma_sems(6)
        + dma_sems(n // 2)
        + dma_sems(n // 2 - 1)
        + dma_sems(n // 2 - 1),
        compiler_params=remote_params(0),
        name="gather_in",
    )(tokens, attention_weight, expand_weight)


def final_kernel(
    heads, n, base_hbm, pieces_hbm, w_hbm, con_ref, out_ref, att_ref, exp_ref, vec_ref, late_ref,
    tok_o, g_con, g_out, g_exp, g_att, r_vec2, r_late2,
    base_v, pieces_v, w_v, r_con, h_att, m_att, r_att, r_vec, r_late,
    l_in, *sems,
):
    s, w = lax.axis_index("seq"), lax.axis_index("wt")
    z, c = w // 2, lax.rem(w, 2)
    nz = n // 2
    others = [flip(s, k) for k in (1, 2, 3)]
    seq_peers = [(p, w) for p in others]
    mate = (s, flip(w, 1))
    wt_peers = [(s, lax.rem(w + j, n)) for j in range(1, n)]
    names = ("pair", "vec", "late", "con", "out2", "att", "vec2", "late2", "con2", "exp2", "att2")
    sem = {name: (sems[2 * k], sems[2 * k + 1]) for k, name in enumerate(names)}
    loads = [
        pltpu.make_async_copy(src, dst, l_in.at[k])
        for k, (src, dst) in enumerate(((pieces_hbm, pieces_v), (w_hbm, w_v), (base_hbm, base_v)))
    ]
    for copy in loads:
        copy.start()
    meet(seq_peers + wt_peers)
    pair = [send(att_ref.at[2 * k + 1 - c], h_att.at[k], sem["pair"], k, mate) for k in range(nz)]
    cons = [send(con_ref.at[p], r_con.at[s], sem["con"], k, (p, w)) for k, p in enumerate(others)]
    far = [lax.rem(z + j, nz) for j in range(1, nz)]
    exp2 = [send(exp_ref, g_exp.at[s], sem["exp2"], k, p) for k, p in enumerate(seq_peers)]
    out2 = [send(out_ref, g_out.at[s], sem["out2"], k, p) for k, p in enumerate(seq_peers)]
    vecs = [
        send(vec_ref.at[lax.rem(w + j, n)], r_vec.at[w], sem["vec"], j - 1, wt_peers[j - 1])
        for j in range(1, n)
    ]
    lates = [send(late_ref, r_late.at[w], sem["late"], j, p) for j, p in enumerate(wt_peers)]
    r_con[s] = con_ref[s]
    g_exp[s] = exp_ref[...]
    r_vec[w] = vec_ref[w]
    r_late[w] = late_ref[...]
    g_out[s] = out_ref[...]
    for copy in pair:
        copy.wait_recv()
    for k in range(nz):
        m_att[k] = (att_ref[2 * k + c].astype(f32) + h_att[k].astype(f32)).astype(bf16)
    atts = [send(m_att.at[k], r_att.at[z], sem["att"], j, (s, 2 * k + c)) for j, k in enumerate(far)]
    r_att[z] = m_att[z]
    for copy in loads:
        copy.wait()
    cols = 3 * HD
    rows = tok_o.shape[0]
    block = rows // 3

    def total_of(ref, count):
        total = ref[0].astype(f32)
        for k in range(1, count):
            total = total + ref[k].astype(f32)
        return total

    own = [ref.at[s] for ref in (g_con, r_vec2, r_late2, g_att)]
    con2, vec2, late2, att2 = (
        [remote(ref, ref, sem[name], k, p) for k, p in enumerate(seq_peers)]
        for ref, name in zip(own, ("con2", "vec2", "late2", "att2"), strict=True)
    )

    def tokens_block(i, carry):
        there = pl.ds(pl.multiple_of(i * block, block), block)
        total = base_v[there, :]
        for h in range(heads):
            for k in range(4):
                at = (heads * k + h) * cols
                total = total + mm(pieces_v[h, k, :, there].T, w_v[:, at : at + cols], NT)
        tok_o[there, :] = total

        @pl.when(i == 0)
        def _():
            for copy in cons:
                copy.wait_recv()
            g_con[s] = total_of(r_con, 4).astype(bf16)
            for copy in con2:
                copy.start()
            for copy in vecs + lates:
                copy.wait_recv()
            r_vec2[s] = total_of(r_vec, n)
            r_late2[s] = total_of(r_late, n)
            for copy in vec2 + late2:
                copy.start()

        @pl.when(i == 1)
        def _():
            for copy in atts:
                copy.wait_recv()
            g_att[s] = total_of(r_att, nz).astype(bf16)
            for copy in att2:
                copy.start()

        return carry

    lax.fori_loop(0, 3, tokens_block, 0)
    for copy in out2 + con2 + vec2 + late2 + exp2 + att2:
        copy.wait_recv()
    for copy in pair + cons + vecs + lates + atts + con2 + vec2 + late2 + exp2 + out2 + att2:
        copy.wait_send()


def final(n, base, pieces, weight, con, out, att, exp_part, vec, late):
    heads = pieces.shape[0]
    r, d = con.shape[1:]
    cols = att.shape[2]
    nz = n // 2
    counts = (nz, n - 1, n - 1, 3, 3, nz - 1, 3, 3, 3, 3, 3)
    return pl.pallas_call(
        functools.partial(final_kernel, heads, n),
        out_shape=(
            jax.ShapeDtypeStruct(base.shape, f32),
            jax.ShapeDtypeStruct((4, r, d), bf16),
            jax.ShapeDtypeStruct((4,) + out.shape, bf16),
            jax.ShapeDtypeStruct((4,) + exp_part.shape, bf16),
            jax.ShapeDtypeStruct((4, r, cols), bf16),
            jax.ShapeDtypeStruct((4,) + vec.shape[1:], f32),
            jax.ShapeDtypeStruct((4,) + late.shape, f32),
        ),
        in_specs=[ANYWHERE] * 3 + [IN_VMEM] * 6,
        out_specs=(IN_VMEM,) * 7,
        scratch_shapes=[
            pltpu.VMEM(base.shape, f32),
            pltpu.VMEM(pieces.shape, bf16),
            pltpu.VMEM(weight.shape, bf16),
            pltpu.VMEM((4, r, d), bf16),
            pltpu.VMEM((nz, r, cols), bf16),
            pltpu.VMEM((nz, r, cols), bf16),
            pltpu.VMEM((nz, r, cols), bf16),
            pltpu.VMEM((n,) + vec.shape[1:], f32),
            pltpu.VMEM((n,) + late.shape, f32),
            pltpu.SemaphoreType.DMA((3,)),
        ]
        + [sem for count in counts for sem in dma_sems(count)],
        compiler_params=remote_params(3),
        cost_estimate=pl.CostEstimate(
            flops=8 * base.shape[0] * d * cols, bytes_accessed=8 * d * cols, transcendentals=0
        ),
        name="final",
    )(base, pieces, weight, con, out, att, exp_part, vec, late)


def finish_kernel(n, heads, gate_ref, mask_ref, *refs):
    sources, rest = refs[:7], refs[7:]
    con_o, out_o, exp_o, att_o, tok_o = rest[:5]
    vec_os, unit_os, query_o, value_o, gate_o = rest[5:12], rest[12:14], rest[14], rest[15], rest[16]
    con_v, out_v, exp_v, att_v, vec_v, late_v, sem = rest[17:]
    loads = [
        pltpu.make_async_copy(src, dst, sem.at[k])
        for k, (src, dst) in enumerate(
            zip(sources, (con_v, out_v, exp_v, att_v, vec_v, late_v, tok_o), strict=True)
        )
    ]
    for copy in loads:
        copy.start()

    def add4(parts):
        return (parts[0] + parts[1]) + (parts[2] + parts[3])

    for copy in loads:
        copy.wait()
    wide, cols, part = exp_v.shape[2], att_v.shape[2], out_v.shape[2]
    for k in range(4):
        con_o[k] = con_v[k].astype(f32)
        exp_o[:, k * wide : (k + 1) * wide] = exp_v[k].astype(f32)
        att_o[:, k * cols : (k + 1) * cols] = att_v[k].astype(f32)
        out_o[:, k * part : (k + 1) * part] = out_v[k].astype(f32)
    vec = add4([vec_v[k] for k in range(4)])
    own = vec_os[0].shape[0]
    for k, ref in enumerate(vec_os):
        ref[...] = vec[k, 0:own]
    for k, ref in enumerate(unit_os):
        ref[...] = vec[8 + k]
    rows = [jnp.concatenate([late_v[k, j : j + 1, :] for k in range(4)], axis=1) for j in range(2)]
    for k in range(n):

        @pl.when(lax.axis_index("wt") == k)
        def _(k=k):
            query_o[...] = rows[0][0, k * own : (k + 1) * own]
            value_o[...] = rows[1][0, k * own : (k + 1) * own]

    gates = []
    for k in range(4):
        for h in range(heads):
            part_sum = jnp.sum(late_v[k, 2:3, HD * h : HD * (h + 1)], axis=1, keepdims=True)
            kept = mask_ref[heads * k + h].astype(f32) / gate_ref[heads * k + h]
            gates.append(part_sum * kept)
    gate_o[...] = jnp.concatenate(gates, axis=1)[0]


def finish(n, heads, gate, mask, con, out, exp_all, att, vec, late, tok):
    r = out.shape[1]
    wide, cols, part = exp_all.shape[2], att.shape[2], out.shape[2]
    units = vec.shape[2]
    row = jax.ShapeDtypeStruct((r,), f32)
    return pl.pallas_call(
        functools.partial(finish_kernel, n, heads),
        out_shape=(
            jax.ShapeDtypeStruct(con.shape, f32),
            jax.ShapeDtypeStruct((r, 4 * part), f32),
            jax.ShapeDtypeStruct((r, 4 * wide), f32),
            jax.ShapeDtypeStruct((r, 4 * cols), f32),
            jax.ShapeDtypeStruct(tok.shape, f32),
        )
        + (row,) * 7
        + (jax.ShapeDtypeStruct((units,), f32),) * 2
        + (row,) * 2
        + (jax.ShapeDtypeStruct((4 * heads,), f32),),
        in_specs=[IN_SMEM] * 2 + [ANYWHERE] * 7,
        out_specs=(IN_VMEM,) * 17,
        scratch_shapes=[pltpu.VMEM(x.shape, x.dtype) for x in (con, out, exp_all, att, vec, late)]
        + [pltpu.SemaphoreType.DMA((7,))],
        compiler_params=pltpu.CompilerParams(vmem_limit_bytes=56 * 2**20),
        name="finish",
    )(gate, mask, con, out, exp_all, att, vec, late, tok)


(OUT_BIAS, GAIN1, SHIFT1, HIDDEN_SCALE, CON_BIAS, GAIN2, SHIFT2, HIDDEN_MASK) = range(8)
(S_OUT_BIAS, S_GAIN1, S_SHIFT1, S_CON_BIAS, S_GAIN2, S_SHIFT2, S_HIDDEN) = range(7)


def gelu_parts(x):
    bell = jnp.exp(-0.5 * (x * x))
    t = 1.0 / (1.0 + (0.3275911 * root_half) * jnp.abs(x))
    poly = t * (
        0.127414796 + t * (-0.142248368 + t * (0.7107068705 + t * (-0.7265760135 + t * 0.5307027145)))
    )
    tail = poly * bell
    cumulative = jnp.where(x < 0.0, tail, 1.0 - tail)
    return x * cumulative, cumulative + x * bell * density_scale


def norm_parts(summed):
    centre = summed - jnp.mean(summed, axis=-1, keepdims=True)
    inverse = lax.rsqrt(jnp.mean(centre * centre, axis=-1, keepdims=True) + epsilon)
    return (centre * inverse, inverse)


def norm_back(grad_normed, normed, inverse):
    return inverse * (
        grad_normed
        - jnp.mean(grad_normed, axis=-1, keepdims=True)
        - normed * jnp.mean(grad_normed * normed, axis=-1, keepdims=True)
    )


def feed_forward_kernel(
    steps, chunk,
    kept_ref, ctx_ref, tok_ref, cot_ref, wo_ref, we_hbm, wc_hbm,
    ob_ref, g1_ref, t1_ref, hg_ref, hm_ref, cb_ref, g2_ref, t2_ref, eb_ref, ug_ref, um_ref,
    lo_ref, dt1_ref, g_all, vec_ref, dwc_hbm, dwe_hbm, dwo_ref,
    we_ref, wc_ref, dwc_ref, dwe_ref, g_sc,
    wide_ref, unit_ref, sw_ref, su_ref, act_sc, gh_sc, low_sc, gb_sc, ga_sc, ctx_sc, gelu_sc, slope_sc,
    l_w, l_o, l_g, s_g, r_g,
):
    i = pl.program_id(0)
    block = tok_ref.shape[0]
    units = we_ref.shape[1]
    rows = pl.ds(pl.multiple_of(i * block, block), block)
    s, w = lax.axis_index("seq"), lax.axis_index("wt")
    others = [flip(s, k) for k in (1, 2, 3)]
    part_rows = g_all.shape[0]
    weights = [
        pltpu.make_async_copy(we_hbm, we_ref, l_w.at[0]),
        pltpu.make_async_copy(wc_hbm, wc_ref, l_w.at[1]),
    ]

    def leaving(t):
        there = g_all.at[:, pl.ds(pl.multiple_of((s * steps + t) * block, 128), block)]

        def part(p):
            lanes = pl.ds(pl.multiple_of(t * block, 128), block)
            return g_sc.at[pl.ds(pl.multiple_of(p * part_rows, 16), part_rows), lanes]

        copies = [
            remote(part(p), there, (s_g, r_g), 3 * t + k, (p, w)) for k, p in enumerate(others)
        ]
        return copies + [pltpu.make_async_copy(part(s), there, l_g.at[t])]

    @pl.when(i == 0)
    def _():
        for copy in weights:
            copy.start()
        meet([(p, w) for p in others])
        sw_ref[...] = jnp.zeros_like(sw_ref)
        su_ref[...] = jnp.zeros_like(su_ref)

        def row(ref):
            return ref[...].astype(f32).reshape(1, ref.shape[0])

        plain = ((OUT_BIAS, ob_ref), (GAIN1, g1_ref), (SHIFT1, t1_ref), (CON_BIAS, cb_ref))
        for k, ref in plain + ((GAIN2, g2_ref), (SHIFT2, t2_ref), (HIDDEN_MASK, hm_ref)):
            wide_ref[k : k + 1, :] = row(ref)
        wide_ref[HIDDEN_SCALE : HIDDEN_SCALE + 1, :] = row(hm_ref) * row(hg_ref)
        kept = row(um_ref) * kept_ref[lax.axis_index("wt")].astype(f32)
        unit_ref[0:1, :] = row(eb_ref)
        unit_ref[1:2, :] = kept * row(ug_ref)
        unit_ref[2:3, :] = kept

    def wide(k):
        return wide_ref[k : k + 1, :]

    def add_sum(ref, k, cols, value):
        ref[k : k + 1, cols] += jnp.sum(value, axis=0, keepdims=True)

    full = slice(None)
    ctx = ctx_ref[...]
    ctx_sc[:, rows] = ctx
    summed = mm(ctx, wo_ref[...], TN) + wide(OUT_BIAS) + tok_ref[...].astype(f32)
    n1, inv1 = norm_parts(summed)
    s1 = n1 * wide(GAIN1) + wide(SHIFT1)
    hs = wide(HIDDEN_SCALE)
    first = s1 * hs
    low = first.astype(bf16)
    low_sc[rows, :] = low
    branch = first + wide(CON_BIAS)

    @pl.when(i == 0)
    def _():
        for copy in weights:
            copy.wait()

    for j in range(units // chunk):
        cols = slice(j * chunk, (j + 1) * chunk)
        hidden = mm(low, we_ref[:, cols]) + unit_ref[0:1, cols]
        gelu, slope = gelu_parts(hidden)
        scale = unit_ref[1:2, cols]
        gelu_sc[:, cols] = gelu.astype(gelu_sc.dtype)
        slope_sc[:, cols] = (slope * scale).astype(slope_sc.dtype)
        act = (gelu * scale).astype(bf16)
        act_sc[rows, cols] = act
        branch = branch + mm(act, wc_ref[cols, :])
    n2, inv2 = norm_parts(branch)
    s2 = n2 * wide(GAIN2) + wide(SHIFT2)
    lo_ref[...] = (s2 * hs).astype(bf16)
    dy = cot_ref[...].astype(f32)
    e2 = dy * hs
    add_sum(sw_ref, S_GAIN2, full, e2 * n2)
    add_sum(sw_ref, S_SHIFT2, full, e2)
    dt2 = norm_back(e2 * wide(GAIN2), n2, inv2)
    gb = dt2.astype(bf16)
    gb_sc[rows, :] = gb
    add_sum(sw_ref, S_CON_BIAS, full, gb.astype(f32))
    d_first = dt2
    for j in range(units // chunk):
        cols = slice(j * chunk, (j + 1) * chunk)
        d_act = mm(gb, wc_ref[cols, :], NT)
        add_sum(su_ref, 1, cols, d_act * gelu_sc[:, cols].astype(f32))
        gh = d_act * slope_sc[:, cols].astype(f32)
        add_sum(su_ref, 0, cols, gh)
        gh = gh.astype(bf16)
        gh_sc[rows, cols] = gh
        d_first = d_first + mm(gh, we_ref[:, cols], NT)
    e1 = d_first * hs
    add_sum(sw_ref, S_GAIN1, full, e1 * n1)
    add_sum(sw_ref, S_SHIFT1, full, e1)
    add_sum(sw_ref, S_HIDDEN, full, dy * s2 + d_first * s1)
    dt1 = norm_back(e1 * wide(GAIN1), n1, inv1)
    dt1_ref[...] = dt1
    ga = dt1.astype(bf16)
    ga_sc[rows, :] = ga
    add_sum(sw_ref, S_OUT_BIAS, full, ga.astype(f32))
    g_sc[:, rows] = mm(wo_ref[...], ga, NT).astype(bf16)
    for copy in leaving(i):
        copy.start()

    @pl.when(i == steps - 1)
    def _():
        own, wide_cols = dwe_ref.shape[3:]

        def weight_grads(j, carry):
            cols = pl.ds(pl.multiple_of(j * wide_cols, 128), wide_cols)
            dwc_ref[cols, :] = mm(act_sc[:, cols], gb_sc[...], TN).astype(bf16)
            part = mm(low_sc[...], gh_sc[:, cols], TN).astype(bf16)
            for k in range(2 * dwe_ref.shape[2]):
                dwe_ref[k % 2, j, k // 2] = part[k * own : (k + 1) * own]
            for copy in given(j):
                copy.start()
            return carry

        def given(j):
            there = pl.ds(pl.multiple_of(j * wide_cols, 128), wide_cols)
            return [
                pltpu.make_async_copy(dwc_ref.at[there], dwc_hbm.at[there], l_o.at[j]),
                pltpu.make_async_copy(dwe_ref.at[:, j], dwe_hbm.at[:, j], l_o.at[4 + j]),
            ]

        lax.fori_loop(0, 4, weight_grads, 0)
        own, part_cols = dwo_ref.shape[3:]
        for q in range(4):
            part = mm(ctx_sc[...], ga_sc[:, q * part_cols : (q + 1) * part_cols]).astype(bf16)
            for k in range(2 * dwo_ref.shape[2]):
                dwo_ref[k % 2, q, k // 2] = part[k * own : (k + 1) * own]
        vec_ref[...] = jnp.zeros_like(vec_ref)
        sw_ref[S_HIDDEN : S_HIDDEN + 1, :] *= wide(HIDDEN_MASK)
        su_ref[1:2, :] *= unit_ref[2:3, :]
        own_wide, own_units = dwe_ref.shape[3], vec_ref.shape[2]
        for k in range(vec_ref.shape[0]):
            vec_ref[k, 0:8, 0:own_wide] = sw_ref[:, k * own_wide : (k + 1) * own_wide]
            vec_ref[k, 8:16, :] = su_ref[:, k * own_units : (k + 1) * own_units]
        for t in range(steps):
            for copy in leaving(t):
                copy.wait()
        for j in range(4):
            for copy in given(j):
                copy.wait()


def feed_forward(n, kept, ctx_t, tokens, cotangent, wo, we, wc, *vectors):
    steps, chunk, keep = 3, 768, f32
    rows, d = tokens.shape
    units = we.shape[1]
    block = rows // steps
    halves = (2, 4, n // 2, d // n, units // 4)
    out_halves = (2, 4, n // 2, d // n, d // 4)
    tile = pl.BlockSpec((block, d), lambda i: (i, 0))
    lanes = pl.BlockSpec((d, block), lambda i: (0, i))

    def once(shape):
        return pl.BlockSpec(shape, lambda i: (0, 0), pipeline_mode=pl.Buffered(1))

    def once3(shape):
        return pl.BlockSpec(shape, lambda i: (0, 0, 0), pipeline_mode=pl.Buffered(1))

    def once5(shape):
        return pl.BlockSpec(shape, lambda i: (0, 0, 0, 0, 0), pipeline_mode=pl.Buffered(1))

    return pl.pallas_call(
        functools.partial(feed_forward_kernel, steps, chunk),
        out_shape=(
            jax.ShapeDtypeStruct((rows, d), bf16),
            jax.ShapeDtypeStruct((rows, d), f32),
            jax.ShapeDtypeStruct((d // 4, 4 * rows), bf16),
            jax.ShapeDtypeStruct((n, 16, units // n), f32),
            jax.ShapeDtypeStruct((units, d), bf16),
            jax.ShapeDtypeStruct(halves, bf16),
            jax.ShapeDtypeStruct(out_halves, bf16),
        ),
        grid=(steps,),
        in_specs=[
            pl.BlockSpec(memory_space=pltpu.SMEM),
            lanes, tile, tile, once((d, d)), ANYWHERE, ANYWHERE,
        ]
        + [IN_VMEM] * len(vectors),
        out_specs=(
            tile, tile, ANYWHERE, once3((n, 16, units // n)), ANYWHERE,
            ANYWHERE, once5(out_halves),
        ),
        scratch_shapes=[
            pltpu.VMEM((d, units), bf16),
            pltpu.VMEM((units, d), bf16),
            pltpu.VMEM((units, d), bf16),
            pltpu.VMEM(halves, bf16),
            pltpu.VMEM((d, rows), bf16),
            pltpu.VMEM((8, d), f32),
            pltpu.VMEM((8, units), f32),
            pltpu.VMEM((8, d), f32),
            pltpu.VMEM((8, units), f32),
            pltpu.VMEM((rows, units), bf16),
            pltpu.VMEM((rows, units), bf16),
            pltpu.VMEM((rows, d), bf16),
            pltpu.VMEM((rows, d), bf16),
            pltpu.VMEM((rows, d), bf16),
            pltpu.VMEM((d, rows), bf16),
            pltpu.VMEM((block, units), keep),
            pltpu.VMEM((block, units), keep),
            pltpu.SemaphoreType.DMA((2,)),
            pltpu.SemaphoreType.DMA((8,)),
            pltpu.SemaphoreType.DMA((steps,)),
        ]
        + dma_sems(3 * steps),
        compiler_params=pltpu.CompilerParams(
            collective_id=4, has_side_effects=True, vmem_limit_bytes=62 * 2**20
        ),
        cost_estimate=pl.CostEstimate(
            flops=rows * d * (12 * units + 6 * d),
            bytes_accessed=4 * d * (4 * units + 2 * d) + 12 * rows * d,
            transcendentals=2 * rows * units,
        ),
        name="feed_forward",
    )(kept, ctx_t, tokens, cotangent, wo, we, wc, *vectors)


def local(
    tokens,
    output_cotangent,
    attention_weight,
    query_bias,
    value_bias,
    output_weight,
    output_bias,
    first_gain,
    first_shift,
    expand_weight,
    expand_bias,
    contract_weight,
    contract_bias,
    second_gain,
    second_shift,
    head_gate,
    hidden_gate,
    unit_gate,
    head_mask,
    hidden_mask,
    unit_mask,
    attention_mask,
    feedforward_mask,
    continuation_lengths,
):
    seq_count = lax.axis_size("seq")
    wt_count = lax.axis_size("wt")
    model_width = hidden_gate.shape[0]
    local_heads = head_gate.shape[0] // seq_count
    own_wide = model_width // wt_count
    tokens_all, own_weight, exp_quarter = gather_in(wt_count, tokens, attention_weight, expand_weight)
    contract_weight, own_weight = lax.optimization_barrier((contract_weight, own_weight))
    full_contract = lax.all_gather(contract_weight, "wt", axis=0, tiled=True)
    full_attention = lax.all_gather(attention_weight, "wt", axis=0, tiled=True)
    full_output = lax.all_gather(output_weight, "wt", axis=0, tiled=True)
    packed, own_context, log_sums, context_t, full_expand = attend(
        wt_count,
        continuation_lengths,
        attention_mask,
        head_gate,
        head_mask,
        query_bias,
        value_bias,
        tokens_all,
        own_weight.reshape(model_width, -1),
        exp_quarter,
        local_heads,
    )
    (
        layer_output,
        grad_total_one,
        grad_context_t,
        vec_sums,
        contract_weight_grad,
        exp_parts,
        out_parts,
    ) = feed_forward(
        wt_count,
        feedforward_mask,
        context_t,
        tokens,
        output_cotangent,
        full_output,
        full_expand.reshape(model_width, -1),
        full_contract,
        output_bias,
        first_gain,
        first_shift,
        hidden_gate,
        hidden_mask,
        contract_bias,
        second_gain,
        second_shift,
        expand_bias,
        unit_gate,
        unit_mask,
    )
    con_piece = lax.psum_scatter(contract_weight_grad, "wt", scatter_dimension=0, tiled=True)
    pieces, projection_grad, exp_part, out_part, late_sums = attend_back(
        wt_count,
        continuation_lengths,
        attention_mask,
        head_gate,
        head_mask,
        packed,
        own_context,
        grad_context_t,
        log_sums,
        tokens_all,
        exp_parts,
        out_parts,
    )
    tokens_grad, con_all, out_all, exp_all, att_all, vec_all, late_all = final(
        wt_count,
        grad_total_one,
        pieces,
        full_attention,
        con_piece.reshape(seq_count, own_wide, model_width),
        out_part,
        projection_grad,
        exp_part,
        vec_sums,
        late_sums,
    )
    con_sum, out_sum, exp_sum, att_sum, tokens_grad, *rows = finish(
        wt_count,
        local_heads,
        head_gate,
        head_mask,
        con_all,
        out_all,
        exp_all,
        att_all,
        vec_all,
        late_all,
        tokens_grad,
    )
    return (
        layer_output,
        tokens_grad,
        att_sum,
        rows[9],
        rows[10],
        out_sum,
        rows[S_OUT_BIAS],
        rows[S_GAIN1],
        rows[S_SHIFT1],
        exp_sum,
        rows[7],
        con_sum.reshape(seq_count * own_wide, model_width),
        rows[S_CON_BIAS],
        rows[S_GAIN2],
        rows[S_SHIFT2],
        rows[11],
        rows[S_HIDDEN],
        rows[8],
    )


def solution(mesh):
    return jax.shard_map(
        local,
        mesh=mesh,
        in_specs=(
            P(("wt", "seq"), None),
            P(("wt", "seq"), None),
            P("wt", None),
            P(),
            P(),
            P("wt", None),
            P(),
            P(),
            P(),
            P("wt", None),
            P(),
            P("wt", None),
            P(),
            P(),
            P(),
            P(),
            P(),
            P(),
            P(),
            P(),
            P(),
            P(),
            P(),
            P(),
        ),
        out_specs=(
            P(("wt", "seq"), None),
            P(("wt", "seq"), None),
            P("wt", None),
            P("wt"),
            P("wt"),
            P("wt", None),
            P("wt"),
            P("wt"),
            P("wt"),
            P("wt", None),
            P("wt"),
            P("wt", None),
            P("wt"),
            P("wt"),
            P("wt"),
            P(),
            P("wt"),
            P("wt"),
        ),
        check_vma=False,
    )
```

```python
import functools

import jax
import jax.numpy as jnp
from jax import lax
from jax.experimental import pallas as pl
from jax.experimental.pallas import tpu as pltpu
from jax.sharding import PartitionSpec as P

PROMPT = 1024
GRP_WT = 1
GLEN = 3072
SHORT = 512
LONG = 1536
HD = 64
TQ = 512
KC = 512

epsilon = 1e-06
score_scale = 0.125
exp2_scale = 0.125 * 1.4426950408889634
root_half = 0.7071067811865476
density_scale = 0.3989422804014327
bf16 = jnp.bfloat16
f32 = jnp.float32

NT = (((1,), (1,)), ((), ()))
NN = (((1,), (0,)), ((), ()))
TN = (((0,), (0,)), ((), ()))


def mm(a, b, dims=NN):
    return lax.dot_general(a, b, dims, preferred_element_type=f32)


def natural_at(short_first, i):
    other = jnp.where(i == 2, 5, i - 1)
    return jnp.where(short_first | (i < 2), i, other)


def ordered_at(short_first, j):
    other = jnp.where(j == 5, 2, j + 1)
    return jnp.where(short_first | (j < 2), j, other)


def query_tiles(tile):
    def prompt(i, carry):
        tile(i, ())
        return carry

    def longer(i, carry):
        tile(i, (3, 4, 5))
        return carry

    lax.fori_loop(0, 2, prompt, 0)
    tile(2, (2,))
    lax.fori_loop(3, 6, longer, 0)


def remote(src, dst, sems, k, peer):
    return pltpu.make_async_remote_copy(
        src_ref=src,
        dst_ref=dst,
        send_sem=sems[0].at[k],
        recv_sem=sems[1].at[k],
        device_id=peer,
        device_id_type=pl.DeviceIdType.MESH,
    )


def send(src, dst, sems, k, peer):
    copy = remote(src, dst, sems, k, peer)
    copy.start()
    return copy


def value_scale(head, group, kept_ref, gate_ref, mask_ref):
    return mask_ref[head].astype(f32) * gate_ref[head] * kept_ref[group].astype(f32)


def attend_kernel(
    heads, n, lens_ref, kept_ref, gate_ref, mask_ref, qb_ref, vb_ref, tok_ref, w_ref, exp_ref,
    q_sc, k_sc, v_ref, kt_ref, ctx_ref, lse_ref, full_ref, exp_all,
    vt_sc, ct_sc, vec_ref, exp_buf,
    local_sem, s_sem, r_sem, s_e, r_e,
):
    s, w = lax.axis_index("seq"), lax.axis_index("wt")
    others = [flip(s, k) for k in (1, 2, 3)]
    mate = (s, flip(w, 1))
    short_first = lens_ref[w, 0] == SHORT
    come = pltpu.make_async_copy(exp_ref, exp_buf, local_sem.at[heads])
    come.start()
    meet([(p, w) for p in others] + [mate])
    core, quarter = lax.rem(w, 2), exp_ref.shape[2]

    def exp_place(p):
        return exp_all.at[:, core, :, pl.ds(pl.multiple_of(p * quarter, 128), quarter)]

    spread = [
        send(exp_ref, exp_place(s), (s_e, r_e), k, (p, w)) for k, p in enumerate(others)
    ] + [send(exp_ref, exp_place(s), (s_e, r_e), 3, mate)]
    width = heads * HD
    count = GLEN // 4
    vec_ref[...] = jnp.zeros_like(vec_ref)
    for k in range(4):

        @pl.when(s == k)
        def _(k=k):
            query = qb_ref[...].astype(f32).reshape(1, 4 * width)
            value = vb_ref[...].astype(f32).reshape(1, 4 * width)
            for h in range(heads):
                own = slice(k * width + h * HD, k * width + (h + 1) * HD)
                at = 3 * HD * h
                vec_ref[0:1, at : at + HD] = query[:, own]
                vec_ref[0:1, at + 2 * HD : at + 3 * HD] = value[:, own]

    for h in range(heads):
        at = 3 * HD * h
        vec_ref[1:2, at : at + 2 * HD] = jnp.ones((1, 2 * HD), f32)
        scale = value_scale(s * heads + h, w, kept_ref, gate_ref, mask_ref)
        vec_ref[1:2, at + 2 * HD : at + 3 * HD] = jnp.full((1, HD), scale, f32)
    come.wait()
    own_part = pltpu.make_async_copy(exp_buf, exp_place(s), local_sem.at[heads])
    own_part.start()

    def project(i, carry):
        rows = pl.ds(pl.multiple_of(i * TQ, TQ), TQ)
        x = mm(tok_ref[natural_at(short_first, i)], w_ref[...]) + vec_ref[0:1, :]
        x = (x * vec_ref[1:2, :]).astype(bf16)
        for h in range(heads):
            at = 3 * HD * h
            q_sc[h, rows, :] = x[:, at : at + HD]
            k = x[:, at + HD : at + 2 * HD]
            k_sc[h, rows, :] = k
            kt_ref[h, i] = k.T
            v = x[:, at + 2 * HD : at + 3 * HD]
            v_ref[h, rows, :] = v
            vt_sc[h, :, rows] = v.T
        return carry

    lax.fori_loop(0, GLEN // TQ, project, 0)

    def leaving(h):
        rows = pl.ds(pl.multiple_of(h * HD, HD), HD)
        there = full_ref.at[pl.ds(pl.multiple_of(s * width + h * HD, HD), HD), :]

        def part(p):
            return ctx_ref.at[rows, pl.ds(pl.multiple_of(p * count, 128), count)]

        copies = [
            remote(part(p), there, (s_sem, r_sem), 3 * h + k, (p, w)) for k, p in enumerate(others)
        ]
        return copies, pltpu.make_async_copy(part(s), there, local_sem.at[h])

    passed = [
        (spread[k], remote(exp_place(p), exp_place(p), (s_e, r_e), 4 + k, mate))
        for k, p in enumerate(others)
    ]

    def one_head(h, carry):
        @pl.when(h == heads - 1)
        def _():
            for came, copy in passed:
                came.wait_recv()
                copy.start()

        def tile(i, own_blocks):
            rows = pl.ds(pl.multiple_of(i * TQ, TQ), TQ)
            q = q_sc[h, rows, :]
            s1 = mm(k_sc[h, 0:PROMPT, :], q, NT)
            top = jnp.max(s1, axis=0, keepdims=True)
            if own_blocks:
                own = slice(own_blocks[0] * KC, (own_blocks[-1] + 1) * KC)
                s2 = mm(k_sc[h, own, :], q, NT)
                top = jnp.maximum(top, jnp.max(s2, axis=0, keepdims=True))
            top = top * exp2_scale
            p1 = jnp.exp2(s1 * exp2_scale - top)
            o = mm(vt_sc[h, :, 0:PROMPT], p1.astype(bf16))
            total = jnp.sum(p1, axis=0, keepdims=True)
            if own_blocks:
                p2 = jnp.exp2(s2 * exp2_scale - top)
                o = o + mm(vt_sc[h, :, own], p2.astype(bf16))
                total = total + jnp.sum(p2, axis=0, keepdims=True)
            ct_sc[i] = (o / total).astype(bf16)
            lse_ref[h, :, rows] = top + jnp.log2(total)

        query_tiles(tile)

        def settle(j, carry):
            rows = pl.ds(pl.multiple_of(h * HD, HD), HD)
            lanes = pl.ds(pl.multiple_of(j * SHORT, SHORT), SHORT)
            ctx_ref[rows, lanes] = ct_sc[ordered_at(short_first, j)]
            return carry

        lax.fori_loop(0, GLEN // SHORT, settle, 0)
        copies, own = leaving(h)
        for copy in copies:
            copy.start()
        own.start()
        return carry

    lax.fori_loop(0, heads, one_head, 0)
    own_part.wait()
    spread[3].wait_recv()
    for _, copy in passed:
        copy.wait()
    for copy in spread:
        copy.wait_send()
    for h in range(heads):
        copies, own = leaving(h)
        own.wait()
        for copy in copies:
            copy.wait()


def attend(n, lens, kept, gate, mask, query_bias, value_bias, tokens_all, weight, exp_part, heads):
    width = 3 * HD * heads
    return pl.pallas_call(
        functools.partial(attend_kernel, heads, n),
        out_shape=(
            jax.ShapeDtypeStruct((heads, GLEN, HD), bf16),
            jax.ShapeDtypeStruct((heads, GLEN, HD), bf16),
            jax.ShapeDtypeStruct((heads, GLEN, HD), bf16),
            jax.ShapeDtypeStruct((heads, GLEN // TQ, HD, TQ), bf16),
            jax.ShapeDtypeStruct((HD * heads, GLEN), bf16),
            jax.ShapeDtypeStruct((heads, 1, GLEN), f32),
            jax.ShapeDtypeStruct((4 * HD * heads, GLEN // 4), bf16),
            jax.ShapeDtypeStruct((n // 2, 2, exp_part.shape[1], 4 * exp_part.shape[2]), bf16),
        ),
        in_specs=[IN_SMEM] * 4 + [IN_VMEM] * 4 + [ANYWHERE],
        out_specs=(IN_VMEM,) * 6 + (ANYWHERE, ANYWHERE),
        scratch_shapes=[
            pltpu.VMEM((heads, HD, GLEN), bf16),
            pltpu.VMEM((GLEN // TQ, HD, TQ), bf16),
            pltpu.VMEM((2, width), f32),
            pltpu.VMEM(exp_part.shape, bf16),
            pltpu.SemaphoreType.DMA((heads + 1,)),
        ]
        + dma_sems(3 * heads)
        + dma_sems(7),
        compiler_params=remote_params(1),
        cost_estimate=pl.CostEstimate(
            flops=2 * GLEN * 768 * width + heads * 4 * 256 * 5767168,
            bytes_accessed=2 * GLEN * (768 + width),
            transcendentals=heads * 5767168,
        ),
        name="attend",
    )(
        lens, kept, gate, mask, query_bias, value_bias,
        tokens_all.reshape(GLEN // TQ, TQ, -1), weight, exp_part,
    )


def attend_back_kernel(
    heads, n, lens_ref, kept_ref, gate_ref, mask_ref, q_hbm, k_hbm, v_hbm, kt_hbm,
    ctx_ref, gctx_ref, lse_ref, tok_hbm,
    e_own_hbm, e_got_hbm, o_own_hbm, o_got_hbm, pieces_o, dw_o, exp_o, out_o, late_o,
    tok_v, e_own, o_own, e_got, o_got, e_all, o_all, e_sum, o_sum, e_z, o_z, stage, late_sc, row_sc,
    q_all, k_all, v_all, kt_all, g_sc, g_nat, delta_sc, delta_nat, dqt_sc, dk_sc, dv_sc, acc,
    l_in, l_out, s_p, r_p, s_e, r_e, s_z, r_z,
):
    s, w = lax.axis_index("seq"), lax.axis_index("wt")
    others = [flip(s, k) for k in (1, 2, 3)]
    z, c, nz = w // 2, lax.rem(w, 2), n // 2
    far = [lax.rem(z + j, nz) for j in range(1, nz)]
    short_first = lens_ref[w, 0] == SHORT
    count = GLEN // 4
    width = heads * HD
    def taken(h):
        pairs = ((q_hbm, q_all), (k_hbm, k_all), (v_hbm, v_all), (kt_hbm, kt_all))
        return [
            pltpu.make_async_copy(src.at[h], dst.at[h], l_in.at[4 * h + k])
            for k, (src, dst) in enumerate(pairs)
        ]

    loads = [
        pltpu.make_async_copy(e_own_hbm, e_own, l_in.at[4 * heads]),
        pltpu.make_async_copy(e_got_hbm, e_got, l_in.at[4 * heads + 1]),
        pltpu.make_async_copy(o_own_hbm, o_own, l_in.at[4 * heads + 2]),
        pltpu.make_async_copy(o_got_hbm, o_got, l_in.at[4 * heads + 3]),
        pltpu.make_async_copy(tok_hbm, tok_v, l_in.at[4 * heads + 4]),
    ]
    for copy in loads[:4] + taken(0):
        copy.start()
    for h in range(1, heads):
        for copy in taken(h):
            copy.start()
    loads[4].start()
    meet([(p, w) for p in others] + [(s, 2 * k + c) for k in far])

    def leaving(h, own=False):
        if own:
            return pltpu.make_async_copy(stage.at[h, s], pieces_o.at[h, s], l_out.at[h])
        return [
            remote(stage.at[h, p], pieces_o.at[h, s], (s_p, r_p), 3 * h + k, (p, w))
            for k, p in enumerate(others)
        ]

    over_plane = [
        remote(e_got.at[p], e_all.at[s], (s_e, r_e), k, (p, w)) for k, p in enumerate(others)
    ] + [remote(o_got.at[p], o_all.at[s], (s_e, r_e), 3 + k, (p, w)) for k, p in enumerate(others)]
    over_z = [
        remote(e_sum.at[k], e_z.at[z], (s_z, r_z), j, (s, 2 * k + c)) for j, k in enumerate(far)
    ] + [
        remote(o_sum.at[k], o_z.at[z], (s_z, r_z), nz - 1 + j, (s, 2 * k + c))
        for j, k in enumerate(far)
    ]
    for copy in loads[:4]:
        copy.wait()

    def pair_sum(i, carry):
        q, k = i // nz, lax.rem(i, nz)
        e_got[q, k] = (e_got[q, k].astype(f32) + e_own[q, k].astype(f32)).astype(bf16)
        o_got[q, k] = (o_got[q, k].astype(f32) + o_own[q, k].astype(f32)).astype(bf16)
        return carry

    lax.fori_loop(0, 4 * nz, pair_sum, 0)
    for copy in over_plane:
        copy.start()
    e_all[s] = e_got[s]
    o_all[s] = o_got[s]
    late_sc[...] = jnp.zeros_like(late_sc)
    row_sc[...] = jnp.zeros_like(row_sc)
    for h in range(heads):
        for copy in taken(h):
            copy.wait()

    def prologue(h):
        dk_sc[...] = jnp.zeros_like(dk_sc)
        dv_sc[...] = jnp.zeros_like(dv_sc)
        def inner(i, carry):
            lanes = pl.ds(pl.multiple_of(i * TQ, TQ), TQ)
            own = pl.ds(pl.multiple_of(h * HD, HD), HD)
            g_nat[i] = gctx_ref[own, lanes]
            product = g_nat[i].astype(f32) * ctx_ref[own, lanes].astype(f32)
            delta_nat[i] = jnp.sum(product, axis=0, keepdims=True)
            return carry

        def order(i, carry):
            g_sc[i] = g_nat[natural_at(short_first, i)]
            delta_sc[i] = delta_nat[natural_at(short_first, i)]
            return carry

        lax.fori_loop(0, GLEN // TQ, inner, 0)
        lax.fori_loop(0, GLEN // TQ, order, 0)

    def halfway():
        for copy in over_plane:
            copy.wait_recv()

        def add4(ref, k):
            t = [ref[q, k].astype(f32) for q in range(4)]
            return ((t[0] + t[1]) + (t[2] + t[3])).astype(bf16)

        def plane_sum(k, carry):
            e_sum[k] = add4(e_all, k)
            o_sum[k] = add4(o_all, k)
            return carry

        lax.fori_loop(0, nz, plane_sum, 0)
        for copy in over_z:
            copy.start()
        e_z[z] = e_sum[z]
        o_z[z] = o_sum[z]

    def epilogue(h, first, last):
        half = SHORT // 2
        scale = value_scale(s * heads + h, w, kept_ref, gate_ref, mask_ref)

        def settle(j, carry):
            i = ordered_at(short_first, j)
            dq = dqt_sc[i].astype(bf16)
            dk = (dk_sc[i] * score_scale).astype(bf16).T
            dv = dv_sc[i].astype(bf16).astype(f32)
            gate = jnp.sum(dv * v_all[h, i].astype(f32), axis=0, keepdims=True)
            dv = (dv * scale).astype(bf16)
            row_sc[h, 0:1, :] += jnp.sum(dv.astype(f32), axis=0, keepdims=True)
            row_sc[h, 1:2, :] += gate
            dv = dv.T
            x = dq.astype(f32)
            late_sc[h] += (x[:, 0:128] + x[:, 128:256]) + (x[:, 256:384] + x[:, 384:512])
            for r in range(2):
                u = 2 * j + r
                p, there = u // 3, pl.ds(pl.multiple_of(lax.rem(u, 3) * half, half), half)
                cols = slice(r * half, (r + 1) * half)
                stage[h, p, 0:HD, there] = dq[:, cols]
                stage[h, p, HD : 2 * HD, there] = dk[:, cols]
                stage[h, p, 2 * HD : 3 * HD, there] = dv[:, cols]
            return carry

        lax.fori_loop(first, last, settle, 0)
        for p, copy in zip(others, leaving(h), strict=True):

            @pl.when(p // 2 == (0 if first == 0 else 1))
            def _(copy=copy):
                copy.start()

        if first == 0:
            leaving(h, True).start()

    def tile_of(h):
        def tile(i, own_blocks):
            q = q_all[h, i]
            g = g_sc[i]
            lse = lse_ref[h, :, pl.ds(pl.multiple_of(i * TQ, TQ), TQ)]
            delta = delta_sc[i]
            dq = jnp.zeros((HD, TQ), f32)
            for j in (0, 1) + own_blocks:
                sc = mm(k_all[h, j], q, NT)
                p = jnp.exp2(sc * exp2_scale - lse)
                dp = mm(v_all[h, j], g)
                ds = (p * (dp - delta)).astype(bf16)
                dv_sc[j] += mm(p.astype(bf16), g, NT)
                dk_sc[j] += mm(ds, q)
                dq = dq + mm(kt_all[h, j], ds)
            dqt_sc[i] = dq * score_scale

        return tile

    def one_head(h, carry):
        prologue(h)
        def longer(i, carry):
            tile_of(h)(i, (3, 4, 5))
            return carry

        def prompt(i, carry):
            tile_of(h)(i, ())
            return carry

        tile_of(h)(2, (2,))
        pl.when(h == heads - 1)(halfway)

        lax.fori_loop(3, 6, longer, 0)
        epilogue(h, 2, 6)
        lax.fori_loop(0, 2, prompt, 0)
        epilogue(h, 0, 2)
        return carry

    lax.fori_loop(0, heads, one_head, 0)
    loads[4].wait()
    acc[...] = jnp.zeros_like(acc)

    def weight_grad(p, carry):
        x = tok_v[pl.ds(pl.multiple_of(p * count, count), count), :]
        for h in range(heads):
            acc[3 * HD * h : 3 * HD * (h + 1), :] += mm(stage[h, p], x)
        return carry

    lax.fori_loop(0, 4, weight_grad, 0)
    own_rows = dw_o.shape[1]
    grad = acc[...].T.astype(bf16)
    for k in range(n):
        dw_o[k] = grad[k * own_rows : (k + 1) * own_rows, :]
    late_o[...] = jnp.zeros_like(late_o)
    for h in range(heads):
        own = slice(HD * h, HD * (h + 1))
        late_o[0:1, own] = jnp.sum(late_sc[h].T, axis=0, keepdims=True)
        late_o[1:3, own] = row_sc[h, 0:2, :]
    for copy in over_z:
        copy.wait_recv()
    for ref, out in ((e_z, exp_o), (o_z, out_o)):
        total = ref[0].astype(f32)
        for k in range(1, nz):
            total = total + ref[k].astype(f32)
        out[...] = total.astype(bf16)
    for h in range(heads):
        for copy in [leaving(h, True)] + leaving(h):
            copy.wait()
    for copy in over_plane + over_z:
        copy.wait_send()


def attend_back(n, lens, kept, gate, mask, q, k, v, kt, ctx, g, lse, tokens_all, *parts):
    heads = q.shape[0]
    width = 3 * HD * heads
    d = tokens_all.shape[1]
    count = GLEN // 4
    nz = n // 2
    own, wide = parts[0].shape[2:]
    part = parts[2].shape[3]
    blocks = GLEN // TQ
    rows64 = pltpu.VMEM((heads, blocks, TQ, HD), bf16)
    blocks64 = pltpu.VMEM((blocks, HD, TQ), bf16)
    quarters = [pltpu.VMEM(parts[0].shape, bf16), pltpu.VMEM(parts[2].shape, bf16)]
    return pl.pallas_call(
        functools.partial(attend_back_kernel, heads, n),
        out_shape=(
            jax.ShapeDtypeStruct((heads, 4, 3 * HD, count), bf16),
            jax.ShapeDtypeStruct((n, d // n, width), bf16),
            jax.ShapeDtypeStruct((own, wide), bf16),
            jax.ShapeDtypeStruct((own, part), bf16),
            jax.ShapeDtypeStruct((8, HD * heads), f32),
        ),
        in_specs=[IN_SMEM] * 4
        + [ANYWHERE] * 4
        + [IN_VMEM, IN_VMEM, IN_VMEM, ANYWHERE]
        + [ANYWHERE] * 4,
        out_specs=(ANYWHERE, IN_VMEM, IN_VMEM, IN_VMEM, IN_VMEM),
        scratch_shapes=[
            pltpu.VMEM(tokens_all.shape, bf16),
        ]
        + quarters * 3
        + [pltpu.VMEM((nz, own, wide), bf16), pltpu.VMEM((nz, own, part), bf16)] * 2
        + [pltpu.VMEM((heads, 4, 3 * HD, count), bf16), pltpu.VMEM((heads, HD, 128), f32)]
        + [pltpu.VMEM((heads, 8, HD), f32)]
        + [
            rows64,
            rows64,
            rows64,
            pltpu.VMEM(kt.shape, bf16),
            blocks64,
            blocks64,
            pltpu.VMEM((blocks, 1, TQ), f32),
            pltpu.VMEM((blocks, 1, TQ), f32),
            pltpu.VMEM((blocks, HD, TQ), f32),
            pltpu.VMEM((blocks, TQ, HD), f32),
            pltpu.VMEM((blocks, TQ, HD), f32),
            pltpu.VMEM((width, d), f32),
            pltpu.SemaphoreType.DMA((4 * heads + 5,)),
            pltpu.SemaphoreType.DMA((heads,)),
        ]
        + dma_sems(3 * heads)
        + dma_sems(6)
        + dma_sems(2 * nz - 2),
        compiler_params=remote_params(2),
        cost_estimate=pl.CostEstimate(
            flops=heads * 10 * 256 * 5767168 + 2 * GLEN * d * width,
            bytes_accessed=2 * GLEN * (3 * width + d),
            transcendentals=heads * 5767168,
        ),
        name="attend_back",
    )(
        lens, kept, gate, mask,
        *(x.reshape(heads, blocks, TQ, HD) for x in (q, k, v)),
        kt, ctx, g, lse, tokens_all, *parts,
    )


def meet(peers):
    barrier = pltpu.get_barrier_semaphore()
    for peer in peers:
        pl.semaphore_signal(barrier, inc=1, device_id=peer, device_id_type=pl.DeviceIdType.MESH)
    pl.semaphore_wait(barrier, len(peers))


def flip(index, bits):
    for bit in (1, 2):
        if bits & bit:
            index = index + bit - 2 * bit * ((index // bit) % 2)
    return index


def remote_params(number):
    return pltpu.CompilerParams(
        collective_id=number, has_side_effects=True, vmem_limit_bytes=56 * 2**20
    )


ANYWHERE = pl.BlockSpec(memory_space=pl.ANY)
IN_VMEM = pl.BlockSpec(memory_space=pltpu.VMEM)
IN_SMEM = pl.BlockSpec(memory_space=pltpu.SMEM)


def dma_sems(count):
    return [pltpu.SemaphoreType.DMA((count,)), pltpu.SemaphoreType.DMA((count,))]


def gather_kernel(
    n, tok_ref, weight_ref, exp_ref, tok_all, cols_all, exp_all, tok_buf, cols_buf, exp_buf,
    local_sem, s_tok, r_tok, s_w, r_w, s_f, r_f, s_e, r_e,
):
    s, w = lax.axis_index("seq"), lax.axis_index("wt")
    rows = tok_ref.shape[0]
    half = rows // 2
    wide = cols_buf.shape[1]
    for k in range(4):

        @pl.when(s == k)
        def _(k=k):
            cols_buf[...] = weight_ref[:, k * wide : (k + 1) * wide]

    by_x, by_y, mate = (flip(s, 1), w), (flip(s, 2), w), (s, flip(w, 1))
    far = [(s, lax.rem(w + 2 * j, n)) for j in range(1, n // 2)]
    quarter = exp_buf.shape[1]
    exp_own = exp_ref.at[:, pl.ds(pl.multiple_of(s * quarter, 128), quarter)]
    come = [
        pltpu.make_async_copy(tok_ref, tok_buf, local_sem.at[0]),
        pltpu.make_async_copy(exp_own, exp_buf, local_sem.at[2]),
    ]
    for copy in come:
        copy.start()
    meet([by_x, by_y, mate] + far)

    def part(owner, k):
        return pl.ds(pl.multiple_of(owner * rows + k * half, half), half)

    tok = (s_tok, r_tok)
    first = [pl.ds(0, half), pl.ds(half, half)]
    x0 = send(tok_ref.at[first[0]], tok_all.at[part(s, 0)], tok, 0, by_x)
    y1 = send(tok_ref.at[first[1]], tok_all.at[part(s, 1)], tok, 1, by_y)
    x1 = send(tok_ref.at[first[1]], tok_all.at[part(s, 1)], tok, 2, by_x)
    y0 = send(tok_ref.at[first[0]], tok_all.at[part(s, 0)], tok, 3, by_y)
    held = [
        send(cols_buf, cols_all.at[w], (s_w, r_w), k, peer) for k, peer in enumerate(far + [mate])
    ]
    along = [
        send(exp_own, exp_all.at[w // 2], (s_e, r_e), k, peer) for k, peer in enumerate(far)
    ]
    for copy in come:
        copy.wait()
    own = [
        pltpu.make_async_copy(exp_buf, exp_all.at[w // 2], local_sem.at[2]),
        pltpu.make_async_copy(
            tok_buf, tok_all.at[pl.ds(pl.multiple_of(s * rows, rows), rows)], local_sem.at[0]
        ),
        pltpu.make_async_copy(cols_buf, cols_all.at[w], local_sem.at[1]),
    ]
    for copy in own:
        copy.start()
    passed = []
    for j in range(1, n // 2):
        origin = lax.rem(w + n - 2 * j, n)
        held[j - 1].wait_recv()
        passed.append(send(cols_all.at[origin], cols_all.at[origin], (s_f, r_f), j - 1, mate))
    x0.wait_recv()
    there = tok_all.at[part(flip(s, 1), 0)]
    passed.append(send(there, there, tok, 4, by_y))
    y1.wait_recv()
    there = tok_all.at[part(flip(s, 2), 1)]
    passed.append(send(there, there, tok, 5, by_x))
    for copy in own:
        copy.wait()
    for copy in [x1, y0, held[-1]] + passed + along:
        copy.wait_recv()
    for copy in [x0, x1, y0, y1] + held + passed + along:
        copy.wait_send()


def gather_in(n, tokens, attention_weight, expand_weight):
    rows, d = tokens.shape
    own, width = attention_weight.shape
    quarter = expand_weight.shape[1] // 4
    return pl.pallas_call(
        functools.partial(gather_kernel, n),
        out_shape=(
            jax.ShapeDtypeStruct((4 * rows, d), bf16),
            jax.ShapeDtypeStruct((n, own, width // 4), bf16),
            jax.ShapeDtypeStruct((n // 2, own, quarter), bf16),
        ),
        in_specs=[ANYWHERE, IN_VMEM, ANYWHERE],
        out_specs=(ANYWHERE,) * 3,
        scratch_shapes=[
            pltpu.VMEM(tokens.shape, bf16),
            pltpu.VMEM((own, width // 4), bf16),
            pltpu.VMEM((own, quarter), bf16),
            pltpu.SemaphoreType.DMA((3,)),
        ]
        + dma_sems(6)
        + dma_sems(n // 2)
        + dma_sems(n // 2 - 1)
        + dma_sems(n // 2 - 1),
        compiler_params=remote_params(0),
        name="gather_in",
    )(tokens, attention_weight, expand_weight)


def final_kernel(
    heads, n, base_hbm, pieces_hbm, w_hbm, con_ref, out_ref, att_ref, exp_ref, vec_ref, late_ref,
    tok_o, g_con, g_out, g_exp, g_att, r_vec2, r_late2,
    base_v, pieces_v, w_v, r_con, h_att, m_att, r_att, r_vec, r_late,
    l_in, *sems,
):
    s, w = lax.axis_index("seq"), lax.axis_index("wt")
    z, c = w // 2, lax.rem(w, 2)
    nz = n // 2
    others = [flip(s, k) for k in (1, 2, 3)]
    seq_peers = [(p, w) for p in others]
    mate = (s, flip(w, 1))
    wt_peers = [(s, lax.rem(w + j, n)) for j in range(1, n)]
    names = ("pair", "vec", "late", "con", "out2", "att", "vec2", "late2", "con2", "exp2", "att2")
    sem = {name: (sems[2 * k], sems[2 * k + 1]) for k, name in enumerate(names)}
    loads = [
        pltpu.make_async_copy(src, dst, l_in.at[k])
        for k, (src, dst) in enumerate(((pieces_hbm, pieces_v), (w_hbm, w_v), (base_hbm, base_v)))
    ]
    for copy in loads:
        copy.start()
    meet(seq_peers + wt_peers)
    pair = [send(att_ref.at[2 * k + 1 - c], h_att.at[k], sem["pair"], k, mate) for k in range(nz)]
    cons = [send(con_ref.at[p], r_con.at[s], sem["con"], k, (p, w)) for k, p in enumerate(others)]
    far = [lax.rem(z + j, nz) for j in range(1, nz)]
    exp2 = [send(exp_ref, g_exp.at[s], sem["exp2"], k, p) for k, p in enumerate(seq_peers)]
    out2 = [send(out_ref, g_out.at[s], sem["out2"], k, p) for k, p in enumerate(seq_peers)]
    vecs = [
        send(vec_ref.at[lax.rem(w + j, n)], r_vec.at[w], sem["vec"], j - 1, wt_peers[j - 1])
        for j in range(1, n)
    ]
    lates = [send(late_ref, r_late.at[w], sem["late"], j, p) for j, p in enumerate(wt_peers)]
    r_con[s] = con_ref[s]
    g_exp[s] = exp_ref[...]
    r_vec[w] = vec_ref[w]
    r_late[w] = late_ref[...]
    g_out[s] = out_ref[...]
    for copy in pair:
        copy.wait_recv()
    for k in range(nz):
        m_att[k] = (att_ref[2 * k + c].astype(f32) + h_att[k].astype(f32)).astype(bf16)
    atts = [send(m_att.at[k], r_att.at[z], sem["att"], j, (s, 2 * k + c)) for j, k in enumerate(far)]
    r_att[z] = m_att[z]
    for copy in loads:
        copy.wait()
    cols = 3 * HD
    rows = tok_o.shape[0]
    block = rows // 3

    def total_of(ref, count):
        total = ref[0].astype(f32)
        for k in range(1, count):
            total = total + ref[k].astype(f32)
        return total

    own = [ref.at[s] for ref in (g_con, r_vec2, r_late2, g_att)]
    con2, vec2, late2, att2 = (
        [remote(ref, ref, sem[name], k, p) for k, p in enumerate(seq_peers)]
        for ref, name in zip(own, ("con2", "vec2", "late2", "att2"), strict=True)
    )

    def tokens_block(i, carry):
        there = pl.ds(pl.multiple_of(i * block, block), block)
        total = base_v[there, :]
        for h in range(heads):
            for k in range(4):
                at = (heads * k + h) * cols
                total = total + mm(pieces_v[h, k, :, there].T, w_v[:, at : at + cols], NT)
        tok_o[there, :] = total

        @pl.when(i == 0)
        def _():
            for copy in cons:
                copy.wait_recv()
            g_con[s] = total_of(r_con, 4).astype(bf16)
            for copy in con2:
                copy.start()
            for copy in vecs + lates:
                copy.wait_recv()
            r_vec2[s] = total_of(r_vec, n)
            r_late2[s] = total_of(r_late, n)
            for copy in vec2 + late2:
                copy.start()

        @pl.when(i == 1)
        def _():
            for copy in atts:
                copy.wait_recv()
            g_att[s] = total_of(r_att, nz).astype(bf16)
            for copy in att2:
                copy.start()

        return carry

    lax.fori_loop(0, 3, tokens_block, 0)
    for copy in out2 + con2 + vec2 + late2 + exp2 + att2:
        copy.wait_recv()
    for copy in pair + cons + vecs + lates + atts + con2 + vec2 + late2 + exp2 + out2 + att2:
        copy.wait_send()


def final(n, base, pieces, weight, con, out, att, exp_part, vec, late):
    heads = pieces.shape[0]
    r, d = con.shape[1:]
    cols = att.shape[2]
    nz = n // 2
    counts = (nz, n - 1, n - 1, 3, 3, nz - 1, 3, 3, 3, 3, 3)
    return pl.pallas_call(
        functools.partial(final_kernel, heads, n),
        out_shape=(
            jax.ShapeDtypeStruct(base.shape, f32),
            jax.ShapeDtypeStruct((4, r, d), bf16),
            jax.ShapeDtypeStruct((4,) + out.shape, bf16),
            jax.ShapeDtypeStruct((4,) + exp_part.shape, bf16),
            jax.ShapeDtypeStruct((4, r, cols), bf16),
            jax.ShapeDtypeStruct((4,) + vec.shape[1:], f32),
            jax.ShapeDtypeStruct((4,) + late.shape, f32),
        ),
        in_specs=[ANYWHERE] * 3 + [IN_VMEM] * 6,
        out_specs=(IN_VMEM,) * 7,
        scratch_shapes=[
            pltpu.VMEM(base.shape, f32),
            pltpu.VMEM(pieces.shape, bf16),
            pltpu.VMEM(weight.shape, bf16),
            pltpu.VMEM((4, r, d), bf16),
            pltpu.VMEM((nz, r, cols), bf16),
            pltpu.VMEM((nz, r, cols), bf16),
            pltpu.VMEM((nz, r, cols), bf16),
            pltpu.VMEM((n,) + vec.shape[1:], f32),
            pltpu.VMEM((n,) + late.shape, f32),
            pltpu.SemaphoreType.DMA((3,)),
        ]
        + [sem for count in counts for sem in dma_sems(count)],
        compiler_params=remote_params(3),
        cost_estimate=pl.CostEstimate(
            flops=8 * base.shape[0] * d * cols, bytes_accessed=8 * d * cols, transcendentals=0
        ),
        name="final",
    )(base, pieces, weight, con, out, att, exp_part, vec, late)


def finish_kernel(n, heads, gate_ref, mask_ref, *refs):
    sources, rest = refs[:8], refs[8:]
    con_o, exp_o, att_o, tok_o, low_o, out_o = rest[:6]
    vec_os, unit_os, query_o, value_o, gate_o = rest[6:13], rest[13:15], rest[15], rest[16], rest[17]
    con_v, exp_v, att_v, tok_v, low_v, out_v, vec_v, late_v, con_f, exp_f, att_f, l_in, l_out = rest[18:]
    inside = (con_v, exp_v, att_v, tok_v, low_v, out_v, vec_v, late_v)
    loads = [
        pltpu.make_async_copy(src, dst, l_in.at[k])
        for k, (src, dst) in enumerate(zip(sources, inside, strict=True))
    ]
    for copy in loads:
        copy.start()
    outside = ((con_f, con_o), (exp_f, exp_o), (att_f, att_o), (tok_v, tok_o), (low_v, low_o))
    stores = [pltpu.make_async_copy(src, dst, l_out.at[k]) for k, (src, dst) in enumerate(outside)]

    def add4(parts):
        return (parts[0] + parts[1]) + (parts[2] + parts[3])

    wide, cols, part = exp_v.shape[2], att_v.shape[2], out_v.shape[2]
    loads[0].wait()
    con_f[...] = con_v[...].astype(f32)
    stores[0].start()
    loads[1].wait()
    for k in range(4):
        exp_f[:, k * wide : (k + 1) * wide] = exp_v[k].astype(f32)
    stores[1].start()
    loads[2].wait()
    for k in range(4):
        att_f[:, k * cols : (k + 1) * cols] = att_v[k].astype(f32)
    stores[2].start()
    for k in (3, 4):
        loads[k].wait()
        stores[k].start()
    for copy in loads[5:]:
        copy.wait()
    for k in range(4):
        out_o[:, k * part : (k + 1) * part] = out_v[k].astype(f32)
    vec = add4([vec_v[k] for k in range(4)])
    own = vec_os[0].shape[0]
    for k, ref in enumerate(vec_os):
        ref[...] = vec[k, 0:own]
    for k, ref in enumerate(unit_os):
        ref[...] = vec[8 + k]
    rows = [jnp.concatenate([late_v[k, j : j + 1, :] for k in range(4)], axis=1) for j in range(2)]
    for k in range(n):

        @pl.when(lax.axis_index("wt") == k)
        def _(k=k):
            query_o[...] = rows[0][0, k * own : (k + 1) * own]
            value_o[...] = rows[1][0, k * own : (k + 1) * own]

    gates = []
    for k in range(4):
        for h in range(heads):
            part_sum = jnp.sum(late_v[k, 2:3, HD * h : HD * (h + 1)], axis=1, keepdims=True)
            kept = mask_ref[heads * k + h].astype(f32) / gate_ref[heads * k + h]
            gates.append(part_sum * kept)
    gate_o[...] = jnp.concatenate(gates, axis=1)[0]
    for copy in stores:
        copy.wait()


def finish(n, heads, gate, mask, con, exp_all, att, tok, low, out, vec, late):
    r = out.shape[1]
    wide, cols, part = exp_all.shape[2], att.shape[2], out.shape[2]
    units = vec.shape[2]
    row = jax.ShapeDtypeStruct((r,), f32)
    con_f, exp_f, att_f = (
        con.shape,
        (r, 4 * wide),
        (r, 4 * cols),
    )
    return pl.pallas_call(
        functools.partial(finish_kernel, n, heads),
        out_shape=(
            jax.ShapeDtypeStruct(con_f, f32),
            jax.ShapeDtypeStruct(exp_f, f32),
            jax.ShapeDtypeStruct(att_f, f32),
            jax.ShapeDtypeStruct(tok.shape, f32),
            jax.ShapeDtypeStruct(low.shape, low.dtype),
            jax.ShapeDtypeStruct((r, 4 * part), f32),
        )
        + (row,) * 7
        + (jax.ShapeDtypeStruct((units,), f32),) * 2
        + (row,) * 2
        + (jax.ShapeDtypeStruct((4 * heads,), f32),),
        in_specs=[IN_SMEM] * 2 + [ANYWHERE] * 8,
        out_specs=(ANYWHERE,) * 5 + (IN_VMEM,) * 13,
        scratch_shapes=[
            pltpu.VMEM(x.shape, x.dtype) for x in (con, exp_all, att, tok, low, out, vec, late)
        ]
        + [pltpu.VMEM(x, f32) for x in (con_f, exp_f, att_f)]
        + [pltpu.SemaphoreType.DMA((8,)), pltpu.SemaphoreType.DMA((5,))],
        compiler_params=pltpu.CompilerParams(vmem_limit_bytes=56 * 2**20),
        name="finish",
    )(gate, mask, con, exp_all, att, tok, low, out, vec, late)


(OUT_BIAS, GAIN1, SHIFT1, HIDDEN_SCALE, CON_BIAS, GAIN2, SHIFT2, HIDDEN_MASK) = range(8)
(S_OUT_BIAS, S_GAIN1, S_SHIFT1, S_CON_BIAS, S_GAIN2, S_SHIFT2, S_HIDDEN) = range(7)


def gelu_parts(x):
    bell = jnp.exp(-0.5 * (x * x))
    t = 1.0 / (1.0 + (0.3275911 * root_half) * jnp.abs(x))
    poly = t * (
        0.127414796 + t * (-0.142248368 + t * (0.7107068705 + t * (-0.7265760135 + t * 0.5307027145)))
    )
    tail = poly * bell
    cumulative = jnp.where(x < 0.0, tail, 1.0 - tail)
    return x * cumulative, cumulative + x * bell * density_scale


def norm_parts(summed):
    centre = summed - jnp.mean(summed, axis=-1, keepdims=True)
    inverse = lax.rsqrt(jnp.mean(centre * centre, axis=-1, keepdims=True) + epsilon)
    return (centre * inverse, inverse)


def norm_back(grad_normed, normed, inverse):
    return inverse * (
        grad_normed
        - jnp.mean(grad_normed, axis=-1, keepdims=True)
        - normed * jnp.mean(grad_normed * normed, axis=-1, keepdims=True)
    )


def feed_forward_kernel(
    steps, chunk,
    kept_ref, ctx_ref, tok_ref, cot_ref, wo_ref, we_hbm, wc_hbm,
    ob_ref, g1_ref, t1_ref, hg_ref, hm_ref, cb_ref, g2_ref, t2_ref, eb_ref, ug_ref, um_ref,
    lo_ref, dt1_ref, g_all, vec_ref, dwc_hbm, e_own, e_got, o_own, o_got,
    we_ref, wc_ref, dwc_ref, dwe_ref, dwo_ref, g_sc,
    wide_ref, unit_ref, sw_ref, su_ref, act_sc, gh_sc, low_sc, gb_sc, ga_sc, ctx_sc, gelu_sc, slope_sc,
    l_w, l_o, l_g, s_g, r_g, s_p, r_p,
):
    i = pl.program_id(0)
    block = tok_ref.shape[0]
    units = we_ref.shape[1]
    rows = pl.ds(pl.multiple_of(i * block, block), block)
    s, w = lax.axis_index("seq"), lax.axis_index("wt")
    others = [flip(s, k) for k in (1, 2, 3)]
    mate, core = (s, flip(w, 1)), lax.rem(w, 2)
    part_rows = g_all.shape[0]
    weights = [
        pltpu.make_async_copy(we_hbm, we_ref, l_w.at[0]),
        pltpu.make_async_copy(wc_hbm, wc_ref, l_w.at[1]),
    ]

    def leaving(t):
        there = g_all.at[:, pl.ds(pl.multiple_of((s * steps + t) * block, 128), block)]

        def part(p):
            lanes = pl.ds(pl.multiple_of(t * block, 128), block)
            return g_sc.at[pl.ds(pl.multiple_of(p * part_rows, 16), part_rows), lanes]

        copies = [
            remote(part(p), there, (s_g, r_g), 3 * t + k, (p, w)) for k, p in enumerate(others)
        ]
        return copies + [pltpu.make_async_copy(part(s), there, l_g.at[t])]

    @pl.when(i == 0)
    def _():
        for copy in weights:
            copy.start()
        meet([(p, w) for p in others] + [mate])
        sw_ref[...] = jnp.zeros_like(sw_ref)
        su_ref[...] = jnp.zeros_like(su_ref)

        def row(ref):
            return ref[...].astype(f32).reshape(1, ref.shape[0])

        plain = ((OUT_BIAS, ob_ref), (GAIN1, g1_ref), (SHIFT1, t1_ref), (CON_BIAS, cb_ref))
        for k, ref in plain + ((GAIN2, g2_ref), (SHIFT2, t2_ref), (HIDDEN_MASK, hm_ref)):
            wide_ref[k : k + 1, :] = row(ref)
        wide_ref[HIDDEN_SCALE : HIDDEN_SCALE + 1, :] = row(hm_ref) * row(hg_ref)
        kept = row(um_ref) * kept_ref[lax.axis_index("wt")].astype(f32)
        unit_ref[0:1, :] = row(eb_ref)
        unit_ref[1:2, :] = kept * row(ug_ref)
        unit_ref[2:3, :] = kept

    def wide(k):
        return wide_ref[k : k + 1, :]

    def add_sum(ref, k, cols, value):
        ref[k : k + 1, cols] += jnp.sum(value, axis=0, keepdims=True)

    full = slice(None)
    ctx = ctx_ref[...]
    ctx_sc[:, rows] = ctx
    summed = mm(ctx, wo_ref[...], TN) + wide(OUT_BIAS) + tok_ref[...].astype(f32)
    n1, inv1 = norm_parts(summed)
    s1 = n1 * wide(GAIN1) + wide(SHIFT1)
    hs = wide(HIDDEN_SCALE)
    first = s1 * hs
    low = first.astype(bf16)
    low_sc[rows, :] = low
    branch = first + wide(CON_BIAS)

    @pl.when(i == 0)
    def _():
        for copy in weights:
            copy.wait()

    for j in range(units // chunk):
        cols = slice(j * chunk, (j + 1) * chunk)
        hidden = mm(low, we_ref[:, cols]) + unit_ref[0:1, cols]
        gelu, slope = gelu_parts(hidden)
        scale = unit_ref[1:2, cols]
        gelu_sc[:, cols] = gelu.astype(gelu_sc.dtype)
        slope_sc[:, cols] = (slope * scale).astype(slope_sc.dtype)
        act = (gelu * scale).astype(bf16)
        act_sc[rows, cols] = act
        branch = branch + mm(act, wc_ref[cols, :])
    n2, inv2 = norm_parts(branch)
    s2 = n2 * wide(GAIN2) + wide(SHIFT2)
    lo_ref[...] = (s2 * hs).astype(bf16)
    dy = cot_ref[...].astype(f32)
    e2 = dy * hs
    add_sum(sw_ref, S_GAIN2, full, e2 * n2)
    add_sum(sw_ref, S_SHIFT2, full, e2)
    dt2 = norm_back(e2 * wide(GAIN2), n2, inv2)
    gb = dt2.astype(bf16)
    gb_sc[rows, :] = gb
    add_sum(sw_ref, S_CON_BIAS, full, gb.astype(f32))
    d_first = dt2
    for j in range(units // chunk):
        cols = slice(j * chunk, (j + 1) * chunk)
        d_act = mm(gb, wc_ref[cols, :], NT)
        add_sum(su_ref, 1, cols, d_act * gelu_sc[:, cols].astype(f32))
        gh = d_act * slope_sc[:, cols].astype(f32)
        add_sum(su_ref, 0, cols, gh)
        gh = gh.astype(bf16)
        gh_sc[rows, cols] = gh
        d_first = d_first + mm(gh, we_ref[:, cols], NT)
    e1 = d_first * hs
    add_sum(sw_ref, S_GAIN1, full, e1 * n1)
    add_sum(sw_ref, S_SHIFT1, full, e1)
    add_sum(sw_ref, S_HIDDEN, full, dy * s2 + d_first * s1)
    dt1 = norm_back(e1 * wide(GAIN1), n1, inv1)
    dt1_ref[...] = dt1
    ga = dt1.astype(bf16)
    ga_sc[rows, :] = ga
    add_sum(sw_ref, S_OUT_BIAS, full, ga.astype(f32))
    g_sc[:, rows] = mm(wo_ref[...], ga, NT).astype(bf16)
    for copy in leaving(i):
        copy.start()

    @pl.when(i == steps - 1)
    def _():
        own, wide_cols = dwe_ref.shape[3:]

        def weight_grads(j, carry):
            cols = pl.ds(pl.multiple_of(j * wide_cols, 128), wide_cols)
            dwc_ref[cols, :] = mm(act_sc[:, cols], gb_sc[...], TN).astype(bf16)
            part = mm(low_sc[...], gh_sc[:, cols], TN).astype(bf16)
            for k in range(2 * dwe_ref.shape[2]):
                dwe_ref[k % 2, j, k // 2] = part[k * own : (k + 1) * own]
            for copy in given(j):
                copy.start()
            return carry

        def given(j):
            there = pl.ds(pl.multiple_of(j * wide_cols, 128), wide_cols)
            return [
                pltpu.make_async_copy(dwc_ref.at[there], dwc_hbm.at[there], l_o.at[j]),
                pltpu.make_async_copy(dwe_ref.at[core, j], e_own.at[j], l_o.at[4 + j]),
                remote(dwe_ref.at[1 - core, j], e_got.at[j], (s_p, r_p), j, mate),
            ]

        part_cols = dwo_ref.shape[4]
        for q in range(4):
            part = mm(ctx_sc[...], ga_sc[:, q * part_cols : (q + 1) * part_cols]).astype(bf16)
            for k in range(2 * dwo_ref.shape[2]):
                dwo_ref[k % 2, q, k // 2] = part[k * own : (k + 1) * own]
        over = [
            pltpu.make_async_copy(dwo_ref.at[core], o_own, l_o.at[8]),
            remote(dwo_ref.at[1 - core], o_got, (s_p, r_p), 4, mate),
        ]
        for copy in over:
            copy.start()
        lax.fori_loop(0, 4, weight_grads, 0)
        vec_ref[...] = jnp.zeros_like(vec_ref)
        sw_ref[S_HIDDEN : S_HIDDEN + 1, :] *= wide(HIDDEN_MASK)
        su_ref[1:2, :] *= unit_ref[2:3, :]
        own_wide, own_units = dwe_ref.shape[3], vec_ref.shape[2]
        for k in range(vec_ref.shape[0]):
            vec_ref[k, 0:8, 0:own_wide] = sw_ref[:, k * own_wide : (k + 1) * own_wide]
            vec_ref[k, 8:16, :] = su_ref[:, k * own_units : (k + 1) * own_units]
        for t in range(steps):
            for copy in leaving(t):
                copy.wait()
        for copy in over:
            copy.wait()
        for j in range(4):
            for copy in given(j):
                copy.wait()


def feed_forward(n, kept, ctx_t, tokens, cotangent, wo, we, wc, *vectors):
    steps, chunk, keep = 3, 768, f32
    rows, d = tokens.shape
    units = we.shape[1]
    block = rows // steps
    halves = (2, 4, n // 2, d // n, units // 4)
    out_halves = (2, 4, n // 2, d // n, d // 4)
    tile = pl.BlockSpec((block, d), lambda i: (i, 0))
    lanes = pl.BlockSpec((d, block), lambda i: (0, i))

    def once(shape):
        return pl.BlockSpec(shape, lambda i: (0, 0), pipeline_mode=pl.Buffered(1))

    def once3(shape):
        return pl.BlockSpec(shape, lambda i: (0, 0, 0), pipeline_mode=pl.Buffered(1))

    return pl.pallas_call(
        functools.partial(feed_forward_kernel, steps, chunk),
        out_shape=(
            jax.ShapeDtypeStruct((rows, d), bf16),
            jax.ShapeDtypeStruct((rows, d), f32),
            jax.ShapeDtypeStruct((d // 4, 4 * rows), bf16),
            jax.ShapeDtypeStruct((n, 16, units // n), f32),
            jax.ShapeDtypeStruct((units, d), bf16),
            jax.ShapeDtypeStruct(halves[1:], bf16),
            jax.ShapeDtypeStruct(halves[1:], bf16),
            jax.ShapeDtypeStruct(out_halves[1:], bf16),
            jax.ShapeDtypeStruct(out_halves[1:], bf16),
        ),
        grid=(steps,),
        in_specs=[
            pl.BlockSpec(memory_space=pltpu.SMEM),
            lanes, tile, tile, once((d, d)), ANYWHERE, ANYWHERE,
        ]
        + [IN_VMEM] * len(vectors),
        out_specs=(
            tile, tile, ANYWHERE, once3((n, 16, units // n)), ANYWHERE,
            ANYWHERE, ANYWHERE, ANYWHERE, ANYWHERE,
        ),
        scratch_shapes=[
            pltpu.VMEM((d, units), bf16),
            pltpu.VMEM((units, d), bf16),
            pltpu.VMEM((units, d), bf16),
            pltpu.VMEM(halves, bf16),
            pltpu.VMEM(out_halves, bf16),
            pltpu.VMEM((d, rows), bf16),
            pltpu.VMEM((8, d), f32),
            pltpu.VMEM((8, units), f32),
            pltpu.VMEM((8, d), f32),
            pltpu.VMEM((8, units), f32),
            pltpu.VMEM((rows, units), bf16),
            pltpu.VMEM((rows, units), bf16),
            pltpu.VMEM((rows, d), bf16),
            pltpu.VMEM((rows, d), bf16),
            pltpu.VMEM((rows, d), bf16),
            pltpu.VMEM((d, rows), bf16),
            pltpu.VMEM((block, units), keep),
            pltpu.VMEM((block, units), keep),
            pltpu.SemaphoreType.DMA((2,)),
            pltpu.SemaphoreType.DMA((9,)),
            pltpu.SemaphoreType.DMA((steps,)),
        ]
        + dma_sems(3 * steps)
        + dma_sems(5),
        compiler_params=pltpu.CompilerParams(
            collective_id=4, has_side_effects=True, vmem_limit_bytes=62 * 2**20
        ),
        cost_estimate=pl.CostEstimate(
            flops=rows * d * (12 * units + 6 * d),
            bytes_accessed=4 * d * (4 * units + 2 * d) + 12 * rows * d,
            transcendentals=2 * rows * units,
        ),
        name="feed_forward",
    )(kept, ctx_t, tokens, cotangent, wo, we, wc, *vectors)


def local(
    tokens,
    output_cotangent,
    attention_weight,
    query_bias,
    value_bias,
    output_weight,
    output_bias,
    first_gain,
    first_shift,
    expand_weight,
    expand_bias,
    contract_weight,
    contract_bias,
    second_gain,
    second_shift,
    head_gate,
    hidden_gate,
    unit_gate,
    head_mask,
    hidden_mask,
    unit_mask,
    attention_mask,
    feedforward_mask,
    continuation_lengths,
):
    seq_count = lax.axis_size("seq")
    wt_count = lax.axis_size("wt")
    model_width = hidden_gate.shape[0]
    local_heads = head_gate.shape[0] // seq_count
    own_wide = model_width // wt_count
    tokens_all, own_weight, exp_quarter = gather_in(wt_count, tokens, attention_weight, expand_weight)
    contract_weight, own_weight = lax.optimization_barrier((contract_weight, own_weight))
    full_contract = lax.all_gather(contract_weight, "wt", axis=0, tiled=True)
    full_attention = lax.all_gather(attention_weight, "wt", axis=0, tiled=True)
    full_output = lax.all_gather(output_weight, "wt", axis=0, tiled=True)
    q, k, v, kt, own_context, log_sums, context_t, full_expand = attend(
        wt_count,
        continuation_lengths,
        attention_mask,
        head_gate,
        head_mask,
        query_bias,
        value_bias,
        tokens_all,
        own_weight.reshape(model_width, -1),
        exp_quarter,
        local_heads,
    )
    (
        layer_output,
        grad_total_one,
        grad_context_t,
        vec_sums,
        contract_weight_grad,
        *parts,
    ) = feed_forward(
        wt_count,
        feedforward_mask,
        context_t,
        tokens,
        output_cotangent,
        full_output,
        full_expand.reshape(model_width, -1),
        full_contract,
        output_bias,
        first_gain,
        first_shift,
        hidden_gate,
        hidden_mask,
        contract_bias,
        second_gain,
        second_shift,
        expand_bias,
        unit_gate,
        unit_mask,
    )
    con_piece = lax.psum_scatter(contract_weight_grad, "wt", scatter_dimension=0, tiled=True)
    pieces, projection_grad, exp_part, out_part, late_sums = attend_back(
        wt_count,
        continuation_lengths,
        attention_mask,
        head_gate,
        head_mask,
        q,
        k,
        v,
        kt,
        own_context,
        grad_context_t,
        log_sums,
        tokens_all,
        *parts,
    )
    tokens_grad, con_all, out_all, exp_all, att_all, vec_all, late_all = final(
        wt_count,
        grad_total_one,
        pieces,
        full_attention,
        con_piece.reshape(seq_count, own_wide, model_width),
        out_part,
        projection_grad,
        exp_part,
        vec_sums,
        late_sums,
    )
    con_sum, exp_sum, att_sum, tokens_grad, layer_output, out_sum, *rows = finish(
        wt_count,
        local_heads,
        head_gate,
        head_mask,
        con_all,
        exp_all,
        att_all,
        tokens_grad,
        layer_output,
        out_all,
        vec_all,
        late_all,
    )
    return (
        layer_output,
        tokens_grad,
        att_sum,
        rows[9],
        rows[10],
        out_sum,
        rows[S_OUT_BIAS],
        rows[S_GAIN1],
        rows[S_SHIFT1],
        exp_sum,
        rows[7],
        con_sum.reshape(seq_count * own_wide, model_width),
        rows[S_CON_BIAS],
        rows[S_GAIN2],
        rows[S_SHIFT2],
        rows[11],
        rows[S_HIDDEN],
        rows[8],
    )


def solution(mesh):
    return jax.shard_map(
        local,
        mesh=mesh,
        in_specs=(
            P(("wt", "seq"), None),
            P(("wt", "seq"), None),
            P("wt", None),
            P(),
            P(),
            P("wt", None),
            P(),
            P(),
            P(),
            P("wt", None),
            P(),
            P("wt", None),
            P(),
            P(),
            P(),
            P(),
            P(),
            P(),
            P(),
            P(),
            P(),
            P(),
            P(),
            P(),
        ),
        out_specs=(
            P(("wt", "seq"), None),
            P(("wt", "seq"), None),
            P("wt", None),
            P("wt"),
            P("wt"),
            P("wt", None),
            P("wt"),
            P("wt"),
            P("wt"),
            P("wt", None),
            P("wt"),
            P("wt", None),
            P("wt"),
            P("wt"),
            P("wt"),
            P(),
            P("wt"),
            P("wt"),
        ),
        check_vma=False,
    )
```

```python
import functools

import jax
import jax.numpy as jnp
from jax import lax
from jax.experimental import pallas as pl
from jax.experimental.pallas import tpu as pltpu
from jax.sharding import PartitionSpec as P

PROMPT = 1024
GRP_WT = 1
GLEN = 3072
SHORT = 512
LONG = 1536
HD = 64
TQ = 512
KC = 512

epsilon = 1e-06
score_scale = 0.125
exp2_scale = 0.125 * 1.4426950408889634
root_half = 0.7071067811865476
density_scale = 0.3989422804014327
bf16 = jnp.bfloat16
f32 = jnp.float32

NT = (((1,), (1,)), ((), ()))
NN = (((1,), (0,)), ((), ()))
TN = (((0,), (0,)), ((), ()))


def mm(a, b, dims=NN):
    return lax.dot_general(a, b, dims, preferred_element_type=f32)


def natural_at(short_first, i):
    other = jnp.where(i == 2, 5, i - 1)
    return jnp.where(short_first | (i < 2), i, other)


def ordered_at(short_first, j):
    other = jnp.where(j == 5, 2, j + 1)
    return jnp.where(short_first | (j < 2), j, other)


def query_tiles(tile):
    def prompt(i, carry):
        tile(i, ())
        return carry

    def longer(i, carry):
        tile(i, (3, 4, 5))
        return carry

    lax.fori_loop(0, 2, prompt, 0)
    tile(2, (2,))
    lax.fori_loop(3, 6, longer, 0)


def remote(src, dst, sems, k, peer):
    return pltpu.make_async_remote_copy(
        src_ref=src,
        dst_ref=dst,
        send_sem=sems[0].at[k],
        recv_sem=sems[1].at[k],
        device_id=peer,
        device_id_type=pl.DeviceIdType.MESH,
    )


def send(src, dst, sems, k, peer):
    copy = remote(src, dst, sems, k, peer)
    copy.start()
    return copy


def value_scale(head, group, kept_ref, gate_ref, mask_ref):
    return mask_ref[head].astype(f32) * gate_ref[head] * kept_ref[group].astype(f32)


def attend_kernel(
    heads, n, lens_ref, kept_ref, gate_ref, mask_ref, qb_ref, vb_ref, tok_hbm, w_hbm, exp_ref,
    q_sc, k_sc, v_ref, kt_ref, ctx_ref, lse_ref, full_ref, exp_all,
    tok_ref, w_ref, vt_sc, ct_sc, vec_ref, exp_buf,
    local_sem, s_sem, r_sem, s_e, r_e,
):
    s, w = lax.axis_index("seq"), lax.axis_index("wt")
    others = [flip(s, k) for k in (1, 2, 3)]
    mate = (s, flip(w, 1))
    short_first = lens_ref[w, 0] == SHORT
    operands = [
        pltpu.make_async_copy(tok_hbm, tok_ref, local_sem.at[heads + 1]),
        pltpu.make_async_copy(w_hbm, w_ref, local_sem.at[heads + 2]),
    ]
    come = pltpu.make_async_copy(exp_ref, exp_buf, local_sem.at[heads])
    for copy in operands + [come]:
        copy.start()
    meet([(p, w) for p in others] + [mate])
    core, quarter = lax.rem(w, 2), exp_ref.shape[2]

    def exp_place(p):
        return exp_all.at[:, core, :, pl.ds(pl.multiple_of(p * quarter, 128), quarter)]

    spread = [
        send(exp_ref, exp_place(s), (s_e, r_e), k, (p, w)) for k, p in enumerate(others)
    ] + [send(exp_ref, exp_place(s), (s_e, r_e), 3, mate)]
    width = heads * HD
    count = GLEN // 4
    vec_ref[...] = jnp.zeros_like(vec_ref)
    for k in range(4):

        @pl.when(s == k)
        def _(k=k):
            query = qb_ref[...].astype(f32).reshape(1, 4 * width)
            value = vb_ref[...].astype(f32).reshape(1, 4 * width)
            for h in range(heads):
                own = slice(k * width + h * HD, k * width + (h + 1) * HD)
                at = 3 * HD * h
                vec_ref[0:1, at : at + HD] = query[:, own]
                vec_ref[0:1, at + 2 * HD : at + 3 * HD] = value[:, own]

    for h in range(heads):
        at = 3 * HD * h
        vec_ref[1:2, at : at + 2 * HD] = jnp.ones((1, 2 * HD), f32)
        scale = value_scale(s * heads + h, w, kept_ref, gate_ref, mask_ref)
        vec_ref[1:2, at + 2 * HD : at + 3 * HD] = jnp.full((1, HD), scale, f32)
    come.wait()
    own_part = pltpu.make_async_copy(exp_buf, exp_place(s), local_sem.at[heads])
    own_part.start()
    for copy in operands:
        copy.wait()

    def project(i, carry):
        rows = pl.ds(pl.multiple_of(i * TQ, TQ), TQ)
        x = mm(tok_ref[natural_at(short_first, i)], w_ref[...]) + vec_ref[0:1, :]
        x = (x * vec_ref[1:2, :]).astype(bf16)
        for h in range(heads):
            at = 3 * HD * h
            q_sc[h, rows, :] = x[:, at : at + HD]
            k = x[:, at + HD : at + 2 * HD]
            k_sc[h, rows, :] = k
            kt_ref[h, i] = k.T
            v = x[:, at + 2 * HD : at + 3 * HD]
            v_ref[h, rows, :] = v
            vt_sc[h, :, rows] = v.T
        return carry

    lax.fori_loop(0, GLEN // TQ, project, 0)

    def leaving(h):
        rows = pl.ds(pl.multiple_of(h * HD, HD), HD)
        there = full_ref.at[pl.ds(pl.multiple_of(s * width + h * HD, HD), HD), :]

        def part(p):
            return ctx_ref.at[rows, pl.ds(pl.multiple_of(p * count, 128), count)]

        copies = [
            remote(part(p), there, (s_sem, r_sem), 3 * h + k, (p, w)) for k, p in enumerate(others)
        ]
        return copies, pltpu.make_async_copy(part(s), there, local_sem.at[h])

    passed = [
        (spread[k], remote(exp_place(p), exp_place(p), (s_e, r_e), 4 + k, mate))
        for k, p in enumerate(others)
    ]

    def one_head(h, carry):
        @pl.when(h == heads - 1)
        def _():
            for came, copy in passed:
                came.wait_recv()
                copy.start()

        def tile(i, own_blocks):
            rows = pl.ds(pl.multiple_of(i * TQ, TQ), TQ)
            q = q_sc[h, rows, :]
            s1 = mm(k_sc[h, 0:PROMPT, :], q, NT)
            top = jnp.max(s1, axis=0, keepdims=True)
            if own_blocks:
                own = slice(own_blocks[0] * KC, (own_blocks[-1] + 1) * KC)
                s2 = mm(k_sc[h, own, :], q, NT)
                top = jnp.maximum(top, jnp.max(s2, axis=0, keepdims=True))
            top = top * exp2_scale
            p1 = jnp.exp2(s1 * exp2_scale - top)
            o = mm(vt_sc[h, :, 0:PROMPT], p1.astype(bf16))
            total = jnp.sum(p1, axis=0, keepdims=True)
            if own_blocks:
                p2 = jnp.exp2(s2 * exp2_scale - top)
                o = o + mm(vt_sc[h, :, own], p2.astype(bf16))
                total = total + jnp.sum(p2, axis=0, keepdims=True)
            ct_sc[i] = (o / total).astype(bf16)
            lse_ref[h, :, rows] = top + jnp.log2(total)

        query_tiles(tile)

        def settle(j, carry):
            rows = pl.ds(pl.multiple_of(h * HD, HD), HD)
            lanes = pl.ds(pl.multiple_of(j * SHORT, SHORT), SHORT)
            ctx_ref[rows, lanes] = ct_sc[ordered_at(short_first, j)]
            return carry

        lax.fori_loop(0, GLEN // SHORT, settle, 0)
        copies, own = leaving(h)
        for copy in copies:
            copy.start()
        own.start()
        return carry

    lax.fori_loop(0, heads, one_head, 0)
    own_part.wait()
    spread[3].wait_recv()
    for _, copy in passed:
        copy.wait()
    for copy in spread:
        copy.wait_send()
    for h in range(heads):
        copies, own = leaving(h)
        own.wait()
        for copy in copies:
            copy.wait()


def attend(n, lens, kept, gate, mask, query_bias, value_bias, tokens_all, weight, exp_part, heads):
    width = 3 * HD * heads
    return pl.pallas_call(
        functools.partial(attend_kernel, heads, n),
        out_shape=(
            jax.ShapeDtypeStruct((heads, GLEN, HD), bf16),
            jax.ShapeDtypeStruct((heads, GLEN, HD), bf16),
            jax.ShapeDtypeStruct((heads, GLEN, HD), bf16),
            jax.ShapeDtypeStruct((heads, GLEN // TQ, HD, TQ), bf16),
            jax.ShapeDtypeStruct((HD * heads, GLEN), bf16),
            jax.ShapeDtypeStruct((heads, 1, GLEN), f32),
            jax.ShapeDtypeStruct((4 * HD * heads, GLEN // 4), bf16),
            jax.ShapeDtypeStruct((n // 2, 2, exp_part.shape[1], 4 * exp_part.shape[2]), bf16),
        ),
        in_specs=[IN_SMEM] * 4 + [IN_VMEM] * 2 + [ANYWHERE] * 3,
        out_specs=(IN_VMEM,) * 6 + (ANYWHERE, ANYWHERE),
        scratch_shapes=[
            pltpu.VMEM((GLEN // TQ, TQ, tokens_all.shape[1]), bf16),
            pltpu.VMEM(weight.shape, bf16),
            pltpu.VMEM((heads, HD, GLEN), bf16),
            pltpu.VMEM((GLEN // TQ, HD, TQ), bf16),
            pltpu.VMEM((2, width), f32),
            pltpu.VMEM(exp_part.shape, bf16),
            pltpu.SemaphoreType.DMA((heads + 3,)),
        ]
        + dma_sems(3 * heads)
        + dma_sems(7),
        compiler_params=remote_params(1),
        cost_estimate=pl.CostEstimate(
            flops=2 * GLEN * 768 * width + heads * 4 * 256 * 5767168,
            bytes_accessed=2 * GLEN * (768 + width),
            transcendentals=heads * 5767168,
        ),
        name="attend",
    )(
        lens, kept, gate, mask, query_bias, value_bias,
        tokens_all.reshape(GLEN // TQ, TQ, -1), weight, exp_part,
    )


def attend_back_kernel(
    heads, n, lens_ref, kept_ref, gate_ref, mask_ref, q_hbm, k_hbm, v_hbm, kt_hbm,
    ctx_hbm, gctx_hbm, lse_hbm, tok_hbm,
    e_own_hbm, e_got_hbm, o_own_hbm, o_got_hbm, pieces_o, dw_o, exp_o, out_o, late_o,
    ctx_ref, gctx_ref, lse_ref, tok_v, e_own, o_own, e_got, o_got, e_all, o_all, e_sum, o_sum, e_z, o_z, stage, late_sc, row_sc,
    q_all, k_all, v_all, kt_all, g_sc, g_nat, delta_sc, delta_nat, dqt_sc, dk_sc, dv_sc, acc,
    l_in, l_out, s_p, r_p, s_e, r_e, s_z, r_z,
):
    s, w = lax.axis_index("seq"), lax.axis_index("wt")
    others = [flip(s, k) for k in (1, 2, 3)]
    z, c, nz = w // 2, lax.rem(w, 2), n // 2
    far = [lax.rem(z + j, nz) for j in range(1, nz)]
    short_first = lens_ref[w, 0] == SHORT
    count = GLEN // 4
    width = heads * HD
    def taken(h):
        pairs = ((q_hbm, q_all), (k_hbm, k_all), (v_hbm, v_all), (kt_hbm, kt_all))
        return [
            pltpu.make_async_copy(src.at[h], dst.at[h], l_in.at[4 * h + k])
            for k, (src, dst) in enumerate(pairs)
        ]

    loads = [
        pltpu.make_async_copy(e_own_hbm, e_own, l_in.at[4 * heads]),
        pltpu.make_async_copy(e_got_hbm, e_got, l_in.at[4 * heads + 1]),
        pltpu.make_async_copy(o_own_hbm, o_own, l_in.at[4 * heads + 2]),
        pltpu.make_async_copy(o_got_hbm, o_got, l_in.at[4 * heads + 3]),
        pltpu.make_async_copy(tok_hbm, tok_v, l_in.at[4 * heads + 4]),
        pltpu.make_async_copy(ctx_hbm, ctx_ref, l_in.at[4 * heads + 5]),
        pltpu.make_async_copy(gctx_hbm, gctx_ref, l_in.at[4 * heads + 6]),
        pltpu.make_async_copy(lse_hbm, lse_ref, l_in.at[4 * heads + 7]),
    ]
    for copy in loads[:4] + loads[5:] + taken(0):
        copy.start()
    for h in range(1, heads):
        for copy in taken(h):
            copy.start()
    loads[4].start()
    meet([(p, w) for p in others] + [(s, 2 * k + c) for k in far])

    def leaving(h, own=False):
        if own:
            return pltpu.make_async_copy(stage.at[h, s], pieces_o.at[h, s], l_out.at[h])
        return [
            remote(stage.at[h, p], pieces_o.at[h, s], (s_p, r_p), 3 * h + k, (p, w))
            for k, p in enumerate(others)
        ]

    over_plane = [
        remote(e_got.at[p], e_all.at[s], (s_e, r_e), k, (p, w)) for k, p in enumerate(others)
    ] + [remote(o_got.at[p], o_all.at[s], (s_e, r_e), 3 + k, (p, w)) for k, p in enumerate(others)]
    over_z = [
        remote(e_sum.at[k], e_z.at[z], (s_z, r_z), j, (s, 2 * k + c)) for j, k in enumerate(far)
    ] + [
        remote(o_sum.at[k], o_z.at[z], (s_z, r_z), nz - 1 + j, (s, 2 * k + c))
        for j, k in enumerate(far)
    ]
    for copy in loads[:4]:
        copy.wait()

    def pair_sum(i, carry):
        q, k = i // nz, lax.rem(i, nz)
        e_got[q, k] = (e_got[q, k].astype(f32) + e_own[q, k].astype(f32)).astype(bf16)
        o_got[q, k] = (o_got[q, k].astype(f32) + o_own[q, k].astype(f32)).astype(bf16)
        return carry

    lax.fori_loop(0, 4 * nz, pair_sum, 0)
    for copy in over_plane:
        copy.start()
    e_all[s] = e_got[s]
    o_all[s] = o_got[s]
    late_sc[...] = jnp.zeros_like(late_sc)
    row_sc[...] = jnp.zeros_like(row_sc)
    for copy in loads[5:]:
        copy.wait()
    for h in range(heads):
        for copy in taken(h):
            copy.wait()

    def prologue(h):
        dk_sc[...] = jnp.zeros_like(dk_sc)
        dv_sc[...] = jnp.zeros_like(dv_sc)
        def inner(i, carry):
            lanes = pl.ds(pl.multiple_of(i * TQ, TQ), TQ)
            own = pl.ds(pl.multiple_of(h * HD, HD), HD)
            g_nat[i] = gctx_ref[own, lanes]
            product = g_nat[i].astype(f32) * ctx_ref[own, lanes].astype(f32)
            delta_nat[i] = jnp.sum(product, axis=0, keepdims=True)
            return carry

        def order(i, carry):
            g_sc[i] = g_nat[natural_at(short_first, i)]
            delta_sc[i] = delta_nat[natural_at(short_first, i)]
            return carry

        lax.fori_loop(0, GLEN // TQ, inner, 0)
        lax.fori_loop(0, GLEN // TQ, order, 0)

    def halfway():
        for copy in over_plane:
            copy.wait_recv()

        def add4(ref, k):
            t = [ref[q, k].astype(f32) for q in range(4)]
            return ((t[0] + t[1]) + (t[2] + t[3])).astype(bf16)

        def plane_sum(k, carry):
            e_sum[k] = add4(e_all, k)
            o_sum[k] = add4(o_all, k)
            return carry

        lax.fori_loop(0, nz, plane_sum, 0)
        for copy in over_z:
            copy.start()
        e_z[z] = e_sum[z]
        o_z[z] = o_sum[z]

    def epilogue(h, first, last):
        half = SHORT // 2
        scale = value_scale(s * heads + h, w, kept_ref, gate_ref, mask_ref)

        def settle(j, carry):
            i = ordered_at(short_first, j)
            dq = dqt_sc[i].astype(bf16)
            dk = (dk_sc[i] * score_scale).astype(bf16).T
            dv = dv_sc[i].astype(bf16).astype(f32)
            gate = jnp.sum(dv * v_all[h, i].astype(f32), axis=0, keepdims=True)
            dv = (dv * scale).astype(bf16)
            row_sc[h, 0:1, :] += jnp.sum(dv.astype(f32), axis=0, keepdims=True)
            row_sc[h, 1:2, :] += gate
            dv = dv.T
            x = dq.astype(f32)
            late_sc[h] += (x[:, 0:128] + x[:, 128:256]) + (x[:, 256:384] + x[:, 384:512])
            for r in range(2):
                u = 2 * j + r
                p, there = u // 3, pl.ds(pl.multiple_of(lax.rem(u, 3) * half, half), half)
                cols = slice(r * half, (r + 1) * half)
                stage[h, p, 0:HD, there] = dq[:, cols]
                stage[h, p, HD : 2 * HD, there] = dk[:, cols]
                stage[h, p, 2 * HD : 3 * HD, there] = dv[:, cols]
            return carry

        lax.fori_loop(first, last, settle, 0)
        for p, copy in zip(others, leaving(h), strict=True):

            @pl.when(p // 2 == (0 if first == 0 else 1))
            def _(copy=copy):
                copy.start()

        if first == 0:
            leaving(h, True).start()

    def tile_of(h):
        def tile(i, own_blocks):
            q = q_all[h, i]
            g = g_sc[i]
            lse = lse_ref[h, :, pl.ds(pl.multiple_of(i * TQ, TQ), TQ)]
            delta = delta_sc[i]
            dq = jnp.zeros((HD, TQ), f32)
            for j in (0, 1) + own_blocks:
                sc = mm(k_all[h, j], q, NT)
                p = jnp.exp2(sc * exp2_scale - lse)
                dp = mm(v_all[h, j], g)
                ds = (p * (dp - delta)).astype(bf16)
                dv_sc[j] += mm(p.astype(bf16), g, NT)
                dk_sc[j] += mm(ds, q)
                dq = dq + mm(kt_all[h, j], ds)
            dqt_sc[i] = dq * score_scale

        return tile

    def one_head(h, carry):
        prologue(h)
        def longer(i, carry):
            tile_of(h)(i, (3, 4, 5))
            return carry

        def prompt(i, carry):
            tile_of(h)(i, ())
            return carry

        tile_of(h)(2, (2,))
        pl.when(h == heads - 1)(halfway)

        lax.fori_loop(3, 6, longer, 0)
        epilogue(h, 2, 6)
        lax.fori_loop(0, 2, prompt, 0)
        epilogue(h, 0, 2)
        return carry

    lax.fori_loop(0, heads, one_head, 0)
    loads[4].wait()
    acc[...] = jnp.zeros_like(acc)

    def weight_grad(p, carry):
        x = tok_v[pl.ds(pl.multiple_of(p * count, count), count), :]
        for h in range(heads):
            acc[3 * HD * h : 3 * HD * (h + 1), :] += mm(stage[h, p], x)
        return carry

    lax.fori_loop(0, 4, weight_grad, 0)
    own_rows = dw_o.shape[1]
    grad = acc[...].T.astype(bf16)
    for k in range(n):
        dw_o[k] = grad[k * own_rows : (k + 1) * own_rows, :]
    late_o[...] = jnp.zeros_like(late_o)
    for h in range(heads):
        own = slice(HD * h, HD * (h + 1))
        late_o[0:1, own] = jnp.sum(late_sc[h].T, axis=0, keepdims=True)
        late_o[1:3, own] = row_sc[h, 0:2, :]
    for copy in over_z:
        copy.wait_recv()
    for ref, out in ((e_z, exp_o), (o_z, out_o)):
        total = ref[0].astype(f32)
        for k in range(1, nz):
            total = total + ref[k].astype(f32)
        out[...] = total.astype(bf16)
    for h in range(heads):
        for copy in [leaving(h, True)] + leaving(h):
            copy.wait()
    for copy in over_plane + over_z:
        copy.wait_send()


def attend_back(n, lens, kept, gate, mask, q, k, v, kt, ctx, g, lse, tokens_all, *parts):
    heads = q.shape[0]
    width = 3 * HD * heads
    d = tokens_all.shape[1]
    count = GLEN // 4
    nz = n // 2
    own, wide = parts[0].shape[2:]
    part = parts[2].shape[3]
    blocks = GLEN // TQ
    rows64 = pltpu.VMEM((heads, blocks, TQ, HD), bf16)
    blocks64 = pltpu.VMEM((blocks, HD, TQ), bf16)
    quarters = [pltpu.VMEM(parts[0].shape, bf16), pltpu.VMEM(parts[2].shape, bf16)]
    return pl.pallas_call(
        functools.partial(attend_back_kernel, heads, n),
        out_shape=(
            jax.ShapeDtypeStruct((heads, 4, 3 * HD, count), bf16),
            jax.ShapeDtypeStruct((n, d // n, width), bf16),
            jax.ShapeDtypeStruct((own, wide), bf16),
            jax.ShapeDtypeStruct((own, part), bf16),
            jax.ShapeDtypeStruct((8, HD * heads), f32),
        ),
        in_specs=[IN_SMEM] * 4
        + [ANYWHERE] * 4
        + [ANYWHERE] * 8,
        out_specs=(ANYWHERE, IN_VMEM, IN_VMEM, IN_VMEM, IN_VMEM),
        scratch_shapes=[
            pltpu.VMEM(ctx.shape, bf16),
            pltpu.VMEM(g.shape, bf16),
            pltpu.VMEM(lse.shape, f32),
            pltpu.VMEM(tokens_all.shape, bf16),
        ]
        + quarters * 3
        + [pltpu.VMEM((nz, own, wide), bf16), pltpu.VMEM((nz, own, part), bf16)] * 2
        + [pltpu.VMEM((heads, 4, 3 * HD, count), bf16), pltpu.VMEM((heads, HD, 128), f32)]
        + [pltpu.VMEM((heads, 8, HD), f32)]
        + [
            rows64,
            rows64,
            rows64,
            pltpu.VMEM(kt.shape, bf16),
            blocks64,
            blocks64,
            pltpu.VMEM((blocks, 1, TQ), f32),
            pltpu.VMEM((blocks, 1, TQ), f32),
            pltpu.VMEM((blocks, HD, TQ), f32),
            pltpu.VMEM((blocks, TQ, HD), f32),
            pltpu.VMEM((blocks, TQ, HD), f32),
            pltpu.VMEM((width, d), f32),
            pltpu.SemaphoreType.DMA((4 * heads + 8,)),
            pltpu.SemaphoreType.DMA((heads,)),
        ]
        + dma_sems(3 * heads)
        + dma_sems(6)
        + dma_sems(2 * nz - 2),
        compiler_params=remote_params(2),
        cost_estimate=pl.CostEstimate(
            flops=heads * 10 * 256 * 5767168 + 2 * GLEN * d * width,
            bytes_accessed=2 * GLEN * (3 * width + d),
            transcendentals=heads * 5767168,
        ),
        name="attend_back",
    )(
        lens, kept, gate, mask,
        *(x.reshape(heads, blocks, TQ, HD) for x in (q, k, v)),
        kt, ctx, g, lse, tokens_all, *parts,
    )


def meet(peers):
    barrier = pltpu.get_barrier_semaphore()
    for peer in peers:
        pl.semaphore_signal(barrier, inc=1, device_id=peer, device_id_type=pl.DeviceIdType.MESH)
    pl.semaphore_wait(barrier, len(peers))


def flip(index, bits):
    for bit in (1, 2):
        if bits & bit:
            index = index + bit - 2 * bit * ((index // bit) % 2)
    return index


def remote_params(number):
    return pltpu.CompilerParams(
        collective_id=number, has_side_effects=True, vmem_limit_bytes=56 * 2**20
    )


ANYWHERE = pl.BlockSpec(memory_space=pl.ANY)
IN_VMEM = pl.BlockSpec(memory_space=pltpu.VMEM)
IN_SMEM = pl.BlockSpec(memory_space=pltpu.SMEM)


def dma_sems(count):
    return [pltpu.SemaphoreType.DMA((count,)), pltpu.SemaphoreType.DMA((count,))]


def gather_kernel(
    n, tok_ref, weight_ref, exp_ref, tok_all, cols_all, exp_all, tok_buf, cols_buf, exp_buf,
    local_sem, s_tok, r_tok, s_w, r_w, s_f, r_f, s_e, r_e,
):
    s, w = lax.axis_index("seq"), lax.axis_index("wt")
    rows = tok_ref.shape[0]
    half = rows // 2
    wide = cols_buf.shape[1]
    for k in range(4):

        @pl.when(s == k)
        def _(k=k):
            cols_buf[...] = weight_ref[:, k * wide : (k + 1) * wide]

    by_x, by_y, mate = (flip(s, 1), w), (flip(s, 2), w), (s, flip(w, 1))
    far = [(s, lax.rem(w + 2 * j, n)) for j in range(1, n // 2)]
    quarter = exp_buf.shape[1]
    exp_own = exp_ref.at[:, pl.ds(pl.multiple_of(s * quarter, 128), quarter)]
    come = [
        pltpu.make_async_copy(tok_ref, tok_buf, local_sem.at[0]),
        pltpu.make_async_copy(exp_own, exp_buf, local_sem.at[2]),
    ]
    for copy in come:
        copy.start()
    meet([by_x, by_y, mate] + far)

    def part(owner, k):
        return pl.ds(pl.multiple_of(owner * rows + k * half, half), half)

    tok = (s_tok, r_tok)
    first = [pl.ds(0, half), pl.ds(half, half)]
    x0 = send(tok_ref.at[first[0]], tok_all.at[part(s, 0)], tok, 0, by_x)
    y1 = send(tok_ref.at[first[1]], tok_all.at[part(s, 1)], tok, 1, by_y)
    x1 = send(tok_ref.at[first[1]], tok_all.at[part(s, 1)], tok, 2, by_x)
    y0 = send(tok_ref.at[first[0]], tok_all.at[part(s, 0)], tok, 3, by_y)
    held = [
        send(cols_buf, cols_all.at[w], (s_w, r_w), k, peer) for k, peer in enumerate(far + [mate])
    ]
    along = [
        send(exp_own, exp_all.at[w // 2], (s_e, r_e), k, peer) for k, peer in enumerate(far)
    ]
    for copy in come:
        copy.wait()
    own = [
        pltpu.make_async_copy(exp_buf, exp_all.at[w // 2], local_sem.at[2]),
        pltpu.make_async_copy(
            tok_buf, tok_all.at[pl.ds(pl.multiple_of(s * rows, rows), rows)], local_sem.at[0]
        ),
        pltpu.make_async_copy(cols_buf, cols_all.at[w], local_sem.at[1]),
    ]
    for copy in own:
        copy.start()
    passed = []
    for j in range(1, n // 2):
        origin = lax.rem(w + n - 2 * j, n)
        held[j - 1].wait_recv()
        passed.append(send(cols_all.at[origin], cols_all.at[origin], (s_f, r_f), j - 1, mate))
    x0.wait_recv()
    there = tok_all.at[part(flip(s, 1), 0)]
    passed.append(send(there, there, tok, 4, by_y))
    y1.wait_recv()
    there = tok_all.at[part(flip(s, 2), 1)]
    passed.append(send(there, there, tok, 5, by_x))
    for copy in own:
        copy.wait()
    for copy in [x1, y0, held[-1]] + passed + along:
        copy.wait_recv()
    for copy in [x0, x1, y0, y1] + held + passed + along:
        copy.wait_send()


def gather_in(n, tokens, attention_weight, expand_weight):
    rows, d = tokens.shape
    own, width = attention_weight.shape
    quarter = expand_weight.shape[1] // 4
    return pl.pallas_call(
        functools.partial(gather_kernel, n),
        out_shape=(
            jax.ShapeDtypeStruct((4 * rows, d), bf16),
            jax.ShapeDtypeStruct((n, own, width // 4), bf16),
            jax.ShapeDtypeStruct((n // 2, own, quarter), bf16),
        ),
        in_specs=[ANYWHERE, IN_VMEM, ANYWHERE],
        out_specs=(ANYWHERE,) * 3,
        scratch_shapes=[
            pltpu.VMEM(tokens.shape, bf16),
            pltpu.VMEM((own, width // 4), bf16),
            pltpu.VMEM((own, quarter), bf16),
            pltpu.SemaphoreType.DMA((3,)),
        ]
        + dma_sems(6)
        + dma_sems(n // 2)
        + dma_sems(n // 2 - 1)
        + dma_sems(n // 2 - 1),
        compiler_params=remote_params(0),
        name="gather_in",
    )(tokens, attention_weight, expand_weight)


def final_kernel(
    heads, n, base_hbm, pieces_hbm, w_hbm, con_ref, att_ref, out_ref, exp_ref, vec_ref, late_ref,
    tok_o, g_con, g_out, g_exp, g_att, r_vec2, r_late2,
    base_v, pieces_v, w_v, a_own, r_con, h_att, m_att, r_att, r_vec, r_late,
    l_in, *sems,
):
    s, w = lax.axis_index("seq"), lax.axis_index("wt")
    z, c = w // 2, lax.rem(w, 2)
    nz = n // 2
    others = [flip(s, k) for k in (1, 2, 3)]
    seq_peers = [(p, w) for p in others]
    mate = (s, flip(w, 1))
    wt_peers = [(s, lax.rem(w + j, n)) for j in range(1, n)]
    names = ("pair", "vec", "late", "con", "out2", "att", "vec2", "late2", "con2", "exp2", "att2")
    sem = {name: (sems[2 * k], sems[2 * k + 1]) for k, name in enumerate(names)}
    loads = [
        pltpu.make_async_copy(src, dst, l_in.at[k])
        for k, (src, dst) in enumerate(((pieces_hbm, pieces_v), (w_hbm, w_v), (base_hbm, base_v)))
    ]
    first = [pltpu.make_async_copy(con_ref.at[s], r_con.at[s], l_in.at[3])] + [
        pltpu.make_async_copy(att_ref.at[2 * k + c], a_own.at[k], l_in.at[4 + k]) for k in range(nz)
    ]
    for copy in first + loads:
        copy.start()
    meet(seq_peers + wt_peers)
    pair = [send(att_ref.at[2 * k + 1 - c], h_att.at[k], sem["pair"], k, mate) for k in range(nz)]
    cons = [send(con_ref.at[p], r_con.at[s], sem["con"], k, (p, w)) for k, p in enumerate(others)]
    far = [lax.rem(z + j, nz) for j in range(1, nz)]
    exp2 = [send(exp_ref, g_exp.at[s], sem["exp2"], k, p) for k, p in enumerate(seq_peers)]
    out2 = [send(out_ref, g_out.at[s], sem["out2"], k, p) for k, p in enumerate(seq_peers)]
    vecs = [
        send(vec_ref.at[lax.rem(w + j, n)], r_vec.at[w], sem["vec"], j - 1, wt_peers[j - 1])
        for j in range(1, n)
    ]
    lates = [send(late_ref, r_late.at[w], sem["late"], j, p) for j, p in enumerate(wt_peers)]
    g_exp[s] = exp_ref[...]
    r_vec[w] = vec_ref[w]
    r_late[w] = late_ref[...]
    g_out[s] = out_ref[...]
    for copy in first:
        copy.wait()
    for copy in pair:
        copy.wait_recv()
    for k in range(nz):
        m_att[k] = (a_own[k].astype(f32) + h_att[k].astype(f32)).astype(bf16)
    atts = [send(m_att.at[k], r_att.at[z], sem["att"], j, (s, 2 * k + c)) for j, k in enumerate(far)]
    r_att[z] = m_att[z]
    for copy in loads:
        copy.wait()
    cols = 3 * HD
    rows = tok_o.shape[0]
    block = rows // 3

    def total_of(ref, count):
        total = ref[0].astype(f32)
        for k in range(1, count):
            total = total + ref[k].astype(f32)
        return total

    own = [ref.at[s] for ref in (g_con, r_vec2, r_late2, g_att)]
    con2, vec2, late2, att2 = (
        [remote(ref, ref, sem[name], k, p) for k, p in enumerate(seq_peers)]
        for ref, name in zip(own, ("con2", "vec2", "late2", "att2"), strict=True)
    )

    def tokens_block(i, carry):
        there = pl.ds(pl.multiple_of(i * block, block), block)
        total = base_v[there, :]
        for h in range(heads):
            for k in range(4):
                at = (heads * k + h) * cols
                total = total + mm(pieces_v[h, k, :, there].T, w_v[:, at : at + cols], NT)
        tok_o[there, :] = total

        @pl.when(i == 0)
        def _():
            for copy in cons:
                copy.wait_recv()
            g_con[s] = total_of(r_con, 4).astype(bf16)
            for copy in con2:
                copy.start()
            for copy in vecs + lates:
                copy.wait_recv()
            r_vec2[s] = total_of(r_vec, n)
            r_late2[s] = total_of(r_late, n)
            for copy in vec2 + late2:
                copy.start()

        @pl.when(i == 1)
        def _():
            for copy in atts:
                copy.wait_recv()
            g_att[s] = total_of(r_att, nz).astype(bf16)
            for copy in att2:
                copy.start()

        return carry

    lax.fori_loop(0, 3, tokens_block, 0)
    for copy in out2 + con2 + vec2 + late2 + exp2 + att2:
        copy.wait_recv()
    for copy in pair + cons + vecs + lates + atts + con2 + vec2 + late2 + exp2 + out2 + att2:
        copy.wait_send()


def final(n, base, pieces, weight, con, att, out, exp_part, vec, late):
    heads = pieces.shape[0]
    r, d = con.shape[1:]
    cols = att.shape[2]
    nz = n // 2
    counts = (nz, n - 1, n - 1, 3, 3, nz - 1, 3, 3, 3, 3, 3)
    return pl.pallas_call(
        functools.partial(final_kernel, heads, n),
        out_shape=(
            jax.ShapeDtypeStruct(base.shape, f32),
            jax.ShapeDtypeStruct((4, r, d), bf16),
            jax.ShapeDtypeStruct((4,) + out.shape, bf16),
            jax.ShapeDtypeStruct((4,) + exp_part.shape, bf16),
            jax.ShapeDtypeStruct((4, r, cols), bf16),
            jax.ShapeDtypeStruct((4,) + vec.shape[1:], f32),
            jax.ShapeDtypeStruct((4,) + late.shape, f32),
        ),
        in_specs=[ANYWHERE] * 5 + [IN_VMEM] * 4,
        out_specs=(IN_VMEM,) * 7,
        scratch_shapes=[
            pltpu.VMEM(base.shape, f32),
            pltpu.VMEM(pieces.shape, bf16),
            pltpu.VMEM(weight.shape, bf16),
            pltpu.VMEM((nz, r, cols), bf16),
            pltpu.VMEM((4, r, d), bf16),
            pltpu.VMEM((nz, r, cols), bf16),
            pltpu.VMEM((nz, r, cols), bf16),
            pltpu.VMEM((nz, r, cols), bf16),
            pltpu.VMEM((n,) + vec.shape[1:], f32),
            pltpu.VMEM((n,) + late.shape, f32),
            pltpu.SemaphoreType.DMA((4 + nz,)),
        ]
        + [sem for count in counts for sem in dma_sems(count)],
        compiler_params=remote_params(3),
        cost_estimate=pl.CostEstimate(
            flops=8 * base.shape[0] * d * cols, bytes_accessed=8 * d * cols, transcendentals=0
        ),
        name="final",
    )(base, pieces, weight, con, att, out, exp_part, vec, late)


def finish_kernel(n, heads, gate_ref, mask_ref, *refs):
    sources, rest = refs[:8], refs[8:]
    con_o, exp_o, att_o, tok_o, low_o, out_o = rest[:6]
    vec_os, unit_os, query_o, value_o, gate_o = rest[6:13], rest[13:15], rest[15], rest[16], rest[17]
    con_v, exp_v, att_v, tok_v, low_v, out_v, vec_v, late_v, con_f, exp_f, att_f, l_in, l_out = rest[18:]
    inside = (con_v, exp_v, att_v, tok_v, low_v, out_v, vec_v, late_v)
    loads = [
        pltpu.make_async_copy(src, dst, l_in.at[k])
        for k, (src, dst) in enumerate(zip(sources, inside, strict=True))
    ]
    for copy in loads:
        copy.start()
    outside = ((con_f, con_o), (exp_f, exp_o), (att_f, att_o), (tok_v, tok_o), (low_v, low_o))
    stores = [pltpu.make_async_copy(src, dst, l_out.at[k]) for k, (src, dst) in enumerate(outside)]

    def add4(parts):
        return (parts[0] + parts[1]) + (parts[2] + parts[3])

    wide, cols, part = exp_v.shape[2], att_v.shape[2], out_v.shape[2]
    loads[0].wait()
    con_f[...] = con_v[...].astype(f32)
    stores[0].start()
    loads[1].wait()
    for k in range(4):
        exp_f[:, k * wide : (k + 1) * wide] = exp_v[k].astype(f32)
    stores[1].start()
    loads[2].wait()
    for k in range(4):
        att_f[:, k * cols : (k + 1) * cols] = att_v[k].astype(f32)
    stores[2].start()
    for k in (3, 4):
        loads[k].wait()
        stores[k].start()
    for copy in loads[5:]:
        copy.wait()
    for k in range(4):
        out_o[:, k * part : (k + 1) * part] = out_v[k].astype(f32)
    vec = add4([vec_v[k] for k in range(4)])
    own = vec_os[0].shape[0]
    for k, ref in enumerate(vec_os):
        ref[...] = vec[k, 0:own]
    for k, ref in enumerate(unit_os):
        ref[...] = vec[8 + k]
    rows = [jnp.concatenate([late_v[k, j : j + 1, :] for k in range(4)], axis=1) for j in range(2)]
    for k in range(n):

        @pl.when(lax.axis_index("wt") == k)
        def _(k=k):
            query_o[...] = rows[0][0, k * own : (k + 1) * own]
            value_o[...] = rows[1][0, k * own : (k + 1) * own]

    gates = []
    for k in range(4):
        for h in range(heads):
            part_sum = jnp.sum(late_v[k, 2:3, HD * h : HD * (h + 1)], axis=1, keepdims=True)
            kept = mask_ref[heads * k + h].astype(f32) / gate_ref[heads * k + h]
            gates.append(part_sum * kept)
    gate_o[...] = jnp.concatenate(gates, axis=1)[0]
    for copy in stores:
        copy.wait()


def finish(n, heads, gate, mask, con, exp_all, att, tok, low, out, vec, late):
    r = out.shape[1]
    wide, cols, part = exp_all.shape[2], att.shape[2], out.shape[2]
    units = vec.shape[2]
    row = jax.ShapeDtypeStruct((r,), f32)
    con_f, exp_f, att_f = (
        con.shape,
        (r, 4 * wide),
        (r, 4 * cols),
    )
    return pl.pallas_call(
        functools.partial(finish_kernel, n, heads),
        out_shape=(
            jax.ShapeDtypeStruct(con_f, f32),
            jax.ShapeDtypeStruct(exp_f, f32),
            jax.ShapeDtypeStruct(att_f, f32),
            jax.ShapeDtypeStruct(tok.shape, f32),
            jax.ShapeDtypeStruct(low.shape, low.dtype),
            jax.ShapeDtypeStruct((r, 4 * part), f32),
        )
        + (row,) * 7
        + (jax.ShapeDtypeStruct((units,), f32),) * 2
        + (row,) * 2
        + (jax.ShapeDtypeStruct((4 * heads,), f32),),
        in_specs=[IN_SMEM] * 2 + [ANYWHERE] * 8,
        out_specs=(ANYWHERE,) * 5 + (IN_VMEM,) * 13,
        scratch_shapes=[
            pltpu.VMEM(x.shape, x.dtype) for x in (con, exp_all, att, tok, low, out, vec, late)
        ]
        + [pltpu.VMEM(x, f32) for x in (con_f, exp_f, att_f)]
        + [pltpu.SemaphoreType.DMA((8,)), pltpu.SemaphoreType.DMA((5,))],
        compiler_params=pltpu.CompilerParams(vmem_limit_bytes=56 * 2**20),
        name="finish",
    )(gate, mask, con, exp_all, att, tok, low, out, vec, late)


(OUT_BIAS, GAIN1, SHIFT1, HIDDEN_SCALE, CON_BIAS, GAIN2, SHIFT2, HIDDEN_MASK) = range(8)
(S_OUT_BIAS, S_GAIN1, S_SHIFT1, S_CON_BIAS, S_GAIN2, S_SHIFT2, S_HIDDEN) = range(7)


def gelu_parts(x):
    bell = jnp.exp(-0.5 * (x * x))
    t = 1.0 / (1.0 + (0.3275911 * root_half) * jnp.abs(x))
    poly = t * (
        0.127414796 + t * (-0.142248368 + t * (0.7107068705 + t * (-0.7265760135 + t * 0.5307027145)))
    )
    tail = poly * bell
    cumulative = jnp.where(x < 0.0, tail, 1.0 - tail)
    return x * cumulative, cumulative + x * bell * density_scale


def norm_parts(summed):
    centre = summed - jnp.mean(summed, axis=-1, keepdims=True)
    inverse = lax.rsqrt(jnp.mean(centre * centre, axis=-1, keepdims=True) + epsilon)
    return (centre * inverse, inverse)


def norm_back(grad_normed, normed, inverse):
    return inverse * (
        grad_normed
        - jnp.mean(grad_normed, axis=-1, keepdims=True)
        - normed * jnp.mean(grad_normed * normed, axis=-1, keepdims=True)
    )


def feed_forward_kernel(
    steps, chunk,
    kept_ref, ctx_ref, tok_ref, cot_ref, wo_ref, we_hbm, wc_hbm,
    ob_ref, g1_ref, t1_ref, hg_ref, hm_ref, cb_ref, g2_ref, t2_ref, eb_ref, ug_ref, um_ref,
    lo_ref, dt1_ref, g_all, vec_ref, dwc_hbm, e_own, e_got, o_own, o_got,
    we_ref, wc_ref, dwc_ref, dwe_ref, dwo_ref, g_sc,
    wide_ref, unit_ref, sw_ref, su_ref, act_sc, gh_sc, low_sc, gb_sc, ga_sc, ctx_sc, gelu_sc, slope_sc,
    l_w, l_o, l_g, s_g, r_g, s_p, r_p,
):
    i = pl.program_id(0)
    block = tok_ref.shape[0]
    units = we_ref.shape[1]
    rows = pl.ds(pl.multiple_of(i * block, block), block)
    s, w = lax.axis_index("seq"), lax.axis_index("wt")
    others = [flip(s, k) for k in (1, 2, 3)]
    mate, core = (s, flip(w, 1)), lax.rem(w, 2)
    part_rows = g_all.shape[0]
    weights = [
        pltpu.make_async_copy(we_hbm, we_ref, l_w.at[0]),
        pltpu.make_async_copy(wc_hbm, wc_ref, l_w.at[1]),
    ]

    def leaving(t):
        there = g_all.at[:, pl.ds(pl.multiple_of((s * steps + t) * block, 128), block)]

        def part(p):
            lanes = pl.ds(pl.multiple_of(t * block, 128), block)
            return g_sc.at[pl.ds(pl.multiple_of(p * part_rows, 16), part_rows), lanes]

        copies = [
            remote(part(p), there, (s_g, r_g), 3 * t + k, (p, w)) for k, p in enumerate(others)
        ]
        return copies + [pltpu.make_async_copy(part(s), there, l_g.at[t])]

    @pl.when(i == 0)
    def _():
        for copy in weights:
            copy.start()
        meet([(p, w) for p in others] + [mate])
        sw_ref[...] = jnp.zeros_like(sw_ref)
        su_ref[...] = jnp.zeros_like(su_ref)

        def row(ref):
            return ref[...].astype(f32).reshape(1, ref.shape[0])

        plain = ((OUT_BIAS, ob_ref), (GAIN1, g1_ref), (SHIFT1, t1_ref), (CON_BIAS, cb_ref))
        for k, ref in plain + ((GAIN2, g2_ref), (SHIFT2, t2_ref), (HIDDEN_MASK, hm_ref)):
            wide_ref[k : k + 1, :] = row(ref)
        wide_ref[HIDDEN_SCALE : HIDDEN_SCALE + 1, :] = row(hm_ref) * row(hg_ref)
        kept = row(um_ref) * kept_ref[lax.axis_index("wt")].astype(f32)
        unit_ref[0:1, :] = row(eb_ref)
        unit_ref[1:2, :] = kept * row(ug_ref)
        unit_ref[2:3, :] = kept

    def wide(k):
        return wide_ref[k : k + 1, :]

    def add_sum(ref, k, cols, value):
        ref[k : k + 1, cols] += jnp.sum(value, axis=0, keepdims=True)

    full = slice(None)
    ctx = ctx_ref[...]
    ctx_sc[:, rows] = ctx
    summed = mm(ctx, wo_ref[...], TN) + wide(OUT_BIAS) + tok_ref[...].astype(f32)
    n1, inv1 = norm_parts(summed)
    s1 = n1 * wide(GAIN1) + wide(SHIFT1)
    hs = wide(HIDDEN_SCALE)
    first = s1 * hs
    low = first.astype(bf16)
    low_sc[rows, :] = low
    branch = first + wide(CON_BIAS)

    @pl.when(i == 0)
    def _():
        for copy in weights:
            copy.wait()

    for j in range(units // chunk):
        cols = slice(j * chunk, (j + 1) * chunk)
        hidden = mm(low, we_ref[:, cols]) + unit_ref[0:1, cols]
        gelu, slope = gelu_parts(hidden)
        scale = unit_ref[1:2, cols]
        gelu_sc[:, cols] = gelu.astype(gelu_sc.dtype)
        slope_sc[:, cols] = (slope * scale).astype(slope_sc.dtype)
        act = (gelu * scale).astype(bf16)
        act_sc[rows, cols] = act
        branch = branch + mm(act, wc_ref[cols, :])
    n2, inv2 = norm_parts(branch)
    s2 = n2 * wide(GAIN2) + wide(SHIFT2)
    lo_ref[...] = (s2 * hs).astype(bf16)
    dy = cot_ref[...].astype(f32)
    e2 = dy * hs
    add_sum(sw_ref, S_GAIN2, full, e2 * n2)
    add_sum(sw_ref, S_SHIFT2, full, e2)
    dt2 = norm_back(e2 * wide(GAIN2), n2, inv2)
    gb = dt2.astype(bf16)
    gb_sc[rows, :] = gb
    add_sum(sw_ref, S_CON_BIAS, full, gb.astype(f32))
    d_first = dt2
    for j in range(units // chunk):
        cols = slice(j * chunk, (j + 1) * chunk)
        d_act = mm(gb, wc_ref[cols, :], NT)
        add_sum(su_ref, 1, cols, d_act * gelu_sc[:, cols].astype(f32))
        gh = d_act * slope_sc[:, cols].astype(f32)
        add_sum(su_ref, 0, cols, gh)
        gh = gh.astype(bf16)
        gh_sc[rows, cols] = gh
        d_first = d_first + mm(gh, we_ref[:, cols], NT)
    e1 = d_first * hs
    add_sum(sw_ref, S_GAIN1, full, e1 * n1)
    add_sum(sw_ref, S_SHIFT1, full, e1)
    add_sum(sw_ref, S_HIDDEN, full, dy * s2 + d_first * s1)
    dt1 = norm_back(e1 * wide(GAIN1), n1, inv1)
    dt1_ref[...] = dt1
    ga = dt1.astype(bf16)
    ga_sc[rows, :] = ga
    add_sum(sw_ref, S_OUT_BIAS, full, ga.astype(f32))
    g_sc[:, rows] = mm(wo_ref[...], ga, NT).astype(bf16)
    for copy in leaving(i):
        copy.start()

    @pl.when(i == steps - 1)
    def _():
        own, wide_cols = dwe_ref.shape[3:]

        def weight_grads(j, carry):
            cols = pl.ds(pl.multiple_of(j * wide_cols, 128), wide_cols)
            dwc_ref[cols, :] = mm(act_sc[:, cols], gb_sc[...], TN).astype(bf16)
            part = mm(low_sc[...], gh_sc[:, cols], TN).astype(bf16)
            for k in range(2 * dwe_ref.shape[2]):
                dwe_ref[k % 2, j, k // 2] = part[k * own : (k + 1) * own]
            for copy in given(j):
                copy.start()
            return carry

        def given(j):
            there = pl.ds(pl.multiple_of(j * wide_cols, 128), wide_cols)
            return [
                pltpu.make_async_copy(dwc_ref.at[there], dwc_hbm.at[there], l_o.at[j]),
                pltpu.make_async_copy(dwe_ref.at[core, j], e_own.at[j], l_o.at[4 + j]),
                remote(dwe_ref.at[1 - core, j], e_got.at[j], (s_p, r_p), j, mate),
            ]

        part_cols = dwo_ref.shape[4]
        for q in range(4):
            part = mm(ctx_sc[...], ga_sc[:, q * part_cols : (q + 1) * part_cols]).astype(bf16)
            for k in range(2 * dwo_ref.shape[2]):
                dwo_ref[k % 2, q, k // 2] = part[k * own : (k + 1) * own]
        over = [
            pltpu.make_async_copy(dwo_ref.at[core], o_own, l_o.at[8]),
            remote(dwo_ref.at[1 - core], o_got, (s_p, r_p), 4, mate),
        ]
        for copy in over:
            copy.start()
        lax.fori_loop(0, 4, weight_grads, 0)
        vec_ref[...] = jnp.zeros_like(vec_ref)
        sw_ref[S_HIDDEN : S_HIDDEN + 1, :] *= wide(HIDDEN_MASK)
        su_ref[1:2, :] *= unit_ref[2:3, :]
        own_wide, own_units = dwe_ref.shape[3], vec_ref.shape[2]
        for k in range(vec_ref.shape[0]):
            vec_ref[k, 0:8, 0:own_wide] = sw_ref[:, k * own_wide : (k + 1) * own_wide]
            vec_ref[k, 8:16, :] = su_ref[:, k * own_units : (k + 1) * own_units]
        for t in range(steps):
            for copy in leaving(t):
                copy.wait()
        for copy in over:
            copy.wait()
        for j in range(4):
            for copy in given(j):
                copy.wait()


def feed_forward(n, kept, ctx_t, tokens, cotangent, wo, we, wc, *vectors):
    steps, chunk, keep = 3, 768, f32
    rows, d = tokens.shape
    units = we.shape[1]
    block = rows // steps
    halves = (2, 4, n // 2, d // n, units // 4)
    out_halves = (2, 4, n // 2, d // n, d // 4)
    tile = pl.BlockSpec((block, d), lambda i: (i, 0))
    lanes = pl.BlockSpec((d, block), lambda i: (0, i))

    def once(shape):
        return pl.BlockSpec(shape, lambda i: (0, 0), pipeline_mode=pl.Buffered(1))

    def once3(shape):
        return pl.BlockSpec(shape, lambda i: (0, 0, 0), pipeline_mode=pl.Buffered(1))

    return pl.pallas_call(
        functools.partial(feed_forward_kernel, steps, chunk),
        out_shape=(
            jax.ShapeDtypeStruct((rows, d), bf16),
            jax.ShapeDtypeStruct((rows, d), f32),
            jax.ShapeDtypeStruct((d // 4, 4 * rows), bf16),
            jax.ShapeDtypeStruct((n, 16, units // n), f32),
            jax.ShapeDtypeStruct((units, d), bf16),
            jax.ShapeDtypeStruct(halves[1:], bf16),
            jax.ShapeDtypeStruct(halves[1:], bf16),
            jax.ShapeDtypeStruct(out_halves[1:], bf16),
            jax.ShapeDtypeStruct(out_halves[1:], bf16),
        ),
        grid=(steps,),
        in_specs=[
            pl.BlockSpec(memory_space=pltpu.SMEM),
            lanes, tile, tile, once((d, d)), ANYWHERE, ANYWHERE,
        ]
        + [IN_VMEM] * len(vectors),
        out_specs=(
            tile, tile, ANYWHERE, once3((n, 16, units // n)), ANYWHERE,
            ANYWHERE, ANYWHERE, ANYWHERE, ANYWHERE,
        ),
        scratch_shapes=[
            pltpu.VMEM((d, units), bf16),
            pltpu.VMEM((units, d), bf16),
            pltpu.VMEM((units, d), bf16),
            pltpu.VMEM(halves, bf16),
            pltpu.VMEM(out_halves, bf16),
            pltpu.VMEM((d, rows), bf16),
            pltpu.VMEM((8, d), f32),
            pltpu.VMEM((8, units), f32),
            pltpu.VMEM((8, d), f32),
            pltpu.VMEM((8, units), f32),
            pltpu.VMEM((rows, units), bf16),
            pltpu.VMEM((rows, units), bf16),
            pltpu.VMEM((rows, d), bf16),
            pltpu.VMEM((rows, d), bf16),
            pltpu.VMEM((rows, d), bf16),
            pltpu.VMEM((d, rows), bf16),
            pltpu.VMEM((block, units), keep),
            pltpu.VMEM((block, units), keep),
            pltpu.SemaphoreType.DMA((2,)),
            pltpu.SemaphoreType.DMA((9,)),
            pltpu.SemaphoreType.DMA((steps,)),
        ]
        + dma_sems(3 * steps)
        + dma_sems(5),
        compiler_params=pltpu.CompilerParams(
            collective_id=4, has_side_effects=True, vmem_limit_bytes=62 * 2**20
        ),
        cost_estimate=pl.CostEstimate(
            flops=rows * d * (12 * units + 6 * d),
            bytes_accessed=4 * d * (4 * units + 2 * d) + 12 * rows * d,
            transcendentals=2 * rows * units,
        ),
        name="feed_forward",
    )(kept, ctx_t, tokens, cotangent, wo, we, wc, *vectors)


def local(
    tokens,
    output_cotangent,
    attention_weight,
    query_bias,
    value_bias,
    output_weight,
    output_bias,
    first_gain,
    first_shift,
    expand_weight,
    expand_bias,
    contract_weight,
    contract_bias,
    second_gain,
    second_shift,
    head_gate,
    hidden_gate,
    unit_gate,
    head_mask,
    hidden_mask,
    unit_mask,
    attention_mask,
    feedforward_mask,
    continuation_lengths,
):
    seq_count = lax.axis_size("seq")
    wt_count = lax.axis_size("wt")
    model_width = hidden_gate.shape[0]
    local_heads = head_gate.shape[0] // seq_count
    own_wide = model_width // wt_count
    tokens_all, own_weight, exp_quarter = gather_in(wt_count, tokens, attention_weight, expand_weight)
    contract_weight, own_weight = lax.optimization_barrier((contract_weight, own_weight))
    full_contract = lax.all_gather(contract_weight, "wt", axis=0, tiled=True)
    full_attention = lax.all_gather(attention_weight, "wt", axis=0, tiled=True)
    full_output = lax.all_gather(output_weight, "wt", axis=0, tiled=True)
    q, k, v, kt, own_context, log_sums, context_t, full_expand = attend(
        wt_count,
        continuation_lengths,
        attention_mask,
        head_gate,
        head_mask,
        query_bias,
        value_bias,
        tokens_all,
        own_weight.reshape(model_width, -1),
        exp_quarter,
        local_heads,
    )
    (
        layer_output,
        grad_total_one,
        grad_context_t,
        vec_sums,
        contract_weight_grad,
        *parts,
    ) = feed_forward(
        wt_count,
        feedforward_mask,
        context_t,
        tokens,
        output_cotangent,
        full_output,
        full_expand.reshape(model_width, -1),
        full_contract,
        output_bias,
        first_gain,
        first_shift,
        hidden_gate,
        hidden_mask,
        contract_bias,
        second_gain,
        second_shift,
        expand_bias,
        unit_gate,
        unit_mask,
    )
    con_piece = lax.psum_scatter(contract_weight_grad, "wt", scatter_dimension=0, tiled=True)
    pieces, projection_grad, exp_part, out_part, late_sums = attend_back(
        wt_count,
        continuation_lengths,
        attention_mask,
        head_gate,
        head_mask,
        q,
        k,
        v,
        kt,
        own_context,
        grad_context_t,
        log_sums,
        tokens_all,
        *parts,
    )
    tokens_grad, con_all, out_all, exp_all, att_all, vec_all, late_all = final(
        wt_count,
        grad_total_one,
        pieces,
        full_attention,
        con_piece.reshape(seq_count, own_wide, model_width),
        projection_grad,
        out_part,
        exp_part,
        vec_sums,
        late_sums,
    )
    con_sum, exp_sum, att_sum, tokens_grad, layer_output, out_sum, *rows = finish(
        wt_count,
        local_heads,
        head_gate,
        head_mask,
        con_all,
        exp_all,
        att_all,
        tokens_grad,
        layer_output,
        out_all,
        vec_all,
        late_all,
    )
    return (
        layer_output,
        tokens_grad,
        att_sum,
        rows[9],
        rows[10],
        out_sum,
        rows[S_OUT_BIAS],
        rows[S_GAIN1],
        rows[S_SHIFT1],
        exp_sum,
        rows[7],
        con_sum.reshape(seq_count * own_wide, model_width),
        rows[S_CON_BIAS],
        rows[S_GAIN2],
        rows[S_SHIFT2],
        rows[11],
        rows[S_HIDDEN],
        rows[8],
    )


def solution(mesh):
    return jax.shard_map(
        local,
        mesh=mesh,
        in_specs=(
            P(("wt", "seq"), None),
            P(("wt", "seq"), None),
            P("wt", None),
            P(),
            P(),
            P("wt", None),
            P(),
            P(),
            P(),
            P("wt", None),
            P(),
            P("wt", None),
            P(),
            P(),
            P(),
            P(),
            P(),
            P(),
            P(),
            P(),
            P(),
            P(),
            P(),
            P(),
        ),
        out_specs=(
            P(("wt", "seq"), None),
            P(("wt", "seq"), None),
            P("wt", None),
            P("wt"),
            P("wt"),
            P("wt", None),
            P("wt"),
            P("wt"),
            P("wt"),
            P("wt", None),
            P("wt"),
            P("wt", None),
            P("wt"),
            P("wt"),
            P("wt"),
            P(),
            P("wt"),
            P("wt"),
        ),
        check_vma=False,
    )
```

```python
import functools

import jax
import jax.numpy as jnp
from jax import lax
from jax.experimental import pallas as pl
from jax.experimental.pallas import tpu as pltpu
from jax.sharding import PartitionSpec as P

PROMPT = 1024
GRP_WT = 1
GLEN = 3072
SHORT = 512
LONG = 1536
HD = 64
TQ = 512
KC = 512

epsilon = 1e-06
score_scale = 0.125
exp2_scale = 0.125 * 1.4426950408889634
root_half = 0.7071067811865476
density_scale = 0.3989422804014327
bf16 = jnp.bfloat16
f32 = jnp.float32

NT = (((1,), (1,)), ((), ()))
NN = (((1,), (0,)), ((), ()))
TN = (((0,), (0,)), ((), ()))


def mm(a, b, dims=NN):
    return lax.dot_general(a, b, dims, preferred_element_type=f32)


def natural_at(short_first, i):
    other = jnp.where(i == 2, 5, i - 1)
    return jnp.where(short_first | (i < 2), i, other)


def ordered_at(short_first, j):
    other = jnp.where(j == 5, 2, j + 1)
    return jnp.where(short_first | (j < 2), j, other)


def query_tiles(tile):
    def prompt(i, carry):
        tile(i, ())
        return carry

    def longer(i, carry):
        tile(i, (3, 4, 5))
        return carry

    lax.fori_loop(0, 2, prompt, 0)
    tile(2, (2,))
    lax.fori_loop(3, 6, longer, 0)


def remote(src, dst, sems, k, peer):
    return pltpu.make_async_remote_copy(
        src_ref=src,
        dst_ref=dst,
        send_sem=sems[0].at[k],
        recv_sem=sems[1].at[k],
        device_id=peer,
        device_id_type=pl.DeviceIdType.MESH,
    )


def send(src, dst, sems, k, peer):
    copy = remote(src, dst, sems, k, peer)
    copy.start()
    return copy


def value_scale(head, group, kept_ref, gate_ref, mask_ref):
    return mask_ref[head].astype(f32) * gate_ref[head] * kept_ref[group].astype(f32)


def attend_kernel(
    heads, n, lens_ref, kept_ref, gate_ref, mask_ref, qb_ref, vb_ref, tok_hbm, w_hbm, exp_ref,
    q_o, k_o, v_o, kt_o, ctx_ref, lse_ref, full_ref, exp_all,
    tok_ref, w_ref, q_sc, k_sc, v_ref, kt_ref, vt_sc, ct_sc, vec_ref, exp_buf,
    local_sem, s_sem, r_sem, s_e, r_e,
):
    s, w = lax.axis_index("seq"), lax.axis_index("wt")
    others = [flip(s, k) for k in (1, 2, 3)]
    mate = (s, flip(w, 1))
    short_first = lens_ref[w, 0] == SHORT
    operands = [
        pltpu.make_async_copy(tok_hbm, tok_ref, local_sem.at[heads + 1]),
        pltpu.make_async_copy(w_hbm, w_ref, local_sem.at[heads + 2]),
    ]
    come = pltpu.make_async_copy(exp_ref, exp_buf, local_sem.at[heads])
    for copy in operands + [come]:
        copy.start()
    meet([(p, w) for p in others] + [mate])
    core, quarter = lax.rem(w, 2), exp_ref.shape[2]

    def exp_place(p):
        return exp_all.at[:, core, :, pl.ds(pl.multiple_of(p * quarter, 128), quarter)]

    spread = [
        send(exp_ref, exp_place(s), (s_e, r_e), k, (p, w)) for k, p in enumerate(others)
    ] + [send(exp_ref, exp_place(s), (s_e, r_e), 3, mate)]
    width = heads * HD
    count = GLEN // 4
    vec_ref[...] = jnp.zeros_like(vec_ref)
    for k in range(4):

        @pl.when(s == k)
        def _(k=k):
            query = qb_ref[...].astype(f32).reshape(1, 4 * width)
            value = vb_ref[...].astype(f32).reshape(1, 4 * width)
            for h in range(heads):
                own = slice(k * width + h * HD, k * width + (h + 1) * HD)
                at = 3 * HD * h
                vec_ref[0:1, at : at + HD] = query[:, own]
                vec_ref[0:1, at + 2 * HD : at + 3 * HD] = value[:, own]

    for h in range(heads):
        at = 3 * HD * h
        vec_ref[1:2, at : at + 2 * HD] = jnp.ones((1, 2 * HD), f32)
        scale = value_scale(s * heads + h, w, kept_ref, gate_ref, mask_ref)
        vec_ref[1:2, at + 2 * HD : at + 3 * HD] = jnp.full((1, HD), scale, f32)
    come.wait()
    own_part = pltpu.make_async_copy(exp_buf, exp_place(s), local_sem.at[heads])
    own_part.start()
    for copy in operands:
        copy.wait()

    def project(i, carry):
        rows = pl.ds(pl.multiple_of(i * TQ, TQ), TQ)
        x = mm(tok_ref[natural_at(short_first, i)], w_ref[...]) + vec_ref[0:1, :]
        x = (x * vec_ref[1:2, :]).astype(bf16)
        for h in range(heads):
            at = 3 * HD * h
            q_sc[h, rows, :] = x[:, at : at + HD]
            k = x[:, at + HD : at + 2 * HD]
            k_sc[h, rows, :] = k
            kt_ref[h, i] = k.T
            v = x[:, at + 2 * HD : at + 3 * HD]
            v_ref[h, rows, :] = v
            vt_sc[h, :, rows] = v.T
        return carry

    lax.fori_loop(0, GLEN // TQ, project, 0)
    handed = [
        pltpu.make_async_copy(src, dst, local_sem.at[heads + 3 + k])
        for k, (src, dst) in enumerate(((q_sc, q_o), (k_sc, k_o), (v_ref, v_o), (kt_ref, kt_o)))
    ]
    for copy in handed:
        copy.start()

    def leaving(h):
        rows = pl.ds(pl.multiple_of(h * HD, HD), HD)
        there = full_ref.at[pl.ds(pl.multiple_of(s * width + h * HD, HD), HD), :]

        def part(p):
            return ctx_ref.at[rows, pl.ds(pl.multiple_of(p * count, 128), count)]

        copies = [
            remote(part(p), there, (s_sem, r_sem), 3 * h + k, (p, w)) for k, p in enumerate(others)
        ]
        return copies, pltpu.make_async_copy(part(s), there, local_sem.at[h])

    passed = [
        (spread[k], remote(exp_place(p), exp_place(p), (s_e, r_e), 4 + k, mate))
        for k, p in enumerate(others)
    ]

    def one_head(h, carry):
        @pl.when(h == heads - 1)
        def _():
            for came, copy in passed:
                came.wait_recv()
                copy.start()

        def tile(i, own_blocks):
            rows = pl.ds(pl.multiple_of(i * TQ, TQ), TQ)
            q = q_sc[h, rows, :]
            s1 = mm(k_sc[h, 0:PROMPT, :], q, NT)
            top = jnp.max(s1, axis=0, keepdims=True)
            if own_blocks:
                own = slice(own_blocks[0] * KC, (own_blocks[-1] + 1) * KC)
                s2 = mm(k_sc[h, own, :], q, NT)
                top = jnp.maximum(top, jnp.max(s2, axis=0, keepdims=True))
            top = top * exp2_scale
            p1 = jnp.exp2(s1 * exp2_scale - top)
            o = mm(vt_sc[h, :, 0:PROMPT], p1.astype(bf16))
            total = jnp.sum(p1, axis=0, keepdims=True)
            if own_blocks:
                p2 = jnp.exp2(s2 * exp2_scale - top)
                o = o + mm(vt_sc[h, :, own], p2.astype(bf16))
                total = total + jnp.sum(p2, axis=0, keepdims=True)
            ct_sc[i] = (o / total).astype(bf16)
            lse_ref[h, :, rows] = top + jnp.log2(total)

        query_tiles(tile)

        def settle(j, carry):
            rows = pl.ds(pl.multiple_of(h * HD, HD), HD)
            lanes = pl.ds(pl.multiple_of(j * SHORT, SHORT), SHORT)
            ctx_ref[rows, lanes] = ct_sc[ordered_at(short_first, j)]
            return carry

        lax.fori_loop(0, GLEN // SHORT, settle, 0)
        copies, own = leaving(h)
        for copy in copies:
            copy.start()
        own.start()
        return carry

    lax.fori_loop(0, heads, one_head, 0)
    for copy in handed:
        copy.wait()
    own_part.wait()
    spread[3].wait_recv()
    for _, copy in passed:
        copy.wait()
    for copy in spread:
        copy.wait_send()
    for h in range(heads):
        copies, own = leaving(h)
        own.wait()
        for copy in copies:
            copy.wait()


def attend(n, lens, kept, gate, mask, query_bias, value_bias, tokens_all, weight, exp_part, heads):
    width = 3 * HD * heads
    return pl.pallas_call(
        functools.partial(attend_kernel, heads, n),
        out_shape=(
            jax.ShapeDtypeStruct((heads, GLEN, HD), bf16),
            jax.ShapeDtypeStruct((heads, GLEN, HD), bf16),
            jax.ShapeDtypeStruct((heads, GLEN, HD), bf16),
            jax.ShapeDtypeStruct((heads, GLEN // TQ, HD, TQ), bf16),
            jax.ShapeDtypeStruct((HD * heads, GLEN), bf16),
            jax.ShapeDtypeStruct((heads, 1, GLEN), f32),
            jax.ShapeDtypeStruct((4 * HD * heads, GLEN // 4), bf16),
            jax.ShapeDtypeStruct((n // 2, 2, exp_part.shape[1], 4 * exp_part.shape[2]), bf16),
        ),
        in_specs=[IN_SMEM] * 4 + [IN_VMEM] * 2 + [ANYWHERE] * 3,
        out_specs=(ANYWHERE,) * 4 + (IN_VMEM,) * 2 + (ANYWHERE, ANYWHERE),
        scratch_shapes=[
            pltpu.VMEM((GLEN // TQ, TQ, tokens_all.shape[1]), bf16),
            pltpu.VMEM(weight.shape, bf16),
            pltpu.VMEM((heads, GLEN, HD), bf16),
            pltpu.VMEM((heads, GLEN, HD), bf16),
            pltpu.VMEM((heads, GLEN, HD), bf16),
            pltpu.VMEM((heads, GLEN // TQ, HD, TQ), bf16),
            pltpu.VMEM((heads, HD, GLEN), bf16),
            pltpu.VMEM((GLEN // TQ, HD, TQ), bf16),
            pltpu.VMEM((2, width), f32),
            pltpu.VMEM(exp_part.shape, bf16),
            pltpu.SemaphoreType.DMA((heads + 7,)),
        ]
        + dma_sems(3 * heads)
        + dma_sems(7),
        compiler_params=remote_params(1),
        cost_estimate=pl.CostEstimate(
            flops=2 * GLEN * 768 * width + heads * 4 * 256 * 5767168,
            bytes_accessed=2 * GLEN * (768 + width),
            transcendentals=heads * 5767168,
        ),
        name="attend",
    )(
        lens, kept, gate, mask, query_bias, value_bias,
        tokens_all.reshape(GLEN // TQ, TQ, -1), weight, exp_part,
    )


def attend_back_kernel(
    heads, n, lens_ref, kept_ref, gate_ref, mask_ref, q_hbm, k_hbm, v_hbm, kt_hbm,
    ctx_hbm, gctx_hbm, lse_hbm, tok_hbm,
    e_own_hbm, e_got_hbm, o_own_hbm, o_got_hbm, pieces_o, dw_o, exp_o, out_o, late_o,
    ctx_ref, gctx_ref, lse_ref, tok_v, e_own, o_own, e_got, o_got, e_all, o_all, e_sum, o_sum, e_z, o_z, stage, late_sc, row_sc,
    q_all, k_all, v_all, kt_all, g_sc, g_nat, delta_sc, delta_nat, dqt_sc, dk_sc, dv_sc, acc,
    l_in, l_out, s_p, r_p, s_e, r_e, s_z, r_z,
):
    s, w = lax.axis_index("seq"), lax.axis_index("wt")
    others = [flip(s, k) for k in (1, 2, 3)]
    z, c, nz = w // 2, lax.rem(w, 2), n // 2
    far = [lax.rem(z + j, nz) for j in range(1, nz)]
    short_first = lens_ref[w, 0] == SHORT
    count = GLEN // 4
    width = heads * HD
    def taken(h):
        pairs = ((q_hbm, q_all), (k_hbm, k_all), (v_hbm, v_all), (kt_hbm, kt_all))
        return [
            pltpu.make_async_copy(src.at[h], dst.at[h], l_in.at[4 * h + k])
            for k, (src, dst) in enumerate(pairs)
        ]

    loads = [
        pltpu.make_async_copy(e_own_hbm, e_own, l_in.at[4 * heads]),
        pltpu.make_async_copy(e_got_hbm, e_got, l_in.at[4 * heads + 1]),
        pltpu.make_async_copy(o_own_hbm, o_own, l_in.at[4 * heads + 2]),
        pltpu.make_async_copy(o_got_hbm, o_got, l_in.at[4 * heads + 3]),
        pltpu.make_async_copy(tok_hbm, tok_v, l_in.at[4 * heads + 4]),
        pltpu.make_async_copy(ctx_hbm, ctx_ref, l_in.at[4 * heads + 5]),
        pltpu.make_async_copy(gctx_hbm, gctx_ref, l_in.at[4 * heads + 6]),
        pltpu.make_async_copy(lse_hbm, lse_ref, l_in.at[4 * heads + 7]),
    ]
    for copy in loads[:4] + loads[5:] + taken(0):
        copy.start()
    for h in range(1, heads):
        for copy in taken(h):
            copy.start()
    loads[4].start()
    meet([(p, w) for p in others] + [(s, 2 * k + c) for k in far])

    def leaving(h, own=False):
        if own:
            return pltpu.make_async_copy(stage.at[h, s], pieces_o.at[h, s], l_out.at[h])
        return [
            remote(stage.at[h, p], pieces_o.at[h, s], (s_p, r_p), 3 * h + k, (p, w))
            for k, p in enumerate(others)
        ]

    over_plane = [
        remote(e_got.at[p], e_all.at[s], (s_e, r_e), k, (p, w)) for k, p in enumerate(others)
    ] + [remote(o_got.at[p], o_all.at[s], (s_e, r_e), 3 + k, (p, w)) for k, p in enumerate(others)]
    over_z = [
        remote(e_sum.at[k], e_z.at[z], (s_z, r_z), j, (s, 2 * k + c)) for j, k in enumerate(far)
    ] + [
        remote(o_sum.at[k], o_z.at[z], (s_z, r_z), nz - 1 + j, (s, 2 * k + c))
        for j, k in enumerate(far)
    ]
    for copy in loads[:4]:
        copy.wait()

    def pair_sum(i, carry):
        q, k = i // nz, lax.rem(i, nz)
        e_got[q, k] = (e_got[q, k].astype(f32) + e_own[q, k].astype(f32)).astype(bf16)
        o_got[q, k] = (o_got[q, k].astype(f32) + o_own[q, k].astype(f32)).astype(bf16)
        return carry

    lax.fori_loop(0, 4 * nz, pair_sum, 0)
    for copy in over_plane:
        copy.start()
    e_all[s] = e_got[s]
    o_all[s] = o_got[s]
    late_sc[...] = jnp.zeros_like(late_sc)
    row_sc[...] = jnp.zeros_like(row_sc)
    for copy in loads[5:]:
        copy.wait()
    for h in range(heads):
        for copy in taken(h):
            copy.wait()

    def prologue(h):
        dk_sc[...] = jnp.zeros_like(dk_sc)
        dv_sc[...] = jnp.zeros_like(dv_sc)
        def inner(i, carry):
            lanes = pl.ds(pl.multiple_of(i * TQ, TQ), TQ)
            own = pl.ds(pl.multiple_of(h * HD, HD), HD)
            g_nat[i] = gctx_ref[own, lanes]
            product = g_nat[i].astype(f32) * ctx_ref[own, lanes].astype(f32)
            delta_nat[i] = jnp.sum(product, axis=0, keepdims=True)
            return carry

        def order(i, carry):
            g_sc[i] = g_nat[natural_at(short_first, i)]
            delta_sc[i] = delta_nat[natural_at(short_first, i)]
            return carry

        lax.fori_loop(0, GLEN // TQ, inner, 0)
        lax.fori_loop(0, GLEN // TQ, order, 0)

    def halfway():
        for copy in over_plane:
            copy.wait_recv()

        def add4(ref, k):
            t = [ref[q, k].astype(f32) for q in range(4)]
            return ((t[0] + t[1]) + (t[2] + t[3])).astype(bf16)

        def plane_sum(k, carry):
            e_sum[k] = add4(e_all, k)
            o_sum[k] = add4(o_all, k)
            return carry

        lax.fori_loop(0, nz, plane_sum, 0)
        for copy in over_z:
            copy.start()
        e_z[z] = e_sum[z]
        o_z[z] = o_sum[z]

    def epilogue(h, first, last):
        half = SHORT // 2
        scale = value_scale(s * heads + h, w, kept_ref, gate_ref, mask_ref)

        def settle(j, carry):
            i = ordered_at(short_first, j)
            dq = dqt_sc[i].astype(bf16)
            dk = (dk_sc[i] * score_scale).astype(bf16).T
            dv = dv_sc[i].astype(bf16).astype(f32)
            gate = jnp.sum(dv * v_all[h, i].astype(f32), axis=0, keepdims=True)
            dv = (dv * scale).astype(bf16)
            row_sc[h, 0:1, :] += jnp.sum(dv.astype(f32), axis=0, keepdims=True)
            row_sc[h, 1:2, :] += gate
            dv = dv.T
            x = dq.astype(f32)
            late_sc[h] += (x[:, 0:128] + x[:, 128:256]) + (x[:, 256:384] + x[:, 384:512])
            for r in range(2):
                u = 2 * j + r
                p, there = u // 3, pl.ds(pl.multiple_of(lax.rem(u, 3) * half, half), half)
                cols = slice(r * half, (r + 1) * half)
                stage[h, p, 0:HD, there] = dq[:, cols]
                stage[h, p, HD : 2 * HD, there] = dk[:, cols]
                stage[h, p, 2 * HD : 3 * HD, there] = dv[:, cols]
            return carry

        lax.fori_loop(first, last, settle, 0)
        for p, copy in zip(others, leaving(h), strict=True):

            @pl.when(p // 2 == (0 if first == 0 else 1))
            def _(copy=copy):
                copy.start()

        if first == 0:
            leaving(h, True).start()

    def tile_of(h):
        def tile(i, own_blocks):
            q = q_all[h, i]
            g = g_sc[i]
            lse = lse_ref[h, :, pl.ds(pl.multiple_of(i * TQ, TQ), TQ)]
            delta = delta_sc[i]
            dq = jnp.zeros((HD, TQ), f32)
            for j in (0, 1) + own_blocks:
                sc = mm(k_all[h, j], q, NT)
                p = jnp.exp2(sc * exp2_scale - lse)
                dp = mm(v_all[h, j], g)
                ds = (p * (dp - delta)).astype(bf16)
                dv_sc[j] += mm(p.astype(bf16), g, NT)
                dk_sc[j] += mm(ds, q)
                dq = dq + mm(kt_all[h, j], ds)
            dqt_sc[i] = dq * score_scale

        return tile

    def one_head(h, carry):
        prologue(h)
        def longer(i, carry):
            tile_of(h)(i, (3, 4, 5))
            return carry

        def prompt(i, carry):
            tile_of(h)(i, ())
            return carry

        tile_of(h)(2, (2,))
        pl.when(h == heads - 1)(halfway)

        lax.fori_loop(3, 6, longer, 0)
        epilogue(h, 2, 6)
        lax.fori_loop(0, 2, prompt, 0)
        epilogue(h, 0, 2)
        return carry

    lax.fori_loop(0, heads, one_head, 0)
    loads[4].wait()
    acc[...] = jnp.zeros_like(acc)

    def weight_grad(p, carry):
        x = tok_v[pl.ds(pl.multiple_of(p * count, count), count), :]
        for h in range(heads):
            acc[3 * HD * h : 3 * HD * (h + 1), :] += mm(stage[h, p], x)
        return carry

    lax.fori_loop(0, 4, weight_grad, 0)
    own_rows = dw_o.shape[1]
    grad = acc[...].T.astype(bf16)
    for k in range(n):
        dw_o[k] = grad[k * own_rows : (k + 1) * own_rows, :]
    late_o[...] = jnp.zeros_like(late_o)
    for h in range(heads):
        own = slice(HD * h, HD * (h + 1))
        late_o[0:1, own] = jnp.sum(late_sc[h].T, axis=0, keepdims=True)
        late_o[1:3, own] = row_sc[h, 0:2, :]
    for copy in over_z:
        copy.wait_recv()
    for ref, out in ((e_z, exp_o), (o_z, out_o)):
        total = ref[0].astype(f32)
        for k in range(1, nz):
            total = total + ref[k].astype(f32)
        out[...] = total.astype(bf16)
    for h in range(heads):
        for copy in [leaving(h, True)] + leaving(h):
            copy.wait()
    for copy in over_plane + over_z:
        copy.wait_send()


def attend_back(n, lens, kept, gate, mask, q, k, v, kt, ctx, g, lse, tokens_all, *parts):
    heads = q.shape[0]
    width = 3 * HD * heads
    d = tokens_all.shape[1]
    count = GLEN // 4
    nz = n // 2
    own, wide = parts[0].shape[2:]
    part = parts[2].shape[3]
    blocks = GLEN // TQ
    rows64 = pltpu.VMEM((heads, blocks, TQ, HD), bf16)
    blocks64 = pltpu.VMEM((blocks, HD, TQ), bf16)
    quarters = [pltpu.VMEM(parts[0].shape, bf16), pltpu.VMEM(parts[2].shape, bf16)]
    return pl.pallas_call(
        functools.partial(attend_back_kernel, heads, n),
        out_shape=(
            jax.ShapeDtypeStruct((heads, 4, 3 * HD, count), bf16),
            jax.ShapeDtypeStruct((n, d // n, width), bf16),
            jax.ShapeDtypeStruct((own, wide), bf16),
            jax.ShapeDtypeStruct((own, part), bf16),
            jax.ShapeDtypeStruct((8, HD * heads), f32),
        ),
        in_specs=[IN_SMEM] * 4
        + [ANYWHERE] * 4
        + [ANYWHERE] * 8,
        out_specs=(ANYWHERE, IN_VMEM, IN_VMEM, IN_VMEM, IN_VMEM),
        scratch_shapes=[
            pltpu.VMEM(ctx.shape, bf16),
            pltpu.VMEM(g.shape, bf16),
            pltpu.VMEM(lse.shape, f32),
            pltpu.VMEM(tokens_all.shape, bf16),
        ]
        + quarters * 3
        + [pltpu.VMEM((nz, own, wide), bf16), pltpu.VMEM((nz, own, part), bf16)] * 2
        + [pltpu.VMEM((heads, 4, 3 * HD, count), bf16), pltpu.VMEM((heads, HD, 128), f32)]
        + [pltpu.VMEM((heads, 8, HD), f32)]
        + [
            rows64,
            rows64,
            rows64,
            pltpu.VMEM(kt.shape, bf16),
            blocks64,
            blocks64,
            pltpu.VMEM((blocks, 1, TQ), f32),
            pltpu.VMEM((blocks, 1, TQ), f32),
            pltpu.VMEM((blocks, HD, TQ), f32),
            pltpu.VMEM((blocks, TQ, HD), f32),
            pltpu.VMEM((blocks, TQ, HD), f32),
            pltpu.VMEM((width, d), f32),
            pltpu.SemaphoreType.DMA((4 * heads + 8,)),
            pltpu.SemaphoreType.DMA((heads,)),
        ]
        + dma_sems(3 * heads)
        + dma_sems(6)
        + dma_sems(2 * nz - 2),
        compiler_params=remote_params(2),
        cost_estimate=pl.CostEstimate(
            flops=heads * 10 * 256 * 5767168 + 2 * GLEN * d * width,
            bytes_accessed=2 * GLEN * (3 * width + d),
            transcendentals=heads * 5767168,
        ),
        name="attend_back",
    )(
        lens, kept, gate, mask,
        *(x.reshape(heads, blocks, TQ, HD) for x in (q, k, v)),
        kt, ctx, g, lse, tokens_all, *parts,
    )


def meet(peers):
    barrier = pltpu.get_barrier_semaphore()
    for peer in peers:
        pl.semaphore_signal(barrier, inc=1, device_id=peer, device_id_type=pl.DeviceIdType.MESH)
    pl.semaphore_wait(barrier, len(peers))


def flip(index, bits):
    for bit in (1, 2):
        if bits & bit:
            index = index + bit - 2 * bit * ((index // bit) % 2)
    return index


def remote_params(number):
    return pltpu.CompilerParams(
        collective_id=number, has_side_effects=True, vmem_limit_bytes=56 * 2**20
    )


ANYWHERE = pl.BlockSpec(memory_space=pl.ANY)
IN_VMEM = pl.BlockSpec(memory_space=pltpu.VMEM)
IN_SMEM = pl.BlockSpec(memory_space=pltpu.SMEM)


def dma_sems(count):
    return [pltpu.SemaphoreType.DMA((count,)), pltpu.SemaphoreType.DMA((count,))]


def gather_kernel(
    n, tok_ref, weight_ref, exp_ref, tok_all, cols_all, exp_all, tok_buf, cols_buf, exp_buf,
    local_sem, s_tok, r_tok, s_w, r_w, s_f, r_f, s_e, r_e,
):
    s, w = lax.axis_index("seq"), lax.axis_index("wt")
    rows = tok_ref.shape[0]
    half = rows // 2
    wide = cols_buf.shape[1]
    for k in range(4):

        @pl.when(s == k)
        def _(k=k):
            cols_buf[...] = weight_ref[:, k * wide : (k + 1) * wide]

    by_x, by_y, mate = (flip(s, 1), w), (flip(s, 2), w), (s, flip(w, 1))
    far = [(s, lax.rem(w + 2 * j, n)) for j in range(1, n // 2)]
    quarter = exp_buf.shape[1]
    exp_own = exp_ref.at[:, pl.ds(pl.multiple_of(s * quarter, 128), quarter)]
    come = [
        pltpu.make_async_copy(tok_ref, tok_buf, local_sem.at[0]),
        pltpu.make_async_copy(exp_own, exp_buf, local_sem.at[2]),
    ]
    for copy in come:
        copy.start()
    meet([by_x, by_y, mate] + far)

    def part(owner, k):
        return pl.ds(pl.multiple_of(owner * rows + k * half, half), half)

    tok = (s_tok, r_tok)
    first = [pl.ds(0, half), pl.ds(half, half)]
    x0 = send(tok_ref.at[first[0]], tok_all.at[part(s, 0)], tok, 0, by_x)
    y1 = send(tok_ref.at[first[1]], tok_all.at[part(s, 1)], tok, 1, by_y)
    x1 = send(tok_ref.at[first[1]], tok_all.at[part(s, 1)], tok, 2, by_x)
    y0 = send(tok_ref.at[first[0]], tok_all.at[part(s, 0)], tok, 3, by_y)
    held = [
        send(cols_buf, cols_all.at[w], (s_w, r_w), k, peer) for k, peer in enumerate(far + [mate])
    ]
    along = [
        send(exp_own, exp_all.at[w // 2], (s_e, r_e), k, peer) for k, peer in enumerate(far)
    ]
    for copy in come:
        copy.wait()
    own = [
        pltpu.make_async_copy(exp_buf, exp_all.at[w // 2], local_sem.at[2]),
        pltpu.make_async_copy(
            tok_buf, tok_all.at[pl.ds(pl.multiple_of(s * rows, rows), rows)], local_sem.at[0]
        ),
        pltpu.make_async_copy(cols_buf, cols_all.at[w], local_sem.at[1]),
    ]
    for copy in own:
        copy.start()
    passed = []
    for j in range(1, n // 2):
        origin = lax.rem(w + n - 2 * j, n)
        held[j - 1].wait_recv()
        passed.append(send(cols_all.at[origin], cols_all.at[origin], (s_f, r_f), j - 1, mate))
    x0.wait_recv()
    there = tok_all.at[part(flip(s, 1), 0)]
    passed.append(send(there, there, tok, 4, by_y))
    y1.wait_recv()
    there = tok_all.at[part(flip(s, 2), 1)]
    passed.append(send(there, there, tok, 5, by_x))
    for copy in own:
        copy.wait()
    for copy in [x1, y0, held[-1]] + passed + along:
        copy.wait_recv()
    for copy in [x0, x1, y0, y1] + held + passed + along:
        copy.wait_send()


def gather_in(n, tokens, attention_weight, expand_weight):
    rows, d = tokens.shape
    own, width = attention_weight.shape
    quarter = expand_weight.shape[1] // 4
    return pl.pallas_call(
        functools.partial(gather_kernel, n),
        out_shape=(
            jax.ShapeDtypeStruct((4 * rows, d), bf16),
            jax.ShapeDtypeStruct((n, own, width // 4), bf16),
            jax.ShapeDtypeStruct((n // 2, own, quarter), bf16),
        ),
        in_specs=[ANYWHERE, IN_VMEM, ANYWHERE],
        out_specs=(ANYWHERE,) * 3,
        scratch_shapes=[
            pltpu.VMEM(tokens.shape, bf16),
            pltpu.VMEM((own, width // 4), bf16),
            pltpu.VMEM((own, quarter), bf16),
            pltpu.SemaphoreType.DMA((3,)),
        ]
        + dma_sems(6)
        + dma_sems(n // 2)
        + dma_sems(n // 2 - 1)
        + dma_sems(n // 2 - 1),
        compiler_params=remote_params(0),
        name="gather_in",
    )(tokens, attention_weight, expand_weight)


def final_kernel(
    heads, n, base_hbm, pieces_hbm, w_hbm, con_ref, att_ref, out_ref, exp_ref, vec_ref, late_ref,
    tok_hbm, g_con, g_out, g_exp, g_att, r_vec2, r_late2,
    tok_o, base_v, pieces_v, w_v, a_own, r_con, h_att, m_att, r_att, r_vec, r_late,
    l_in, *sems,
):
    s, w = lax.axis_index("seq"), lax.axis_index("wt")
    z, c = w // 2, lax.rem(w, 2)
    nz = n // 2
    others = [flip(s, k) for k in (1, 2, 3)]
    seq_peers = [(p, w) for p in others]
    mate = (s, flip(w, 1))
    wt_peers = [(s, lax.rem(w + j, n)) for j in range(1, n)]
    names = ("pair", "vec", "late", "con", "out2", "att", "vec2", "late2", "con2", "exp2", "att2")
    sem = {name: (sems[2 * k], sems[2 * k + 1]) for k, name in enumerate(names)}
    loads = [
        pltpu.make_async_copy(src, dst, l_in.at[k])
        for k, (src, dst) in enumerate(((pieces_hbm, pieces_v), (w_hbm, w_v), (base_hbm, base_v)))
    ]
    first = [pltpu.make_async_copy(con_ref.at[s], r_con.at[s], l_in.at[3])] + [
        pltpu.make_async_copy(att_ref.at[2 * k + c], a_own.at[k], l_in.at[4 + k]) for k in range(nz)
    ]
    for copy in first + loads:
        copy.start()
    meet(seq_peers + wt_peers)
    pair = [send(att_ref.at[2 * k + 1 - c], h_att.at[k], sem["pair"], k, mate) for k in range(nz)]
    cons = [send(con_ref.at[p], r_con.at[s], sem["con"], k, (p, w)) for k, p in enumerate(others)]
    far = [lax.rem(z + j, nz) for j in range(1, nz)]
    exp2 = [send(exp_ref, g_exp.at[s], sem["exp2"], k, p) for k, p in enumerate(seq_peers)]
    out2 = [send(out_ref, g_out.at[s], sem["out2"], k, p) for k, p in enumerate(seq_peers)]
    vecs = [
        send(vec_ref.at[lax.rem(w + j, n)], r_vec.at[w], sem["vec"], j - 1, wt_peers[j - 1])
        for j in range(1, n)
    ]
    lates = [send(late_ref, r_late.at[w], sem["late"], j, p) for j, p in enumerate(wt_peers)]
    g_exp[s] = exp_ref[...]
    r_vec[w] = vec_ref[w]
    r_late[w] = late_ref[...]
    g_out[s] = out_ref[...]
    for copy in first:
        copy.wait()
    for copy in pair:
        copy.wait_recv()
    for k in range(nz):
        m_att[k] = (a_own[k].astype(f32) + h_att[k].astype(f32)).astype(bf16)
    atts = [send(m_att.at[k], r_att.at[z], sem["att"], j, (s, 2 * k + c)) for j, k in enumerate(far)]
    r_att[z] = m_att[z]
    for copy in loads:
        copy.wait()
    cols = 3 * HD
    rows = tok_o.shape[0]
    block = rows // 3

    def total_of(ref, count):
        total = ref[0].astype(f32)
        for k in range(1, count):
            total = total + ref[k].astype(f32)
        return total

    own = [ref.at[s] for ref in (g_con, r_vec2, r_late2, g_att)]
    con2, vec2, late2, att2 = (
        [remote(ref, ref, sem[name], k, p) for k, p in enumerate(seq_peers)]
        for ref, name in zip(own, ("con2", "vec2", "late2", "att2"), strict=True)
    )

    def given(i):
        there = pl.ds(pl.multiple_of(i * block, block), block)
        return pltpu.make_async_copy(tok_o.at[there], tok_hbm.at[there], l_in.at[4 + nz + i])

    def tokens_block(i, carry):
        there = pl.ds(pl.multiple_of(i * block, block), block)
        total = base_v[there, :]
        for h in range(heads):
            for k in range(4):
                at = (heads * k + h) * cols
                total = total + mm(pieces_v[h, k, :, there].T, w_v[:, at : at + cols], NT)
        tok_o[there, :] = total
        given(i).start()

        @pl.when(i == 0)
        def _():
            for copy in cons:
                copy.wait_recv()
            g_con[s] = total_of(r_con, 4).astype(bf16)
            for copy in con2:
                copy.start()
            for copy in vecs + lates:
                copy.wait_recv()
            r_vec2[s] = total_of(r_vec, n)
            r_late2[s] = total_of(r_late, n)
            for copy in vec2 + late2:
                copy.start()

        @pl.when(i == 1)
        def _():
            for copy in atts:
                copy.wait_recv()
            g_att[s] = total_of(r_att, nz).astype(bf16)
            for copy in att2:
                copy.start()

        return carry

    lax.fori_loop(0, 3, tokens_block, 0)
    for i in range(3):
        given(i).wait()
    for copy in out2 + con2 + vec2 + late2 + exp2 + att2:
        copy.wait_recv()
    for copy in pair + cons + vecs + lates + atts + con2 + vec2 + late2 + exp2 + out2 + att2:
        copy.wait_send()


def final(n, base, pieces, weight, con, att, out, exp_part, vec, late):
    heads = pieces.shape[0]
    r, d = con.shape[1:]
    cols = att.shape[2]
    nz = n // 2
    counts = (nz, n - 1, n - 1, 3, 3, nz - 1, 3, 3, 3, 3, 3)
    return pl.pallas_call(
        functools.partial(final_kernel, heads, n),
        out_shape=(
            jax.ShapeDtypeStruct(base.shape, f32),
            jax.ShapeDtypeStruct((4, r, d), bf16),
            jax.ShapeDtypeStruct((4,) + out.shape, bf16),
            jax.ShapeDtypeStruct((4,) + exp_part.shape, bf16),
            jax.ShapeDtypeStruct((4, r, cols), bf16),
            jax.ShapeDtypeStruct((4,) + vec.shape[1:], f32),
            jax.ShapeDtypeStruct((4,) + late.shape, f32),
        ),
        in_specs=[ANYWHERE] * 5 + [IN_VMEM] * 4,
        out_specs=(ANYWHERE,) + (IN_VMEM,) * 6,
        scratch_shapes=[
            pltpu.VMEM(base.shape, f32),
            pltpu.VMEM(base.shape, f32),
            pltpu.VMEM(pieces.shape, bf16),
            pltpu.VMEM(weight.shape, bf16),
            pltpu.VMEM((nz, r, cols), bf16),
            pltpu.VMEM((4, r, d), bf16),
            pltpu.VMEM((nz, r, cols), bf16),
            pltpu.VMEM((nz, r, cols), bf16),
            pltpu.VMEM((nz, r, cols), bf16),
            pltpu.VMEM((n,) + vec.shape[1:], f32),
            pltpu.VMEM((n,) + late.shape, f32),
            pltpu.SemaphoreType.DMA((7 + nz,)),
        ]
        + [sem for count in counts for sem in dma_sems(count)],
        compiler_params=remote_params(3),
        cost_estimate=pl.CostEstimate(
            flops=8 * base.shape[0] * d * cols, bytes_accessed=8 * d * cols, transcendentals=0
        ),
        name="final",
    )(base, pieces, weight, con, att, out, exp_part, vec, late)


def finish_kernel(n, heads, gate_ref, mask_ref, *refs):
    sources, rest = refs[:8], refs[8:]
    con_o, exp_o, att_o, tok_o, low_o, out_o = rest[:6]
    vec_os, unit_os, query_o, value_o, gate_o = rest[6:13], rest[13:15], rest[15], rest[16], rest[17]
    con_v, exp_v, att_v, tok_v, low_v, out_v, vec_v, late_v, con_f, exp_f, att_f, l_in, l_out = rest[18:]
    inside = (con_v, exp_v, att_v, tok_v, low_v, out_v, vec_v, late_v)
    loads = [
        pltpu.make_async_copy(src, dst, l_in.at[k])
        for k, (src, dst) in enumerate(zip(sources, inside, strict=True))
    ]
    for copy in loads:
        copy.start()
    outside = ((con_f, con_o), (exp_f, exp_o), (att_f, att_o), (tok_v, tok_o), (low_v, low_o))
    stores = [pltpu.make_async_copy(src, dst, l_out.at[k]) for k, (src, dst) in enumerate(outside)]

    def add4(parts):
        return (parts[0] + parts[1]) + (parts[2] + parts[3])

    wide, cols, part = exp_v.shape[2], att_v.shape[2], out_v.shape[2]
    loads[0].wait()
    con_f[...] = con_v[...].astype(f32)
    stores[0].start()
    loads[1].wait()
    for k in range(4):
        exp_f[:, k * wide : (k + 1) * wide] = exp_v[k].astype(f32)
    stores[1].start()
    loads[2].wait()
    for k in range(4):
        att_f[:, k * cols : (k + 1) * cols] = att_v[k].astype(f32)
    stores[2].start()
    for k in (3, 4):
        loads[k].wait()
        stores[k].start()
    for copy in loads[5:]:
        copy.wait()
    for k in range(4):
        out_o[:, k * part : (k + 1) * part] = out_v[k].astype(f32)
    vec = add4([vec_v[k] for k in range(4)])
    own = vec_os[0].shape[0]
    for k, ref in enumerate(vec_os):
        ref[...] = vec[k, 0:own]
    for k, ref in enumerate(unit_os):
        ref[...] = vec[8 + k]
    rows = [jnp.concatenate([late_v[k, j : j + 1, :] for k in range(4)], axis=1) for j in range(2)]
    for k in range(n):

        @pl.when(lax.axis_index("wt") == k)
        def _(k=k):
            query_o[...] = rows[0][0, k * own : (k + 1) * own]
            value_o[...] = rows[1][0, k * own : (k + 1) * own]

    gates = []
    for k in range(4):
        for h in range(heads):
            part_sum = jnp.sum(late_v[k, 2:3, HD * h : HD * (h + 1)], axis=1, keepdims=True)
            kept = mask_ref[heads * k + h].astype(f32) / gate_ref[heads * k + h]
            gates.append(part_sum * kept)
    gate_o[...] = jnp.concatenate(gates, axis=1)[0]
    for copy in stores:
        copy.wait()


def finish(n, heads, gate, mask, con, exp_all, att, tok, low, out, vec, late):
    r = out.shape[1]
    wide, cols, part = exp_all.shape[2], att.shape[2], out.shape[2]
    units = vec.shape[2]
    row = jax.ShapeDtypeStruct((r,), f32)
    con_f, exp_f, att_f = (
        con.shape,
        (r, 4 * wide),
        (r, 4 * cols),
    )
    return pl.pallas_call(
        functools.partial(finish_kernel, n, heads),
        out_shape=(
            jax.ShapeDtypeStruct(con_f, f32),
            jax.ShapeDtypeStruct(exp_f, f32),
            jax.ShapeDtypeStruct(att_f, f32),
            jax.ShapeDtypeStruct(tok.shape, f32),
            jax.ShapeDtypeStruct(low.shape, low.dtype),
            jax.ShapeDtypeStruct((r, 4 * part), f32),
        )
        + (row,) * 7
        + (jax.ShapeDtypeStruct((units,), f32),) * 2
        + (row,) * 2
        + (jax.ShapeDtypeStruct((4 * heads,), f32),),
        in_specs=[IN_SMEM] * 2 + [ANYWHERE] * 8,
        out_specs=(ANYWHERE,) * 5 + (IN_VMEM,) * 13,
        scratch_shapes=[
            pltpu.VMEM(x.shape, x.dtype) for x in (con, exp_all, att, tok, low, out, vec, late)
        ]
        + [pltpu.VMEM(x, f32) for x in (con_f, exp_f, att_f)]
        + [pltpu.SemaphoreType.DMA((8,)), pltpu.SemaphoreType.DMA((5,))],
        compiler_params=pltpu.CompilerParams(vmem_limit_bytes=56 * 2**20),
        name="finish",
    )(gate, mask, con, exp_all, att, tok, low, out, vec, late)


(OUT_BIAS, GAIN1, SHIFT1, HIDDEN_SCALE, CON_BIAS, GAIN2, SHIFT2, HIDDEN_MASK) = range(8)
(S_OUT_BIAS, S_GAIN1, S_SHIFT1, S_CON_BIAS, S_GAIN2, S_SHIFT2, S_HIDDEN) = range(7)


def gelu_parts(x):
    bell = jnp.exp(-0.5 * (x * x))
    t = 1.0 / (1.0 + (0.3275911 * root_half) * jnp.abs(x))
    poly = t * (
        0.127414796 + t * (-0.142248368 + t * (0.7107068705 + t * (-0.7265760135 + t * 0.5307027145)))
    )
    tail = poly * bell
    cumulative = jnp.where(x < 0.0, tail, 1.0 - tail)
    return x * cumulative, cumulative + x * bell * density_scale


def norm_parts(summed):
    centre = summed - jnp.mean(summed, axis=-1, keepdims=True)
    inverse = lax.rsqrt(jnp.mean(centre * centre, axis=-1, keepdims=True) + epsilon)
    return (centre * inverse, inverse)


def norm_back(grad_normed, normed, inverse):
    return inverse * (
        grad_normed
        - jnp.mean(grad_normed, axis=-1, keepdims=True)
        - normed * jnp.mean(grad_normed * normed, axis=-1, keepdims=True)
    )


def feed_forward_kernel(
    steps, chunk,
    kept_ref, ctx_ref, tok_ref, cot_ref, wo_ref, we_hbm, wc_hbm,
    ob_ref, g1_ref, t1_ref, hg_ref, hm_ref, cb_ref, g2_ref, t2_ref, eb_ref, ug_ref, um_ref,
    lo_ref, dt1_ref, g_all, vec_ref, dwc_hbm, e_own, e_got, o_own, o_got,
    we_ref, wc_ref, dwc_ref, dwe_ref, dwo_ref, g_sc,
    wide_ref, unit_ref, sw_ref, su_ref, act_sc, gh_sc, low_sc, gb_sc, ga_sc, ctx_sc, gelu_sc, slope_sc,
    l_w, l_o, l_g, s_g, r_g, s_p, r_p,
):
    i = pl.program_id(0)
    block = tok_ref.shape[0]
    units = we_ref.shape[1]
    rows = pl.ds(pl.multiple_of(i * block, block), block)
    s, w = lax.axis_index("seq"), lax.axis_index("wt")
    others = [flip(s, k) for k in (1, 2, 3)]
    mate, core = (s, flip(w, 1)), lax.rem(w, 2)
    part_rows = g_all.shape[0]
    weights = [
        pltpu.make_async_copy(we_hbm, we_ref, l_w.at[0]),
        pltpu.make_async_copy(wc_hbm, wc_ref, l_w.at[1]),
    ]

    def leaving(t):
        there = g_all.at[:, pl.ds(pl.multiple_of((s * steps + t) * block, 128), block)]

        def part(p):
            lanes = pl.ds(pl.multiple_of(t * block, 128), block)
            return g_sc.at[pl.ds(pl.multiple_of(p * part_rows, 16), part_rows), lanes]

        copies = [
            remote(part(p), there, (s_g, r_g), 3 * t + k, (p, w)) for k, p in enumerate(others)
        ]
        return copies + [pltpu.make_async_copy(part(s), there, l_g.at[t])]

    @pl.when(i == 0)
    def _():
        for copy in weights:
            copy.start()
        meet([(p, w) for p in others] + [mate])
        sw_ref[...] = jnp.zeros_like(sw_ref)
        su_ref[...] = jnp.zeros_like(su_ref)

        def row(ref):
            return ref[...].astype(f32).reshape(1, ref.shape[0])

        plain = ((OUT_BIAS, ob_ref), (GAIN1, g1_ref), (SHIFT1, t1_ref), (CON_BIAS, cb_ref))
        for k, ref in plain + ((GAIN2, g2_ref), (SHIFT2, t2_ref), (HIDDEN_MASK, hm_ref)):
            wide_ref[k : k + 1, :] = row(ref)
        wide_ref[HIDDEN_SCALE : HIDDEN_SCALE + 1, :] = row(hm_ref) * row(hg_ref)
        kept = row(um_ref) * kept_ref[lax.axis_index("wt")].astype(f32)
        unit_ref[0:1, :] = row(eb_ref)
        unit_ref[1:2, :] = kept * row(ug_ref)
        unit_ref[2:3, :] = kept

    def wide(k):
        return wide_ref[k : k + 1, :]

    def add_sum(ref, k, cols, value):
        ref[k : k + 1, cols] += jnp.sum(value, axis=0, keepdims=True)

    full = slice(None)
    ctx = ctx_ref[...]
    ctx_sc[:, rows] = ctx
    summed = mm(ctx, wo_ref[...], TN) + wide(OUT_BIAS) + tok_ref[...].astype(f32)
    n1, inv1 = norm_parts(summed)
    s1 = n1 * wide(GAIN1) + wide(SHIFT1)
    hs = wide(HIDDEN_SCALE)
    first = s1 * hs
    low = first.astype(bf16)
    low_sc[rows, :] = low
    branch = first + wide(CON_BIAS)

    @pl.when(i == 0)
    def _():
        for copy in weights:
            copy.wait()

    for j in range(units // chunk):
        cols = slice(j * chunk, (j + 1) * chunk)
        hidden = mm(low, we_ref[:, cols]) + unit_ref[0:1, cols]
        gelu, slope = gelu_parts(hidden)
        scale = unit_ref[1:2, cols]
        gelu_sc[:, cols] = gelu.astype(gelu_sc.dtype)
        slope_sc[:, cols] = (slope * scale).astype(slope_sc.dtype)
        act = (gelu * scale).astype(bf16)
        act_sc[rows, cols] = act
        branch = branch + mm(act, wc_ref[cols, :])
    n2, inv2 = norm_parts(branch)
    s2 = n2 * wide(GAIN2) + wide(SHIFT2)
    lo_ref[...] = (s2 * hs).astype(bf16)
    dy = cot_ref[...].astype(f32)
    e2 = dy * hs
    add_sum(sw_ref, S_GAIN2, full, e2 * n2)
    add_sum(sw_ref, S_SHIFT2, full, e2)
    dt2 = norm_back(e2 * wide(GAIN2), n2, inv2)
    gb = dt2.astype(bf16)
    gb_sc[rows, :] = gb
    add_sum(sw_ref, S_CON_BIAS, full, gb.astype(f32))
    d_first = dt2
    for j in range(units // chunk):
        cols = slice(j * chunk, (j + 1) * chunk)
        d_act = mm(gb, wc_ref[cols, :], NT)
        add_sum(su_ref, 1, cols, d_act * gelu_sc[:, cols].astype(f32))
        gh = d_act * slope_sc[:, cols].astype(f32)
        add_sum(su_ref, 0, cols, gh)
        gh = gh.astype(bf16)
        gh_sc[rows, cols] = gh
        d_first = d_first + mm(gh, we_ref[:, cols], NT)
    e1 = d_first * hs
    add_sum(sw_ref, S_GAIN1, full, e1 * n1)
    add_sum(sw_ref, S_SHIFT1, full, e1)
    add_sum(sw_ref, S_HIDDEN, full, dy * s2 + d_first * s1)
    dt1 = norm_back(e1 * wide(GAIN1), n1, inv1)
    dt1_ref[...] = dt1
    ga = dt1.astype(bf16)
    ga_sc[rows, :] = ga
    add_sum(sw_ref, S_OUT_BIAS, full, ga.astype(f32))
    g_sc[:, rows] = mm(wo_ref[...], ga, NT).astype(bf16)
    for copy in leaving(i):
        copy.start()

    @pl.when(i == steps - 1)
    def _():
        own, wide_cols = dwe_ref.shape[3:]

        def weight_grads(j, carry):
            cols = pl.ds(pl.multiple_of(j * wide_cols, 128), wide_cols)
            dwc_ref[cols, :] = mm(act_sc[:, cols], gb_sc[...], TN).astype(bf16)
            part = mm(low_sc[...], gh_sc[:, cols], TN).astype(bf16)
            for k in range(2 * dwe_ref.shape[2]):
                dwe_ref[k % 2, j, k // 2] = part[k * own : (k + 1) * own]
            for copy in given(j):
                copy.start()
            return carry

        def given(j):
            there = pl.ds(pl.multiple_of(j * wide_cols, 128), wide_cols)
            return [
                pltpu.make_async_copy(dwc_ref.at[there], dwc_hbm.at[there], l_o.at[j]),
                pltpu.make_async_copy(dwe_ref.at[core, j], e_own.at[j], l_o.at[4 + j]),
                remote(dwe_ref.at[1 - core, j], e_got.at[j], (s_p, r_p), j, mate),
            ]

        part_cols = dwo_ref.shape[4]
        for q in range(4):
            part = mm(ctx_sc[...], ga_sc[:, q * part_cols : (q + 1) * part_cols]).astype(bf16)
            for k in range(2 * dwo_ref.shape[2]):
                dwo_ref[k % 2, q, k // 2] = part[k * own : (k + 1) * own]
        over = [
            pltpu.make_async_copy(dwo_ref.at[core], o_own, l_o.at[8]),
            remote(dwo_ref.at[1 - core], o_got, (s_p, r_p), 4, mate),
        ]
        for copy in over:
            copy.start()
        lax.fori_loop(0, 4, weight_grads, 0)
        vec_ref[...] = jnp.zeros_like(vec_ref)
        sw_ref[S_HIDDEN : S_HIDDEN + 1, :] *= wide(HIDDEN_MASK)
        su_ref[1:2, :] *= unit_ref[2:3, :]
        own_wide, own_units = dwe_ref.shape[3], vec_ref.shape[2]
        for k in range(vec_ref.shape[0]):
            vec_ref[k, 0:8, 0:own_wide] = sw_ref[:, k * own_wide : (k + 1) * own_wide]
            vec_ref[k, 8:16, :] = su_ref[:, k * own_units : (k + 1) * own_units]
        for t in range(steps):
            for copy in leaving(t):
                copy.wait()
        for copy in over:
            copy.wait()
        for j in range(4):
            for copy in given(j):
                copy.wait()


def feed_forward(n, kept, ctx_t, tokens, cotangent, wo, we, wc, *vectors):
    steps, chunk, keep = 3, 768, f32
    rows, d = tokens.shape
    units = we.shape[1]
    block = rows // steps
    halves = (2, 4, n // 2, d // n, units // 4)
    out_halves = (2, 4, n // 2, d // n, d // 4)
    tile = pl.BlockSpec((block, d), lambda i: (i, 0))
    lanes = pl.BlockSpec((d, block), lambda i: (0, i))

    def once(shape):
        return pl.BlockSpec(shape, lambda i: (0, 0), pipeline_mode=pl.Buffered(1))

    def once3(shape):
        return pl.BlockSpec(shape, lambda i: (0, 0, 0), pipeline_mode=pl.Buffered(1))

    return pl.pallas_call(
        functools.partial(feed_forward_kernel, steps, chunk),
        out_shape=(
            jax.ShapeDtypeStruct((rows, d), bf16),
            jax.ShapeDtypeStruct((rows, d), f32),
            jax.ShapeDtypeStruct((d // 4, 4 * rows), bf16),
            jax.ShapeDtypeStruct((n, 16, units // n), f32),
            jax.ShapeDtypeStruct((units, d), bf16),
            jax.ShapeDtypeStruct(halves[1:], bf16),
            jax.ShapeDtypeStruct(halves[1:], bf16),
            jax.ShapeDtypeStruct(out_halves[1:], bf16),
            jax.ShapeDtypeStruct(out_halves[1:], bf16),
        ),
        grid=(steps,),
        in_specs=[
            pl.BlockSpec(memory_space=pltpu.SMEM),
            lanes, tile, tile, once((d, d)), ANYWHERE, ANYWHERE,
        ]
        + [IN_VMEM] * len(vectors),
        out_specs=(
            tile, tile, ANYWHERE, once3((n, 16, units // n)), ANYWHERE,
            ANYWHERE, ANYWHERE, ANYWHERE, ANYWHERE,
        ),
        scratch_shapes=[
            pltpu.VMEM((d, units), bf16),
            pltpu.VMEM((units, d), bf16),
            pltpu.VMEM((units, d), bf16),
            pltpu.VMEM(halves, bf16),
            pltpu.VMEM(out_halves, bf16),
            pltpu.VMEM((d, rows), bf16),
            pltpu.VMEM((8, d), f32),
            pltpu.VMEM((8, units), f32),
            pltpu.VMEM((8, d), f32),
            pltpu.VMEM((8, units), f32),
            pltpu.VMEM((rows, units), bf16),
            pltpu.VMEM((rows, units), bf16),
            pltpu.VMEM((rows, d), bf16),
            pltpu.VMEM((rows, d), bf16),
            pltpu.VMEM((rows, d), bf16),
            pltpu.VMEM((d, rows), bf16),
            pltpu.VMEM((block, units), keep),
            pltpu.VMEM((block, units), keep),
            pltpu.SemaphoreType.DMA((2,)),
            pltpu.SemaphoreType.DMA((9,)),
            pltpu.SemaphoreType.DMA((steps,)),
        ]
        + dma_sems(3 * steps)
        + dma_sems(5),
        compiler_params=pltpu.CompilerParams(
            collective_id=4, has_side_effects=True, vmem_limit_bytes=62 * 2**20
        ),
        cost_estimate=pl.CostEstimate(
            flops=rows * d * (12 * units + 6 * d),
            bytes_accessed=4 * d * (4 * units + 2 * d) + 12 * rows * d,
            transcendentals=2 * rows * units,
        ),
        name="feed_forward",
    )(kept, ctx_t, tokens, cotangent, wo, we, wc, *vectors)


def local(
    tokens,
    output_cotangent,
    attention_weight,
    query_bias,
    value_bias,
    output_weight,
    output_bias,
    first_gain,
    first_shift,
    expand_weight,
    expand_bias,
    contract_weight,
    contract_bias,
    second_gain,
    second_shift,
    head_gate,
    hidden_gate,
    unit_gate,
    head_mask,
    hidden_mask,
    unit_mask,
    attention_mask,
    feedforward_mask,
    continuation_lengths,
):
    seq_count = lax.axis_size("seq")
    wt_count = lax.axis_size("wt")
    model_width = hidden_gate.shape[0]
    local_heads = head_gate.shape[0] // seq_count
    own_wide = model_width // wt_count
    tokens_all, own_weight, exp_quarter = gather_in(wt_count, tokens, attention_weight, expand_weight)
    contract_weight, own_weight = lax.optimization_barrier((contract_weight, own_weight))
    full_contract = lax.all_gather(contract_weight, "wt", axis=0, tiled=True)
    full_attention = lax.all_gather(attention_weight, "wt", axis=0, tiled=True)
    full_output = lax.all_gather(output_weight, "wt", axis=0, tiled=True)
    q, k, v, kt, own_context, log_sums, context_t, full_expand = attend(
        wt_count,
        continuation_lengths,
        attention_mask,
        head_gate,
        head_mask,
        query_bias,
        value_bias,
        tokens_all,
        own_weight.reshape(model_width, -1),
        exp_quarter,
        local_heads,
    )
    (
        layer_output,
        grad_total_one,
        grad_context_t,
        vec_sums,
        contract_weight_grad,
        *parts,
    ) = feed_forward(
        wt_count,
        feedforward_mask,
        context_t,
        tokens,
        output_cotangent,
        full_output,
        full_expand.reshape(model_width, -1),
        full_contract,
        output_bias,
        first_gain,
        first_shift,
        hidden_gate,
        hidden_mask,
        contract_bias,
        second_gain,
        second_shift,
        expand_bias,
        unit_gate,
        unit_mask,
    )
    con_piece = lax.psum_scatter(contract_weight_grad, "wt", scatter_dimension=0, tiled=True)
    pieces, projection_grad, exp_part, out_part, late_sums = attend_back(
        wt_count,
        continuation_lengths,
        attention_mask,
        head_gate,
        head_mask,
        q,
        k,
        v,
        kt,
        own_context,
        grad_context_t,
        log_sums,
        tokens_all,
        *parts,
    )
    tokens_grad, con_all, out_all, exp_all, att_all, vec_all, late_all = final(
        wt_count,
        grad_total_one,
        pieces,
        full_attention,
        con_piece.reshape(seq_count, own_wide, model_width),
        projection_grad,
        out_part,
        exp_part,
        vec_sums,
        late_sums,
    )
    con_sum, exp_sum, att_sum, tokens_grad, layer_output, out_sum, *rows = finish(
        wt_count,
        local_heads,
        head_gate,
        head_mask,
        con_all,
        exp_all,
        att_all,
        tokens_grad,
        layer_output,
        out_all,
        vec_all,
        late_all,
    )
    return (
        layer_output,
        tokens_grad,
        att_sum,
        rows[9],
        rows[10],
        out_sum,
        rows[S_OUT_BIAS],
        rows[S_GAIN1],
        rows[S_SHIFT1],
        exp_sum,
        rows[7],
        con_sum.reshape(seq_count * own_wide, model_width),
        rows[S_CON_BIAS],
        rows[S_GAIN2],
        rows[S_SHIFT2],
        rows[11],
        rows[S_HIDDEN],
        rows[8],
    )


def solution(mesh):
    return jax.shard_map(
        local,
        mesh=mesh,
        in_specs=(
            P(("wt", "seq"), None),
            P(("wt", "seq"), None),
            P("wt", None),
            P(),
            P(),
            P("wt", None),
            P(),
            P(),
            P(),
            P("wt", None),
            P(),
            P("wt", None),
            P(),
            P(),
            P(),
            P(),
            P(),
            P(),
            P(),
            P(),
            P(),
            P(),
            P(),
            P(),
        ),
        out_specs=(
            P(("wt", "seq"), None),
            P(("wt", "seq"), None),
            P("wt", None),
            P("wt"),
            P("wt"),
            P("wt", None),
            P("wt"),
            P("wt"),
            P("wt"),
            P("wt", None),
            P("wt"),
            P("wt", None),
            P("wt"),
            P("wt"),
            P("wt"),
            P(),
            P("wt"),
            P("wt"),
        ),
        check_vma=False,
    )
```

```python
import functools

import jax
import jax.numpy as jnp
from jax import lax
from jax.experimental import pallas as pl
from jax.experimental.pallas import tpu as pltpu
from jax.sharding import PartitionSpec as P

PROMPT = 1024
GRP_WT = 1
GLEN = 3072
SHORT = 512
LONG = 1536
HD = 64
TQ = 512
KC = 512

epsilon = 1e-06
score_scale = 0.125
exp2_scale = 0.125 * 1.4426950408889634
root_half = 0.7071067811865476
density_scale = 0.3989422804014327
bf16 = jnp.bfloat16
f32 = jnp.float32

NT = (((1,), (1,)), ((), ()))
NN = (((1,), (0,)), ((), ()))
TN = (((0,), (0,)), ((), ()))


def mm(a, b, dims=NN):
    return lax.dot_general(a, b, dims, preferred_element_type=f32)


def natural_at(short_first, i):
    other = jnp.where(i == 2, 5, i - 1)
    return jnp.where(short_first | (i < 2), i, other)


def ordered_at(short_first, j):
    other = jnp.where(j == 5, 2, j + 1)
    return jnp.where(short_first | (j < 2), j, other)


def query_tiles(tile):
    def prompt(i, carry):
        tile(i, ())
        return carry

    def longer(i, carry):
        tile(i, (3, 4, 5))
        return carry

    lax.fori_loop(0, 2, prompt, 0)
    tile(2, (2,))
    lax.fori_loop(3, 6, longer, 0)


def remote(src, dst, sems, k, peer):
    return pltpu.make_async_remote_copy(
        src_ref=src,
        dst_ref=dst,
        send_sem=sems[0].at[k],
        recv_sem=sems[1].at[k],
        device_id=peer,
        device_id_type=pl.DeviceIdType.MESH,
    )


def send(src, dst, sems, k, peer):
    copy = remote(src, dst, sems, k, peer)
    copy.start()
    return copy


def value_scale(head, group, kept_ref, gate_ref, mask_ref):
    return mask_ref[head].astype(f32) * gate_ref[head] * kept_ref[group].astype(f32)


def attend_kernel(
    heads, n, lens_ref, kept_ref, gate_ref, mask_ref, qb_ref, vb_ref, tok_hbm, w_hbm, exp_ref,
    q_o, k_o, v_o, kt_o, ctx_o, lse_ref, full_ref, exp_all,
    ctx_ref, tok_ref, w_ref, q_sc, k_sc, v_ref, kt_ref, vt_sc, ct_sc, vec_ref, exp_buf,
    local_sem, s_sem, r_sem, s_e, r_e,
):
    s, w = lax.axis_index("seq"), lax.axis_index("wt")
    others = [flip(s, k) for k in (1, 2, 3)]
    mate = (s, flip(w, 1))
    short_first = lens_ref[w, 0] == SHORT
    operands = [
        pltpu.make_async_copy(tok_hbm, tok_ref, local_sem.at[heads + 1]),
        pltpu.make_async_copy(w_hbm, w_ref, local_sem.at[heads + 2]),
    ]
    come = pltpu.make_async_copy(exp_ref, exp_buf, local_sem.at[heads])
    for copy in operands + [come]:
        copy.start()
    meet([(p, w) for p in others] + [mate])
    core, quarter = lax.rem(w, 2), exp_ref.shape[2]

    def exp_place(p):
        return exp_all.at[:, core, :, pl.ds(pl.multiple_of(p * quarter, 128), quarter)]

    spread = [
        send(exp_ref, exp_place(s), (s_e, r_e), k, (p, w)) for k, p in enumerate(others)
    ] + [send(exp_ref, exp_place(s), (s_e, r_e), 3, mate)]
    width = heads * HD
    count = GLEN // 4
    vec_ref[...] = jnp.zeros_like(vec_ref)
    for k in range(4):

        @pl.when(s == k)
        def _(k=k):
            query = qb_ref[...].astype(f32).reshape(1, 4 * width)
            value = vb_ref[...].astype(f32).reshape(1, 4 * width)
            for h in range(heads):
                own = slice(k * width + h * HD, k * width + (h + 1) * HD)
                at = 3 * HD * h
                vec_ref[0:1, at : at + HD] = query[:, own]
                vec_ref[0:1, at + 2 * HD : at + 3 * HD] = value[:, own]

    for h in range(heads):
        at = 3 * HD * h
        vec_ref[1:2, at : at + 2 * HD] = jnp.ones((1, 2 * HD), f32)
        scale = value_scale(s * heads + h, w, kept_ref, gate_ref, mask_ref)
        vec_ref[1:2, at + 2 * HD : at + 3 * HD] = jnp.full((1, HD), scale, f32)
    come.wait()
    own_part = pltpu.make_async_copy(exp_buf, exp_place(s), local_sem.at[heads])
    own_part.start()
    for copy in operands:
        copy.wait()

    def project(i, carry):
        rows = pl.ds(pl.multiple_of(i * TQ, TQ), TQ)
        x = mm(tok_ref[natural_at(short_first, i)], w_ref[...]) + vec_ref[0:1, :]
        x = (x * vec_ref[1:2, :]).astype(bf16)
        for h in range(heads):
            at = 3 * HD * h
            q_sc[h, rows, :] = x[:, at : at + HD]
            k = x[:, at + HD : at + 2 * HD]
            k_sc[h, rows, :] = k
            kt_ref[h, i] = k.T
            v = x[:, at + 2 * HD : at + 3 * HD]
            v_ref[h, rows, :] = v
            vt_sc[h, :, rows] = v.T
        return carry

    lax.fori_loop(0, GLEN // TQ, project, 0)
    handed = [
        pltpu.make_async_copy(src, dst, local_sem.at[heads + 3 + k])
        for k, (src, dst) in enumerate(((q_sc, q_o), (k_sc, k_o), (v_ref, v_o), (kt_ref, kt_o)))
    ]
    for copy in handed:
        copy.start()

    def stays(h):
        rows = pl.ds(pl.multiple_of(h * HD, HD), HD)
        return pltpu.make_async_copy(ctx_ref.at[rows], ctx_o.at[rows], local_sem.at[heads + 7 + h])

    def leaving(h):
        rows = pl.ds(pl.multiple_of(h * HD, HD), HD)
        there = full_ref.at[pl.ds(pl.multiple_of(s * width + h * HD, HD), HD), :]

        def part(p):
            return ctx_ref.at[rows, pl.ds(pl.multiple_of(p * count, 128), count)]

        copies = [
            remote(part(p), there, (s_sem, r_sem), 3 * h + k, (p, w)) for k, p in enumerate(others)
        ]
        return copies, pltpu.make_async_copy(part(s), there, local_sem.at[h])

    passed = [
        (spread[k], remote(exp_place(p), exp_place(p), (s_e, r_e), 4 + k, mate))
        for k, p in enumerate(others)
    ]

    def one_head(h, carry):
        @pl.when(h == heads - 1)
        def _():
            for came, copy in passed:
                came.wait_recv()
                copy.start()

        def tile(i, own_blocks):
            rows = pl.ds(pl.multiple_of(i * TQ, TQ), TQ)
            q = q_sc[h, rows, :]
            s1 = mm(k_sc[h, 0:PROMPT, :], q, NT)
            top = jnp.max(s1, axis=0, keepdims=True)
            if own_blocks:
                own = slice(own_blocks[0] * KC, (own_blocks[-1] + 1) * KC)
                s2 = mm(k_sc[h, own, :], q, NT)
                top = jnp.maximum(top, jnp.max(s2, axis=0, keepdims=True))
            top = top * exp2_scale
            p1 = jnp.exp2(s1 * exp2_scale - top)
            o = mm(vt_sc[h, :, 0:PROMPT], p1.astype(bf16))
            total = jnp.sum(p1, axis=0, keepdims=True)
            if own_blocks:
                p2 = jnp.exp2(s2 * exp2_scale - top)
                o = o + mm(vt_sc[h, :, own], p2.astype(bf16))
                total = total + jnp.sum(p2, axis=0, keepdims=True)
            ct_sc[i] = (o / total).astype(bf16)
            lse_ref[h, :, rows] = top + jnp.log2(total)

        query_tiles(tile)

        def settle(j, carry):
            rows = pl.ds(pl.multiple_of(h * HD, HD), HD)
            lanes = pl.ds(pl.multiple_of(j * SHORT, SHORT), SHORT)
            ctx_ref[rows, lanes] = ct_sc[ordered_at(short_first, j)]
            return carry

        lax.fori_loop(0, GLEN // SHORT, settle, 0)
        copies, own = leaving(h)
        for copy in copies:
            copy.start()
        own.start()
        stays(h).start()
        return carry

    lax.fori_loop(0, heads, one_head, 0)
    for copy in handed:
        copy.wait()
    own_part.wait()
    spread[3].wait_recv()
    for _, copy in passed:
        copy.wait()
    for copy in spread:
        copy.wait_send()
    for h in range(heads):
        stays(h).wait()
        copies, own = leaving(h)
        own.wait()
        for copy in copies:
            copy.wait()


def attend(n, lens, kept, gate, mask, query_bias, value_bias, tokens_all, weight, exp_part, heads):
    width = 3 * HD * heads
    return pl.pallas_call(
        functools.partial(attend_kernel, heads, n),
        out_shape=(
            jax.ShapeDtypeStruct((heads, GLEN, HD), bf16),
            jax.ShapeDtypeStruct((heads, GLEN, HD), bf16),
            jax.ShapeDtypeStruct((heads, GLEN, HD), bf16),
            jax.ShapeDtypeStruct((heads, GLEN // TQ, HD, TQ), bf16),
            jax.ShapeDtypeStruct((HD * heads, GLEN), bf16),
            jax.ShapeDtypeStruct((heads, 1, GLEN), f32),
            jax.ShapeDtypeStruct((4 * HD * heads, GLEN // 4), bf16),
            jax.ShapeDtypeStruct((n // 2, 2, exp_part.shape[1], 4 * exp_part.shape[2]), bf16),
        ),
        in_specs=[IN_SMEM] * 4 + [IN_VMEM] * 2 + [ANYWHERE] * 3,
        out_specs=(ANYWHERE,) * 5 + (IN_VMEM,) + (ANYWHERE, ANYWHERE),
        scratch_shapes=[
            pltpu.VMEM((HD * heads, GLEN), bf16),
            pltpu.VMEM((GLEN // TQ, TQ, tokens_all.shape[1]), bf16),
            pltpu.VMEM(weight.shape, bf16),
            pltpu.VMEM((heads, GLEN, HD), bf16),
            pltpu.VMEM((heads, GLEN, HD), bf16),
            pltpu.VMEM((heads, GLEN, HD), bf16),
            pltpu.VMEM((heads, GLEN // TQ, HD, TQ), bf16),
            pltpu.VMEM((heads, HD, GLEN), bf16),
            pltpu.VMEM((GLEN // TQ, HD, TQ), bf16),
            pltpu.VMEM((2, width), f32),
            pltpu.VMEM(exp_part.shape, bf16),
            pltpu.SemaphoreType.DMA((2 * heads + 7,)),
        ]
        + dma_sems(3 * heads)
        + dma_sems(7),
        compiler_params=remote_params(1),
        cost_estimate=pl.CostEstimate(
            flops=2 * GLEN * 768 * width + heads * 4 * 256 * 5767168,
            bytes_accessed=2 * GLEN * (768 + width),
            transcendentals=heads * 5767168,
        ),
        name="attend",
    )(
        lens, kept, gate, mask, query_bias, value_bias,
        tokens_all.reshape(GLEN // TQ, TQ, -1), weight, exp_part,
    )


def attend_back_kernel(
    heads, n, lens_ref, kept_ref, gate_ref, mask_ref, q_hbm, k_hbm, v_hbm, kt_hbm,
    ctx_hbm, gctx_hbm, lse_hbm, tok_hbm,
    e_own_hbm, e_got_hbm, o_own_hbm, o_got_hbm, pieces_o, dw_o, exp_o, out_o, late_o,
    ctx_ref, gctx_ref, lse_ref, tok_v, e_own, o_own, e_got, o_got, e_all, o_all, e_sum, o_sum, e_z, o_z, stage, late_sc, row_sc,
    q_all, k_all, v_all, kt_all, g_sc, g_nat, delta_sc, delta_nat, dqt_sc, dk_sc, dv_sc, acc,
    l_in, l_out, s_p, r_p, s_e, r_e, s_z, r_z,
):
    s, w = lax.axis_index("seq"), lax.axis_index("wt")
    others = [flip(s, k) for k in (1, 2, 3)]
    z, c, nz = w // 2, lax.rem(w, 2), n // 2
    far = [lax.rem(z + j, nz) for j in range(1, nz)]
    short_first = lens_ref[w, 0] == SHORT
    count = GLEN // 4
    width = heads * HD
    def taken(h):
        pairs = ((q_hbm, q_all), (k_hbm, k_all), (v_hbm, v_all), (kt_hbm, kt_all))
        return [
            pltpu.make_async_copy(src.at[h], dst.at[h], l_in.at[4 * h + k])
            for k, (src, dst) in enumerate(pairs)
        ]

    loads = [
        pltpu.make_async_copy(e_own_hbm, e_own, l_in.at[4 * heads]),
        pltpu.make_async_copy(e_got_hbm, e_got, l_in.at[4 * heads + 1]),
        pltpu.make_async_copy(o_own_hbm, o_own, l_in.at[4 * heads + 2]),
        pltpu.make_async_copy(o_got_hbm, o_got, l_in.at[4 * heads + 3]),
        pltpu.make_async_copy(tok_hbm, tok_v, l_in.at[4 * heads + 4]),
        pltpu.make_async_copy(ctx_hbm, ctx_ref, l_in.at[4 * heads + 5]),
        pltpu.make_async_copy(gctx_hbm, gctx_ref, l_in.at[4 * heads + 6]),
        pltpu.make_async_copy(lse_hbm, lse_ref, l_in.at[4 * heads + 7]),
    ]
    for copy in loads[:4] + loads[5:] + taken(0):
        copy.start()
    for h in range(1, heads):
        for copy in taken(h):
            copy.start()
    loads[4].start()
    meet([(p, w) for p in others] + [(s, 2 * k + c) for k in far])

    def leaving(h, own=False):
        if own:
            return pltpu.make_async_copy(stage.at[h, s], pieces_o.at[h, s], l_out.at[h])
        return [
            remote(stage.at[h, p], pieces_o.at[h, s], (s_p, r_p), 3 * h + k, (p, w))
            for k, p in enumerate(others)
        ]

    over_plane = [
        remote(e_got.at[p], e_all.at[s], (s_e, r_e), k, (p, w)) for k, p in enumerate(others)
    ] + [remote(o_got.at[p], o_all.at[s], (s_e, r_e), 3 + k, (p, w)) for k, p in enumerate(others)]
    over_z = [
        remote(e_sum.at[k], e_z.at[z], (s_z, r_z), j, (s, 2 * k + c)) for j, k in enumerate(far)
    ] + [
        remote(o_sum.at[k], o_z.at[z], (s_z, r_z), nz - 1 + j, (s, 2 * k + c))
        for j, k in enumerate(far)
    ]
    for copy in loads[:4]:
        copy.wait()

    def pair_sum(i, carry):
        q, k = i // nz, lax.rem(i, nz)
        e_got[q, k] = (e_got[q, k].astype(f32) + e_own[q, k].astype(f32)).astype(bf16)
        o_got[q, k] = (o_got[q, k].astype(f32) + o_own[q, k].astype(f32)).astype(bf16)
        return carry

    lax.fori_loop(0, 4 * nz, pair_sum, 0)
    for copy in over_plane:
        copy.start()
    e_all[s] = e_got[s]
    o_all[s] = o_got[s]
    late_sc[...] = jnp.zeros_like(late_sc)
    row_sc[...] = jnp.zeros_like(row_sc)
    for copy in loads[5:]:
        copy.wait()
    for h in range(heads):
        for copy in taken(h):
            copy.wait()

    def prologue(h):
        dk_sc[...] = jnp.zeros_like(dk_sc)
        dv_sc[...] = jnp.zeros_like(dv_sc)
        def inner(i, carry):
            lanes = pl.ds(pl.multiple_of(i * TQ, TQ), TQ)
            own = pl.ds(pl.multiple_of(h * HD, HD), HD)
            g_nat[i] = gctx_ref[own, lanes]
            product = g_nat[i].astype(f32) * ctx_ref[own, lanes].astype(f32)
            delta_nat[i] = jnp.sum(product, axis=0, keepdims=True)
            return carry

        def order(i, carry):
            g_sc[i] = g_nat[natural_at(short_first, i)]
            delta_sc[i] = delta_nat[natural_at(short_first, i)]
            return carry

        lax.fori_loop(0, GLEN // TQ, inner, 0)
        lax.fori_loop(0, GLEN // TQ, order, 0)

    def halfway():
        for copy in over_plane:
            copy.wait_recv()

        def add4(ref, k):
            t = [ref[q, k].astype(f32) for q in range(4)]
            return ((t[0] + t[1]) + (t[2] + t[3])).astype(bf16)

        def plane_sum(k, carry):
            e_sum[k] = add4(e_all, k)
            o_sum[k] = add4(o_all, k)
            return carry

        lax.fori_loop(0, nz, plane_sum, 0)
        for copy in over_z:
            copy.start()
        e_z[z] = e_sum[z]
        o_z[z] = o_sum[z]

    def epilogue(h, first, last):
        half = SHORT // 2
        scale = value_scale(s * heads + h, w, kept_ref, gate_ref, mask_ref)

        def settle(j, carry):
            i = ordered_at(short_first, j)
            dq = dqt_sc[i].astype(bf16)
            dk = (dk_sc[i] * score_scale).astype(bf16).T
            dv = dv_sc[i].astype(bf16).astype(f32)
            gate = jnp.sum(dv * v_all[h, i].astype(f32), axis=0, keepdims=True)
            dv = (dv * scale).astype(bf16)
            row_sc[h, 0:1, :] += jnp.sum(dv.astype(f32), axis=0, keepdims=True)
            row_sc[h, 1:2, :] += gate
            dv = dv.T
            x = dq.astype(f32)
            late_sc[h] += (x[:, 0:128] + x[:, 128:256]) + (x[:, 256:384] + x[:, 384:512])
            for r in range(2):
                u = 2 * j + r
                p, there = u // 3, pl.ds(pl.multiple_of(lax.rem(u, 3) * half, half), half)
                cols = slice(r * half, (r + 1) * half)
                stage[h, p, 0:HD, there] = dq[:, cols]
                stage[h, p, HD : 2 * HD, there] = dk[:, cols]
                stage[h, p, 2 * HD : 3 * HD, there] = dv[:, cols]
            return carry

        lax.fori_loop(first, last, settle, 0)
        for p, copy in zip(others, leaving(h), strict=True):

            @pl.when(p // 2 == (0 if first == 0 else 1))
            def _(copy=copy):
                copy.start()

        if first == 0:
            leaving(h, True).start()

    def tile_of(h):
        def tile(i, own_blocks):
            q = q_all[h, i]
            g = g_sc[i]
            lse = lse_ref[h, :, pl.ds(pl.multiple_of(i * TQ, TQ), TQ)]
            delta = delta_sc[i]
            dq = jnp.zeros((HD, TQ), f32)
            for j in (0, 1) + own_blocks:
                sc = mm(k_all[h, j], q, NT)
                p = jnp.exp2(sc * exp2_scale - lse)
                dp = mm(v_all[h, j], g)
                ds = (p * (dp - delta)).astype(bf16)
                dv_sc[j] += mm(p.astype(bf16), g, NT)
                dk_sc[j] += mm(ds, q)
                dq = dq + mm(kt_all[h, j], ds)
            dqt_sc[i] = dq * score_scale

        return tile

    def one_head(h, carry):
        prologue(h)
        def longer(i, carry):
            tile_of(h)(i, (3, 4, 5))
            return carry

        def prompt(i, carry):
            tile_of(h)(i, ())
            return carry

        tile_of(h)(2, (2,))
        pl.when(h == heads - 1)(halfway)

        lax.fori_loop(3, 6, longer, 0)
        epilogue(h, 2, 6)
        lax.fori_loop(0, 2, prompt, 0)
        epilogue(h, 0, 2)
        return carry

    lax.fori_loop(0, heads, one_head, 0)
    loads[4].wait()
    acc[...] = jnp.zeros_like(acc)

    def weight_grad(p, carry):
        x = tok_v[pl.ds(pl.multiple_of(p * count, count), count), :]
        for h in range(heads):
            acc[3 * HD * h : 3 * HD * (h + 1), :] += mm(stage[h, p], x)
        return carry

    lax.fori_loop(0, 4, weight_grad, 0)
    own_rows = dw_o.shape[1]
    grad = acc[...].T.astype(bf16)
    for k in range(n):
        dw_o[k] = grad[k * own_rows : (k + 1) * own_rows, :]
    late_o[...] = jnp.zeros_like(late_o)
    for h in range(heads):
        own = slice(HD * h, HD * (h + 1))
        late_o[0:1, own] = jnp.sum(late_sc[h].T, axis=0, keepdims=True)
        late_o[1:3, own] = row_sc[h, 0:2, :]
    for copy in over_z:
        copy.wait_recv()
    for ref, out in ((e_z, exp_o), (o_z, out_o)):
        total = ref[0].astype(f32)
        for k in range(1, nz):
            total = total + ref[k].astype(f32)
        out[...] = total.astype(bf16)
    for h in range(heads):
        for copy in [leaving(h, True)] + leaving(h):
            copy.wait()
    for copy in over_plane + over_z:
        copy.wait_send()


def attend_back(n, lens, kept, gate, mask, q, k, v, kt, ctx, g, lse, tokens_all, *parts):
    heads = q.shape[0]
    width = 3 * HD * heads
    d = tokens_all.shape[1]
    count = GLEN // 4
    nz = n // 2
    own, wide = parts[0].shape[2:]
    part = parts[2].shape[3]
    blocks = GLEN // TQ
    rows64 = pltpu.VMEM((heads, blocks, TQ, HD), bf16)
    blocks64 = pltpu.VMEM((blocks, HD, TQ), bf16)
    quarters = [pltpu.VMEM(parts[0].shape, bf16), pltpu.VMEM(parts[2].shape, bf16)]
    return pl.pallas_call(
        functools.partial(attend_back_kernel, heads, n),
        out_shape=(
            jax.ShapeDtypeStruct((heads, 4, 3 * HD, count), bf16),
            jax.ShapeDtypeStruct((n, d // n, width), bf16),
            jax.ShapeDtypeStruct((own, wide), bf16),
            jax.ShapeDtypeStruct((own, part), bf16),
            jax.ShapeDtypeStruct((8, HD * heads), f32),
        ),
        in_specs=[IN_SMEM] * 4
        + [ANYWHERE] * 4
        + [ANYWHERE] * 8,
        out_specs=(ANYWHERE, IN_VMEM, IN_VMEM, IN_VMEM, IN_VMEM),
        scratch_shapes=[
            pltpu.VMEM(ctx.shape, bf16),
            pltpu.VMEM(g.shape, bf16),
            pltpu.VMEM(lse.shape, f32),
            pltpu.VMEM(tokens_all.shape, bf16),
        ]
        + quarters * 3
        + [pltpu.VMEM((nz, own, wide), bf16), pltpu.VMEM((nz, own, part), bf16)] * 2
        + [pltpu.VMEM((heads, 4, 3 * HD, count), bf16), pltpu.VMEM((heads, HD, 128), f32)]
        + [pltpu.VMEM((heads, 8, HD), f32)]
        + [
            rows64,
            rows64,
            rows64,
            pltpu.VMEM(kt.shape, bf16),
            blocks64,
            blocks64,
            pltpu.VMEM((blocks, 1, TQ), f32),
            pltpu.VMEM((blocks, 1, TQ), f32),
            pltpu.VMEM((blocks, HD, TQ), f32),
            pltpu.VMEM((blocks, TQ, HD), f32),
            pltpu.VMEM((blocks, TQ, HD), f32),
            pltpu.VMEM((width, d), f32),
            pltpu.SemaphoreType.DMA((4 * heads + 8,)),
            pltpu.SemaphoreType.DMA((heads,)),
        ]
        + dma_sems(3 * heads)
        + dma_sems(6)
        + dma_sems(2 * nz - 2),
        compiler_params=remote_params(2),
        cost_estimate=pl.CostEstimate(
            flops=heads * 10 * 256 * 5767168 + 2 * GLEN * d * width,
            bytes_accessed=2 * GLEN * (3 * width + d),
            transcendentals=heads * 5767168,
        ),
        name="attend_back",
    )(
        lens, kept, gate, mask,
        *(x.reshape(heads, blocks, TQ, HD) for x in (q, k, v)),
        kt, ctx, g, lse, tokens_all, *parts,
    )


def meet(peers):
    barrier = pltpu.get_barrier_semaphore()
    for peer in peers:
        pl.semaphore_signal(barrier, inc=1, device_id=peer, device_id_type=pl.DeviceIdType.MESH)
    pl.semaphore_wait(barrier, len(peers))


def flip(index, bits):
    for bit in (1, 2):
        if bits & bit:
            index = index + bit - 2 * bit * ((index // bit) % 2)
    return index


def remote_params(number):
    return pltpu.CompilerParams(
        collective_id=number, has_side_effects=True, vmem_limit_bytes=56 * 2**20
    )


ANYWHERE = pl.BlockSpec(memory_space=pl.ANY)
IN_VMEM = pl.BlockSpec(memory_space=pltpu.VMEM)
IN_SMEM = pl.BlockSpec(memory_space=pltpu.SMEM)


def dma_sems(count):
    return [pltpu.SemaphoreType.DMA((count,)), pltpu.SemaphoreType.DMA((count,))]


def gather_kernel(
    n, tok_ref, weight_ref, exp_ref, tok_all, cols_all, exp_all, tok_buf, cols_buf, exp_buf,
    local_sem, s_tok, r_tok, s_w, r_w, s_f, r_f, s_e, r_e,
):
    s, w = lax.axis_index("seq"), lax.axis_index("wt")
    rows = tok_ref.shape[0]
    half = rows // 2
    wide = cols_buf.shape[1]
    for k in range(4):

        @pl.when(s == k)
        def _(k=k):
            cols_buf[...] = weight_ref[:, k * wide : (k + 1) * wide]

    by_x, by_y, mate = (flip(s, 1), w), (flip(s, 2), w), (s, flip(w, 1))
    far = [(s, lax.rem(w + 2 * j, n)) for j in range(1, n // 2)]
    quarter = exp_buf.shape[1]
    exp_own = exp_ref.at[:, pl.ds(pl.multiple_of(s * quarter, 128), quarter)]
    come = [
        pltpu.make_async_copy(tok_ref, tok_buf, local_sem.at[0]),
        pltpu.make_async_copy(exp_own, exp_buf, local_sem.at[2]),
    ]
    for copy in come:
        copy.start()
    meet([by_x, by_y, mate] + far)

    def part(owner, k):
        return pl.ds(pl.multiple_of(owner * rows + k * half, half), half)

    tok = (s_tok, r_tok)
    first = [pl.ds(0, half), pl.ds(half, half)]
    x0 = send(tok_ref.at[first[0]], tok_all.at[part(s, 0)], tok, 0, by_x)
    y1 = send(tok_ref.at[first[1]], tok_all.at[part(s, 1)], tok, 1, by_y)
    x1 = send(tok_ref.at[first[1]], tok_all.at[part(s, 1)], tok, 2, by_x)
    y0 = send(tok_ref.at[first[0]], tok_all.at[part(s, 0)], tok, 3, by_y)
    held = [
        send(cols_buf, cols_all.at[w], (s_w, r_w), k, peer) for k, peer in enumerate(far + [mate])
    ]
    along = [
        send(exp_own, exp_all.at[w // 2], (s_e, r_e), k, peer) for k, peer in enumerate(far)
    ]
    for copy in come:
        copy.wait()
    own = [
        pltpu.make_async_copy(exp_buf, exp_all.at[w // 2], local_sem.at[2]),
        pltpu.make_async_copy(
            tok_buf, tok_all.at[pl.ds(pl.multiple_of(s * rows, rows), rows)], local_sem.at[0]
        ),
        pltpu.make_async_copy(cols_buf, cols_all.at[w], local_sem.at[1]),
    ]
    for copy in own:
        copy.start()
    passed = []
    for j in range(1, n // 2):
        origin = lax.rem(w + n - 2 * j, n)
        held[j - 1].wait_recv()
        passed.append(send(cols_all.at[origin], cols_all.at[origin], (s_f, r_f), j - 1, mate))
    x0.wait_recv()
    there = tok_all.at[part(flip(s, 1), 0)]
    passed.append(send(there, there, tok, 4, by_y))
    y1.wait_recv()
    there = tok_all.at[part(flip(s, 2), 1)]
    passed.append(send(there, there, tok, 5, by_x))
    for copy in own:
        copy.wait()
    for copy in [x1, y0, held[-1]] + passed + along:
        copy.wait_recv()
    for copy in [x0, x1, y0, y1] + held + passed + along:
        copy.wait_send()


def gather_in(n, tokens, attention_weight, expand_weight):
    rows, d = tokens.shape
    own, width = attention_weight.shape
    quarter = expand_weight.shape[1] // 4
    return pl.pallas_call(
        functools.partial(gather_kernel, n),
        out_shape=(
            jax.ShapeDtypeStruct((4 * rows, d), bf16),
            jax.ShapeDtypeStruct((n, own, width // 4), bf16),
            jax.ShapeDtypeStruct((n // 2, own, quarter), bf16),
        ),
        in_specs=[ANYWHERE, IN_VMEM, ANYWHERE],
        out_specs=(ANYWHERE,) * 3,
        scratch_shapes=[
            pltpu.VMEM(tokens.shape, bf16),
            pltpu.VMEM((own, width // 4), bf16),
            pltpu.VMEM((own, quarter), bf16),
            pltpu.SemaphoreType.DMA((3,)),
        ]
        + dma_sems(6)
        + dma_sems(n // 2)
        + dma_sems(n // 2 - 1)
        + dma_sems(n // 2 - 1),
        compiler_params=remote_params(0),
        name="gather_in",
    )(tokens, attention_weight, expand_weight)


def final_kernel(
    heads, n, base_hbm, pieces_hbm, w_hbm, con_ref, att_ref, out_ref, exp_ref, vec_ref, late_ref,
    tok_hbm, g_con, g_out, g_exp, g_att, r_vec2, r_late2,
    tok_o, base_v, pieces_v, w_v, a_own, r_con, h_att, m_att, r_att, r_vec, r_late,
    l_in, *sems,
):
    s, w = lax.axis_index("seq"), lax.axis_index("wt")
    z, c = w // 2, lax.rem(w, 2)
    nz = n // 2
    others = [flip(s, k) for k in (1, 2, 3)]
    seq_peers = [(p, w) for p in others]
    mate = (s, flip(w, 1))
    wt_peers = [(s, lax.rem(w + j, n)) for j in range(1, n)]
    names = ("pair", "vec", "late", "con", "out2", "att", "vec2", "late2", "con2", "exp2", "att2")
    sem = {name: (sems[2 * k], sems[2 * k + 1]) for k, name in enumerate(names)}
    loads = [
        pltpu.make_async_copy(src, dst, l_in.at[k])
        for k, (src, dst) in enumerate(((pieces_hbm, pieces_v), (w_hbm, w_v), (base_hbm, base_v)))
    ]
    first = [pltpu.make_async_copy(con_ref.at[s], r_con.at[s], l_in.at[3])] + [
        pltpu.make_async_copy(att_ref.at[2 * k + c], a_own.at[k], l_in.at[4 + k]) for k in range(nz)
    ]
    for copy in first + loads:
        copy.start()
    meet(seq_peers + wt_peers)
    pair = [send(att_ref.at[2 * k + 1 - c], h_att.at[k], sem["pair"], k, mate) for k in range(nz)]
    cons = [send(con_ref.at[p], r_con.at[s], sem["con"], k, (p, w)) for k, p in enumerate(others)]
    far = [lax.rem(z + j, nz) for j in range(1, nz)]
    exp2 = [send(exp_ref, g_exp.at[s], sem["exp2"], k, p) for k, p in enumerate(seq_peers)]
    out2 = [send(out_ref, g_out.at[s], sem["out2"], k, p) for k, p in enumerate(seq_peers)]
    vecs = [
        send(vec_ref.at[lax.rem(w + j, n)], r_vec.at[w], sem["vec"], j - 1, wt_peers[j - 1])
        for j in range(1, n)
    ]
    lates = [send(late_ref, r_late.at[w], sem["late"], j, p) for j, p in enumerate(wt_peers)]
    g_exp[s] = exp_ref[...]
    r_vec[w] = vec_ref[w]
    r_late[w] = late_ref[...]
    g_out[s] = out_ref[...]
    for copy in first:
        copy.wait()
    for copy in pair:
        copy.wait_recv()
    for k in range(nz):
        m_att[k] = (a_own[k].astype(f32) + h_att[k].astype(f32)).astype(bf16)
    atts = [send(m_att.at[k], r_att.at[z], sem["att"], j, (s, 2 * k + c)) for j, k in enumerate(far)]
    r_att[z] = m_att[z]
    for copy in loads:
        copy.wait()
    cols = 3 * HD
    rows = tok_o.shape[0]
    block = rows // 3

    def total_of(ref, count):
        total = ref[0].astype(f32)
        for k in range(1, count):
            total = total + ref[k].astype(f32)
        return total

    own = [ref.at[s] for ref in (g_con, r_vec2, r_late2, g_att)]
    con2, vec2, late2, att2 = (
        [remote(ref, ref, sem[name], k, p) for k, p in enumerate(seq_peers)]
        for ref, name in zip(own, ("con2", "vec2", "late2", "att2"), strict=True)
    )

    def given(i):
        there = pl.ds(pl.multiple_of(i * block, block), block)
        return pltpu.make_async_copy(tok_o.at[there], tok_hbm.at[there], l_in.at[4 + nz + i])

    def tokens_block(i, carry):
        there = pl.ds(pl.multiple_of(i * block, block), block)
        total = base_v[there, :]
        for h in range(heads):
            for k in range(4):
                at = (heads * k + h) * cols
                total = total + mm(pieces_v[h, k, :, there].T, w_v[:, at : at + cols], NT)
        tok_o[there, :] = total
        given(i).start()

        @pl.when(i == 0)
        def _():
            for copy in cons:
                copy.wait_recv()
            g_con[s] = total_of(r_con, 4).astype(bf16)
            for copy in con2:
                copy.start()
            for copy in vecs + lates:
                copy.wait_recv()
            r_vec2[s] = total_of(r_vec, n)
            r_late2[s] = total_of(r_late, n)
            for copy in vec2 + late2:
                copy.start()

        @pl.when(i == 1)
        def _():
            for copy in atts:
                copy.wait_recv()
            g_att[s] = total_of(r_att, nz).astype(bf16)
            for copy in att2:
                copy.start()

        return carry

    lax.fori_loop(0, 3, tokens_block, 0)
    for i in range(3):
        given(i).wait()
    for copy in out2 + con2 + vec2 + late2 + exp2 + att2:
        copy.wait_recv()
    for copy in pair + cons + vecs + lates + atts + con2 + vec2 + late2 + exp2 + out2 + att2:
        copy.wait_send()


def final(n, base, pieces, weight, con, att, out, exp_part, vec, late):
    heads = pieces.shape[0]
    r, d = con.shape[1:]
    cols = att.shape[2]
    nz = n // 2
    counts = (nz, n - 1, n - 1, 3, 3, nz - 1, 3, 3, 3, 3, 3)
    return pl.pallas_call(
        functools.partial(final_kernel, heads, n),
        out_shape=(
            jax.ShapeDtypeStruct(base.shape, f32),
            jax.ShapeDtypeStruct((4, r, d), bf16),
            jax.ShapeDtypeStruct((4,) + out.shape, bf16),
            jax.ShapeDtypeStruct((4,) + exp_part.shape, bf16),
            jax.ShapeDtypeStruct((4, r, cols), bf16),
            jax.ShapeDtypeStruct((4,) + vec.shape[1:], f32),
            jax.ShapeDtypeStruct((4,) + late.shape, f32),
        ),
        in_specs=[ANYWHERE] * 5 + [IN_VMEM] * 4,
        out_specs=(ANYWHERE,) + (IN_VMEM,) * 6,
        scratch_shapes=[
            pltpu.VMEM(base.shape, f32),
            pltpu.VMEM(base.shape, f32),
            pltpu.VMEM(pieces.shape, bf16),
            pltpu.VMEM(weight.shape, bf16),
            pltpu.VMEM((nz, r, cols), bf16),
            pltpu.VMEM((4, r, d), bf16),
            pltpu.VMEM((nz, r, cols), bf16),
            pltpu.VMEM((nz, r, cols), bf16),
            pltpu.VMEM((nz, r, cols), bf16),
            pltpu.VMEM((n,) + vec.shape[1:], f32),
            pltpu.VMEM((n,) + late.shape, f32),
            pltpu.SemaphoreType.DMA((7 + nz,)),
        ]
        + [sem for count in counts for sem in dma_sems(count)],
        compiler_params=remote_params(3),
        cost_estimate=pl.CostEstimate(
            flops=8 * base.shape[0] * d * cols, bytes_accessed=8 * d * cols, transcendentals=0
        ),
        name="final",
    )(base, pieces, weight, con, att, out, exp_part, vec, late)


def finish_kernel(n, heads, gate_ref, mask_ref, *refs):
    sources, rest = refs[:8], refs[8:]
    con_o, exp_o, att_o, tok_o, low_o, out_o = rest[:6]
    vec_os, unit_os, query_o, value_o, gate_o = rest[6:13], rest[13:15], rest[15], rest[16], rest[17]
    con_v, exp_v, att_v, tok_v, low_v, out_v, vec_v, late_v, con_f, exp_f, att_f, l_in, l_out = rest[18:]
    inside = (con_v, exp_v, att_v, tok_v, low_v, out_v, vec_v, late_v)
    loads = [
        pltpu.make_async_copy(src, dst, l_in.at[k])
        for k, (src, dst) in enumerate(zip(sources, inside, strict=True))
    ]
    for k in (3, 4, 0, 1, 2, 5, 6, 7):
        loads[k].start()
    outside = ((con_f, con_o), (exp_f, exp_o), (att_f, att_o), (tok_v, tok_o), (low_v, low_o))
    stores = [pltpu.make_async_copy(src, dst, l_out.at[k]) for k, (src, dst) in enumerate(outside)]

    def add4(parts):
        return (parts[0] + parts[1]) + (parts[2] + parts[3])

    wide, cols, part = exp_v.shape[2], att_v.shape[2], out_v.shape[2]
    for k in (3, 4):
        loads[k].wait()
        stores[k].start()
    loads[0].wait()
    con_f[...] = con_v[...].astype(f32)
    stores[0].start()
    loads[1].wait()
    for k in range(4):
        exp_f[:, k * wide : (k + 1) * wide] = exp_v[k].astype(f32)
    stores[1].start()
    loads[2].wait()
    for k in range(4):
        att_f[:, k * cols : (k + 1) * cols] = att_v[k].astype(f32)
    stores[2].start()
    for copy in loads[5:]:
        copy.wait()
    for k in range(4):
        out_o[:, k * part : (k + 1) * part] = out_v[k].astype(f32)
    vec = add4([vec_v[k] for k in range(4)])
    own = vec_os[0].shape[0]
    for k, ref in enumerate(vec_os):
        ref[...] = vec[k, 0:own]
    for k, ref in enumerate(unit_os):
        ref[...] = vec[8 + k]
    rows = [jnp.concatenate([late_v[k, j : j + 1, :] for k in range(4)], axis=1) for j in range(2)]
    for k in range(n):

        @pl.when(lax.axis_index("wt") == k)
        def _(k=k):
            query_o[...] = rows[0][0, k * own : (k + 1) * own]
            value_o[...] = rows[1][0, k * own : (k + 1) * own]

    gates = []
    for k in range(4):
        for h in range(heads):
            part_sum = jnp.sum(late_v[k, 2:3, HD * h : HD * (h + 1)], axis=1, keepdims=True)
            kept = mask_ref[heads * k + h].astype(f32) / gate_ref[heads * k + h]
            gates.append(part_sum * kept)
    gate_o[...] = jnp.concatenate(gates, axis=1)[0]
    for copy in stores:
        copy.wait()


def finish(n, heads, gate, mask, con, exp_all, att, tok, low, out, vec, late):
    r = out.shape[1]
    wide, cols, part = exp_all.shape[2], att.shape[2], out.shape[2]
    units = vec.shape[2]
    row = jax.ShapeDtypeStruct((r,), f32)
    con_f, exp_f, att_f = (
        con.shape,
        (r, 4 * wide),
        (r, 4 * cols),
    )
    return pl.pallas_call(
        functools.partial(finish_kernel, n, heads),
        out_shape=(
            jax.ShapeDtypeStruct(con_f, f32),
            jax.ShapeDtypeStruct(exp_f, f32),
            jax.ShapeDtypeStruct(att_f, f32),
            jax.ShapeDtypeStruct(tok.shape, f32),
            jax.ShapeDtypeStruct(low.shape, low.dtype),
            jax.ShapeDtypeStruct((r, 4 * part), f32),
        )
        + (row,) * 7
        + (jax.ShapeDtypeStruct((units,), f32),) * 2
        + (row,) * 2
        + (jax.ShapeDtypeStruct((4 * heads,), f32),),
        in_specs=[IN_SMEM] * 2 + [ANYWHERE] * 8,
        out_specs=(ANYWHERE,) * 5 + (IN_VMEM,) * 13,
        scratch_shapes=[
            pltpu.VMEM(x.shape, x.dtype) for x in (con, exp_all, att, tok, low, out, vec, late)
        ]
        + [pltpu.VMEM(x, f32) for x in (con_f, exp_f, att_f)]
        + [pltpu.SemaphoreType.DMA((8,)), pltpu.SemaphoreType.DMA((5,))],
        compiler_params=pltpu.CompilerParams(vmem_limit_bytes=56 * 2**20),
        name="finish",
    )(gate, mask, con, exp_all, att, tok, low, out, vec, late)


(OUT_BIAS, GAIN1, SHIFT1, HIDDEN_SCALE, CON_BIAS, GAIN2, SHIFT2, HIDDEN_MASK) = range(8)
(S_OUT_BIAS, S_GAIN1, S_SHIFT1, S_CON_BIAS, S_GAIN2, S_SHIFT2, S_HIDDEN) = range(7)


def gelu_parts(x):
    bell = jnp.exp(-0.5 * (x * x))
    t = 1.0 / (1.0 + (0.3275911 * root_half) * jnp.abs(x))
    poly = t * (
        0.127414796 + t * (-0.142248368 + t * (0.7107068705 + t * (-0.7265760135 + t * 0.5307027145)))
    )
    tail = poly * bell
    cumulative = jnp.where(x < 0.0, tail, 1.0 - tail)
    return x * cumulative, cumulative + x * bell * density_scale


def norm_parts(summed):
    centre = summed - jnp.mean(summed, axis=-1, keepdims=True)
    inverse = lax.rsqrt(jnp.mean(centre * centre, axis=-1, keepdims=True) + epsilon)
    return (centre * inverse, inverse)


def norm_back(grad_normed, normed, inverse):
    return inverse * (
        grad_normed
        - jnp.mean(grad_normed, axis=-1, keepdims=True)
        - normed * jnp.mean(grad_normed * normed, axis=-1, keepdims=True)
    )


def feed_forward_kernel(
    steps, chunk,
    kept_ref, ctx_ref, tok_ref, cot_ref, wo_ref, we_hbm, wc_hbm,
    ob_ref, g1_ref, t1_ref, hg_ref, hm_ref, cb_ref, g2_ref, t2_ref, eb_ref, ug_ref, um_ref,
    lo_ref, dt1_ref, g_all, vec_ref, dwc_hbm, e_own, e_got, o_own, o_got,
    we_ref, wc_ref, dwc_ref, dwe_ref, dwo_ref, g_sc,
    wide_ref, unit_ref, sw_ref, su_ref, act_sc, gh_sc, low_sc, gb_sc, ga_sc, ctx_sc, gelu_sc, slope_sc,
    l_w, l_o, l_g, s_g, r_g, s_p, r_p,
):
    i = pl.program_id(0)
    block = tok_ref.shape[0]
    units = we_ref.shape[1]
    rows = pl.ds(pl.multiple_of(i * block, block), block)
    s, w = lax.axis_index("seq"), lax.axis_index("wt")
    others = [flip(s, k) for k in (1, 2, 3)]
    mate, core = (s, flip(w, 1)), lax.rem(w, 2)
    part_rows = g_all.shape[0]
    weights = [
        pltpu.make_async_copy(we_hbm, we_ref, l_w.at[0]),
        pltpu.make_async_copy(wc_hbm, wc_ref, l_w.at[1]),
    ]

    def leaving(t):
        there = g_all.at[:, pl.ds(pl.multiple_of((s * steps + t) * block, 128), block)]

        def part(p):
            lanes = pl.ds(pl.multiple_of(t * block, 128), block)
            return g_sc.at[pl.ds(pl.multiple_of(p * part_rows, 16), part_rows), lanes]

        copies = [
            remote(part(p), there, (s_g, r_g), 3 * t + k, (p, w)) for k, p in enumerate(others)
        ]
        return copies + [pltpu.make_async_copy(part(s), there, l_g.at[t])]

    @pl.when(i == 0)
    def _():
        for copy in weights:
            copy.start()
        meet([(p, w) for p in others] + [mate])
        sw_ref[...] = jnp.zeros_like(sw_ref)
        su_ref[...] = jnp.zeros_like(su_ref)

        def row(ref):
            return ref[...].astype(f32).reshape(1, ref.shape[0])

        plain = ((OUT_BIAS, ob_ref), (GAIN1, g1_ref), (SHIFT1, t1_ref), (CON_BIAS, cb_ref))
        for k, ref in plain + ((GAIN2, g2_ref), (SHIFT2, t2_ref), (HIDDEN_MASK, hm_ref)):
            wide_ref[k : k + 1, :] = row(ref)
        wide_ref[HIDDEN_SCALE : HIDDEN_SCALE + 1, :] = row(hm_ref) * row(hg_ref)
        kept = row(um_ref) * kept_ref[lax.axis_index("wt")].astype(f32)
        unit_ref[0:1, :] = row(eb_ref)
        unit_ref[1:2, :] = kept * row(ug_ref)
        unit_ref[2:3, :] = kept

    def wide(k):
        return wide_ref[k : k + 1, :]

    def add_sum(ref, k, cols, value):
        ref[k : k + 1, cols] += jnp.sum(value, axis=0, keepdims=True)

    full = slice(None)
    ctx = ctx_ref[...]
    ctx_sc[:, rows] = ctx
    summed = mm(ctx, wo_ref[...], TN) + wide(OUT_BIAS) + tok_ref[...].astype(f32)
    n1, inv1 = norm_parts(summed)
    s1 = n1 * wide(GAIN1) + wide(SHIFT1)
    hs = wide(HIDDEN_SCALE)
    first = s1 * hs
    low = first.astype(bf16)
    low_sc[rows, :] = low
    branch = first + wide(CON_BIAS)

    @pl.when(i == 0)
    def _():
        for copy in weights:
            copy.wait()

    for j in range(units // chunk):
        cols = slice(j * chunk, (j + 1) * chunk)
        hidden = mm(low, we_ref[:, cols]) + unit_ref[0:1, cols]
        gelu, slope = gelu_parts(hidden)
        scale = unit_ref[1:2, cols]
        gelu_sc[:, cols] = gelu.astype(gelu_sc.dtype)
        slope_sc[:, cols] = (slope * scale).astype(slope_sc.dtype)
        act = (gelu * scale).astype(bf16)
        act_sc[rows, cols] = act
        branch = branch + mm(act, wc_ref[cols, :])
    n2, inv2 = norm_parts(branch)
    s2 = n2 * wide(GAIN2) + wide(SHIFT2)
    lo_ref[...] = (s2 * hs).astype(bf16)
    dy = cot_ref[...].astype(f32)
    e2 = dy * hs
    add_sum(sw_ref, S_GAIN2, full, e2 * n2)
    add_sum(sw_ref, S_SHIFT2, full, e2)
    dt2 = norm_back(e2 * wide(GAIN2), n2, inv2)
    gb = dt2.astype(bf16)
    gb_sc[rows, :] = gb
    add_sum(sw_ref, S_CON_BIAS, full, gb.astype(f32))
    d_first = dt2
    for j in range(units // chunk):
        cols = slice(j * chunk, (j + 1) * chunk)
        d_act = mm(gb, wc_ref[cols, :], NT)
        add_sum(su_ref, 1, cols, d_act * gelu_sc[:, cols].astype(f32))
        gh = d_act * slope_sc[:, cols].astype(f32)
        add_sum(su_ref, 0, cols, gh)
        gh = gh.astype(bf16)
        gh_sc[rows, cols] = gh
        d_first = d_first + mm(gh, we_ref[:, cols], NT)
    e1 = d_first * hs
    add_sum(sw_ref, S_GAIN1, full, e1 * n1)
    add_sum(sw_ref, S_SHIFT1, full, e1)
    add_sum(sw_ref, S_HIDDEN, full, dy * s2 + d_first * s1)
    dt1 = norm_back(e1 * wide(GAIN1), n1, inv1)
    dt1_ref[...] = dt1
    ga = dt1.astype(bf16)
    ga_sc[rows, :] = ga
    add_sum(sw_ref, S_OUT_BIAS, full, ga.astype(f32))
    g_sc[:, rows] = mm(wo_ref[...], ga, NT).astype(bf16)
    for copy in leaving(i):
        copy.start()

    @pl.when(i == steps - 1)
    def _():
        own, wide_cols = dwe_ref.shape[3:]

        def weight_grads(j, carry):
            cols = pl.ds(pl.multiple_of(j * wide_cols, 128), wide_cols)
            dwc_ref[cols, :] = mm(act_sc[:, cols], gb_sc[...], TN).astype(bf16)
            part = mm(low_sc[...], gh_sc[:, cols], TN).astype(bf16)
            for k in range(2 * dwe_ref.shape[2]):
                dwe_ref[k % 2, j, k // 2] = part[k * own : (k + 1) * own]
            for copy in given(j):
                copy.start()
            return carry

        def given(j):
            there = pl.ds(pl.multiple_of(j * wide_cols, 128), wide_cols)
            return [
                pltpu.make_async_copy(dwc_ref.at[there], dwc_hbm.at[there], l_o.at[j]),
                pltpu.make_async_copy(dwe_ref.at[core, j], e_own.at[j], l_o.at[4 + j]),
                remote(dwe_ref.at[1 - core, j], e_got.at[j], (s_p, r_p), j, mate),
            ]

        part_cols = dwo_ref.shape[4]
        for q in range(4):
            part = mm(ctx_sc[...], ga_sc[:, q * part_cols : (q + 1) * part_cols]).astype(bf16)
            for k in range(2 * dwo_ref.shape[2]):
                dwo_ref[k % 2, q, k // 2] = part[k * own : (k + 1) * own]
        over = [
            pltpu.make_async_copy(dwo_ref.at[core], o_own, l_o.at[8]),
            remote(dwo_ref.at[1 - core], o_got, (s_p, r_p), 4, mate),
        ]
        for copy in over:
            copy.start()
        lax.fori_loop(0, 4, weight_grads, 0)
        vec_ref[...] = jnp.zeros_like(vec_ref)
        sw_ref[S_HIDDEN : S_HIDDEN + 1, :] *= wide(HIDDEN_MASK)
        su_ref[1:2, :] *= unit_ref[2:3, :]
        own_wide, own_units = dwe_ref.shape[3], vec_ref.shape[2]
        for k in range(vec_ref.shape[0]):
            vec_ref[k, 0:8, 0:own_wide] = sw_ref[:, k * own_wide : (k + 1) * own_wide]
            vec_ref[k, 8:16, :] = su_ref[:, k * own_units : (k + 1) * own_units]
        for t in range(steps):
            for copy in leaving(t):
                copy.wait()
        for copy in over:
            copy.wait()
        for j in range(4):
            for copy in given(j):
                copy.wait()


def feed_forward(n, kept, ctx_t, tokens, cotangent, wo, we, wc, *vectors):
    steps, chunk, keep = 3, 768, f32
    rows, d = tokens.shape
    units = we.shape[1]
    block = rows // steps
    halves = (2, 4, n // 2, d // n, units // 4)
    out_halves = (2, 4, n // 2, d // n, d // 4)
    tile = pl.BlockSpec((block, d), lambda i: (i, 0))
    lanes = pl.BlockSpec((d, block), lambda i: (0, i))

    def once(shape):
        return pl.BlockSpec(shape, lambda i: (0, 0), pipeline_mode=pl.Buffered(1))

    def once3(shape):
        return pl.BlockSpec(shape, lambda i: (0, 0, 0), pipeline_mode=pl.Buffered(1))

    return pl.pallas_call(
        functools.partial(feed_forward_kernel, steps, chunk),
        out_shape=(
            jax.ShapeDtypeStruct((rows, d), bf16),
            jax.ShapeDtypeStruct((rows, d), f32),
            jax.ShapeDtypeStruct((d // 4, 4 * rows), bf16),
            jax.ShapeDtypeStruct((n, 16, units // n), f32),
            jax.ShapeDtypeStruct((units, d), bf16),
            jax.ShapeDtypeStruct(halves[1:], bf16),
            jax.ShapeDtypeStruct(halves[1:], bf16),
            jax.ShapeDtypeStruct(out_halves[1:], bf16),
            jax.ShapeDtypeStruct(out_halves[1:], bf16),
        ),
        grid=(steps,),
        in_specs=[
            pl.BlockSpec(memory_space=pltpu.SMEM),
            lanes, tile, tile, once((d, d)), ANYWHERE, ANYWHERE,
        ]
        + [IN_VMEM] * len(vectors),
        out_specs=(
            tile, tile, ANYWHERE, once3((n, 16, units // n)), ANYWHERE,
            ANYWHERE, ANYWHERE, ANYWHERE, ANYWHERE,
        ),
        scratch_shapes=[
            pltpu.VMEM((d, units), bf16),
            pltpu.VMEM((units, d), bf16),
            pltpu.VMEM((units, d), bf16),
            pltpu.VMEM(halves, bf16),
            pltpu.VMEM(out_halves, bf16),
            pltpu.VMEM((d, rows), bf16),
            pltpu.VMEM((8, d), f32),
            pltpu.VMEM((8, units), f32),
            pltpu.VMEM((8, d), f32),
            pltpu.VMEM((8, units), f32),
            pltpu.VMEM((rows, units), bf16),
            pltpu.VMEM((rows, units), bf16),
            pltpu.VMEM((rows, d), bf16),
            pltpu.VMEM((rows, d), bf16),
            pltpu.VMEM((rows, d), bf16),
            pltpu.VMEM((d, rows), bf16),
            pltpu.VMEM((block, units), keep),
            pltpu.VMEM((block, units), keep),
            pltpu.SemaphoreType.DMA((2,)),
            pltpu.SemaphoreType.DMA((9,)),
            pltpu.SemaphoreType.DMA((steps,)),
        ]
        + dma_sems(3 * steps)
        + dma_sems(5),
        compiler_params=pltpu.CompilerParams(
            collective_id=4, has_side_effects=True, vmem_limit_bytes=62 * 2**20
        ),
        cost_estimate=pl.CostEstimate(
            flops=rows * d * (12 * units + 6 * d),
            bytes_accessed=4 * d * (4 * units + 2 * d) + 12 * rows * d,
            transcendentals=2 * rows * units,
        ),
        name="feed_forward",
    )(kept, ctx_t, tokens, cotangent, wo, we, wc, *vectors)


def local(
    tokens,
    output_cotangent,
    attention_weight,
    query_bias,
    value_bias,
    output_weight,
    output_bias,
    first_gain,
    first_shift,
    expand_weight,
    expand_bias,
    contract_weight,
    contract_bias,
    second_gain,
    second_shift,
    head_gate,
    hidden_gate,
    unit_gate,
    head_mask,
    hidden_mask,
    unit_mask,
    attention_mask,
    feedforward_mask,
    continuation_lengths,
):
    seq_count = lax.axis_size("seq")
    wt_count = lax.axis_size("wt")
    model_width = hidden_gate.shape[0]
    local_heads = head_gate.shape[0] // seq_count
    own_wide = model_width // wt_count
    tokens_all, own_weight, exp_quarter = gather_in(wt_count, tokens, attention_weight, expand_weight)
    contract_weight, own_weight = lax.optimization_barrier((contract_weight, own_weight))
    full_contract = lax.all_gather(contract_weight, "wt", axis=0, tiled=True)
    full_attention = lax.all_gather(attention_weight, "wt", axis=0, tiled=True)
    full_output = lax.all_gather(output_weight, "wt", axis=0, tiled=True)
    q, k, v, kt, own_context, log_sums, context_t, full_expand = attend(
        wt_count,
        continuation_lengths,
        attention_mask,
        head_gate,
        head_mask,
        query_bias,
        value_bias,
        tokens_all,
        own_weight.reshape(model_width, -1),
        exp_quarter,
        local_heads,
    )
    (
        layer_output,
        grad_total_one,
        grad_context_t,
        vec_sums,
        contract_weight_grad,
        *parts,
    ) = feed_forward(
        wt_count,
        feedforward_mask,
        context_t,
        tokens,
        output_cotangent,
        full_output,
        full_expand.reshape(model_width, -1),
        full_contract,
        output_bias,
        first_gain,
        first_shift,
        hidden_gate,
        hidden_mask,
        contract_bias,
        second_gain,
        second_shift,
        expand_bias,
        unit_gate,
        unit_mask,
    )
    con_piece = lax.psum_scatter(contract_weight_grad, "wt", scatter_dimension=0, tiled=True)
    pieces, projection_grad, exp_part, out_part, late_sums = attend_back(
        wt_count,
        continuation_lengths,
        attention_mask,
        head_gate,
        head_mask,
        q,
        k,
        v,
        kt,
        own_context,
        grad_context_t,
        log_sums,
        tokens_all,
        *parts,
    )
    tokens_grad, con_all, out_all, exp_all, att_all, vec_all, late_all = final(
        wt_count,
        grad_total_one,
        pieces,
        full_attention,
        con_piece.reshape(seq_count, own_wide, model_width),
        projection_grad,
        out_part,
        exp_part,
        vec_sums,
        late_sums,
    )
    con_sum, exp_sum, att_sum, tokens_grad, layer_output, out_sum, *rows = finish(
        wt_count,
        local_heads,
        head_gate,
        head_mask,
        con_all,
        exp_all,
        att_all,
        tokens_grad,
        layer_output,
        out_all,
        vec_all,
        late_all,
    )
    return (
        layer_output,
        tokens_grad,
        att_sum,
        rows[9],
        rows[10],
        out_sum,
        rows[S_OUT_BIAS],
        rows[S_GAIN1],
        rows[S_SHIFT1],
        exp_sum,
        rows[7],
        con_sum.reshape(seq_count * own_wide, model_width),
        rows[S_CON_BIAS],
        rows[S_GAIN2],
        rows[S_SHIFT2],
        rows[11],
        rows[S_HIDDEN],
        rows[8],
    )


def solution(mesh):
    return jax.shard_map(
        local,
        mesh=mesh,
        in_specs=(
            P(("wt", "seq"), None),
            P(("wt", "seq"), None),
            P("wt", None),
            P(),
            P(),
            P("wt", None),
            P(),
            P(),
            P(),
            P("wt", None),
            P(),
            P("wt", None),
            P(),
            P(),
            P(),
            P(),
            P(),
            P(),
            P(),
            P(),
            P(),
            P(),
            P(),
            P(),
        ),
        out_specs=(
            P(("wt", "seq"), None),
            P(("wt", "seq"), None),
            P("wt", None),
            P("wt"),
            P("wt"),
            P("wt", None),
            P("wt"),
            P("wt"),
            P("wt"),
            P("wt", None),
            P("wt"),
            P("wt", None),
            P("wt"),
            P("wt"),
            P("wt"),
            P(),
            P("wt"),
            P("wt"),
        ),
        check_vma=False,
    )
```
